32 devices in a mesh: dp: 8 (over y, x, core), head: 4 (over z).
Axes of the slice: x: 2, y: 2, z: 4, core: 2. Of those that a mesh axis runs over, the one named last changes fastest.
Arguments:
- tokens: bfloat16 [6400, 384], P(('dp', 'head')), may hold values from -6 to 6
- grad_out: bfloat16 [1600, 768], P(('dp', 'head')), may hold values from -6 to 6
- video_ids: int32 [16], replicated, may hold values from 0 to 3, never falling along the last dimension, each value on 1 to 8 neighbouring positions
- offsets: int32 [16, 2], P('dp'), may hold values from 0 to 7
- gain_one: float32 [384], replicated, may hold values from 0.25 to 1.75
- qkv_one: bfloat16 [384, 1152], P(None, 'head'), may hold values from -0.3125 to 0.3125
- pools_one: float32 [3, 27, 96], replicated, may hold values from -1.25 to 1.25
- memory_one: float32 [2, 4, 96], replicated, may hold values from -3 to 3
- table_one: float32 [4, 15], P('head'), may hold values from -6 to 6
- proj_one: bfloat16 [384, 384], P('head'), may hold values from -0.3125 to 0.3125
- gain_two: float32 [384], replicated, may hold values from 0.25 to 1.75
- up_one: bfloat16 [384, 1536], P(None, 'head'), may hold values from -0.3125 to 0.3125
- down_one: bfloat16 [1536, 384], P('head'), may hold values from -0.15625 to 0.15625
- gain_three: float32 [384], replicated, may hold values from 0.25 to 1.75
- qkv_two: bfloat16 [384, 2304], P(None, 'head'), may hold values from -0.3125 to 0.3125
- residual_two: bfloat16 [384, 768], replicated, may hold values from -0.3125 to 0.3125
- pools_two: float32 [3, 27, 96], replicated, may hold values from -1.25 to 1.25
- memory_two: float32 [2, 4, 96], replicated, may hold values from -3 to 3
- table_two: float32 [8, 15], P('head'), may hold values from -6 to 6
- proj_two: bfloat16 [768, 768], P('head'), may hold values from -0.21875 to 0.21875
- gain_four: float32 [768], replicated, may hold values from 0.25 to 1.75
- up_two: bfloat16 [768, 3072], P(None, 'head'), may hold values from -0.21875 to 0.21875
- down_two: bfloat16 [3072, 768], P('head'), may hold values from -0.109375 to 0.109375
Outputs:
- blocks_out: bfloat16 [1600, 768], P(('dp', 'head'))
- grad_tokens: bfloat16 [6400, 384], P(('dp', 'head'))
- grad_gain_one: float32 [384], replicated
- grad_qkv_one: float32 [384, 1152], P(None, 'head')
- grad_pools_one: float32 [3, 27, 96], replicated
- grad_memory_one: float32 [2, 4, 96], replicated
- grad_table_one: float32 [4, 15], P('head')
- grad_proj_one: float32 [384, 384], P('head')
- grad_gain_two: float32 [384], replicated
- grad_up_one: float32 [384, 1536], P(None, 'head')
- grad_down_one: float32 [1536, 384], P('head')
- grad_gain_three: float32 [384], replicated
- grad_qkv_two: float32 [384, 2304], P(None, 'head')
- grad_residual_two: float32 [384, 768], replicated
- grad_pools_two: float32 [3, 27, 96], replicated
- grad_memory_two: float32 [2, 4, 96], replicated
- grad_table_two: float32 [8, 15], P('head')
- grad_proj_two: float32 [768, 768], P('head')
- grad_gain_four: float32 [768], replicated
- grad_up_two: float32 [768, 3072], P(None, 'head')
- grad_down_two: float32 [3072, 768], P('head')
The draws below stay inside these ranges and needn't reach their ends.
Inputs may be any that keep to these rules, and one draw needn't show every extreme that they name: video_ids never falls along the clips; each video has 1 to 8 consecutive clips.
All inputs are finite; a program needn't handle non-finite values.
Results may differ from the reference program's by a relative error of at most 0.04.
Values may be sent and summed in bfloat16 or wider, within the bound.
No kernel may reach another device: no remote copies, remote signals or barrier semaphores. Data moves between devices by JAX's collectives and lax.ppermute only.
A program may use at most 256 MiB of HBM per device.

```python
import math
import jax
import jax.numpy as jnp
import numpy as np
from jax import lax

D1 = 384
D2 = 768
HD = 96
HA = 4
HB = 8
FA = 1536
FB = 3072
FR = 4
SIDE = 10
NOFF = 8
CLIPS = 16
VIDEOS = 4
TOK_CLIP = 400
LP = 100
NBIN = 15


def set_ends(entries, key, low, high):
    spot = [jax.random.randint(jax.random.fold_in(key, axis), (), 0, length) for axis, length in enumerate(entries.shape)]
    main_axis = entries.shape.index(max(entries.shape))
    next_to = spot[:main_axis] + [(spot[main_axis] + 1) % entries.shape[main_axis]] + spot[main_axis + 1:]
    return entries.at[tuple(spot)].set(low).at[tuple(next_to)].set(high)


def level_of(rng, extent, cuts, least, high):
    def one(dim, blocks):
        draws = jax.random.uniform(jax.random.fold_in(jax.random.fold_in(rng, 6), dim), (blocks,), jnp.float32, least / len(cuts), high / len(cuts))
        return jnp.repeat(jnp.exp(draws), extent[dim] // blocks).reshape((-1,) + (1,) * (len(extent) - dim - 1))

    level = one(*cuts[0])
    for cut in cuts[1:]:
        level = level * one(*cut)
    return level


def profile(number_of, total, limit, skew):
    loads = [(1 << 20) // math.isqrt(standing ** skew) + 1 for standing in range(2, number_of + 1)]
    spare, given = total - limit - (number_of - 1), [1] * (number_of - 1)
    while spare > 0:
        candidates = [i for i in range(number_of - 1) if given[i] < limit]
        mass, budget = sum([loads[i] for i in candidates]), spare
        for i in candidates:
            addition = min(limit - given[i], max(1, budget * loads[i] // mass), spare)
            given[i] = given[i] + addition
            spare = spare - addition
    return np.array([limit] + given)


def uneven(key, amount, total, most, skew):
    if amount == 2:
        one = jax.random.randint(key, (), max(1, total - most), min(most, total - 1) + 1)
        return jnp.stack([one, total - one])
    sizes = jnp.asarray(profile(amount, total, most, skew), jnp.int32)
    twos = (amount - 1) // 2
    donor, taker = sizes[1:1 + 2 * twos:2], sizes[2:2 + 2 * twos:2]
    room = jnp.minimum(donor - 1, most - taker)
    moved = jax.random.randint(jax.random.fold_in(key, 1), (twos,), 0, 1 << 20) % (room + 1)
    sizes = sizes.at[1:1 + 2 * twos:2].set(donor - moved).at[2:2 + 2 * twos:2].set(taker + moved)
    return sizes[jax.random.permutation(jax.random.fold_in(key, 2), amount)]


def centred(own_key, shape, deviation, reach, cuts=(), held_as=jnp.bfloat16):
    entries = deviation * jax.random.normal(own_key, shape, jnp.float32)
    if cuts:
        entries = entries * level_of(own_key, shape, cuts, -0.22, 0.18)
    return jnp.clip(entries, -reach, reach).astype(held_as)


def setup_inputs(seed: int = 0) -> dict:
    key_list = jax.random.split(jax.random.key(seed), 24)
    tokens = centred(key_list[0], (CLIPS * TOK_CLIP, D1), 1.0, 6.0, ((0, 32),))
    grad_out = centred(key_list[1], (CLIPS * LP, D2), 1.0, 6.0, ((0, 32),))
    video_ids = jnp.searchsorted(jnp.cumsum(uneven(key_list[2], VIDEOS, CLIPS, 8, 0)), jnp.arange(CLIPS), side="right").astype(jnp.int32)
    offsets = set_ends(jax.random.randint(key_list[3], (CLIPS, 2), 0, NOFF), jax.random.fold_in(key_list[3], 1), 0, NOFF - 1).astype(jnp.int32)
    gain_one = jnp.clip(1.0 + 0.15 * jax.random.normal(key_list[4], (D1,), jnp.float32), 0.25, 1.75)
    qkv_one = centred(key_list[5], (D1, 3 * D1), D1 ** -0.5, 0.3125, ((1, 4),))
    pools_one = centred(key_list[6], (3, 27, HD), 0.2, 1.25, (), jnp.float32)
    memory_one = centred(key_list[7], (2, 4, HD), 0.5, 3.0, (), jnp.float32)
    table_one = centred(key_list[8], (HA, NBIN), 1.0, 6.0, ((0, 4),), jnp.float32)
    proj_one = centred(key_list[9], (D1, D1), D1 ** -0.5, 0.3125, ((0, 4),))
    gain_two = jnp.clip(1.0 + 0.15 * jax.random.normal(key_list[10], (D1,), jnp.float32), 0.25, 1.75)
    up_one = centred(key_list[11], (D1, FA), D1 ** -0.5, 0.3125, ((1, 4),))
    down_one = centred(key_list[12], (FA, D1), FA ** -0.5, 0.15625, ((0, 4),))
    gain_three = jnp.clip(1.0 + 0.15 * jax.random.normal(key_list[13], (D1,), jnp.float32), 0.25, 1.75)
    qkv_two = centred(key_list[14], (D1, 3 * D2), D1 ** -0.5, 0.3125, ((1, 4),))
    residual_two = centred(key_list[15], (D1, D2), D1 ** -0.5, 0.3125)
    pools_two = centred(key_list[16], (3, 27, HD), 0.2, 1.25, (), jnp.float32)
    memory_two = centred(key_list[17], (2, 4, HD), 0.5, 3.0, (), jnp.float32)
    table_two = centred(key_list[18], (HB, NBIN), 1.0, 6.0, ((0, 4),), jnp.float32)
    proj_two = centred(key_list[19], (D2, D2), D2 ** -0.5, 0.21875, ((0, 4),))
    gain_four = jnp.clip(1.0 + 0.15 * jax.random.normal(key_list[20], (D2,), jnp.float32), 0.25, 1.75)
    up_two = centred(key_list[21], (D2, FB), D2 ** -0.5, 0.21875, ((1, 4),))
    down_two = centred(key_list[22], (FB, D2), FB ** -0.5, 0.109375, ((0, 4),))
    return {"tokens": tokens, "grad_out": grad_out, "video_ids": video_ids, "offsets": offsets, "gain_one": gain_one, "qkv_one": qkv_one, "pools_one": pools_one, "memory_one": memory_one, "table_one": table_one, "proj_one": proj_one, "gain_two": gain_two, "up_one": up_one, "down_one": down_one, "gain_three": gain_three, "qkv_two": qkv_two, "residual_two": residual_two, "pools_two": pools_two, "memory_two": memory_two, "table_two": table_two, "proj_two": proj_two, "gain_four": gain_four, "up_two": up_two, "down_two": down_two}


HIGH = lax.Precision.HIGHEST
EPSILON = 1e-06
NEGATIVE = -1e+30

@jax.custom_vjp
def low(v):
    return lax.optimization_barrier(v.astype(jnp.bfloat16)).astype(jnp.float32)

@jax.custom_vjp
def low_back(v):
    return v

def low_keep(v):
    return (low(v), None)

def low_pass(kept, grad):
    return (grad,)

def back_keep(v):
    return (v, None)

def back_low(kept, grad):
    return (low(grad),)
low.defvjp(low_keep, low_pass)
low_back.defvjp(back_keep, back_low)

def layer_norm(values, gain):
    centered = values - lax.optimization_barrier(jnp.mean(values, axis=-1, keepdims=True))
    variance = lax.optimization_barrier(jnp.mean(centered * centered, axis=-1, keepdims=True))
    return centered * lax.rsqrt(variance + EPSILON) * gain

def pool_conv(fields, weight, stride):
    frames = fields.shape[1]
    side = fields.shape[2]
    padded = jnp.pad(fields, ((0, 0), (1, 1), (1, 1), (1, 1), (0, 0)))
    summed = jnp.zeros((fields.shape[0], frames, side // stride, side // stride, fields.shape[4]), jnp.float32)
    for time_tap in range(3):
        for row_tap in range(3):
            for col_tap in range(3):
                tap_number = 9 * time_tap + 3 * row_tap + col_tap
                window = padded[:, time_tap:time_tap + frames, row_tap:row_tap + side:stride, col_tap:col_tap + side:stride, :]
                summed = summed + window * weight[tap_number]
    return summed

def compress(fields, weight):
    clip_total = fields.shape[0]
    frames = fields.shape[1]
    side = fields.shape[2]
    grouped = fields.reshape(clip_total, frames // 4, 4, side * side, fields.shape[4])
    return lax.optimization_barrier(jnp.sum(grouped * weight[None, None, :, None, :], axis=2)).reshape(clip_total, frames // 4 * side * side, fields.shape[4])

def shape_fields(projected, pools, memory, head_count, stride, key_stride):
    columns = projected.reshape(-1, FR, SIDE, SIDE, head_count, 3, HD)
    clip_total = columns.shape[0]
    channels = head_count * HD

    def take_field(which):
        return columns[:, :, :, :, :, which, :].reshape(clip_total, FR, SIDE, SIDE, channels)

    def tiled(kernel):
        return jnp.tile(kernel, (1, head_count))
    query_pool = pool_conv(take_field(0), tiled(pools[0]), stride)
    key_pool = pool_conv(take_field(1), tiled(pools[1]), key_stride)
    value_pool = pool_conv(take_field(2), tiled(pools[2]), key_stride)
    key_memory = compress(key_pool, tiled(memory[0]))
    value_memory = compress(value_pool, tiled(memory[1]))
    return (query_pool.reshape(clip_total, -1, channels), key_pool.reshape(clip_total, -1, channels), value_pool.reshape(clip_total, -1, channels), key_memory, value_memory)

def relative_bias(table, pair, key_side):
    area = key_side * key_side
    quarter = FR // 4
    query_frame = lax.broadcasted_iota(jnp.int32, (FR, FR * area), 0)
    key_frame = lax.broadcasted_iota(jnp.int32, (FR, FR * area), 1) // area
    own_bins = query_frame - key_frame + FR - 1
    memory_frame = lax.broadcasted_iota(jnp.int32, (FR, quarter * area), 1) // area
    first_bins = 2 * FR - 1 + pair[0] * quarter + memory_frame
    second_bins = 2 * FR - 1 + pair[1] * quarter + memory_frame
    bin_index = jnp.concatenate([own_bins, first_bins, second_bins], 1)
    levels = lax.broadcasted_iota(jnp.int32, (1, 1, table.shape[1]), 2)
    onehot = (bin_index[:, :, None] == levels).astype(jnp.float32)
    return jnp.einsum('tkb,hb->htk', onehot, table, precision=HIGH)

def skip_pool(values):
    frames = values.shape[0] // (SIDE * SIDE)
    grid = values.reshape(frames, SIDE // 2, 2, SIDE // 2, 2, values.shape[1])
    return lax.optimization_barrier(jnp.mean(grid, axis=(2, 4))).reshape(frames * (SIDE // 2) * (SIDE // 2), values.shape[1])

def run_block(clips, weights, residual_weight, stride, key_stride, valid_one, valid_two, offsets):
    gain_first, qkv_weight, pools, memory, table, proj_weight, gain_second, up_weight, down_weight = weights
    head_count = qkv_weight.shape[1] // (3 * HD)
    clip_total = clips.shape[0]
    key_side = SIDE // key_stride
    own_count = FR * key_side * key_side
    memory_count = FR // 4 * key_side * key_side
    keep_rows = jnp.concatenate([jnp.ones((clip_total, own_count), jnp.bool_), jnp.broadcast_to(valid_one[:, None], (clip_total, memory_count)), jnp.broadcast_to(valid_two[:, None], (clip_total, memory_count))], 1)

    def front_part(one_clip):
        normed = low(layer_norm(one_clip, gain_first))
        projected = low_back(jnp.dot(normed, qkv_weight, precision=HIGH))
        query_pool, key_pool, value_pool, key_memory, value_memory = shape_fields(projected, pools, memory, head_count, stride, key_stride)
        if residual_weight is None:
            skip_path = one_clip
        else:
            skip_path = skip_pool(low_back(jnp.dot(normed, residual_weight, precision=HIGH)))
        return (query_pool[0], key_pool[0], value_pool[0], low(key_memory[0]), low(value_memory[0]), skip_path)
    query_pool, key_pool, value_pool, key_memory, value_memory, skip_path = lax.map(jax.checkpoint(front_part), clips)
    prior_key_one = jnp.concatenate([jnp.zeros_like(key_memory[:1]), key_memory[:-1]], 0)
    prior_value_one = jnp.concatenate([jnp.zeros_like(value_memory[:1]), value_memory[:-1]], 0)
    prior_key_two = jnp.concatenate([jnp.zeros_like(key_memory[:2]), key_memory[:-2]], 0)
    prior_value_two = jnp.concatenate([jnp.zeros_like(value_memory[:2]), value_memory[:-2]], 0)

    def back_part(inputs):
        query_field, key_field, value_field, key_one, value_one, key_two, value_two, keep, pair, skip_rows = inputs
        rows = query_field.shape[0]
        queries = low(query_field)
        keys_all = jnp.concatenate([low(key_field), key_one, key_two], 0)
        values_all = jnp.concatenate([low(value_field), value_one, value_two], 0)
        raw = jnp.einsum('ihd,jhd->hij', queries.reshape(rows, head_count, HD), keys_all.reshape(-1, head_count, HD), precision=HIGH) * HD ** (-0.5)
        raw = (raw.reshape(head_count, FR, rows // FR, -1) + relative_bias(table, pair, key_side)[:, :, None, :]).reshape(head_count, rows, -1)
        scores = jnp.where(keep[None, None, :], low_back(raw), NEGATIVE)
        probs = jax.nn.softmax(scores, axis=-1)
        mixture = jnp.einsum('hij,jhd->ihd', low(probs), values_all.reshape(-1, head_count, HD), precision=HIGH).reshape(rows, -1)
        attention = low_back(low(mixture + query_field))
        middle = skip_rows + low_back(jnp.dot(attention, proj_weight, precision=HIGH))
        normed_mlp = low(layer_norm(middle, gain_second))
        up_proj = low_back(jnp.dot(normed_mlp, up_weight, precision=HIGH))
        hidden = low(jax.nn.gelu(up_proj))
        return middle + low_back(jnp.dot(hidden, down_weight, precision=HIGH))
    return lax.map(jax.checkpoint(back_part), (query_pool, key_pool, value_pool, prior_key_one, prior_value_one, prior_key_two, prior_value_two, keep_rows, offsets, skip_path))

def reference(tokens, grad_out, video_ids, offsets, gain_one, qkv_one, pools_one, memory_one, table_one, proj_one, gain_two, up_one, down_one, gain_three, qkv_two, residual_two, pools_two, memory_two, table_two, proj_two, gain_four, up_two, down_two):
    padded = jnp.concatenate([jnp.full((2,), -1, jnp.int32), video_ids.astype(jnp.int32)])
    valid_one = padded[1:-1] == video_ids
    valid_two = padded[:-2] == video_ids
    params = tuple((item.astype(jnp.float32) for item in (gain_one, qkv_one, pools_one, memory_one, table_one, proj_one, gain_two, up_one, down_one, gain_three, qkv_two, residual_two, pools_two, memory_two, table_two, proj_two, gain_four, up_two, down_two)))

    def forward(stream, *weights):
        first = weights[0:9]
        second = (weights[9], weights[10], weights[12], weights[13], weights[14], weights[15], weights[16], weights[17], weights[18])
        clips = stream.reshape(CLIPS, TOK_CLIP, D1)
        middle = run_block(clips, first, None, 1, 2, valid_one, valid_two, offsets)
        final = run_block(middle, second, weights[11], 2, 1, valid_one, valid_two, offsets)
        return final.reshape(CLIPS * LP, D2)
    result, pull = jax.vjp(forward, tokens.astype(jnp.float32), *params)
    grads = pull(grad_out.astype(jnp.float32))
    return (result.astype(jnp.bfloat16), grads[0].astype(jnp.bfloat16), grads[1], grads[2], grads[3], grads[4], grads[5], grads[6], grads[7], grads[8], grads[9], grads[10], grads[11], grads[12], grads[13], grads[14], grads[15], grads[16], grads[17], grads[18], grads[19])
```

```python
import jax
import jax.numpy as jnp
from jax import lax
from jax.sharding import PartitionSpec as P

HD = 96
FR = 4
SIDE = 10


HIGH = lax.Precision.HIGHEST
EPSILON = 1e-06
NEGATIVE = -1e30


def passed_along(block, axis, distance):
    devices = range(lax.axis_size(axis))
    route = [(i - distance, i) for i in devices if i - distance in devices]
    return lax.ppermute(block, axis, route)


def layer_norm(values, gain):
    centered = values - jnp.mean(values, axis=-1, keepdims=True)
    variance = jnp.mean(centered * centered, axis=-1, keepdims=True)
    return centered * lax.rsqrt(variance + EPSILON) * gain


def pool_conv(fields, weight, stride):
    frames = fields.shape[1]
    side = fields.shape[2]
    padded = jnp.pad(fields, ((0, 0), (1, 1), (1, 1), (1, 1), (0, 0)))
    summed = jnp.zeros(fields.shape, jnp.float32)
    for time_tap in range(3):
        for row_tap in range(3):
            for col_tap in range(3):
                tap_number = 9 * time_tap + 3 * row_tap + col_tap
                window = padded[
                    :,
                    time_tap : time_tap + frames,
                    row_tap : row_tap + side,
                    col_tap : col_tap + side,
                    :,
                ]
                summed = summed + window * weight[tap_number]
    if stride > 1:
        small = side // stride
        grid = summed.reshape(
            fields.shape[0], frames, small, stride, small, stride, fields.shape[4]
        )
        summed = grid[:, :, :, 0, :, 0, :]
    return summed


def compress(fields, weight):
    clip_total = fields.shape[0]
    frames = fields.shape[1]
    side = fields.shape[2]
    grouped = fields.reshape(clip_total, frames // 4, 4, side * side, fields.shape[4])
    return jnp.sum(grouped * weight[None, None, :, None, :], axis=2).reshape(
        clip_total, frames // 4 * side * side, fields.shape[4]
    )


def shape_fields(projected, pools, memory, head_count, stride, key_stride):
    columns = projected.reshape(-1, FR, SIDE, SIDE, head_count, 3, HD)
    clip_total = columns.shape[0]
    channels = head_count * HD

    def take_field(which):
        return columns[:, :, :, :, :, which, :].reshape(clip_total, FR, SIDE, SIDE, channels)

    def tiled(kernel):
        return jnp.tile(kernel, (1, head_count))

    query_pool = pool_conv(take_field(0), tiled(pools[0]), stride)
    key_pool = pool_conv(take_field(1), tiled(pools[1]), key_stride)
    value_pool = pool_conv(take_field(2), tiled(pools[2]), key_stride)
    key_memory = compress(key_pool, tiled(memory[0]))
    value_memory = compress(value_pool, tiled(memory[1]))
    return (
        query_pool.reshape(clip_total, -1, channels),
        key_pool.reshape(clip_total, -1, channels),
        value_pool.reshape(clip_total, -1, channels),
        key_memory,
        value_memory,
    )


def relative_bias(table, pair, key_side):
    area = key_side * key_side
    quarter = FR // 4
    query_frame = lax.broadcasted_iota(jnp.int32, (FR, FR * area), 0)
    key_frame = lax.broadcasted_iota(jnp.int32, (FR, FR * area), 1) // area
    own_bins = query_frame - key_frame + FR - 1
    memory_frame = lax.broadcasted_iota(jnp.int32, (FR, quarter * area), 1) // area
    first_bins = 2 * FR - 1 + pair[0] * quarter + memory_frame
    second_bins = 2 * FR - 1 + pair[1] * quarter + memory_frame
    bin_index = jnp.concatenate([own_bins, first_bins, second_bins], 1)
    levels = lax.broadcasted_iota(jnp.int32, (1, 1, table.shape[1]), 2)
    onehot = (bin_index[:, :, None] == levels).astype(jnp.float32)
    return jnp.einsum("tkb,hb->htk", onehot, table, precision=HIGH)


def skip_pool(values):
    frames = values.shape[0] // (SIDE * SIDE)
    grid = values.reshape(frames, SIDE // 2, 2, SIDE // 2, 2, values.shape[1])
    return jnp.mean(grid, axis=(2, 4)).reshape(frames * (SIDE // 2) * (SIDE // 2), values.shape[1])


def spread(normed, weight):
    return jnp.dot(
        lax.all_gather(normed, "head", axis=0, tiled=True),
        weight,
        preferred_element_type=jnp.float32,
    )


def collect(values, weight):
    return lax.psum_scatter(
        jnp.dot(values, weight, preferred_element_type=jnp.float32).astype(jnp.bfloat16),
        "head",
        scatter_dimension=0,
        tiled=True,
    ).astype(jnp.float32)


def branch_back(grad_rows, kept, weight):
    piece = lax.all_gather(grad_rows, "head", axis=0, tiled=True)
    weight_sum = lax.dot_general(
        kept, piece, (((0,), (0,)), ((), ())), preferred_element_type=jnp.float32
    )
    rows_grad = lax.dot_general(
        piece, weight, (((1,), (1,)), ((), ())), preferred_element_type=jnp.float32
    )
    return (weight_sum, rows_grad)


def weight_grad(normed, grads):
    return lax.dot_general(
        lax.all_gather(normed, "head", axis=0, tiled=True),
        grads,
        (((0,), (0,)), ((), ())),
        preferred_element_type=jnp.float32,
    )


def input_grad(grads, weight):
    return lax.psum_scatter(
        lax.dot_general(
            grads, weight, (((1,), (1,)), ((), ())), preferred_element_type=jnp.float32
        ).astype(jnp.bfloat16),
        "head",
        scatter_dimension=0,
        tiled=True,
    ).astype(jnp.float32)


def scores_of(queries, keys_all, bias_grid, keep, head_count):
    rows = queries.shape[0]
    raw = jnp.einsum(
        "ihd,jhd->hij",
        queries.reshape(rows, head_count, HD),
        keys_all.reshape(-1, head_count, HD),
        preferred_element_type=jnp.float32,
    ) * HD ** (-0.5)
    raw = (raw.reshape(head_count, FR, rows // FR, -1) + bias_grid[:, :, None, :]).reshape(
        head_count, rows, -1
    )
    return jnp.where(keep[None, None, :], raw, NEGATIVE)


def attend(queries, keys_all, values_all, bias_grid, keep, head_count):
    rows = queries.shape[0]
    scores = scores_of(queries, keys_all, bias_grid, keep, head_count)
    top = jnp.max(scores, axis=-1, keepdims=True)
    weights = jnp.exp(scores - top)
    total = jnp.sum(weights, axis=-1, keepdims=True)
    probs = (weights / total).astype(jnp.bfloat16)
    mixture = jnp.einsum(
        "hij,jhd->ihd",
        probs,
        values_all.reshape(-1, head_count, HD),
        preferred_element_type=jnp.float32,
    )
    return (mixture.reshape(rows, -1), top + jnp.log(total))


def attend_back(queries, keys_all, values_all, bias_grid, keep, log_total, grad_mix, head_count):
    rows = queries.shape[0]
    scale = HD ** (-0.5)
    scores = scores_of(queries, keys_all, bias_grid, keep, head_count)
    probs = jnp.exp(scores - log_total)
    grad_heads = grad_mix.reshape(rows, head_count, HD)
    key_heads = keys_all.reshape(-1, head_count, HD)
    value_heads = values_all.reshape(-1, head_count, HD)
    query_heads = queries.reshape(rows, head_count, HD)
    grad_probs = jnp.einsum(
        "ihd,jhd->hij", grad_heads, value_heads, preferred_element_type=jnp.float32
    )
    inner = jnp.sum(grad_probs * probs, axis=-1, keepdims=True)
    grad_scores = (probs * (grad_probs - inner)).astype(jnp.bfloat16)
    query_grad = (
        jnp.einsum("hij,jhd->ihd", grad_scores, key_heads, preferred_element_type=jnp.float32)
        * scale
    )
    key_grad = (
        jnp.einsum("hij,ihd->jhd", grad_scores, query_heads, preferred_element_type=jnp.float32)
        * scale
    )
    value_grad = jnp.einsum(
        "hij,ihd->jhd", probs.astype(jnp.bfloat16), grad_heads, preferred_element_type=jnp.float32
    )
    bias_grad = jnp.sum(
        grad_scores.astype(jnp.float32).reshape(head_count, FR, rows // FR, -1), axis=2
    )
    return (
        query_grad.reshape(rows, -1),
        key_grad.reshape(key_heads.shape[0], -1),
        value_grad.reshape(value_heads.shape[0], -1),
        bias_grad,
    )


def block_forward(stream, weights, residual_weight, stride, key_stride, valids, offsets):
    (
        gain_first,
        qkv_weight,
        pools,
        memory,
        table,
        proj_weight,
        gain_second,
        up_weight,
        down_weight,
    ) = weights
    head_count = qkv_weight.shape[1] // (3 * HD)
    channels = head_count * HD
    clip_count = offsets.shape[0]
    key_side = SIDE // key_stride
    own_count = FR * key_side * key_side
    memory_count = FR // 4 * key_side * key_side
    keep_all = jnp.concatenate(
        [
            jnp.ones((clip_count, own_count), jnp.bool_),
            jnp.broadcast_to(valids[0][:, None], (clip_count, memory_count)),
            jnp.broadcast_to(valids[1][:, None], (clip_count, memory_count)),
        ],
        1,
    )
    normed = layer_norm(stream, gain_first).astype(jnp.bfloat16)
    projected = spread(normed, qkv_weight)
    query_pool, key_pool, value_pool, key_memory, value_memory = shape_fields(
        projected, pools, memory, head_count, stride, key_stride
    )
    key_low = key_memory.astype(jnp.bfloat16)
    value_low = value_memory.astype(jnp.bfloat16)
    prior_key, prior_value = passed_along((key_low, value_low), "dp", 1)
    key_ext = jnp.concatenate([prior_key, key_low], 0)
    value_ext = jnp.concatenate([prior_value, value_low], 0)
    keys_all = jnp.concatenate(
        [key_pool.astype(jnp.bfloat16), key_ext[1 : clip_count + 1], key_ext[:clip_count]], 1
    )
    values_all = jnp.concatenate(
        [value_pool.astype(jnp.bfloat16), value_ext[1 : clip_count + 1], value_ext[:clip_count]], 1
    )
    queries = query_pool.astype(jnp.bfloat16)
    bias_all = jax.vmap(lambda pair: relative_bias(table, pair, key_side))(offsets)

    def attend_clip(inputs):
        return attend(inputs[0], inputs[1], inputs[2], inputs[3], inputs[4], head_count)

    mixture, log_total = lax.map(attend_clip, (queries, keys_all, values_all, bias_all, keep_all))
    attention_rows = (mixture + query_pool).astype(jnp.bfloat16).reshape(-1, channels)
    branch = collect(attention_rows, proj_weight)
    if residual_weight is None:
        skip_linear = None
        middle = stream + branch
    else:
        skip_linear = jnp.dot(normed, residual_weight, preferred_element_type=jnp.float32)
        middle = skip_pool(skip_linear) + branch
    normed_mlp = layer_norm(middle, gain_second).astype(jnp.bfloat16)
    up_proj = spread(normed_mlp, up_weight)
    hidden = jax.nn.gelu(up_proj).astype(jnp.bfloat16)
    output = middle + collect(hidden, down_weight)
    kept = (
        stream,
        normed,
        projected,
        queries,
        keys_all,
        values_all,
        bias_all,
        log_total,
        attention_rows,
        skip_linear,
        middle,
        normed_mlp,
        up_proj,
        hidden,
        keep_all,
    )
    return (output, kept)


def block_backward(grad_output, kept, weights, residual_weight, stride, key_stride, offsets):
    (
        gain_first,
        qkv_weight,
        pools,
        memory,
        table,
        proj_weight,
        gain_second,
        up_weight,
        down_weight,
    ) = weights
    (
        stream,
        normed,
        projected,
        queries,
        keys_all,
        values_all,
        bias_all,
        log_total,
        attention_rows,
        skip_linear,
        middle,
        normed_mlp,
        up_proj,
        hidden,
        keep_all,
    ) = kept
    head_count = qkv_weight.shape[1] // (3 * HD)
    key_side = SIDE // key_stride
    own_count = FR * key_side * key_side
    memory_count = FR // 4 * key_side * key_side
    down_grad, hidden_grad = branch_back(grad_output.astype(jnp.bfloat16), hidden, down_weight)
    _, gelu_pull = jax.vjp(jax.nn.gelu, up_proj)
    up_grad = gelu_pull(hidden_grad)[0].astype(jnp.bfloat16)
    up_weight_grad = weight_grad(normed_mlp, up_grad)
    normed_mlp_grad = input_grad(up_grad, up_weight)
    _, second_pull = jax.vjp(layer_norm, middle, gain_second)
    middle_norm_grad, gain_second_grad = second_pull(normed_mlp_grad)
    middle_grad = grad_output + middle_norm_grad
    proj_grad, attention_grad = branch_back(
        middle_grad.astype(jnp.bfloat16), attention_rows, proj_weight
    )
    attention_low = attention_grad.astype(jnp.bfloat16).reshape(queries.shape)

    def clip_back(inputs):
        return attend_back(
            inputs[0], inputs[1], inputs[2], inputs[3], inputs[4], inputs[5], inputs[6], head_count
        )

    query_grad, keys_grad, values_grad, bias_grad = lax.map(
        clip_back, (queries, keys_all, values_all, bias_all, keep_all, log_total, attention_low)
    )

    def table_map(bias_table):
        return jax.vmap(lambda pair: relative_bias(bias_table, pair, key_side))(offsets)

    _, table_pull = jax.vjp(table_map, table)
    table_grad = table_pull(bias_grad)[0]
    query_pool_grad = query_grad + attention_low.astype(jnp.float32)
    edges = ((0, 0), (0, 0))
    first_end = own_count + memory_count
    key_ext_grad = jnp.pad(keys_grad[:, own_count:first_end], ((1, 1),) + edges) + jnp.pad(
        keys_grad[:, first_end:], ((0, 2),) + edges
    )
    value_ext_grad = jnp.pad(values_grad[:, own_count:first_end], ((1, 1),) + edges) + jnp.pad(
        values_grad[:, first_end:], ((0, 2),) + edges
    )
    later_key, later_value = (
        passed_along(key_ext_grad[:2].astype(jnp.bfloat16), "dp", -1).astype(jnp.float32),
        passed_along(value_ext_grad[:2].astype(jnp.bfloat16), "dp", -1).astype(jnp.float32),
    )
    key_memory_grad = key_ext_grad[2:] + later_key
    value_memory_grad = value_ext_grad[2:] + later_value

    def field_map(rows, pool_weights, memory_weights):
        return shape_fields(rows, pool_weights, memory_weights, head_count, stride, key_stride)

    _, field_pull = jax.vjp(field_map, projected, pools, memory)
    projected_grad, pools_grad, memory_grad = field_pull(
        (
            query_pool_grad,
            keys_grad[:, :own_count],
            values_grad[:, :own_count],
            key_memory_grad,
            value_memory_grad,
        )
    )
    projected_low = projected_grad.astype(jnp.bfloat16)
    qkv_grad = weight_grad(normed, projected_low)
    normed_grad = input_grad(projected_low, qkv_weight)
    if residual_weight is None:
        residual_grad = None
        stream_grad = middle_grad
    else:
        _, skip_pull = jax.vjp(skip_pool, skip_linear)
        linear_grad = skip_pull(middle_grad)[0].astype(jnp.bfloat16)
        residual_grad = lax.dot_general(
            normed, linear_grad, (((0,), (0,)), ((), ())), preferred_element_type=jnp.float32
        )
        normed_grad = normed_grad + lax.dot_general(
            linear_grad,
            residual_weight,
            (((1,), (1,)), ((), ())),
            preferred_element_type=jnp.float32,
        )
        stream_grad = jnp.zeros_like(stream)
    _, first_pull = jax.vjp(layer_norm, stream, gain_first)
    stream_norm_grad, gain_first_grad = first_pull(normed_grad)
    grads = (
        gain_first_grad,
        qkv_grad,
        pools_grad,
        memory_grad,
        table_grad,
        proj_grad,
        gain_second_grad,
        up_weight_grad,
        down_grad,
    )
    return (stream_grad + stream_norm_grad, grads, residual_grad)


def local(
    tokens,
    grad_out,
    video_ids,
    offsets,
    gain_one,
    qkv_one,
    pools_one,
    memory_one,
    table_one,
    proj_one,
    gain_two,
    up_one,
    down_one,
    gain_three,
    qkv_two,
    residual_two,
    pools_two,
    memory_two,
    table_two,
    proj_two,
    gain_four,
    up_two,
    down_two,
):
    clip_count = offsets.shape[0]
    first_clip = lax.axis_index("dp") * clip_count
    padded = jnp.concatenate([jnp.full((2,), -1, jnp.int32), video_ids])
    window = lax.dynamic_slice_in_dim(padded, first_clip, clip_count + 2)
    own_video = window[2:]
    valid_one = window[1 : clip_count + 1] == own_video
    valid_two = window[:clip_count] == own_video
    valids = (valid_one, valid_two)
    weights_first = (
        gain_one,
        qkv_one,
        pools_one,
        memory_one,
        table_one,
        proj_one,
        gain_two,
        up_one,
        down_one,
    )
    weights_second = (
        gain_three,
        qkv_two,
        pools_two,
        memory_two,
        table_two,
        proj_two,
        gain_four,
        up_two,
        down_two,
    )
    stream = tokens.astype(jnp.float32)
    middle_stream, kept_first = block_forward(stream, weights_first, None, 1, 2, valids, offsets)
    final, kept_second = block_forward(
        middle_stream, weights_second, residual_two, 2, 1, valids, offsets
    )
    middle_grad, grads_second, residual_grad = block_backward(
        grad_out.astype(jnp.float32), kept_second, weights_second, residual_two, 2, 1, offsets
    )
    tokens_grad, grads_first, unused = block_backward(
        middle_grad, kept_first, weights_first, None, 1, 2, offsets
    )
    summed = lax.psum(
        (
            grads_first[1],
            grads_first[4],
            grads_first[5],
            grads_first[7],
            grads_first[8],
            grads_second[1],
            grads_second[4],
            grads_second[5],
            grads_second[7],
            grads_second[8],
        ),
        "dp",
    )
    sums_first = summed[0:5]
    sums_second = summed[5:10]
    shared = lax.psum(
        (
            grads_first[0],
            grads_first[2],
            grads_first[3],
            grads_first[6],
            grads_second[0],
            residual_grad,
            grads_second[2],
            grads_second[3],
            grads_second[6],
        ),
        ("dp", "head"),
    )
    return (
        final.astype(jnp.bfloat16),
        tokens_grad.astype(jnp.bfloat16),
        shared[0],
        sums_first[0],
        shared[1],
        shared[2],
        sums_first[1],
        sums_first[2],
        shared[3],
        sums_first[3],
        sums_first[4],
        shared[4],
        sums_second[0],
        shared[5],
        shared[6],
        shared[7],
        sums_second[1],
        sums_second[2],
        shared[8],
        sums_second[3],
        sums_second[4],
    )


def solution(mesh):
    in_specs = (
        P(("dp", "head"), None),
        P(("dp", "head"), None),
        P(),
        P("dp", None),
        P(),
        P(None, "head"),
        P(),
        P(),
        P("head", None),
        P("head", None),
        P(),
        P(None, "head"),
        P("head", None),
        P(),
        P(None, "head"),
        P(),
        P(),
        P(),
        P("head", None),
        P("head", None),
        P(),
        P(None, "head"),
        P("head", None),
    )
    out_specs = (
        P(("dp", "head"), None),
        P(("dp", "head"), None),
        P(),
        P(None, "head"),
        P(),
        P(),
        P("head", None),
        P("head", None),
        P(),
        P(None, "head"),
        P("head", None),
        P(),
        P(None, "head"),
        P(),
        P(),
        P(),
        P("head", None),
        P("head", None),
        P(),
        P(None, "head"),
        P("head", None),
    )
    return jax.shard_map(local, mesh=mesh, in_specs=in_specs, out_specs=out_specs, check_vma=False)
```

```python
import functools

import jax
import jax.numpy as jnp
import numpy as np
from jax import lax
from jax.experimental import pallas as pl
from jax.experimental.pallas import tpu as pltpu
from jax.sharding import Mesh, PartitionSpec as P

HD = 96
FR = 4
SIDE = 10
LANES = 128
GRID = SIDE + 2
SLAB = GRID * 2 * FR
PADDED = GRID * SLAB
EPSILON = 1e-06
NEGATIVE = -1e30
SCALE = HD**-0.5
GELU_A = float(np.sqrt(2.0 / np.pi))
GELU_B = 0.044715

BF = jnp.bfloat16
F32 = jnp.float32


def nn(a, b):
    return lax.dot_general(a, b, (((1,), (0,)), ((), ())), preferred_element_type=F32)


def nt(a, b):
    return lax.dot_general(a, b, (((1,), (1,)), ((), ())), preferred_element_type=F32)


def tn(a, b):
    return lax.dot_general(a, b, (((0,), (0,)), ((), ())), preferred_element_type=F32)


def iota(shape, dim):
    return lax.broadcasted_iota(jnp.int32, shape, dim)


def widen(values):
    fill = jnp.zeros((values.shape[0], LANES - values.shape[1]), values.dtype)
    return jnp.concatenate([values, fill], axis=1)


def split(values):
    high = values.astype(BF)
    return high, (values - high.astype(F32)).astype(BF)


def norm_parts(values):
    centered = values - jnp.mean(values, axis=-1, keepdims=True)
    variance = jnp.mean(centered * centered, axis=-1, keepdims=True)
    scale = lax.rsqrt(variance + EPSILON)
    return centered * scale, scale


def norm_back(grad, values, gain):
    unit, scale = norm_parts(values)
    scaled = grad * gain
    mean_one = jnp.mean(scaled, axis=-1, keepdims=True)
    mean_two = jnp.mean(scaled * unit, axis=-1, keepdims=True)
    gain_grad = jnp.sum(grad * unit, axis=0, keepdims=True)
    return scale * (scaled - mean_one - unit * mean_two), gain_grad


def gelu_parts(values):
    square = values * values
    bent = jnp.tanh(GELU_A * values * (1.0 + GELU_B * square))
    half = 0.5 * (1.0 + bent)
    slope = half + 0.5 * values * (1.0 - bent * bent) * GELU_A * (1.0 + 3.0 * GELU_B * square)
    return values * half, slope


def pick(flag, one, two):
    return jnp.where(flag, one, two)


def slots(flag, sources, index=slice(None)):
    own, first, second, third = sources
    return (
        jnp.where(flag, own[index], second[index]),
        jnp.where(flag, first[index], third[index]),
    )


def token_rows(half):
    rows, cols = iota((FR * SIDE * SIDE, 2 * SIDE * SIDE), 0), iota((FR * SIDE * SIDE, 2 * SIDE * SIDE), 1)
    frame, place = rows % FR - 2 * half, rows // FR
    return jnp.where((frame >= 0) & (frame < 2) & (cols == SIDE * SIDE * frame + place), 1.0, 0.0).astype(BF)


def half_rows(half, area):
    rows, cols = iota((2 * area, FR * area), 0), iota((2 * area, FR * area), 1)
    upper = jnp.where(rows >= area, 1, 0)
    return jnp.where(cols == FR * (rows - area * upper) + 2 * half + upper, 1.0, 0.0).astype(BF)


def cells():
    small = SIDE // 2
    shape = (FR * small * small, FR * SIDE * SIDE)
    rows, cols = iota(shape, 0), iota(shape, 1)
    place, spot = rows // FR, cols // FR
    match = (
        (rows % FR == cols % FR)
        & (place // small == spot // (2 * SIDE))
        & (place % small == (spot % SIDE) // 2)
    )
    return jnp.where(match, 1.0, 0.0).astype(BF)


def fill_weights(wide, pools, field, flip):
    for tap in range(27):
        source = 26 - tap if flip else tap
        line = widen(pools[field, source : source + 1, :])
        wide[8 * tap : 8 * tap + 8, :] = jnp.broadcast_to(line, (8, LANES))


def fill_rolled(source, before, after, blocks):
    values = source.reshape(blocks, 8, LANES)
    lane = iota((blocks, 8, LANES), 1)
    before[0 : 8 * blocks, :] = jnp.where(lane >= 2, pltpu.roll(values, 2, 1), 0.0).reshape(8 * blocks, LANES)
    after[0 : 8 * blocks, :] = jnp.where(lane < 6, pltpu.roll(values, 6, 1), 0.0).reshape(8 * blocks, LANES)


def load_row(ref, index):
    return ref[pl.ds(pl.multiple_of(SLAB * index, SLAB), SLAB), :].reshape(GRID, 8, LANES)


def conv_rows(sources, wide, result, stride):
    count = SIDE // stride

    def one_row(i, carry):
        sums = [jnp.zeros((8, LANES), F32) for _ in range(count)]
        for a in range(3):
            for b in range(3):
                line = load_row(sources[a], stride * i + b)
                for e in range(3):
                    tap = 9 * a + 3 * b + e
                    weight = wide[8 * tap : 8 * tap + 8, :]
                    for j in range(count):
                        sums[j] = sums[j] + weight * line[stride * j + e]
        for j in range(count):
            result[pl.ds(pl.multiple_of(8 * count * i + 8 * j, 8), 8), :] = sums[j]
        return carry

    lax.fori_loop(0, count, one_row, 0)


def conv_back_two(sources, wide, result):
    count = SIDE // 2

    def one_row(m, carry):
        even = [jnp.zeros((8, LANES), F32) for _ in range(SIDE)]
        odd = [jnp.zeros((8, LANES), F32) for _ in range(SIDE)]
        for a in range(3):
            now, later = load_row(sources[2 - a], m + 1), load_row(sources[2 - a], m + 2)
            for sums, b, line in ((even, 1, now), (odd, 0, later), (odd, 2, now)):
                taps = [wide[8 * (9 * a + 3 * b + e) : 8 * (9 * a + 3 * b + e) + 8, :] for e in range(3)]
                for n in range(count):
                    sums[2 * n] = sums[2 * n] + taps[1] * line[n + 1]
                    sums[2 * n + 1] = sums[2 * n + 1] + taps[0] * line[n + 2] + taps[2] * line[n + 1]
        for j in range(SIDE):
            result[pl.ds(pl.multiple_of(16 * SIDE * m + 8 * j, 8), 8), :] = even[j]
            result[pl.ds(pl.multiple_of(16 * SIDE * m + 8 * SIDE + 8 * j, 8), 8), :] = odd[j]
        return carry

    lax.fori_loop(0, count, one_row, 0)


def conv_weight(sources, grads, totals, stride):
    count = SIDE // stride
    totals[...] = jnp.zeros((27 * 8, LANES), F32)

    def one_row(i, carry):
        cotangent = load_row(grads, i + 1)
        for a in range(3):
            for b in range(3):
                line = load_row(sources[a], stride * i + b)
                for e in range(3):
                    spot = 8 * (9 * a + 3 * b + e)
                    total = totals[spot : spot + 8, :]
                    for j in range(count):
                        total = total + line[stride * j + e] * cotangent[j + 1]
                    totals[spot : spot + 8, :] = total
        return carry

    lax.fori_loop(0, count, one_row, 0)


def weights_of_rows(totals):
    return jnp.sum(totals[...].reshape(27, 8, LANES), axis=1)


def put_rows(target, values, head, count):
    for i in range(count):
        start = ((i + 1) * GRID + 1) * 8 + head
        target[pl.ds(start, FR * count, stride=2), :] = values[FR * count * i : FR * count * (i + 1), :]


def pairs_of(heads):
    return [((0, 0), (1, 0))] if heads == 2 else [((0, 0), (0, 1)), ((1, 0), (1, 1))]


def shared(heads, head, turn):
    nh = heads // 2
    return (turn if head // nh == 0 else 1 - turn) * nh + head % nh


def front_body(heads, turn, strides, normed, weights, pools, memory, fields, pooled, passed, work):
    before, after, wide, result = work
    nh = heads // 2
    lines = [nn(normed, weights[s]) for s in range(2)]
    for field in range(3):
        fill_weights(wide, pools, field, False)
        stride = strides[field]
        count = SIDE // stride
        for number, pair in enumerate(pairs_of(heads)):
            group = fields.at[field * (heads // 2) + number]
            group[...] = jnp.zeros((PADDED, LANES), F32)
            for head, (slot, place) in enumerate(pair):
                start = HD * (3 * place + field)
                put_rows(group, widen(lines[slot][:, start : start + HD]), head, SIDE)
            fill_rolled(group[...], before, after, PADDED // 8)
            conv_rows((before, group, after), wide, result, stride)
            for head in range(2):
                pooled[field][2 * number + head] = result[pl.ds(head, FR * count * count, stride=2), :]
    area = (SIDE // strides[1]) ** 2
    for which in range(2):
        for head in range(heads):
            total = jnp.zeros((area, LANES), F32)
            for t in range(FR):
                line = widen(memory[which, t : t + 1, :])
                total = total + line * pooled[1 + which][head, pl.ds(t, area, stride=FR), :]
            passed[which * heads + shared(heads, head, turn)] = total.astype(BF)


def front_one(scal, own, first, second, gain, wa, wb, wc, wd, pools, memory, x_out, normed_out, fields, qp, kp, vp, passed, *work):
    match, turn = scal[0] == 1, scal[1] == 1
    near = pick(match, own[...], first[...])
    far = pick(match, first[...], second[...])
    low, high = pick(turn, far, near), pick(turn, near, far)
    rows = nn(token_rows(0), low) + nn(token_rows(1), high)
    x_out[...] = rows.astype(BF)
    normed = (norm_parts(rows)[0] * gain[...]).astype(BF)
    normed_out[...] = normed
    weights = slots(scal[6] == 1, (wa, wb, wc, wd))
    front_body(2, scal[1], (1, 2, 2), normed, weights, pools, memory, fields, (qp, kp, vp), passed, work)


def front_two(scal, middle, part, other, gain, wa, wb, wc, wd, residual, pools, memory, x_out, normed_out, skip, fields, qp, kp, vp, passed, *work):
    rows = middle[...] + (part[...].astype(F32) + other[...].astype(F32))
    x_out[...] = rows
    normed = (norm_parts(rows)[0] * gain[...]).astype(BF)
    normed_out[...] = normed
    high, low = split(nn(cells(), normed))
    skip[...] = 0.25 * (nn(high, residual[...]) + nn(low, residual[...]))
    weights = slots(scal[6] == 1, (wa, wb, wc, wd))
    front_body(4, scal[1], (2, 1, 1), normed, weights, pools, memory, fields, (qp, kp, vp), passed, work)


def table_of(flag, sources, block, slot, place):
    line = slots(flag, sources)[slot].astype(F32)
    row = 3 * (place if block == 0 else 1 + place)
    return line[row : row + 1, :] + line[row + 1 : row + 2, :] + line[row + 2 : row + 3, :]


def own_bias(bins, table):
    values = jnp.zeros(bins.shape, F32)
    for number in range(2 * FR - 1):
        values = jnp.where(bins == number, table[:, number : number + 1], values)
    return values


def far_bias(table, offset):
    lanes = iota(table.shape, 1)
    return jnp.sum(jnp.where(lanes == offset + 2 * FR - 1, table, 0.0), axis=1, keepdims=True)


def probs_of(scal, bins, table, query, keys):
    parts = [nt(query, keys[0]) * SCALE + own_bias(bins, table)]
    for j in range(2):
        raw = nt(query, keys[1 + j]) * SCALE + far_bias(table, scal[4 + j])
        parts.append(jnp.where(scal[2 + j] == 1, raw, NEGATIVE))
    top = functools.reduce(jnp.maximum, [jnp.max(part, axis=1, keepdims=True) for part in parts])
    parts = [jnp.exp(part - top) for part in parts]
    total = sum(jnp.sum(part, axis=1, keepdims=True) for part in parts)
    return [part / total for part in parts]


def heads_of(heads, block):
    return [(slot, place) for slot in range(2) for place in range(heads // 2)]


def attend(block, scal, ta, tb, tc, td, qp, kp, vp, near, far, wa, wb, wc, wd, rows_out, part_out):
    heads = qp.shape[0]
    flag = scal[6] == 1
    shape = (qp.shape[1], kp.shape[1])
    bins = iota(shape, 0) % FR - iota(shape, 1) % FR + FR - 1
    weights = slots(flag, (wa, wb, wc, wd))
    total = jnp.zeros(part_out.shape, F32)
    for head, (slot, place) in enumerate(heads_of(heads, block)):
        table = table_of(flag, (ta, tb, tc, td), block, slot, place)
        pool = qp[head]
        spot = shared(heads, head, scal[1])
        keys = (kp[head].astype(BF), near[spot], far[spot])
        values = (vp[head].astype(BF), near[heads + spot], far[heads + spot])
        probs = probs_of(scal, bins, table, pool.astype(BF), keys)
        mixture = sum(nn(p.astype(BF), v) for p, v in zip(probs, values))
        line = (mixture + pool).astype(BF)
        rows_out[head] = line
        total = total + nn(line[:, :HD], weights[slot][HD * place : HD * place + HD, :])
    part_out[...] = total.astype(BF)


def attend_back(block, scal, ta, tb, tc, td, qp, kp, vp, near, far, wa, wb, wc, wd, rows, middle_grad, dq, dk, dv, d_near, d_far, proj_grad, table_grad):
    heads = qp.shape[0]
    flag = scal[6] == 1
    shape = (qp.shape[1], kp.shape[1])
    bins = iota(shape, 0) % FR - iota(shape, 1) % FR + FR - 1
    weights = slots(flag, (wa, wb, wc, wd))
    branch = middle_grad.astype(BF)
    lanes = iota((1, LANES), 1)
    table_lines = []
    for head, (slot, place) in enumerate(heads_of(heads, block)):
        table = table_of(flag, (ta, tb, tc, td), block, slot, place)
        weight = weights[slot][HD * place : HD * place + HD, :]
        found = tn(rows[head][:, :HD], branch).astype(BF)
        for column in range(proj_grad.shape[1] // (HD * (heads // 2))):
            start = HD * (heads // 2) * column + HD * place
            proj_grad[slot, start : start + HD, :] = found[:, proj_grad.shape[2] * column : proj_grad.shape[2] * (column + 1)]
        grad = widen(nt(branch, weight).astype(BF))
        query = qp[head].astype(BF)
        spot = shared(heads, head, scal[1])
        keys = (kp[head].astype(BF), near[spot], far[spot])
        values = (vp[head].astype(BF), near[heads + spot], far[heads + spot])
        probs = probs_of(scal, bins, table, query, keys)
        grad_probs = [nt(grad, v) for v in values]
        inner = sum(jnp.sum(p * d, axis=1, keepdims=True) for p, d in zip(probs, grad_probs))
        low = [(p * (d - inner)).astype(BF) for p, d in zip(probs, grad_probs)]
        dq[head] = sum(nn(s, k) for s, k in zip(low, keys)) * SCALE + grad.astype(F32)
        key_grads = [tn(s, query) * SCALE for s in low]
        value_grads = [tn(p.astype(BF), grad) for p in probs]
        dk[head], dv[head] = key_grads[0], value_grads[0]
        d_near[spot], d_near[heads + spot] = key_grads[1].astype(BF), value_grads[1].astype(BF)
        d_far[spot], d_far[heads + spot] = key_grads[2].astype(BF), value_grads[2].astype(BF)
        score = low[0].astype(F32)
        line = jnp.zeros((1, LANES), F32)
        for number in range(2 * FR - 1):
            column = jnp.sum(jnp.where(bins == number, score, 0.0), axis=0, keepdims=True)
            line = line + jnp.where(lanes == number, jnp.sum(column, axis=1, keepdims=True), 0.0)
        for j in range(2):
            column = jnp.sum(low[1 + j].astype(F32), axis=0, keepdims=True)
            value = jnp.sum(column, axis=1, keepdims=True)
            line = line + jnp.where(lanes == scal[4 + j] + 2 * FR - 1, value, 0.0)
        table_lines.append(line)
    for head, line in enumerate(table_lines):
        table_grad[head : head + 1, :] = line


def field_back(heads, turn, strides, fields, pooled, grads, near, far, pools, memory, pools_grad, memory_grad, work):
    before, after, wide, result, grid, grid_before, grid_after, totals, rows = work
    half = heads // 2
    back = {}
    area = (SIDE // strides[1]) ** 2
    for field in range(3):
        stride = strides[field]
        count = SIDE // stride
        fill_weights(wide, pools, field, stride == 1)
        weight_sum = jnp.zeros((27, LANES), F32)
        memory_lines = [jnp.zeros((1, LANES), F32) for _ in range(FR)]
        for number, pair in enumerate(pairs_of(heads)):
            grid[...] = jnp.zeros((PADDED, LANES), F32)
            for place in range(2):
                head = 2 * number + place
                if field == 0:
                    put_rows(grid, grads[0][head], place, count)
                else:
                    entry = (field - 1) * heads + shared(heads, head, turn)
                    cotangent = near[entry].astype(F32) + far[entry].astype(F32)
                    for t in range(FR):
                        spot = pl.ds(t, area, stride=FR)
                        line = widen(memory[field - 1, t : t + 1, :])
                        rows[spot, :] = grads[field][head, spot, :] + line * cotangent
                        product = pooled[field - 1][head, spot, :] * cotangent
                        memory_lines[t] = memory_lines[t] + jnp.sum(product, axis=0, keepdims=True)
                    put_rows(grid, rows[0 : FR * area, :], place, count)
            group = fields.at[field * half + number]
            fill_rolled(group[...], before, after, PADDED // 8)
            conv_weight((before, group, after), grid, totals, stride)
            weight_sum = weight_sum + weights_of_rows(totals)
            fill_rolled(grid[...], grid_before, grid_after, PADDED // 8)
            if stride == 1:
                conv_rows((grid_before, grid, grid_after), wide, result, 1)
            else:
                conv_back_two((grid_before, grid, grid_after), wide, result)
            for place, key in enumerate(pair):
                back[key + (field,)] = result[pl.ds(place, FR * SIDE * SIDE, stride=2), :][:, :HD]
        pools_grad[field, 0:27, :] = weight_sum
        if field:
            for t in range(FR):
                memory_grad[field - 1, t : t + 1, :] = memory_lines[t]
    outs = []
    for slot in range(2):
        columns = [back[(slot, place, field)] for place in range(half) for field in range(3)]
        outs.append(jnp.concatenate(columns, axis=1).astype(BF))
    return outs


def mlp_one(scal, x, part, other, gain, ua, ub, uc, ud, da, db, dc, dd, g_own, g_first, g_second, middle_out, normed_out, part_out, g_out):
    middle = x[...].astype(F32) + (part[...].astype(F32) + other[...].astype(F32))
    middle_out[...] = middle
    normed = (norm_parts(middle)[0] * gain[...]).astype(BF)
    normed_out[...] = normed
    flag = scal[6] == 1
    ups, downs = slots(flag, (ua, ub, uc, ud)), slots(flag, (da, db, dc, dd))
    total = jnp.zeros(part_out.shape, F32)
    for slot in range(2):
        hidden = gelu_parts(nn(normed, ups[slot]))[0].astype(BF)
        total = total + nn(hidden, downs[slot])
    part_out[...] = total.astype(BF)
    match, turn = scal[0] == 1, scal[1] == 1
    near = pick(match, g_own[...], g_first[...])
    far = pick(match, g_first[...], g_second[...])
    low, high = pick(turn, far, near), pick(turn, near, far)
    area = (SIDE // 2) ** 2
    total = tn(half_rows(0, area), low) + tn(half_rows(1, area), high)
    g_out[...] = total.astype(BF)


def middle_two(skip, part, other, gain, middle_out, normed_out):
    middle = skip[...] + (part[...].astype(F32) + other[...].astype(F32))
    middle_out[...] = middle
    normed_out[...] = (norm_parts(middle)[0] * gain[...]).astype(BF)


def mlp_two(scal, *refs):
    normed, grads = refs[0:4], refs[4:8]
    up_ref, down_ref = refs[8:10]
    outs, backs = refs[10:14], refs[14:18]
    packed = refs[18]
    width = up_ref.shape[1] // 2
    start = pl.multiple_of(scal[7] * width, LANES)
    up, down = up_ref[:, pl.ds(start, width)], down_ref[pl.ds(start, width), :]
    up_total = jnp.zeros(up.shape, F32)
    down_total = jnp.zeros(down.shape, F32)
    for d in range(4):
        rows, grad = normed[d][...], grads[d][...]
        value, slope = gelu_parts(nn(rows, up))
        hidden = value.astype(BF)
        outs[d][...] = nn(hidden, down).astype(BF)
        up_low = (nt(grad, down) * slope).astype(BF)
        backs[d][...] = nt(up_low, up).astype(BF)
        up_total = up_total + tn(rows, up_low)
        down_total = down_total + tn(hidden, grad)
    size = up.shape[0]
    packed[0:size, :] = up_total.astype(BF)
    packed[size : size + width, :] = down_total[:, :width].astype(BF)
    packed[size + width : size + 2 * width, :] = down_total[:, width:].astype(BF)


def cut(flag, full, keep, send):
    rows = keep.shape[1]
    mine = pl.ds(pl.multiple_of(flag * rows, 16), rows)
    theirs = pl.ds(pl.multiple_of((1 - flag) * rows, 16), rows)
    for slot in range(2):
        keep[slot] = full[slot, mine, :]
        send[slot] = full[slot, theirs, :]


def add_first(number, scal, keep, other, keep_out, send_out, full):
    full[...] = (keep[...].astype(F32) + other[...].astype(F32)).astype(BF)
    cut(scal[number], full, keep_out, send_out)


def add_second(keep, other, one, two):
    one[...] = (keep[0].astype(F32) + other[0].astype(F32)).astype(BF)
    two[...] = (keep[1].astype(F32) + other[1].astype(F32)).astype(BF)


def gather_parts(first, second, scal, parts, full):
    rows = parts[0].shape[0]
    one, two = scal[first], scal[second]
    for part, a, b in zip(parts, (one, one, 1 - one, 1 - one), (two, 1 - two, two, 1 - two)):
        full[pl.ds(pl.multiple_of((2 * a + b) * rows, 16), rows), :] = part[...].astype(F32)


def finish_two(scal, a, b, c, d, qkv, proj, piece, full):
    gather_parts(8, 9, scal, (a, b, c, d), full)
    width = full.shape[1]
    qkv[:, :width] = full[0:384, :]
    qkv[0:192, width:] = full[384:576, :192]
    qkv[192:384, width:] = full[384:576, 192:]
    proj[:, :width] = full[576:768, :]
    proj[:, width:] = full[768:960, :]
    piece[...] = full[960:1152, :].astype(BF)


def finish_mlp(scal, a, b, c, d, up, down, small, full):
    gather_parts(9, 8, scal, (a, b, c, d), full)
    up[...] = full[0:384, :]
    down[...] = full[384:768, :]
    small[...] = full[768:832, :]


def finish_one(scal, a, b, c, d, qkv, proj, table, small, full):
    gather_parts(8, 9, scal, (a, b, c, d), full)
    qkv[...] = full[0:288, :].T
    proj[...] = full[288:384, :]
    table[...] = full[384:392, :]
    small[...] = full[400:464, :]


def finish_wide(scal, own, other, up, down):
    first = scal[7] == 0
    one = jnp.where(first, own[...], other[...]).astype(F32)
    two = jnp.where(first, other[...], own[...]).astype(F32)
    size = up.shape[0]
    width = size // 2
    up[:, :width], up[:, width:] = one[:size, :], two[:size, :]
    down[:width, :width], down[:width, width:] = one[size : size + width, :], one[size + width :, :]
    down[width:, :width], down[width:, width:] = two[size : size + width, :], two[size + width :, :]


def add_two(one, two, out):
    out[...] = (one[...].astype(F32) + two[...].astype(F32)).astype(BF)


def sum_four(a, b, c, d, out):
    total = (a[...].astype(F32) + b[...].astype(F32)) + (c[...].astype(F32) + d[...].astype(F32))
    out[...] = total.astype(BF)


def back_attend_two(scal, part, other, g, middle, gain, *refs):
    ins, outs = refs[0:14], refs[14:]
    grad, gain_grad = norm_back(part[...].astype(F32) + other[...].astype(F32), middle[...], gain[...])
    middle_grad = g[...].astype(F32) + grad
    outs[0][...] = middle_grad
    outs[1][...] = gain_grad
    attend_back(1, scal, *ins, middle_grad, *outs[2:])


def put_small(small, pools_grad, memory_grad):
    small[...] = jnp.zeros(small.shape, F32)
    for field in range(3):
        small[0:27, LANES * field : LANES * (field + 1)] = pools_grad[field, 0:27, :]
    for which in range(2):
        small[32 : 32 + FR, LANES * which : LANES * (which + 1)] = memory_grad[which]


def back_front_two(scal, middle_grad, normed_ref, fields, kp, vp, dq, dk, dv, near, far, wa, wb, wc, wd, residual, pools, memory, proj_grad, gain_grad, part_out, keep, send, small, pools_grad, memory_grad, full, *work):
    normed = normed_ref[...]
    backs = field_back(4, scal[1], (2, 1, 1), fields, (kp, vp), (dq, dk, dv), near, far, pools, memory, pools_grad, memory_grad, work)
    weights = slots(scal[6] == 1, (wa, wb, wc, wd))
    total = jnp.zeros(part_out.shape, F32)
    width = full.shape[2]
    columns = pl.ds(pl.multiple_of(scal[7] * width, LANES), width)
    linear = (0.25 * middle_grad[:, columns]).astype(BF)
    cell = cells()
    high, low = split(nn(cell, normed))
    residual_grad = (tn(high, linear) + tn(low, linear)).astype(BF)
    turned = scal[1] == 1
    upper, under = residual_grad[:192, :], residual_grad[192:, :]
    for slot in range(2):
        found = tn(normed, backs[slot]).astype(BF)
        full[slot, 0:384, :] = found[:, :width]
        full[slot, 384:576, :] = jnp.concatenate([found[0:192, width:], found[192:384, width:]], axis=1)
        full[slot, 576:960, :] = proj_grad[slot]
        full[slot, 960:1152, :] = pick(turned, under, upper) if slot == 0 else pick(turned, upper, under)
        total = total + nt(backs[slot], weights[slot])
    cut(scal[8], full, keep, send)
    high, low = split(nt(linear, residual[:, columns]))
    part_out[...] = (total + tn(cell, high) + tn(cell, low)).astype(BF)
    put_small(small, pools_grad, memory_grad)
    small[40:41, :] = 0.5 * gain_grad[:, :width]
    small[41:42, :] = 0.5 * gain_grad[:, width:]


def back_mlp_one(scal, part, other, x, gain, normed_ref, ua, ub, uc, ud, da, db, dc, dd, small, small_other, grad_out, part_out, gain_grad_ref, keep, send, full):
    grad, gain_grad = norm_back(part[...].astype(F32) + other[...].astype(F32), x[...], gain[...])
    grad_out[...] = grad
    gain_grad_ref[...] = gain_grad
    branch = grad.astype(BF)
    normed = normed_ref[...]
    flag = scal[6] == 1
    ups, downs = slots(flag, (ua, ub, uc, ud)), slots(flag, (da, db, dc, dd))
    total = jnp.zeros(part_out.shape, F32)
    whole = (small[...] + small_other[...]).astype(BF)
    size = normed.shape[1]
    for slot in range(2):
        value, slope = gelu_parts(nn(normed, ups[slot]))
        up_low = (nt(branch, downs[slot]) * slope).astype(BF)
        full[slot, 0:size, :] = tn(normed, up_low).astype(BF)
        full[slot, size : 2 * size, :] = tn(value.astype(BF), branch).astype(BF)
        full[slot, 2 * size : 2 * size + 64, :] = whole
        total = total + nt(up_low, ups[slot])
    part_out[...] = total.astype(BF)
    cut(scal[9], full, keep, send)


def back_attend_one(scal, part, other, g, middle, gain, *refs):
    ins, outs = refs[0:14], refs[14:]
    grad, gain_grad = norm_back(part[...].astype(F32) + other[...].astype(F32), middle[...], gain[...])
    middle_grad = g[...] + grad
    outs[0][...] = middle_grad
    outs[1][...] = gain_grad
    attend_back(0, scal, *ins, middle_grad, *outs[2:])


def back_front_one(scal, normed_ref, fields, kp, vp, dq, dk, dv, near, far, wa, wb, wc, wd, pools, memory, gain_two_grad, gain_three_grad, qkv_grad, part_out, small, pools_grad, memory_grad, *work):
    normed = normed_ref[...]
    backs = field_back(2, scal[1], (1, 2, 2), fields, (kp, vp), (dq, dk, dv), near, far, pools, memory, pools_grad, memory_grad, work)
    weights = slots(scal[6] == 1, (wa, wb, wc, wd))
    total = jnp.zeros(part_out.shape, F32)
    for slot in range(2):
        qkv_grad[slot] = tn(backs[slot], normed).astype(BF)
        total = total + nt(backs[slot], weights[slot])
    part_out[...] = total.astype(BF)
    put_small(small, pools_grad, memory_grad)
    small[40:41, :] = 0.5 * gain_two_grad[...]
    small[41:42, :] = 0.5 * gain_three_grad[...]


def back_tokens(scal, part, other, x, gain, middle_grad, qkv_grad, proj_grad, table_one, table_two, small, small_other, keep_rows, send_rows, keep, send, full):
    grad, gain_grad = norm_back(part[...].astype(F32) + other[...].astype(F32), x[...].astype(F32), gain[...])
    rows = (middle_grad[...] + grad).astype(BF)
    turn = scal[1]
    keep_rows[...] = nn(half_rows(turn, SIDE * SIDE), rows).astype(BF)
    send_rows[...] = nn(half_rows(1 - turn, SIDE * SIDE), rows).astype(BF)
    line = iota((64, 1), 0)
    whole = jnp.where(line == 42, gain_grad, small[...] + small_other[...]).astype(BF)
    for slot in range(2):
        full[slot, 0:288, :] = qkv_grad[slot]
        full[slot, 288:384, :] = proj_grad[slot]
        lines = jnp.concatenate([table_one[slot : slot + 1, :], table_two[2 * slot : 2 * slot + 2, :], jnp.zeros((13, LANES), F32)], axis=0)
        full[slot, 384:400, :] = jnp.concatenate([lines, jnp.zeros((16, 2 * LANES), F32)], axis=1).astype(BF)
        full[slot, 400:464, :] = whole
        full[slot, 464:512, :] = jnp.zeros((48, full.shape[2]), BF)
    cut(scal[8], full, keep, send)


def final_rows(scal, middle, part, other, keep, send):
    rows = (middle[...] + (part[...].astype(F32) + other[...].astype(F32))).astype(BF)
    turn = scal[1]
    area = (SIDE // 2) ** 2
    keep[...] = nn(half_rows(turn, area), rows).astype(BF)
    send[...] = nn(half_rows(1 - turn, area), rows).astype(BF)


SMEM = pl.BlockSpec(memory_space=pltpu.SMEM)


def part_of(block, *index):
    return pl.BlockSpec(block, lambda i: index)


def kernel(body, name, outs, ins, work=(), specs=None, flops=2 * 10**8):
    specs = specs or {}
    in_specs = []
    for number, item in enumerate(ins):
        if number == 0 and item.dtype == jnp.int32:
            in_specs.append(SMEM)
        else:
            in_specs.append(specs.get(number, pl.BlockSpec(memory_space=pltpu.VMEM)))
    moved = sum(int(np.prod(item.shape)) * item.dtype.itemsize for item in ins) + sum(
        int(np.prod(shape)) * jnp.dtype(kind).itemsize for shape, kind in outs
    )
    return pl.pallas_call(
        body,
        **({"grid": (1,)} if specs else {}),
        out_shape=tuple(jax.ShapeDtypeStruct(shape, kind) for shape, kind in outs),
        in_specs=in_specs,
        out_specs=tuple(pl.BlockSpec(memory_space=pltpu.VMEM) for _ in outs),
        scratch_shapes=list(work),
        name=name,
        cost_estimate=pl.CostEstimate(flops=flops, bytes_accessed=moved, transcendentals=0),
        compiler_params=pltpu.CompilerParams(vmem_limit_bytes=48 << 20),
    )(*ins)


def scratch(*rows):
    return [pltpu.VMEM((count, LANES), F32) for count in rows]


FRONT_WORK = (PADDED, PADDED, 216, 800)
BACK_WORK = (PADDED, PADDED, 216, 800, PADDED, PADDED, PADDED, 216, 400)


def chips(z):
    return z // 2, z % 2


def swap(values):
    return lax.ppermute(values, "core", [(0, 1), (1, 0)])


def weight_routes():
    def place(core, z):
        return core * 4 + z

    first, second, third = [], [], []
    for core in range(2):
        low, other = 2 * core, 2 - 2 * core
        first += [(place(core, low), place(core, low + 1)), (place(core, low + 1), place(core, low))]
        second += [(place(core, low), place(core, other)), (place(core, low + 1), place(core, other + 1))]
        third += [(place(core, low + 1), place(core, other)), (place(core, low), place(core, other + 1))]
    return first, second, third


def spread(values):
    return (values,) + tuple(lax.ppermute(values, ("core", "head"), route) for route in weight_routes())


def reverse(route):
    return [(end, start) for start, end in route]


def clip_routes(planes, distance):
    def place(clip):
        slot = clip % 4
        return (clip // 4) * 4 + 2 * (slot % 2) + slot // 2

    total = 4 * planes
    return [(place(clip), place(clip + distance)) for clip in range(total) if 0 <= clip + distance < total]


def half_routes():
    def place(core, a, b):
        return core * 4 + 2 * a + b

    one, two, three = [], [], []
    for a in range(2):
        for b in range(2):
            one += [(place(b, a, b), place(1 - b, a, b)), (place(1 - b, a, b), place(1 - b, a, 1 - b))]
            two += [(place(1 - b, a, b), place(b, a, 1 - b))]
            three += [(place(1 - b, a, b), place(b, a, 1 - b))]
    return one, two, three


def turn_by(values, distance):
    return lax.ppermute(values, "head", [(z, (z + distance) % 4) for z in range(4)])


def local(
    planes,
    tokens,
    grad_out,
    video_ids,
    offsets,
    gain_one,
    qkv_one,
    pools_one,
    memory_one,
    table_one,
    proj_one,
    gain_two,
    up_one,
    down_one,
    gain_three,
    qkv_two,
    residual_two,
    pools_two,
    memory_two,
    table_two,
    proj_two,
    gain_four,
    up_two,
    down_two,
):
    plane, core, head = lax.axis_index("plane"), lax.axis_index("core"), lax.axis_index("head")
    upper, turn = head // 2, head % 2
    clip = 4 * plane + 2 * turn + upper
    match = core == turn
    mine = head // 2 == core
    both = jnp.where(match, offsets, swap(offsets))
    pair = lax.dynamic_slice_in_dim(both, upper, 1, 0)[0]
    padded = jnp.concatenate([jnp.full((2,), -1, jnp.int32), video_ids])
    window = lax.dynamic_slice_in_dim(padded, clip, 3)
    scal = jnp.stack(
        [
            match.astype(jnp.int32),
            turn.astype(jnp.int32),
            (window[1] == window[2]).astype(jnp.int32),
            (window[0] == window[2]).astype(jnp.int32),
            pair[0],
            pair[1],
            mine.astype(jnp.int32),
            core.astype(jnp.int32),
            (plane % 2).astype(jnp.int32),
            (plane // 2 % 2).astype(jnp.int32),
        ]
    )
    gains = [item.reshape(1, -1) for item in (gain_one, gain_two, gain_three, gain_four)]

    tables = jnp.concatenate([table_one, table_two], 0)
    table_high = lax.reduce_precision(tables, 8, 7)
    table_mid = lax.reduce_precision(tables - table_high, 8, 7)
    table_low = tables - table_high - table_mid
    table_rows = jnp.stack([table_high, table_mid, table_low], 1).reshape(9, -1).astype(BF)
    table_rows = jnp.pad(table_rows, ((0, 7), (0, up_one.shape[1] - table_rows.shape[1])))
    proj_bundle = jnp.concatenate([proj_one, table_rows], 0)
    mlp_bundle = jnp.concatenate([up_one, down_one], 0)

    route_one, route_two, route_three = half_routes()
    axes = ("core", "head")
    qkv_one_all = spread(qkv_one)
    tok_one, tok_two = lax.ppermute(tokens, axes, route_one), lax.ppermute(tokens, axes, route_two)
    proj_all = spread(proj_bundle)
    mlp_bundle, late_qkv, late_proj, late_out, gate = lax.optimization_barrier(
        (mlp_bundle, qkv_two, proj_two, grad_out, qkv_one_all)
    )
    qkv_one_all = gate
    mlp_all = spread(mlp_bundle)
    qkv_two_all = spread(late_qkv)
    proj_two_all = spread(late_proj)
    g_one, g_two = lax.ppermute(late_out, axes, route_one), lax.ppermute(late_out, axes, route_two)

    def parts(first, block, index):
        return {first + number: part_of(block, index, 0) for number in range(4)}

    width = qkv_one.shape[0]
    wide = residual_two.shape[1]
    n1, n2 = FR * SIDE * SIDE, FR * SIDE * SIDE // 4
    a1, a2 = n2 // FR, n1 // FR

    def up_specs(first):
        return parts(first, (width, width), 0)

    def down_specs(first):
        return parts(first, (width, width), 1)

    def proj_specs(first):
        return parts(first, (HD, width), 0)

    def table_specs(first):
        return parts(first, (16, width), HD // 16)

    x1, normed1, fields1, qp1, kp1, vp1, passed1 = kernel(
        front_one,
        "front_one",
        [
            ((n1, width), BF),
            ((n1, width), BF),
            ((3, PADDED, LANES), F32),
            ((2, n1, LANES), F32),
            ((2, n2, LANES), F32),
            ((2, n2, LANES), F32),
            ((4, a1, LANES), BF),
        ],
        [scal, tokens, tok_one, tok_two, gains[0], *qkv_one_all, pools_one, memory_one],
        scratch(*FRONT_WORK),
    )
    places = ("plane", "head")
    near1 = lax.ppermute(passed1, places, clip_routes(planes, 1))
    far1 = lax.ppermute(passed1, places, clip_routes(planes, 2))
    attn1_ins = [*proj_all, qp1, kp1, vp1, near1, far1, *proj_all]
    rows1, part1 = kernel(
        functools.partial(attend, 0),
        "attend_one",
        [((2, n1, LANES), BF), ((n1, width), BF)],
        [scal, *attn1_ins],
        specs={**table_specs(1), **proj_specs(10)},
    )
    middle1, mlp_normed1, part_mlp1, g = kernel(
        mlp_one,
        "mlp_one",
        [((n1, width), F32), ((n1, width), BF), ((n1, width), BF), ((n2, wide), BF)],
        [scal, x1, part1, swap(part1), gains[1], *mlp_all, *mlp_all, late_out, g_one, g_two],
        specs={**up_specs(5), **down_specs(9)},
    )
    g_all = [g] + [turn_by(g, d) for d in (1, 2, 3)]
    x2, normed2, skip, fields2, qp2, kp2, vp2, passed2 = kernel(
        front_two,
        "front_two",
        [
            ((n1, width), F32),
            ((n1, width), BF),
            ((n2, wide), F32),
            ((6, PADDED, LANES), F32),
            ((4, n2, LANES), F32),
            ((4, n1, LANES), F32),
            ((4, n1, LANES), F32),
            ((8, a2, LANES), BF),
        ],
        [scal, middle1, part_mlp1, swap(part_mlp1), gains[2], *qkv_two_all, residual_two, pools_two, memory_two],
        scratch(*FRONT_WORK),
    )
    near2 = lax.ppermute(passed2, places, clip_routes(planes, 1))
    far2 = lax.ppermute(passed2, places, clip_routes(planes, 2))
    attn2_ins = [*proj_all, qp2, kp2, vp2, near2, far2, *proj_two_all]
    rows2, part2 = kernel(
        functools.partial(attend, 1),
        "attend_two",
        [((4, n2, LANES), BF), ((n2, wide), BF)],
        [scal, *attn2_ins],
        specs=table_specs(1),
    )
    middle2, mlp_normed2 = kernel(
        middle_two, "middle_two", [((n2, wide), F32), ((n2, wide), BF)], [skip, part2, swap(part2), gains[3]]
    )
    normed_all = [mlp_normed2] + [turn_by(mlp_normed2, d) for d in (1, 2, 3)]
    half = up_two.shape[1] // 2
    found = kernel(
        mlp_two,
        "mlp_two",
        [((n2, wide), BF)] * 8 + [((2 * wide, half), BF)],
        [scal, *normed_all, *g_all, up_two, down_two],
    )
    backs = [found[4]] + [turn_by(found[4 + d], -d) for d in (1, 2, 3)]
    (back_sum,) = kernel(sum_four, "sum_back", [((n2, wide), BF)], backs)
    middle_grad2, gain_four_grad, dq2, dk2, dv2, d_near2, d_far2, proj_two_grad, table_two_grad = kernel(
        back_attend_two,
        "back_attend_two",
        [
            ((n2, wide), F32),
            ((1, wide), F32),
            ((4, n2, LANES), F32),
            ((4, n1, LANES), F32),
            ((4, n1, LANES), F32),
            ((8, a2, LANES), BF),
            ((8, a2, LANES), BF),
            ((2, 4 * HD, width), BF),
            ((4, LANES), F32),
        ],
        [scal, back_sum, swap(back_sum), g, middle2, gains[3], *attn2_ins, rows2],
        specs=table_specs(6),
    )
    near_grad2 = lax.ppermute(d_near2, places, clip_routes(planes, -1))
    far_grad2 = lax.ppermute(d_far2, places, clip_routes(planes, -2))
    part_back2, keep2, send2, small2, _, _ = kernel(
        back_front_two,
        "back_front_two",
        [
            ((n1, width), BF),
            ((2, 576, width), BF),
            ((2, 576, width), BF),
            ((64, width), F32),
            ((3, 32, LANES), F32),
            ((2, FR, LANES), F32),
        ],
        [
            scal, middle_grad2, normed2, fields2, kp2, vp2, dq2, dk2, dv2, near_grad2, far_grad2,
            *qkv_two_all, residual_two, pools_two, memory_two, proj_two_grad, gain_four_grad,
        ],
        [pltpu.VMEM((2, 1152, width), BF)] + scratch(*BACK_WORK),
    )
    grad1, part_mlp_back, gain_three_grad, keep_m, send_m = kernel(
        back_mlp_one,
        "back_mlp_one",
        [((n1, width), F32), ((n1, width), BF), ((1, width), F32), ((2, 416, width), BF), ((2, 416, width), BF)],
        [scal, part_back2, swap(part_back2), x2, gains[2], mlp_normed1, *mlp_all, *mlp_all, small2, swap(small2)],
        [pltpu.VMEM((2, 832, width), BF)],
        specs={**up_specs(6), **down_specs(10)},
    )
    middle_grad1, gain_two_grad, dq1, dk1, dv1, d_near1, d_far1, proj_one_grad, table_one_grad = kernel(
        back_attend_one,
        "back_attend_one",
        [
            ((n1, width), F32),
            ((1, width), F32),
            ((2, n1, LANES), F32),
            ((2, n2, LANES), F32),
            ((2, n2, LANES), F32),
            ((4, a1, LANES), BF),
            ((4, a1, LANES), BF),
            ((2, HD, width), BF),
            ((2, LANES), F32),
        ],
        [scal, part_mlp_back, swap(part_mlp_back), grad1, middle1, gains[1], *attn1_ins, rows1],
        specs={**table_specs(6), **proj_specs(15)},
    )
    near_grad1 = lax.ppermute(d_near1, places, clip_routes(planes, -1))
    far_grad1 = lax.ppermute(d_far1, places, clip_routes(planes, -2))
    qkv_one_grad, part_back1, small1, _, _ = kernel(
        back_front_one,
        "back_front_one",
        [((2, 3 * HD, width), BF), ((n1, width), BF), ((64, width), F32), ((3, 32, LANES), F32), ((2, FR, LANES), F32)],
        [
            scal, normed1, fields1, kp1, vp1, dq1, dk1, dv1, near_grad1, far_grad1,
            *qkv_one_all, pools_one, memory_one, gain_two_grad, gain_three_grad,
        ],
        scratch(*BACK_WORK),
    )
    tok_keep, tok_send, keep1, send1 = kernel(
        back_tokens,
        "back_tokens",
        [((n1 // 2, width), BF), ((n1 // 2, width), BF), ((2, 256, width), BF), ((2, 256, width), BF)],
        [
            scal, part_back1, swap(part_back1), x1, gains[0], middle_grad1, qkv_one_grad, proj_one_grad,
            table_one_grad, table_two_grad, small1, swap(small1),
        ],
        [pltpu.VMEM((2, 512, width), BF)],
    )
    tokens_grad = jnp.where(match, tok_keep, lax.ppermute(tok_send, axes, route_three))

    def across(values, bit):
        return lax.ppermute(values, "plane", [(i, i ^ bit) for i in range(planes)])

    def quarters(keep, send, first, second, label):
        rows = keep.shape[1] // 2
        bits = {8: 1, 9: 2}
        keep, send = kernel(
            functools.partial(add_first, second),
            "add_first_" + label,
            [((2, rows, width), BF)] * 2,
            [scal, keep, across(send, bits[first])],
            [pltpu.VMEM((2, 2 * rows, width), BF)],
        )
        one, two = kernel(add_second, "add_second_" + label, [((rows, width), BF)] * 2, [keep, across(send, bits[second])])
        routes = [reverse(route) for route in weight_routes()]
        (total,) = kernel(
            sum_four,
            "sum_shards_" + label,
            [((rows, width), BF)],
            [one, *(lax.ppermute(item, axes, route) for item, route in zip((two, one, two), routes))],
        )
        bit = 4
        while bit < planes:
            (total,) = kernel(add_two, "add_planes_" + label, [((rows, width), BF)], [total, across(total, bit)])
            bit *= 2
        total = jnp.where(mine, total, swap(total))
        return [total, across(total, bits[second]), across(total, bits[first]), across(total, 3)]

    wide_sum = found[8]
    bit = 1
    while bit < planes:
        (wide_sum,) = kernel(add_two, "add_wide", [((2 * wide, half), BF)], [wide_sum, across(wide_sum, bit)])
        bit *= 2
    up_two_sum, down_two_sum = kernel(
        finish_wide, "finish_wide", [((wide, wide), F32), ((wide, wide), F32)], [scal, wide_sum, swap(wide_sum)]
    )
    qkv_two_sum, proj_two_sum, piece = kernel(
        finish_two,
        "finish_two",
        [(qkv_two.shape, F32), (proj_two.shape, F32), ((192, width), BF)],
        [scal, *quarters(keep2, send2, 8, 9, "two")],
        [pltpu.VMEM((1152, width), F32)],
    )
    pieces = lax.all_gather(piece, "head", axis=0)
    residual_sum = pieces.reshape(2, 2, 192, width).transpose(1, 2, 0, 3).reshape(width, wide).astype(F32)
    up_one_sum, down_one_sum, small_two = kernel(
        finish_mlp,
        "finish_mlp",
        [(up_one.shape, F32), (down_one.shape, F32), ((64, width), F32)],
        [scal, *quarters(keep_m, send_m, 9, 8, "mlp")],
        [pltpu.VMEM((832, width), F32)],
    )
    qkv_one_sum, proj_one_sum, table_sum, small_one = kernel(
        finish_one,
        "finish_one",
        [(qkv_one.shape, F32), (proj_one.shape, F32), ((8, width), F32), ((64, width), F32)],
        [scal, *quarters(keep1, send1, 8, 9, "one")],
        [pltpu.VMEM((512, width), F32)],
    )

    def small_parts(small):
        lines = small[:27].reshape(27, 3, LANES)[:, :, :HD].transpose(1, 0, 2)
        entries = small[32 : 32 + FR, : 2 * LANES].reshape(FR, 2, LANES)[:, :, :HD].transpose(1, 0, 2)
        return lines, entries

    outs = [found[0]] + [turn_by(found[d], -d) for d in (1, 2, 3)]
    (out_sum,) = kernel(sum_four, "sum_out", [((n2, wide), BF)], outs)
    keep, send = kernel(
        final_rows,
        "final_rows",
        [((n2 // 2, wide), BF), ((n2 // 2, wide), BF)],
        [scal, middle2, out_sum, swap(out_sum)],
    )
    blocks_out = jnp.where(match, keep, lax.ppermute(send, axes, route_three))

    pools_one_sum, memory_one_sum = small_parts(small_one)
    pools_two_sum, memory_two_sum = small_parts(small_two)
    bins = table_one.shape[1]
    return (
        blocks_out,
        tokens_grad,
        small_one[42],
        qkv_one_sum,
        pools_one_sum,
        memory_one_sum,
        table_sum[0:1, :bins],
        proj_one_sum,
        small_one[40],
        up_one_sum,
        down_one_sum,
        small_one[41],
        qkv_two_sum,
        residual_sum,
        pools_two_sum,
        memory_two_sum,
        table_sum[1:3, :bins],
        proj_two_sum,
        small_two[40:42].reshape(-1),
        up_two_sum,
        down_two_sum,
    )


def solution(mesh):
    planes = mesh.shape["dp"] // 2
    fine = Mesh(mesh.devices.reshape(planes, 2, mesh.shape["head"]), ("plane", "core", "head"))
    dp = ("plane", "core")
    rows = P(("plane", "core", "head"), None)
    columns, lines, free = P(None, "head"), P("head", None), P()
    in_specs = (
        rows, rows, free, P(dp, None),
        free, columns, free, free, lines, lines, free, columns, lines,
        free, columns, free, free, free, lines, lines, free, columns, lines,
    )
    out_specs = (
        rows, rows,
        free, columns, free, free, lines, lines, free, columns, lines,
        free, columns, free, free, free, lines, lines, free, columns, lines,
    )
    return jax.shard_map(
        functools.partial(local, planes), mesh=fine, in_specs=in_specs, out_specs=out_specs, check_vma=False
    )
```

```python
import functools

import jax
import jax.numpy as jnp
import numpy as np
from jax import lax
from jax.experimental import pallas as pl
from jax.experimental.pallas import tpu as pltpu
from jax.sharding import Mesh, PartitionSpec as P

HD = 96
FR = 4
SIDE = 10
LANES = 128
GRID = SIDE + 2
SLAB = GRID * 2 * FR
PADDED = GRID * SLAB
EPSILON = 1e-06
NEGATIVE = -1e30
SCALE = HD**-0.5
GELU_A = float(np.sqrt(2.0 / np.pi))
GELU_B = 0.044715

BF = jnp.bfloat16
F32 = jnp.float32


def nn(a, b):
    return lax.dot_general(a, b, (((1,), (0,)), ((), ())), preferred_element_type=F32)


def nt(a, b):
    return lax.dot_general(a, b, (((1,), (1,)), ((), ())), preferred_element_type=F32)


def tn(a, b):
    return lax.dot_general(a, b, (((0,), (0,)), ((), ())), preferred_element_type=F32)


def iota(shape, dim):
    return lax.broadcasted_iota(jnp.int32, shape, dim)


def widen(values):
    fill = jnp.zeros((values.shape[0], LANES - values.shape[1]), values.dtype)
    return jnp.concatenate([values, fill], axis=1)


def split(values):
    high = values.astype(BF)
    return high, (values - high.astype(F32)).astype(BF)


def norm_parts(values):
    centered = values - jnp.mean(values, axis=-1, keepdims=True)
    variance = jnp.mean(centered * centered, axis=-1, keepdims=True)
    scale = lax.rsqrt(variance + EPSILON)
    return centered * scale, scale


def norm_back(grad, values, gain):
    unit, scale = norm_parts(values)
    scaled = grad * gain
    mean_one = jnp.mean(scaled, axis=-1, keepdims=True)
    mean_two = jnp.mean(scaled * unit, axis=-1, keepdims=True)
    gain_grad = jnp.sum(grad * unit, axis=0, keepdims=True)
    return scale * (scaled - mean_one - unit * mean_two), gain_grad


def gelu_parts(values):
    square = values * values
    bent = jnp.tanh(GELU_A * values * (1.0 + GELU_B * square))
    half = 0.5 * (1.0 + bent)
    slope = half + 0.5 * values * (1.0 - bent * bent) * GELU_A * (1.0 + 3.0 * GELU_B * square)
    return values * half, slope


def pick(flag, one, two):
    return jnp.where(flag, one, two)


def token_rows(half):
    rows, cols = iota((FR * SIDE * SIDE, 2 * SIDE * SIDE), 0), iota((FR * SIDE * SIDE, 2 * SIDE * SIDE), 1)
    frame, place = rows % FR - 2 * half, rows // FR
    return jnp.where((frame >= 0) & (frame < 2) & (cols == SIDE * SIDE * frame + place), 1.0, 0.0).astype(BF)


def half_rows(half, area):
    rows, cols = iota((2 * area, FR * area), 0), iota((2 * area, FR * area), 1)
    upper = jnp.where(rows >= area, 1, 0)
    return jnp.where(cols == FR * (rows - area * upper) + 2 * half + upper, 1.0, 0.0).astype(BF)


def cells():
    small = SIDE // 2
    shape = (FR * small * small, FR * SIDE * SIDE)
    rows, cols = iota(shape, 0), iota(shape, 1)
    place, spot = rows // FR, cols // FR
    match = (
        (rows % FR == cols % FR)
        & (place // small == spot // (2 * SIDE))
        & (place % small == (spot % SIDE) // 2)
    )
    return jnp.where(match, 1.0, 0.0).astype(BF)


def fill_weights(wide, pools, field, flip):
    for tap in range(27):
        source = 26 - tap if flip else tap
        line = widen(pools[field, source : source + 1, :])
        wide[8 * tap : 8 * tap + 8, :] = jnp.broadcast_to(line, (8, LANES))


def fill_rolled(source, before, after, blocks):
    values = source.reshape(blocks, 8, LANES)
    lane = iota((blocks, 8, LANES), 1)
    before[0 : 8 * blocks, :] = jnp.where(lane >= 2, pltpu.roll(values, 2, 1), 0.0).reshape(8 * blocks, LANES)
    after[0 : 8 * blocks, :] = jnp.where(lane < 6, pltpu.roll(values, 6, 1), 0.0).reshape(8 * blocks, LANES)


def load_row(ref, index):
    return ref[pl.ds(pl.multiple_of(SLAB * index, SLAB), SLAB), :].reshape(GRID, 8, LANES)


def conv_rows(sources, wide, result, stride):
    count = SIDE // stride

    def one_row(i, carry):
        sums = [jnp.zeros((8, LANES), F32) for _ in range(count)]
        for a in range(3):
            for b in range(3):
                line = load_row(sources[a], stride * i + b)
                for e in range(3):
                    tap = 9 * a + 3 * b + e
                    weight = wide[8 * tap : 8 * tap + 8, :]
                    for j in range(count):
                        sums[j] = sums[j] + weight * line[stride * j + e]
        for j in range(count):
            result[pl.ds(pl.multiple_of(8 * count * i + 8 * j, 8), 8), :] = sums[j]
        return carry

    lax.fori_loop(0, count, one_row, 0)


def conv_back_two(sources, wide, result):
    count = SIDE // 2

    def one_row(m, carry):
        even = [jnp.zeros((8, LANES), F32) for _ in range(SIDE)]
        odd = [jnp.zeros((8, LANES), F32) for _ in range(SIDE)]
        for a in range(3):
            now, later = load_row(sources[2 - a], m + 1), load_row(sources[2 - a], m + 2)
            for sums, b, line in ((even, 1, now), (odd, 0, later), (odd, 2, now)):
                taps = [wide[8 * (9 * a + 3 * b + e) : 8 * (9 * a + 3 * b + e) + 8, :] for e in range(3)]
                for n in range(count):
                    sums[2 * n] = sums[2 * n] + taps[1] * line[n + 1]
                    sums[2 * n + 1] = sums[2 * n + 1] + taps[0] * line[n + 2] + taps[2] * line[n + 1]
        for j in range(SIDE):
            result[pl.ds(pl.multiple_of(16 * SIDE * m + 8 * j, 8), 8), :] = even[j]
            result[pl.ds(pl.multiple_of(16 * SIDE * m + 8 * SIDE + 8 * j, 8), 8), :] = odd[j]
        return carry

    lax.fori_loop(0, count, one_row, 0)


def conv_weight(sources, grads, totals, stride):
    count = SIDE // stride
    totals[...] = jnp.zeros((27 * 8, LANES), F32)

    def one_row(i, carry):
        cotangent = load_row(grads, i + 1)
        for a in range(3):
            for b in range(3):
                line = load_row(sources[a], stride * i + b)
                for e in range(3):
                    spot = 8 * (9 * a + 3 * b + e)
                    total = totals[spot : spot + 8, :]
                    for j in range(count):
                        total = total + line[stride * j + e] * cotangent[j + 1]
                    totals[spot : spot + 8, :] = total
        return carry

    lax.fori_loop(0, count, one_row, 0)


def weights_of_rows(totals):
    return jnp.sum(totals[...].reshape(27, 8, LANES), axis=1)


def put_rows(target, values, head, count):
    for i in range(count):
        start = ((i + 1) * GRID + 1) * 8 + head
        target[pl.ds(start, FR * count, stride=2), :] = values[FR * count * i : FR * count * (i + 1), :]


def pairs_of(heads):
    return [((0, 0), (1, 0))] if heads == 2 else [((0, 0), (0, 1)), ((1, 0), (1, 1))]


def pack_heads(lines, turn):
    half = len(lines) // 2
    sides = [jnp.concatenate([line[:, :HD] for line in lines[half * i : half * (i + 1)]], axis=1) for i in range(2)]
    flag = turn == 1
    return jnp.concatenate([pick(flag, sides[1], sides[0]), pick(flag, sides[0], sides[1])], axis=1)


def unpack_heads(values, turn):
    heads = values.shape[1] // HD
    lines = [values[:, HD * head : HD * (head + 1)] for head in range(heads)]
    flag, half = turn == 1, heads // 2
    return [widen(pick(flag, lines[(head + half) % heads], lines[head])) for head in range(heads)]


def front_body(heads, turn, strides, normed, weights, pools, memory, fields, pooled, passed, work):
    before, after, wide, result, held, sent = work
    copies = []
    lines = [nn(normed, weights[s][...]) for s in range(2)]
    for field in range(3):
        fill_weights(wide, pools, field, False)
        stride = strides[field]
        count = SIDE // stride
        for number, pair in enumerate(pairs_of(heads)):
            spot = field * (heads // 2) + number
            group = held.at[spot]
            group[...] = jnp.zeros((PADDED, LANES), F32)
            for head, (slot, place) in enumerate(pair):
                start = HD * (3 * place + field)
                put_rows(group, widen(lines[slot][:, start : start + HD]), head, SIDE)
            copies.append(pltpu.make_async_copy(group, fields.at[spot], sent.at[spot]))
            copies[-1].start()
            fill_rolled(group[...], before, after, PADDED // 8)
            conv_rows((before, group, after), wide, result, stride)
            for head in range(2):
                pooled[field][2 * number + head] = result[pl.ds(head, FR * count * count, stride=2), :]
    area = (SIDE // strides[1]) ** 2
    for which in range(2):
        lines = []
        for head in range(heads):
            total = jnp.zeros((area, LANES), F32)
            for t in range(FR):
                line = widen(memory[which, t : t + 1, :])
                total = total + line * pooled[1 + which][head, pl.ds(t, area, stride=FR), :]
            lines.append(total)
        passed[which] = pack_heads(lines, turn).astype(BF)
    for copy in copies:
        copy.wait()


def front_one(scal, own, first, second, gain, wa, wb, pools, memory, x_out, normed_out, g_out, fields, qp, kp, vp, passed, *work):
    match, turn = scal[0] == 1, scal[1] == 1
    near = pick(match, own[...], first[...])
    far = pick(match, first[...], second[...])
    low, high = pick(turn, far, near), pick(turn, near, far)
    count, area = 2 * SIDE * SIDE, (SIDE // 2) ** 2
    rows = nn(token_rows(0), low[:count]) + nn(token_rows(1), high[:count])
    x_out[...] = rows.astype(BF)
    turns = [half_rows(half, area) for half in range(2)]
    for column in range(2):
        spots = slice(count + 2 * area * column, count + 2 * area * (column + 1))
        g_out[column] = (tn(turns[0], low[spots]) + tn(turns[1], high[spots])).astype(BF)
    normed = (norm_parts(rows)[0] * gain[...]).astype(BF)
    normed_out[...] = normed
    front_body(2, scal[1], (1, 2, 2), normed, (wa, wb), pools, memory, fields, (qp, kp, vp), passed, work)


def front_two(scal, middle, part, other, gain, wa, wb, residual, pools, memory, x_out, normed_out, skip, fields, qp, kp, vp, passed, *work):
    rows = middle[...] + (part[...].astype(F32) + other[...].astype(F32))
    x_out[...] = rows
    normed = (norm_parts(rows)[0] * gain[...]).astype(BF)
    normed_out[...] = normed
    high, low = split(nn(cells(), normed))
    skip[...] = 0.25 * (nn(high, residual[...]) + nn(low, residual[...]))
    front_body(4, scal[1], (2, 1, 1), normed, (wa, wb), pools, memory, fields, (qp, kp, vp), passed, work)


def table_of(shards, block, slot, place):
    line = shards[slot][HD : HD + 16, :].astype(F32)
    row = 3 * (place if block == 0 else 1 + place)
    return line[row : row + 1, :] + line[row + 1 : row + 2, :] + line[row + 2 : row + 3, :]


def own_bias(bins, table):
    values = jnp.zeros(bins.shape, F32)
    for number in range(2 * FR - 1):
        values = jnp.where(bins == number, table[:, number : number + 1], values)
    return values


def far_bias(table, offset):
    lanes = iota(table.shape, 1)
    return jnp.sum(jnp.where(lanes == offset + 2 * FR - 1, table, 0.0), axis=1, keepdims=True)


def probs_of(scal, bins, table, query, keys):
    parts = [nt(query, keys[0]) * SCALE + own_bias(bins, table)]
    for j in range(2):
        raw = nt(query, keys[1 + j]) * SCALE + far_bias(table, scal[4 + j])
        parts.append(jnp.where(scal[2 + j] == 1, raw, NEGATIVE))
    top = functools.reduce(jnp.maximum, [jnp.max(part, axis=1, keepdims=True) for part in parts])
    parts = [jnp.exp(part - top) for part in parts]
    total = sum(jnp.sum(part, axis=1, keepdims=True) for part in parts)
    return [part / total for part in parts]


def heads_of(heads, block):
    return [(slot, place) for slot in range(2) for place in range(heads // 2)]


def attend(block, scal, ta, tb, qp, kp, vp, near, far, wa, wb, rows_out, part_out):
    heads = qp.shape[0]
    shards, weights = (ta, tb), (wa, wb)
    shape = (qp.shape[1], kp.shape[1])
    bins = iota(shape, 0) % FR - iota(shape, 1) % FR + FR - 1
    total = jnp.zeros(part_out.shape, F32)
    nears, fars = ([unpack_heads(item[which], scal[1]) for which in range(2)] for item in (near, far))
    for head, (slot, place) in enumerate(heads_of(heads, block)):
        table = table_of(shards, block, slot, place)
        pool = qp[head]
        keys = (kp[head].astype(BF), nears[0][head], fars[0][head])
        values = (vp[head].astype(BF), nears[1][head], fars[1][head])
        probs = probs_of(scal, bins, table, pool.astype(BF), keys)
        mixture = sum(nn(p.astype(BF), v) for p, v in zip(probs, values))
        line = (mixture + pool).astype(BF)
        rows_out[head] = line
        total = total + nn(line[:, :HD], weights[slot][HD * place : HD * place + HD, :])
    part_out[...] = total.astype(BF)


def attend_back(block, scal, ta, tb, qp, kp, vp, near, far, wa, wb, rows, middle_grad, dq, dk, dv, d_near, d_far, proj_grad, table_grad):
    heads = qp.shape[0]
    shards, weights = (ta, tb), (wa, wb)
    shape = (qp.shape[1], kp.shape[1])
    bins = iota(shape, 0) % FR - iota(shape, 1) % FR + FR - 1
    branch = middle_grad.astype(BF)
    lanes = iota((1, LANES), 1)
    table_lines = []
    nears, fars = ([unpack_heads(item[which], scal[1]) for which in range(2)] for item in (near, far))
    near_lines, far_lines = ([], []), ([], [])
    for head, (slot, place) in enumerate(heads_of(heads, block)):
        table = table_of(shards, block, slot, place)
        weight = weights[slot][HD * place : HD * place + HD, :]
        found = tn(rows[head][:, :HD], branch).astype(BF)
        for column in range(proj_grad.shape[1] // (HD * (heads // 2))):
            start = HD * (heads // 2) * column + HD * place
            proj_grad[slot, start : start + HD, :] = found[:, proj_grad.shape[2] * column : proj_grad.shape[2] * (column + 1)]
        grad = widen(nt(branch, weight).astype(BF))
        query = qp[head].astype(BF)
        keys = (kp[head].astype(BF), nears[0][head], fars[0][head])
        values = (vp[head].astype(BF), nears[1][head], fars[1][head])
        probs = probs_of(scal, bins, table, query, keys)
        grad_probs = [nt(grad, v) for v in values]
        inner = sum(jnp.sum(p * d, axis=1, keepdims=True) for p, d in zip(probs, grad_probs))
        low = [(p * (d - inner)).astype(BF) for p, d in zip(probs, grad_probs)]
        dq[head] = sum(nn(s, k) for s, k in zip(low, keys)) * SCALE + grad.astype(F32)
        key_grads = [tn(s, query) * SCALE for s in low]
        value_grads = [tn(p.astype(BF), grad) for p in probs]
        dk[head], dv[head] = key_grads[0], value_grads[0]
        for which, grads in enumerate((key_grads, value_grads)):
            near_lines[which].append(grads[1])
            far_lines[which].append(grads[2])
        score = low[0].astype(F32)
        line = jnp.zeros((1, LANES), F32)
        for number in range(2 * FR - 1):
            column = jnp.sum(jnp.where(bins == number, score, 0.0), axis=0, keepdims=True)
            line = line + jnp.where(lanes == number, jnp.sum(column, axis=1, keepdims=True), 0.0)
        for j in range(2):
            column = jnp.sum(low[1 + j].astype(F32), axis=0, keepdims=True)
            value = jnp.sum(column, axis=1, keepdims=True)
            line = line + jnp.where(lanes == scal[4 + j] + 2 * FR - 1, value, 0.0)
        table_lines.append(line)
    for which in range(2):
        d_near[which] = pack_heads(near_lines[which], scal[1]).astype(BF)
        d_far[which] = pack_heads(far_lines[which], scal[1]).astype(BF)
    for head, line in enumerate(table_lines):
        table_grad[head : head + 1, :] = line


def field_back(heads, turn, strides, fields, pooled, grads, near, far, pools, memory, pools_grad, memory_grad, work):
    before, after, wide, result, grid, grid_before, grid_after, totals, rows, held, arrived = work
    half = heads // 2
    copies = [pltpu.make_async_copy(fields.at[i], held.at[i], arrived.at[i]) for i in range(3 * half)]
    for copy in copies:
        copy.start()
    back = {}
    area = (SIDE // strides[1]) ** 2
    for field in range(3):
        stride = strides[field]
        count = SIDE // stride
        fill_weights(wide, pools, field, stride == 1)
        weight_sum = jnp.zeros((27, LANES), F32)
        memory_lines = [jnp.zeros((1, LANES), F32) for _ in range(FR)]
        if field:
            passed = unpack_heads(near[field - 1].astype(F32) + far[field - 1].astype(F32), turn)
        for number, pair in enumerate(pairs_of(heads)):
            grid[...] = jnp.zeros((PADDED, LANES), F32)
            for place in range(2):
                head = 2 * number + place
                if field == 0:
                    put_rows(grid, grads[0][head], place, count)
                else:
                    cotangent = passed[head]
                    for t in range(FR):
                        spot = pl.ds(t, area, stride=FR)
                        line = widen(memory[field - 1, t : t + 1, :])
                        rows[spot, :] = grads[field][head, spot, :] + line * cotangent
                        product = pooled[field - 1][head, spot, :] * cotangent
                        memory_lines[t] = memory_lines[t] + jnp.sum(product, axis=0, keepdims=True)
                    put_rows(grid, rows[0 : FR * area, :], place, count)
            group = held.at[field * half + number]
            copies[field * half + number].wait()
            fill_rolled(group[...], before, after, PADDED // 8)
            conv_weight((before, group, after), grid, totals, stride)
            weight_sum = weight_sum + weights_of_rows(totals)
            fill_rolled(grid[...], grid_before, grid_after, PADDED // 8)
            if stride == 1:
                conv_rows((grid_before, grid, grid_after), wide, result, 1)
            else:
                conv_back_two((grid_before, grid, grid_after), wide, result)
            for place, key in enumerate(pair):
                back[key + (field,)] = result[pl.ds(place, FR * SIDE * SIDE, stride=2), :][:, :HD]
        pools_grad[field, 0:27, :] = weight_sum
        if field:
            for t in range(FR):
                memory_grad[field - 1, t : t + 1, :] = memory_lines[t]
    outs = []
    for slot in range(2):
        columns = [back[(slot, place, field)] for place in range(half) for field in range(3)]
        outs.append(jnp.concatenate(columns, axis=1).astype(BF))
    return outs


def mlp_one(scal, x, part, other, gain, wa, wb, middle_out, normed_out, part_out):
    weights = (wa, wb)
    middle = x[...].astype(F32) + (part[...].astype(F32) + other[...].astype(F32))
    middle_out[...] = middle
    normed = (norm_parts(middle)[0] * gain[...]).astype(BF)
    normed_out[...] = normed
    size = normed.shape[1]
    total = jnp.zeros(part_out.shape, F32)
    for slot in range(2):
        hidden = gelu_parts(nn(normed, weights[slot][:size, :]))[0].astype(BF)
        total = total + nn(hidden, weights[slot][size:, :])
    part_out[...] = total.astype(BF)


def middle_two(scal, skip, part, other, gain, g, middle_out, normed_out, half_out):
    middle = skip[...] + (part[...].astype(F32) + other[...].astype(F32))
    middle_out[...] = middle
    normed_out[...] = (norm_parts(middle)[0] * gain[...]).astype(BF)
    width = half_out.shape[2]
    half_out[0] = normed_out[:, pl.ds(pl.multiple_of(scal[7] * width, LANES), width)]
    half_out[1] = g[scal[7]]


def mlp_two(scal, own, own_grad, *refs):
    halves, others = refs[0:3], refs[3:6]
    up_ref, down_ref = refs[6:8]
    keep, give = refs[8:10]
    packed, board, lines = refs[10:13]
    width = up_ref.shape[1] // 2
    core = scal[7]
    start = pl.multiple_of(core * width, LANES)
    rest = pl.multiple_of((1 - core) * width, LANES)
    up, down = up_ref[:, pl.ds(start, width)], down_ref[pl.ds(start, width), :]
    board[0, 0] = own[...]
    for column in range(2):
        board[0, 1, :, width * column : width * (column + 1)] = own_grad[column]
    for d in range(3):
        for which in range(2):
            board[d + 1, which, :, pl.ds(start, width)] = halves[d][which]
            board[d + 1, which, :, pl.ds(rest, width)] = others[d][which]
    up_total = jnp.zeros(up.shape, F32)
    down_total = jnp.zeros(down.shape, F32)
    for d in range(4):
        rows, grad = board[d, 0], board[d, 1]
        value, slope = gelu_parts(nn(rows, up))
        hidden = value.astype(BF)
        lines[0] = nn(hidden, down)
        up_low = (nt(grad, down) * slope).astype(BF)
        lines[1] = nt(up_low, up)
        for which in range(2):
            keep[d, which] = lines[which, :, pl.ds(start, width)].astype(BF)
            give[d, which] = lines[which, :, pl.ds(rest, width)].astype(BF)
        up_total = up_total + tn(rows, up_low)
        down_total = down_total + tn(hidden, grad)
    size = up.shape[0]
    packed[0:size, :] = up_total.astype(BF)
    packed[size : size + width, :] = down_total[:, :width].astype(BF)
    packed[size + width : size + 2 * width, :] = down_total[:, width:].astype(BF)


def quarter_of(scal, peer):
    one = 1 - scal[8] if peer % 2 else scal[8]
    two = 1 - scal[9] if peer // 2 else scal[9]
    return one + 2 * two


def cut(scal, full, parts):
    rows = parts[0].shape[1]
    for peer in range(4):
        spots = pl.ds(pl.multiple_of(quarter_of(scal, peer) * rows, 16), rows)
        for slot in range(2):
            parts[peer][slot] = full[slot, spots, :]


def sum_planes(*refs):
    one, two = refs[-2:]
    start = 0
    for number in range(len(refs) // 4):
        parts = refs[4 * number : 4 * number + 4]
        rows = parts[0].shape[1]
        for slot, out in ((0, one), (1, two)):
            total = (parts[0][slot].astype(F32) + parts[1][slot].astype(F32)) + (
                parts[2][slot].astype(F32) + parts[3][slot].astype(F32)
            )
            out[start : start + rows, :] = total.astype(BF)
        start += rows


def gather_parts(scal, parts, start, full):
    rows = full.shape[0] // 4
    for peer, part in enumerate(parts):
        spots = pl.ds(pl.multiple_of(quarter_of(scal, peer) * rows, 16), rows)
        full[spots, :] = part[start : start + rows, :].astype(F32)


def put_totals(full, start, pools, memory):
    for field in range(3):
        pools[field] = full[start : start + 27, LANES * field : LANES * field + HD]
    for which in range(2):
        memory[which] = full[start + 32 : start + 32 + FR, LANES * which : LANES * which + HD]


def stack_two(scal, own, other, out):
    turn = scal[1]
    out[turn], out[1 - turn] = own[...], other[...]


def finish_residual(scal, own, own_far, other, other_far, out):
    size, width = own.shape[1:]
    upper = scal[10] // 2
    for core, near, far in ((scal[7], own, own_far), (1 - scal[7], other, other_far)):
        for pair, source in ((upper, near), (1 - upper, far)):
            for parity in range(2):
                rows = pl.ds(pl.multiple_of(2 * size * parity + size * core, 16), size)
                columns = pl.ds(pl.multiple_of(width * pair, LANES), width)
                out[rows, columns] = source[parity].astype(F32)


def take_piece(scal, a, b, c, d, piece):
    half = piece.shape[0]
    start = pl.multiple_of(96 + half * scal[7], 16)
    for peer, part in enumerate((a, b, c, d)):

        @pl.when(quarter_of(scal, peer) == 3)
        def _():
            piece[...] = part[pl.ds(start, half), :]


def finish_two(scal, a, b, c, d, qkv, proj, up, down, pools, memory, gain, full, full_mlp):
    parts = (a, b, c, d)
    gather_parts(scal, parts, 0, full)
    gather_parts(scal, parts, full.shape[0] // 4, full_mlp)
    width = full.shape[1]
    qkv[:, :width] = full[0:384, :]
    qkv[0:192, width:] = full[384:576, :192]
    qkv[192:384, width:] = full[384:576, 192:]
    proj[:, :width] = full[576:768, :]
    proj[:, width:] = full[768:960, :]
    up[...] = full_mlp[0:384, :]
    down[...] = full_mlp[384:768, :]
    put_totals(full_mlp, 768, pools, memory)
    gain[:, :width], gain[:, width:] = full_mlp[808:809, :], full_mlp[809:810, :]


def finish_one(scal, a, b, c, d, qkv, proj, table, second_table, pools, memory, gain, second_gain, third_gain, full):
    gather_parts(scal, (a, b, c, d), 0, full)
    qkv[...] = full[0:288, :].T
    proj[...] = full[288:384, :]
    bins = table.shape[1]
    table[...] = full[384:385, :bins]
    second_table[...] = full[385:387, :bins]
    put_totals(full, 400, pools, memory)
    second_gain[...] = full[440:441, :]
    third_gain[...] = full[441:442, :]
    gain[...] = full[442:443, :]


def finish_wide(scal, own, other, up, down):
    first = scal[7] == 0
    one = jnp.where(first, own[...], other[...]).astype(F32)
    two = jnp.where(first, other[...], own[...]).astype(F32)
    size = up.shape[0]
    width = size // 2
    up[:, :width], up[:, width:] = one[:size, :], two[:size, :]
    down[:width, :width], down[:width, width:] = one[size : size + width, :], one[size + width :, :]
    down[width:, :width], down[width:, width:] = two[size : size + width, :], two[size + width :, :]


def add_cores(keep, other, *outs):
    for d in range(4):
        outs[d][...] = (keep[d].astype(F32) + other[d].astype(F32)).astype(BF)


def whole_columns(scal, own, other):
    first = scal[7] == 0
    return jnp.concatenate([pick(first, own, other), pick(first, other, own)], axis=1)


def add_two(one, two, out):
    out[...] = (one[...].astype(F32) + two[...].astype(F32)).astype(BF)


def sum_four(a, b, c, d, out):
    total = (a[...].astype(F32) + b[...].astype(F32)) + (c[...].astype(F32) + d[...].astype(F32))
    out[...] = total.astype(BF)


def back_attend_two(scal, part, other, g, middle, gain, normed, *refs):
    ins, outs = refs[0:10], refs[10:]
    final = (middle[...] + whole_columns(scal, part[0], other[0]).astype(F32)).astype(BF)
    area = (SIDE // 2) ** 2
    outs[10][...] = nn(half_rows(scal[1], area), final).astype(BF)
    outs[11][...] = nn(half_rows(1 - scal[1], area), final).astype(BF)
    grad, gain_grad = norm_back(whole_columns(scal, part[1], other[1]).astype(F32), middle[...], gain[...])
    middle_grad = jnp.concatenate([g[0], g[1]], axis=1).astype(F32) + grad
    outs[0][...] = middle_grad
    outs[1][...] = gain_grad
    width = outs[9].shape[2]
    linear = (0.25 * outs[0][:, pl.ds(pl.multiple_of(scal[7] * width, LANES), width)]).astype(BF)
    high, low = split(nn(cells(), normed[...]))
    found = (tn(high, linear) + tn(low, linear)).astype(BF)
    size = outs[9].shape[1]
    turned = scal[1] == 1
    outs[9][0] = pick(turned, found[size:], found[:size])
    outs[9][1] = pick(turned, found[:size], found[size:])
    attend_back(1, scal, *ins, middle_grad, *outs[2:9])


def put_small(small, pools_grad, memory_grad):
    small[...] = jnp.zeros(small.shape, F32)
    for field in range(3):
        small[0:27, LANES * field : LANES * (field + 1)] = pools_grad[field, 0:27, :]
    for which in range(2):
        small[32 : 32 + FR, LANES * which : LANES * (which + 1)] = memory_grad[which]


def back_front_two(scal, middle_grad, normed_ref, fields, kp, vp, dq, dk, dv, near, far, wa, wb, residual, pools, memory, proj_grad, residual_grad, gain_grad, part_out, keep, one, two, three, small, pools_grad, memory_grad, full, *work):
    weights = (wa, wb)
    normed = normed_ref[...]
    backs = field_back(4, scal[1], (2, 1, 1), fields, (kp, vp), (dq, dk, dv), near, far, pools, memory, pools_grad, memory_grad, work)
    total = jnp.zeros(part_out.shape, F32)
    width = full.shape[2]
    columns = pl.ds(pl.multiple_of(scal[7] * width, LANES), width)
    linear = (0.25 * middle_grad[:, columns]).astype(BF)
    cell = cells()
    for slot in range(2):
        found = tn(normed, backs[slot]).astype(BF)
        full[slot, 0:384, :] = found[:, :width]
        full[slot, 384:576, :] = jnp.concatenate([found[0:192, width:], found[192:384, width:]], axis=1)
        full[slot, 576:960, :] = proj_grad[slot]
        full[slot, 960:1152, :] = residual_grad[slot]
        total = total + nt(backs[slot], weights[slot][...])
    cut(scal, full, (keep, one, two, three))
    high, low = split(nt(linear, residual[:, columns]))
    part_out[...] = (total + tn(cell, high) + tn(cell, low)).astype(BF)
    put_small(small, pools_grad, memory_grad)
    small[40:41, :] = 0.5 * gain_grad[:, :width]
    small[41:42, :] = 0.5 * gain_grad[:, width:]


def back_mlp_one(scal, part, other, x, gain, normed_ref, wa, wb, small, small_other, grad_out, part_out, gain_grad_ref, keep, one, two, three, full):
    weights = (wa, wb)
    grad, gain_grad = norm_back(part[...].astype(F32) + other[...].astype(F32), x[...], gain[...])
    grad_out[...] = grad
    gain_grad_ref[...] = gain_grad
    branch = grad.astype(BF)
    normed = normed_ref[...]
    total = jnp.zeros(part_out.shape, F32)
    whole = (small[...] + small_other[...]).astype(BF)
    size = normed.shape[1]
    for slot in range(2):
        up, down = weights[slot][:size, :], weights[slot][size:, :]
        value, slope = gelu_parts(nn(normed, up))
        up_low = (nt(branch, down) * slope).astype(BF)
        full[slot, 0:size, :] = tn(normed, up_low).astype(BF)
        full[slot, size : 2 * size, :] = tn(value.astype(BF), branch).astype(BF)
        full[slot, 2 * size : 2 * size + 64, :] = whole
        total = total + nt(up_low, up)
    part_out[...] = total.astype(BF)
    cut(scal, full, (keep, one, two, three))


def back_attend_one(scal, part, other, g, middle, gain, *refs):
    ins, outs = refs[0:10], refs[10:]
    grad, gain_grad = norm_back(part[...].astype(F32) + other[...].astype(F32), middle[...], gain[...])
    middle_grad = g[...] + grad
    outs[0][...] = middle_grad
    outs[1][...] = gain_grad
    attend_back(0, scal, *ins, middle_grad, *outs[2:9])


def back_front_one(scal, normed_ref, fields, kp, vp, dq, dk, dv, near, far, wa, wb, pools, memory, gain_two_grad, gain_three_grad, qkv_grad, part_out, small, pools_grad, memory_grad, *work):
    weights = (wa, wb)
    normed = normed_ref[...]
    backs = field_back(2, scal[1], (1, 2, 2), fields, (kp, vp), (dq, dk, dv), near, far, pools, memory, pools_grad, memory_grad, work)
    total = jnp.zeros(part_out.shape, F32)
    for slot in range(2):
        qkv_grad[slot] = tn(backs[slot], normed).astype(BF)
        total = total + nt(backs[slot], weights[slot][...])
    part_out[...] = total.astype(BF)
    put_small(small, pools_grad, memory_grad)
    small[40:41, :] = 0.5 * gain_two_grad[...]
    small[41:42, :] = 0.5 * gain_three_grad[...]


def back_tokens(scal, part, other, x, gain, middle_grad, qkv_grad, proj_grad, table_one, table_two, small, small_other, keep_rows, send_rows, keep, one, two, three, full):
    grad, gain_grad = norm_back(part[...].astype(F32) + other[...].astype(F32), x[...].astype(F32), gain[...])
    rows = (middle_grad[...] + grad).astype(BF)
    turn = scal[1]
    keep_rows[...] = nn(half_rows(turn, SIDE * SIDE), rows).astype(BF)
    send_rows[...] = nn(half_rows(1 - turn, SIDE * SIDE), rows).astype(BF)
    line = iota((64, 1), 0)
    whole = jnp.where(line == 42, gain_grad, small[...] + small_other[...]).astype(BF)
    for slot in range(2):
        full[slot, 0:288, :] = qkv_grad[slot]
        full[slot, 288:384, :] = proj_grad[slot]
        lines = jnp.concatenate([table_one[slot : slot + 1, :], table_two[2 * slot : 2 * slot + 2, :], jnp.zeros((13, LANES), F32)], axis=0)
        full[slot, 384:400, :] = jnp.concatenate([lines, jnp.zeros((16, 2 * LANES), F32)], axis=1).astype(BF)
        full[slot, 400:464, :] = whole
        full[slot, 464:512, :] = jnp.zeros((48, full.shape[2]), BF)
    cut(scal, full, (keep, one, two, three))


SMEM = pl.BlockSpec(memory_space=pltpu.SMEM)


FAR = pl.BlockSpec(memory_space=pltpu.HBM)
NEAR = pl.BlockSpec(memory_space=pltpu.VMEM)


def moved(body, counts, left, early, late, *refs):
    ins_count, outs_count, work_count = counts
    ins, outs = list(refs[:ins_count]), refs[ins_count : ins_count + outs_count]
    spot = ins_count + outs_count
    saved = refs[spot : spot + len(early) + len(late)]
    spot += len(early) + len(late)
    work = refs[spot : spot + work_count]
    buffers, arrived = refs[spot + work_count : -1], refs[-1]
    brought = [pltpu.make_async_copy(ins[item], buffers[i], arrived.at[i]) for i, item in enumerate(left)]
    first = len(left)
    sent = [pltpu.make_async_copy(ins[item], saved[i], arrived.at[first + i]) for i, item in enumerate(early)]
    for copy in brought + sent:
        copy.start()
    for i, item in enumerate(left):
        brought[i].wait()
        ins[item] = buffers[i]
    body(*ins, *outs, *work)
    first += len(early)
    last = [
        pltpu.make_async_copy(outs[item], saved[len(early) + i], arrived.at[first + i]) for i, item in enumerate(late)
    ]
    for copy in last:
        copy.start()
    for copy in sent + last:
        copy.wait()


def kernel(body, name, outs, ins, work=(), left=(), early=(), late=(), raw=(), far_outs=(), flops=2 * 10**8):
    ins = list(ins)
    in_specs = []
    for number, item in enumerate(ins):
        if number == 0 and item.dtype == jnp.int32:
            in_specs.append(SMEM)
        else:
            in_specs.append(FAR if number in left or number in raw else NEAR)
    results = [jax.ShapeDtypeStruct(shape, kind) for shape, kind in outs]
    extra = [jax.ShapeDtypeStruct(ins[item].shape, ins[item].dtype) for item in early] + [results[item] for item in late]
    size = sum(int(np.prod(item.shape)) * item.dtype.itemsize for item in [*ins, *results, *extra])
    work = list(work)
    count = len(work)
    if left or early or late:
        body = functools.partial(moved, body, (len(ins), len(results), count), tuple(left), tuple(early), tuple(late))
        work += [pltpu.VMEM(ins[number].shape, ins[number].dtype) for number in left]
        work.append(pltpu.SemaphoreType.DMA((len(left) + len(early) + len(late),)))
    return pl.pallas_call(
        body,
        out_shape=tuple(results + extra),
        in_specs=in_specs,
        out_specs=tuple([FAR if number in far_outs else NEAR for number in range(len(results))] + [FAR] * len(extra)),
        scratch_shapes=work,
        name=name,
        cost_estimate=pl.CostEstimate(flops=flops, bytes_accessed=size, transcendentals=0),
        compiler_params=pltpu.CompilerParams(vmem_limit_bytes=(32 if left else 16) << 20),
    )(*ins)


def scratch(*rows):
    return [pltpu.VMEM((count, LANES), F32) for count in rows]


def field_work(heads):
    groups = 3 * heads // 2
    return [pltpu.VMEM((groups, PADDED, LANES), F32), pltpu.SemaphoreType.DMA((groups,))]


FRONT_WORK = (PADDED, PADDED, 216, 800)
BACK_WORK = (PADDED, PADDED, 216, 800, PADDED, PADDED, PADDED, 216, 400)


def after(values, events):
    return lax.optimization_barrier((values, events))


def swap(values):
    return lax.ppermute(values, "core", [(0, 1), (1, 0)])


def cross_route():
    route = []
    for core in range(2):
        low, other = 2 * core, 2 - 2 * core
        route += [(core * 4 + low + i, core * 4 + other + i) for i in range(2)]
    return route


def beside(values):
    return lax.ppermute(values, "head", [(z, z ^ 1) for z in range(4)])


def spread(values, mine):
    one = jnp.where(mine, values, lax.ppermute(values, ("core", "head"), cross_route()))
    return one, beside(one)


def reverse(route):
    return [(end, start) for start, end in route]


def clip_routes(planes, distance):
    def place(clip):
        slot = clip % 4
        return (clip // 4) * 4 + 2 * (slot % 2) + slot // 2

    total = 4 * planes
    return [(place(clip), place(clip + distance)) for clip in range(total) if 0 <= clip + distance < total]


def half_routes():
    def place(core, a, b):
        return core * 4 + 2 * a + b

    one, two, three = [], [], []
    for a in range(2):
        for b in range(2):
            one += [(place(b, a, b), place(1 - b, a, b)), (place(1 - b, a, b), place(1 - b, a, 1 - b))]
            two += [(place(1 - b, a, b), place(b, a, 1 - b))]
            three += [(place(1 - b, a, b), place(b, a, 1 - b))]
    return one, two, three


def turn_by(values, distance):
    return lax.ppermute(values, "head", [(z, (z + distance) % 4) for z in range(4)])


def local(
    planes,
    tokens,
    grad_out,
    video_ids,
    offsets,
    gain_one,
    qkv_one,
    pools_one,
    memory_one,
    table_one,
    proj_one,
    gain_two,
    up_one,
    down_one,
    gain_three,
    qkv_two,
    residual_two,
    pools_two,
    memory_two,
    table_two,
    proj_two,
    gain_four,
    up_two,
    down_two,
):
    plane, core, head = lax.axis_index("plane"), lax.axis_index("core"), lax.axis_index("head")
    upper, turn = head // 2, head % 2
    clip = 4 * plane + 2 * turn + upper
    match = core == turn
    mine = head // 2 == core
    both = jnp.where(match, offsets, swap(offsets))
    pair = lax.dynamic_slice_in_dim(both, upper, 1, 0)[0]
    padded = jnp.concatenate([jnp.full((2,), -1, jnp.int32), video_ids])
    window = lax.dynamic_slice_in_dim(padded, clip, 3)
    scal = jnp.stack(
        [
            match.astype(jnp.int32),
            turn.astype(jnp.int32),
            (window[1] == window[2]).astype(jnp.int32),
            (window[0] == window[2]).astype(jnp.int32),
            pair[0],
            pair[1],
            mine.astype(jnp.int32),
            core.astype(jnp.int32),
            (plane % 2).astype(jnp.int32),
            (plane // 2 % 2).astype(jnp.int32),
            head.astype(jnp.int32),
        ]
    )
    gains = [item.reshape(1, -1) for item in (gain_one, gain_two, gain_three, gain_four)]

    tables = jnp.concatenate([table_one, table_two], 0)
    table_high = lax.reduce_precision(tables, 8, 7)
    table_mid = lax.reduce_precision(tables - table_high, 8, 7)
    table_low = tables - table_high - table_mid
    table_rows = jnp.stack([table_high, table_mid, table_low], 1).reshape(9, -1).astype(BF)
    table_rows = jnp.pad(table_rows, ((0, 7), (0, up_one.shape[1] - table_rows.shape[1])))
    proj_bundle = jnp.concatenate([proj_one, table_rows], 0)
    mlp_bundle = jnp.concatenate([up_one, down_one], 0)

    route_one, route_two, route_three = half_routes()
    axes = ("core", "head")
    qkv_one_all = spread(qkv_one, mine)
    half = residual_two.shape[1] // 2
    rows_in = jnp.concatenate([tokens, grad_out[:, :half], grad_out[:, half:]], 0)
    tok_one, tok_two = lax.ppermute(rows_in, axes, route_one), lax.ppermute(rows_in, axes, route_two)
    (proj_bundle, mlp_bundle), (qkv_one_all, tok_one, tok_two) = after(
        (proj_bundle, mlp_bundle), (qkv_one_all, tok_one, tok_two)
    )
    proj_all = spread(proj_bundle, mine)
    mlp_all = spread(mlp_bundle, mine)
    late_qkv, (first,) = after(qkv_two, mlp_all[0:1])
    mlp_all = (first, mlp_all[1])
    qkv_two_all = spread(late_qkv, mine)
    late_proj, (first,) = after(proj_two, qkv_two_all[0:1])
    qkv_two_all = (first, qkv_two_all[1])
    proj_two_all = spread(late_proj, mine)

    width = qkv_one.shape[0]
    wide = residual_two.shape[1]
    n1, n2 = FR * SIDE * SIDE, FR * SIDE * SIDE // 4
    a1, a2 = n2 // FR, n1 // FR

    x1, _, g, fields1, qp1, kp1, vp1, passed1, *saved = kernel(
        front_one,
        "front_one",
        [
            ((n1, width), BF),
            ((n1, width), BF),
            ((2, n2, half), BF),
            ((3, PADDED, LANES), F32),
            ((2, n1, LANES), F32),
            ((2, n2, LANES), F32),
            ((2, n2, LANES), F32),
            ((2, a1, 2 * HD), BF),
        ],
        [scal, rows_in, tok_one, tok_two, gains[0], *qkv_one_all, pools_one, memory_one],
        scratch(*FRONT_WORK) + field_work(2),
        early=(5, 6),
        late=(0, 1, 2, 4, 5, 6),
        far_outs=(3,),
    )
    qkv_one_kept, (x1_kept, normed1, g_kept, qp1_kept, kp1_kept, vp1_kept) = saved[:2], saved[2:]
    places = ("plane", "head")
    near1 = lax.ppermute(passed1, places, clip_routes(planes, 1))
    far1 = lax.ppermute(passed1, places, clip_routes(planes, 2))
    attn1_ins = [*proj_all, qp1, kp1, vp1, near1, far1, *proj_all]
    _, part1, *proj_kept, near1_kept, far1_kept, rows1 = kernel(
        functools.partial(attend, 0),
        "attend_one",
        [((2, n1, LANES), BF), ((n1, width), BF)],
        [scal, *attn1_ins],
        early=(1, 2, 6, 7),
        late=(0,),
    )
    middle1, _, part_mlp1, *mlp_kept, middle1_kept, mlp_normed1 = kernel(
        mlp_one,
        "mlp_one",
        [((n1, width), F32), ((n1, width), BF), ((n1, width), BF)],
        [scal, x1, part1, swap(part1), gains[1], *mlp_all],
        early=(5, 6),
        late=(0, 1),
    )
    _, _, skip, fields2, qp2, kp2, vp2, passed2, *saved = kernel(
        front_two,
        "front_two",
        [
            ((n1, width), F32),
            ((n1, width), BF),
            ((n2, wide), F32),
            ((6, PADDED, LANES), F32),
            ((4, n2, LANES), F32),
            ((4, n1, LANES), F32),
            ((4, n1, LANES), F32),
            ((2, a2, 4 * HD), BF),
        ],
        [scal, middle1, part_mlp1, swap(part_mlp1), gains[2], *qkv_two_all, residual_two, pools_two, memory_two],
        scratch(*FRONT_WORK) + field_work(4),
        early=(5, 6),
        late=(0, 1, 4, 5, 6),
        far_outs=(3,),
    )
    qkv_two_kept, (x2, normed2, qp2_kept, kp2_kept, vp2_kept) = saved[:2], saved[2:]
    near2 = lax.ppermute(passed2, places, clip_routes(planes, 1))
    far2 = lax.ppermute(passed2, places, clip_routes(planes, 2))
    attn2_ins = [*proj_kept, qp2, kp2, vp2, near2, far2, *proj_two_all]
    _, part2, near2_kept, far2_kept, *proj_two_kept, rows2 = kernel(
        functools.partial(attend, 1),
        "attend_two",
        [((4, n2, LANES), BF), ((n2, wide), BF)],
        [scal, *attn2_ins],
        left=(1, 2),
        early=(6, 7, 8, 9),
        late=(0,),
    )
    _, mlp_normed2, own_half, middle2 = kernel(
        middle_two,
        "middle_two",
        [((n2, wide), F32), ((n2, wide), BF), ((2, n2, half), BF)],
        [scal, skip, part2, swap(part2), gains[3], g_kept],
        left=(5,),
        late=(0,),
    )
    halves = [turn_by(own_half, d) for d in (1, 2, 3)]
    found = kernel(
        mlp_two,
        "mlp_two",
        [((4, 2, n2, half), BF)] * 2 + [((2 * wide, half), BF)],
        [scal, mlp_normed2, g_kept, *halves, *(swap(item) for item in halves), up_two, down_two],
        [pltpu.VMEM((4, 2, n2, wide), BF), pltpu.VMEM((2, n2, wide), F32)],
        left=(2, 9, 10),
    )
    sums = kernel(add_cores, "add_cores", [((2, n2, half), BF)] * 4, [found[0], swap(found[1])])
    sums = [sums[0]] + [turn_by(sums[d], -d) for d in (1, 2, 3)]
    (row_sum,) = kernel(sum_four, "sum_rows", [((2, n2, half), BF)], sums)
    middle_grad2, gain_four_grad, dq2, dk2, dv2, d_near2, d_far2, proj_two_grad, table_two_grad, residual_grad, keep, send = kernel(
        back_attend_two,
        "back_attend_two",
        [
            ((n2, wide), F32),
            ((1, wide), F32),
            ((4, n2, LANES), F32),
            ((4, n1, LANES), F32),
            ((4, n1, LANES), F32),
            ((2, a2, 4 * HD), BF),
            ((2, a2, 4 * HD), BF),
            ((2, 4 * HD, width), BF),
            ((4, LANES), F32),
            ((2, 192, half), BF),
            ((n2 // 2, wide), BF),
            ((n2 // 2, wide), BF),
        ],
        [
            scal, row_sum, swap(row_sum), g_kept, middle2, gains[3], normed2,
            *proj_kept, qp2_kept, kp2_kept, vp2_kept, near2_kept, far2_kept, *proj_two_kept, rows2,
        ],
        left=[3, 4, *range(6, 17)],
    )
    near_grad2 = lax.ppermute(d_near2, places, clip_routes(planes, -1))
    far_grad2 = lax.ppermute(d_far2, places, clip_routes(planes, -2))

    def across(values, bit):
        return lax.ppermute(values, "plane", [(i, i ^ bit) for i in range(planes)])

    def peers(parts):
        return [parts[0]] + [across(parts[peer], peer) for peer in (1, 2, 3)]

    def add_wide(values, bit):
        return kernel(add_two, "add_wide", [((2 * wide, half), BF)], [values, across(values, bit)])[0]

    wide_sum = add_wide(found[2], 1)
    (near_grad2, far_grad2), (wide_sum,) = after((near_grad2, far_grad2), (wide_sum,))
    part_back2, *sends2, small2, _, _ = kernel(
        back_front_two,
        "back_front_two",
        [
            ((n1, width), BF),
            *[((2, 288, width), BF)] * 4,
            ((64, width), F32),
            ((3, 32, LANES), F32),
            ((2, FR, LANES), F32),
        ],
        [
            scal, middle_grad2, normed2, fields2, kp2_kept, vp2_kept, dq2, dk2, dv2, near_grad2, far_grad2,
            *qkv_two_kept, residual_two, pools_two, memory_two, proj_two_grad, residual_grad, gain_four_grad,
        ],
        [pltpu.VMEM((2, 1152, width), BF)] + scratch(*BACK_WORK) + field_work(4),
        [2, 4, 5, 11, 12, 13],
        raw=[3],
    )
    received2 = peers(sends2)
    grad1, part_mlp_back, gain_three_grad, *sends_mlp = kernel(
        back_mlp_one,
        "back_mlp_one",
        [((n1, width), F32), ((n1, width), BF), ((1, width), F32)] + [((2, 208, width), BF)] * 4,
        [scal, part_back2, swap(part_back2), x2, gains[2], mlp_normed1, *mlp_kept, small2, swap(small2)],
        [pltpu.VMEM((2, 832, width), BF)],
        [3, 5, 6, 7],
    )
    middle_grad1, gain_two_grad, dq1, dk1, dv1, d_near1, d_far1, proj_one_grad, table_one_grad = kernel(
        back_attend_one,
        "back_attend_one",
        [
            ((n1, width), F32),
            ((1, width), F32),
            ((2, n1, LANES), F32),
            ((2, n2, LANES), F32),
            ((2, n2, LANES), F32),
            ((2, a1, 2 * HD), BF),
            ((2, a1, 2 * HD), BF),
            ((2, HD, width), BF),
            ((2, LANES), F32),
        ],
        [
            scal, part_mlp_back, swap(part_mlp_back), grad1, middle1_kept, gains[1],
            *proj_kept, qp1_kept, kp1_kept, vp1_kept, near1_kept, far1_kept, *proj_kept, rows1,
        ],
        left=[4, *range(6, 16)],
    )
    near_grad1 = lax.ppermute(d_near1, places, clip_routes(planes, -1))
    far_grad1 = lax.ppermute(d_far1, places, clip_routes(planes, -2))
    bit = 2
    while bit < planes:
        wide_sum = add_wide(wide_sum, bit)
        bit *= 2
    received_mlp = peers(sends_mlp)
    (near_grad1, far_grad1), (wide_sum, received2) = after((near_grad1, far_grad1), (wide_sum, received2))
    qkv_one_grad, part_back1, small1, _, _ = kernel(
        back_front_one,
        "back_front_one",
        [((2, 3 * HD, width), BF), ((n1, width), BF), ((64, width), F32), ((3, 32, LANES), F32), ((2, FR, LANES), F32)],
        [
            scal, normed1, fields1, kp1_kept, vp1_kept, dq1, dk1, dv1, near_grad1, far_grad1,
            *qkv_one_kept, pools_one, memory_one, gain_two_grad, gain_three_grad,
        ],
        scratch(*BACK_WORK) + field_work(2),
        [1, 3, 4, 10, 11],
        raw=[2],
    )
    part_back1, (received_mlp,) = after(part_back1, (received_mlp,))
    tok_keep, tok_send, *sends1 = kernel(
        back_tokens,
        "back_tokens",
        [((n1 // 2, width), BF), ((n1 // 2, width), BF)] + [((2, 128, width), BF)] * 4,
        [
            scal, part_back1, swap(part_back1), x1_kept, gains[0], middle_grad1, qkv_one_grad, proj_one_grad,
            table_one_grad, table_two_grad, small1, swap(small1),
        ],
        [pltpu.VMEM((2, 512, width), BF)],
        [3],
    )
    tokens_grad = jnp.where(match, tok_keep, lax.ppermute(tok_send, axes, route_three))

    def combine(body, label, rows, ins, count=1):
        return kernel(body, label, [((rows, width), BF)] * count, ins)

    back_route = reverse(cross_route())
    received1 = peers(sends1)
    rows_two, rows_mlp, rows_one = 288, 208, 128
    one2, two2 = combine(sum_planes, "sum_planes_two", rows_two + rows_mlp, received2 + received_mlp, 2)
    beside2 = beside(two2)
    up_two_sum, down_two_sum = kernel(
        finish_wide, "finish_wide", [((wide, wide), F32), ((wide, wide), F32)], [scal, wide_sum, swap(wide_sum)]
    )
    received1, (up_two_sum, down_two_sum) = after(received1, (up_two_sum, down_two_sum))
    one1, two1 = combine(sum_planes, "sum_planes_one", rows_one, received1, 2)
    beside1 = beside(two1)
    (beside2,), (one1,) = after((beside2,), (one1,))
    (total2,) = combine(add_two, "add_pair_two", rows_two + rows_mlp, [one2, beside2])
    cross2 = lax.ppermute(total2, axes, back_route)
    (beside1,), (total2,) = after((beside1,), (total2,))
    (total1,) = combine(add_two, "add_pair_one", rows_one, [one1, beside1])
    cross1 = lax.ppermute(total1, axes, back_route)
    (cross2,), (total1,) = after((cross2,), (total1,))
    (total2,) = combine(add_two, "add_cross_two", rows_two + rows_mlp, [total2, cross2])
    (total1,) = combine(add_two, "add_cross_one", rows_one, [total1, cross1])
    bit = 4
    while bit < planes:
        (total2,) = combine(add_two, "add_planes_two", rows_two + rows_mlp, [total2, across(total2, bit)])
        (total1,) = combine(add_two, "add_planes_one", rows_one, [total1, across(total1, bit)])
        bit *= 2
    parts2 = peers([jnp.where(mine, total2, swap(total2))] * 4)
    parts1 = peers([jnp.where(mine, total1, swap(total1))] * 4)
    parts2, parts1[0:1] = after(parts2, parts1[0:1])
    (piece,) = kernel(take_piece, "take_piece", [((96, width), BF)], [scal, *parts2])
    small_shapes = [(pools_one.shape, F32), (memory_one.shape, F32)]
    qkv_two_sum, proj_two_sum, up_one_sum, down_one_sum, pools_two_sum, memory_two_sum, gain_four_sum = kernel(
        finish_two,
        "finish_two",
        [(qkv_two.shape, F32), (proj_two.shape, F32), (up_one.shape, F32), (down_one.shape, F32)]
        + small_shapes
        + [((1, wide), F32)],
        [scal, *parts2],
        [pltpu.VMEM((1152, width), F32), pltpu.VMEM((832, width), F32)],
    )
    (qkv_one_sum, proj_one_sum, table_one_sum, table_two_sum, pools_one_sum, memory_one_sum, *gain_sums) = kernel(
        finish_one,
        "finish_one",
        [(qkv_one.shape, F32), (proj_one.shape, F32), (table_one.shape, F32), (table_two.shape, F32)]
        + small_shapes
        + [((1, width), F32)] * 3,
        [scal, *parts1],
        [pltpu.VMEM((512, width), F32)],
    )
    (pieces,) = kernel(stack_two, "stack_pieces", [((2, 96, width), BF)], [scal, piece, beside(piece)])
    far_pieces = lax.ppermute(pieces, "head", [(z, z ^ 2) for z in range(4)])
    (residual_sum,) = kernel(
        finish_residual,
        "finish_residual",
        [(residual_two.shape, F32)],
        [scal, pieces, far_pieces, swap(pieces), swap(far_pieces)],
    )

    blocks_out = jnp.where(match, keep, lax.ppermute(send, axes, route_three))

    return (
        blocks_out,
        tokens_grad,
        gain_sums[0][0],
        qkv_one_sum,
        pools_one_sum,
        memory_one_sum,
        table_one_sum,
        proj_one_sum,
        gain_sums[1][0],
        up_one_sum,
        down_one_sum,
        gain_sums[2][0],
        qkv_two_sum,
        residual_sum,
        pools_two_sum,
        memory_two_sum,
        table_two_sum,
        proj_two_sum,
        gain_four_sum[0],
        up_two_sum,
        down_two_sum,
    )


def solution(mesh):
    planes = mesh.shape["dp"] // 2
    fine = Mesh(mesh.devices.reshape(planes, 2, mesh.shape["head"]), ("plane", "core", "head"))
    dp = ("plane", "core")
    rows = P(("plane", "core", "head"), None)
    columns, lines, free = P(None, "head"), P("head", None), P()
    in_specs = (
        rows, rows, free, P(dp, None),
        free, columns, free, free, lines, lines, free, columns, lines,
        free, columns, free, free, free, lines, lines, free, columns, lines,
    )
    out_specs = (
        rows, rows,
        free, columns, free, free, lines, lines, free, columns, lines,
        free, columns, free, free, free, lines, lines, free, columns, lines,
    )
    return jax.shard_map(
        functools.partial(local, planes), mesh=fine, in_specs=in_specs, out_specs=out_specs, check_vma=False
    )
```

```python
import functools

import jax
import jax.numpy as jnp
import numpy as np
from jax import lax
from jax.experimental import pallas as pl
from jax.experimental.pallas import tpu as pltpu
from jax.sharding import Mesh, PartitionSpec as P

HD = 96
FR = 4
SIDE = 10
LANES = 128
GRID = SIDE + 2
SLAB = GRID * 2 * FR
PADDED = GRID * SLAB
EPSILON = 1e-06
NEGATIVE = -1e30
SCALE = HD**-0.5
GELU_A = float(np.sqrt(2.0 / np.pi))
GELU_B = 0.044715

BF = jnp.bfloat16
F32 = jnp.float32


def nn(a, b):
    return lax.dot_general(a, b, (((1,), (0,)), ((), ())), preferred_element_type=F32)


def nt(a, b):
    return lax.dot_general(a, b, (((1,), (1,)), ((), ())), preferred_element_type=F32)


def tn(a, b):
    return lax.dot_general(a, b, (((0,), (0,)), ((), ())), preferred_element_type=F32)


def iota(shape, dim):
    return lax.broadcasted_iota(jnp.int32, shape, dim)


def widen(values):
    fill = jnp.zeros((values.shape[0], LANES - values.shape[1]), values.dtype)
    return jnp.concatenate([values, fill], axis=1)


def split(values):
    high = values.astype(BF)
    return high, (values - high.astype(F32)).astype(BF)


def norm_parts(values):
    centered = values - jnp.mean(values, axis=-1, keepdims=True)
    variance = jnp.mean(centered * centered, axis=-1, keepdims=True)
    scale = lax.rsqrt(variance + EPSILON)
    return centered * scale, scale


def norm_back(grad, values, gain):
    unit, scale = norm_parts(values)
    scaled = grad * gain
    mean_one = jnp.mean(scaled, axis=-1, keepdims=True)
    mean_two = jnp.mean(scaled * unit, axis=-1, keepdims=True)
    gain_grad = jnp.sum(grad * unit, axis=0, keepdims=True)
    return scale * (scaled - mean_one - unit * mean_two), gain_grad


def gelu_parts(values):
    square = values * values
    bent = jnp.tanh(GELU_A * values * (1.0 + GELU_B * square))
    half = 0.5 * (1.0 + bent)
    slope = half + 0.5 * values * (1.0 - bent * bent) * GELU_A * (1.0 + 3.0 * GELU_B * square)
    return values * half, slope


def pick(flag, one, two):
    return jnp.where(flag, one, two)


def token_rows(half):
    rows, cols = iota((FR * SIDE * SIDE, 2 * SIDE * SIDE), 0), iota((FR * SIDE * SIDE, 2 * SIDE * SIDE), 1)
    frame, place = rows % FR - 2 * half, rows // FR
    return jnp.where((frame >= 0) & (frame < 2) & (cols == SIDE * SIDE * frame + place), 1.0, 0.0).astype(BF)


def half_rows(half, area):
    rows, cols = iota((2 * area, FR * area), 0), iota((2 * area, FR * area), 1)
    upper = jnp.where(rows >= area, 1, 0)
    return jnp.where(cols == FR * (rows - area * upper) + 2 * half + upper, 1.0, 0.0).astype(BF)


def cells():
    small = SIDE // 2
    shape = (FR * small * small, FR * SIDE * SIDE)
    rows, cols = iota(shape, 0), iota(shape, 1)
    place, spot = rows // FR, cols // FR
    match = (
        (rows % FR == cols % FR)
        & (place // small == spot // (2 * SIDE))
        & (place % small == (spot % SIDE) // 2)
    )
    return jnp.where(match, 1.0, 0.0).astype(BF)


def fill_weights(wide, pools, field, flip):
    for tap in range(27):
        source = 26 - tap if flip else tap
        line = widen(pools[field, source : source + 1, :])
        wide[8 * tap : 8 * tap + 8, :] = jnp.broadcast_to(line, (8, LANES))


def fill_rolled(source, before, after, blocks):
    values = source.reshape(blocks, 8, LANES)
    lane = iota((blocks, 8, LANES), 1)
    before[0 : 8 * blocks, :] = jnp.where(lane >= 2, pltpu.roll(values, 2, 1), 0.0).reshape(8 * blocks, LANES)
    after[0 : 8 * blocks, :] = jnp.where(lane < 6, pltpu.roll(values, 6, 1), 0.0).reshape(8 * blocks, LANES)


def load_row(ref, index):
    return ref[pl.ds(pl.multiple_of(SLAB * index, SLAB), SLAB), :].reshape(GRID, 8, LANES)


def conv_rows(sources, wide, result, stride):
    count = SIDE // stride

    def one_row(i, carry):
        sums = [jnp.zeros((8, LANES), F32) for _ in range(count)]
        for a in range(3):
            for b in range(3):
                line = load_row(sources[a], stride * i + b)
                for e in range(3):
                    tap = 9 * a + 3 * b + e
                    weight = wide[8 * tap : 8 * tap + 8, :]
                    for j in range(count):
                        sums[j] = sums[j] + weight * line[stride * j + e]
        for j in range(count):
            result[pl.ds(pl.multiple_of(8 * count * i + 8 * j, 8), 8), :] = sums[j]
        return carry

    lax.fori_loop(0, count, one_row, 0)


def conv_back_two(sources, wide, result):
    count = SIDE // 2

    def one_row(m, carry):
        even = [jnp.zeros((8, LANES), F32) for _ in range(SIDE)]
        odd = [jnp.zeros((8, LANES), F32) for _ in range(SIDE)]
        for a in range(3):
            now, later = load_row(sources[2 - a], m + 1), load_row(sources[2 - a], m + 2)
            for sums, b, line in ((even, 1, now), (odd, 0, later), (odd, 2, now)):
                taps = [wide[8 * (9 * a + 3 * b + e) : 8 * (9 * a + 3 * b + e) + 8, :] for e in range(3)]
                for n in range(count):
                    sums[2 * n] = sums[2 * n] + taps[1] * line[n + 1]
                    sums[2 * n + 1] = sums[2 * n + 1] + taps[0] * line[n + 2] + taps[2] * line[n + 1]
        for j in range(SIDE):
            result[pl.ds(pl.multiple_of(16 * SIDE * m + 8 * j, 8), 8), :] = even[j]
            result[pl.ds(pl.multiple_of(16 * SIDE * m + 8 * SIDE + 8 * j, 8), 8), :] = odd[j]
        return carry

    lax.fori_loop(0, count, one_row, 0)


def conv_weight(sources, grads, totals, stride):
    count = SIDE // stride
    totals[...] = jnp.zeros((27 * 8, LANES), F32)

    def one_row(i, carry):
        cotangent = load_row(grads, i + 1)
        for a in range(3):
            for b in range(3):
                line = load_row(sources[a], stride * i + b)
                for e in range(3):
                    spot = 8 * (9 * a + 3 * b + e)
                    total = totals[spot : spot + 8, :]
                    for j in range(count):
                        total = total + line[stride * j + e] * cotangent[j + 1]
                    totals[spot : spot + 8, :] = total
        return carry

    lax.fori_loop(0, count, one_row, 0)


def weights_of_rows(totals):
    return jnp.sum(totals[...].reshape(27, 8, LANES), axis=1)


def put_rows(target, values, head, count):
    for i in range(count):
        start = ((i + 1) * GRID + 1) * 8 + head
        target[pl.ds(start, FR * count, stride=2), :] = values[FR * count * i : FR * count * (i + 1), :]


def pairs_of(heads):
    return [((0, 0), (1, 0))] if heads == 2 else [((0, 0), (0, 1)), ((1, 0), (1, 1))]


def pack_heads(lines, turn):
    half = len(lines) // 2
    sides = [jnp.concatenate([line[:, :HD] for line in lines[half * i : half * (i + 1)]], axis=1) for i in range(2)]
    flag = turn == 1
    return jnp.concatenate([pick(flag, sides[1], sides[0]), pick(flag, sides[0], sides[1])], axis=1)


def unpack_heads(values, turn):
    heads = values.shape[1] // HD
    lines = [values[:, HD * head : HD * (head + 1)] for head in range(heads)]
    flag, half = turn == 1, heads // 2
    return [widen(pick(flag, lines[(head + half) % heads], lines[head])) for head in range(heads)]


def front_body(heads, turn, strides, normed, weights, pools, memory, fields, pooled, passed, work):
    before, after, wide, result, held, sent = work
    copies = []
    lines = [nt(normed, weights[s][: 3 * HD * heads // 2, :]) for s in range(2)]
    for field in range(3):
        fill_weights(wide, pools, field, False)
        stride = strides[field]
        count = SIDE // stride
        for number, pair in enumerate(pairs_of(heads)):
            spot = field * (heads // 2) + number
            group = held.at[spot]
            group[...] = jnp.zeros((PADDED, LANES), F32)
            for head, (slot, place) in enumerate(pair):
                start = HD * (3 * place + field)
                put_rows(group, widen(lines[slot][:, start : start + HD]), head, SIDE)
            copies.append(pltpu.make_async_copy(group, fields.at[spot], sent.at[spot]))
            copies[-1].start()
            fill_rolled(group[...], before, after, PADDED // 8)
            conv_rows((before, group, after), wide, result, stride)
            for head in range(2):
                pooled[field][2 * number + head] = result[pl.ds(head, FR * count * count, stride=2), :]
    area = (SIDE // strides[1]) ** 2
    for which in range(2):
        lines = []
        for head in range(heads):
            total = jnp.zeros((area, LANES), F32)
            for t in range(FR):
                line = widen(memory[which, t : t + 1, :])
                total = total + line * pooled[1 + which][head, pl.ds(t, area, stride=FR), :]
            lines.append(total)
        passed[which] = pack_heads(lines, turn).astype(BF)
    for copy in copies:
        copy.wait()


def front_one(scal, own, first, second, gain, wa, wb, pools, memory, x_out, normed_out, g_out, fields, qp, kp, vp, passed, *work):
    match, turn = scal[0] == 1, scal[1] == 1
    near = pick(match, own[...], first[...])
    far = pick(match, first[...], second[...])
    low, high = pick(turn, far, near), pick(turn, near, far)
    count, area = 2 * SIDE * SIDE, (SIDE // 2) ** 2
    rows = nn(token_rows(0), low[:count]) + nn(token_rows(1), high[:count])
    x_out[...] = rows.astype(BF)
    turns = [half_rows(half, area) for half in range(2)]
    for column in range(2):
        spots = slice(count + 2 * area * column, count + 2 * area * (column + 1))
        g_out[column] = (tn(turns[0], low[spots]) + tn(turns[1], high[spots])).astype(BF)
    normed = (norm_parts(rows)[0] * gain[...]).astype(BF)
    normed_out[...] = normed
    front_body(2, scal[1], (1, 2, 2), normed, (wa, wb), pools, memory, fields, (qp, kp, vp), passed, work)


def front_two(scal, middle, part, other, gain, wa, wb, residual, pools, memory, x_out, normed_out, skip, fields, qp, kp, vp, passed, *work):
    rows = middle[...] + (part[...].astype(F32) + other[...].astype(F32))
    x_out[...] = rows
    normed = (norm_parts(rows)[0] * gain[...]).astype(BF)
    normed_out[...] = normed
    high, low = split(nn(cells(), normed))
    skip[...] = 0.25 * (nn(high, residual[...]) + nn(low, residual[...]))
    front_body(4, scal[1], (2, 1, 1), normed, (wa, wb), pools, memory, fields, (qp, kp, vp), passed, work)


def table_of(shards, block, slot, place):
    line = shards[slot][4 * HD : 4 * HD + 16, :].astype(F32)
    row = 3 * (place if block == 0 else 1 + place)
    return line[row : row + 1, :] + line[row + 1 : row + 2, :] + line[row + 2 : row + 3, :]


def own_bias(bins, table):
    values = jnp.zeros(bins.shape, F32)
    for number in range(2 * FR - 1):
        values = jnp.where(bins == number, table[:, number : number + 1], values)
    return values


def far_bias(table, offset):
    lanes = iota(table.shape, 1)
    return jnp.sum(jnp.where(lanes == offset + 2 * FR - 1, table, 0.0), axis=1, keepdims=True)


def probs_of(scal, bins, table, query, keys):
    parts = [nt(query, keys[0]) * SCALE + own_bias(bins, table)]
    for j in range(2):
        raw = nt(query, keys[1 + j]) * SCALE + far_bias(table, scal[4 + j])
        parts.append(jnp.where(scal[2 + j] == 1, raw, NEGATIVE))
    top = functools.reduce(jnp.maximum, [jnp.max(part, axis=1, keepdims=True) for part in parts])
    parts = [jnp.exp(part - top) for part in parts]
    total = sum(jnp.sum(part, axis=1, keepdims=True) for part in parts)
    return [part / total for part in parts]


def heads_of(heads, block):
    return [(slot, place) for slot in range(2) for place in range(heads // 2)]


def attend(block, scal, ta, tb, qp, kp, vp, near, far, wa, wb, rows_out, part_out):
    heads = qp.shape[0]
    shards, weights = (ta, tb), (wa, wb)
    base = 0 if block else 3 * HD
    shape = (qp.shape[1], kp.shape[1])
    bins = iota(shape, 0) % FR - iota(shape, 1) % FR + FR - 1
    total = jnp.zeros(part_out.shape, F32)
    nears, fars = ([unpack_heads(item[which], scal[1]) for which in range(2)] for item in (near, far))
    for head, (slot, place) in enumerate(heads_of(heads, block)):
        table = table_of(shards, block, slot, place)
        pool = qp[head]
        keys = (kp[head].astype(BF), nears[0][head], fars[0][head])
        values = (vp[head].astype(BF), nears[1][head], fars[1][head])
        probs = probs_of(scal, bins, table, pool.astype(BF), keys)
        mixture = sum(nn(p.astype(BF), v) for p, v in zip(probs, values))
        line = (mixture + pool).astype(BF)
        rows_out[head] = line
        total = total + nn(line[:, :HD], weights[slot][base + HD * place : base + HD * place + HD, :])
    part_out[...] = total.astype(BF)


def attend_back(block, scal, ta, tb, qp, kp, vp, near, far, wa, wb, rows, middle_grad, dq, dk, dv, d_near, d_far, proj_grad, table_grad):
    heads = qp.shape[0]
    shards, weights = (ta, tb), (wa, wb)
    base = 0 if block else 3 * HD
    shape = (qp.shape[1], kp.shape[1])
    bins = iota(shape, 0) % FR - iota(shape, 1) % FR + FR - 1
    branch = middle_grad.astype(BF)
    lanes = iota((1, LANES), 1)
    table_lines = []
    nears, fars = ([unpack_heads(item[which], scal[1]) for which in range(2)] for item in (near, far))
    near_lines, far_lines = ([], []), ([], [])
    for head, (slot, place) in enumerate(heads_of(heads, block)):
        table = table_of(shards, block, slot, place)
        weight = weights[slot][base + HD * place : base + HD * place + HD, :]
        found = tn(rows[head][:, :HD], branch).astype(BF)
        for column in range(proj_grad.shape[1] // (HD * (heads // 2))):
            start = HD * (heads // 2) * column + HD * place
            proj_grad[slot, start : start + HD, :] = found[:, proj_grad.shape[2] * column : proj_grad.shape[2] * (column + 1)]
        grad = widen(nt(branch, weight).astype(BF))
        query = qp[head].astype(BF)
        keys = (kp[head].astype(BF), nears[0][head], fars[0][head])
        values = (vp[head].astype(BF), nears[1][head], fars[1][head])
        probs = probs_of(scal, bins, table, query, keys)
        grad_probs = [nt(grad, v) for v in values]
        inner = sum(jnp.sum(p * d, axis=1, keepdims=True) for p, d in zip(probs, grad_probs))
        low = [(p * (d - inner)).astype(BF) for p, d in zip(probs, grad_probs)]
        dq[head] = sum(nn(s, k) for s, k in zip(low, keys)) * SCALE + grad.astype(F32)
        key_grads = [tn(s, query) * SCALE for s in low]
        value_grads = [tn(p.astype(BF), grad) for p in probs]
        dk[head], dv[head] = key_grads[0], value_grads[0]
        for which, grads in enumerate((key_grads, value_grads)):
            near_lines[which].append(grads[1])
            far_lines[which].append(grads[2])
        score = low[0].astype(F32)
        line = jnp.zeros((1, LANES), F32)
        for number in range(2 * FR - 1):
            column = jnp.sum(jnp.where(bins == number, score, 0.0), axis=0, keepdims=True)
            line = line + jnp.where(lanes == number, jnp.sum(column, axis=1, keepdims=True), 0.0)
        for j in range(2):
            column = jnp.sum(low[1 + j].astype(F32), axis=0, keepdims=True)
            value = jnp.sum(column, axis=1, keepdims=True)
            line = line + jnp.where(lanes == scal[4 + j] + 2 * FR - 1, value, 0.0)
        table_lines.append(line)
    for which in range(2):
        d_near[which] = pack_heads(near_lines[which], scal[1]).astype(BF)
        d_far[which] = pack_heads(far_lines[which], scal[1]).astype(BF)
    for head, line in enumerate(table_lines):
        table_grad[head : head + 1, :] = line


def field_back(heads, turn, strides, fields, pooled, grads, near, far, pools, memory, pools_grad, memory_grad, work):
    before, after, wide, result, grid, grid_before, grid_after, totals, rows, held, arrived = work
    half = heads // 2
    copies = [pltpu.make_async_copy(fields.at[i], held.at[i], arrived.at[i]) for i in range(3 * half)]
    for copy in copies:
        copy.start()
    back = {}
    area = (SIDE // strides[1]) ** 2
    for field in range(3):
        stride = strides[field]
        count = SIDE // stride
        fill_weights(wide, pools, field, stride == 1)
        weight_sum = jnp.zeros((27, LANES), F32)
        memory_lines = [jnp.zeros((1, LANES), F32) for _ in range(FR)]
        if field:
            passed = unpack_heads(near[field - 1].astype(F32) + far[field - 1].astype(F32), turn)
        for number, pair in enumerate(pairs_of(heads)):
            grid[...] = jnp.zeros((PADDED, LANES), F32)
            for place in range(2):
                head = 2 * number + place
                if field == 0:
                    put_rows(grid, grads[0][head], place, count)
                else:
                    cotangent = passed[head]
                    for t in range(FR):
                        spot = pl.ds(t, area, stride=FR)
                        line = widen(memory[field - 1, t : t + 1, :])
                        rows[spot, :] = grads[field][head, spot, :] + line * cotangent
                        product = pooled[field - 1][head, spot, :] * cotangent
                        memory_lines[t] = memory_lines[t] + jnp.sum(product, axis=0, keepdims=True)
                    put_rows(grid, rows[0 : FR * area, :], place, count)
            group = held.at[field * half + number]
            copies[field * half + number].wait()
            fill_rolled(group[...], before, after, PADDED // 8)
            conv_weight((before, group, after), grid, totals, stride)
            weight_sum = weight_sum + weights_of_rows(totals)
            fill_rolled(grid[...], grid_before, grid_after, PADDED // 8)
            if stride == 1:
                conv_rows((grid_before, grid, grid_after), wide, result, 1)
            else:
                conv_back_two((grid_before, grid, grid_after), wide, result)
            for place, key in enumerate(pair):
                back[key + (field,)] = result[pl.ds(place, FR * SIDE * SIDE, stride=2), :][:, :HD]
        pools_grad[field, 0:27, :] = weight_sum
        if field:
            for t in range(FR):
                memory_grad[field - 1, t : t + 1, :] = memory_lines[t]
    outs = []
    for slot in range(2):
        columns = [back[(slot, place, field)] for place in range(half) for field in range(3)]
        outs.append(jnp.concatenate(columns, axis=1).astype(BF))
    return outs


def mlp_one(scal, x, part, other, gain, wa, wb, middle_out, normed_out, part_out):
    weights = (wa, wb)
    middle = x[...].astype(F32) + (part[...].astype(F32) + other[...].astype(F32))
    middle_out[...] = middle
    normed = (norm_parts(middle)[0] * gain[...]).astype(BF)
    normed_out[...] = normed
    size = normed.shape[1]
    total = jnp.zeros(part_out.shape, F32)
    for slot in range(2):
        hidden = gelu_parts(nn(normed, weights[slot][:size, :]))[0].astype(BF)
        total = total + nn(hidden, weights[slot][size:, :])
    part_out[...] = total.astype(BF)


def middle_two(scal, skip, part, other, gain, g, middle_out, normed_out, half_out):
    middle = skip[...] + (part[...].astype(F32) + other[...].astype(F32))
    middle_out[...] = middle
    normed_out[...] = (norm_parts(middle)[0] * gain[...]).astype(BF)
    width = half_out.shape[2]
    half_out[0] = normed_out[:, pl.ds(pl.multiple_of(scal[7] * width, LANES), width)]
    half_out[1] = g[scal[7]]


def mlp_two(scal, own, own_grad, *refs):
    halves, others = refs[0:3], refs[3:6]
    up_ref, down_ref = refs[6:8]
    keep, give = refs[8:10]
    packed, board, lines = refs[10:13]
    width = up_ref.shape[1] // 2
    core = scal[7]
    start = pl.multiple_of(core * width, LANES)
    rest = pl.multiple_of((1 - core) * width, LANES)
    up, down = up_ref[:, pl.ds(start, width)], down_ref[pl.ds(start, width), :]
    board[0, 0] = own[...]
    for column in range(2):
        board[0, 1, :, width * column : width * (column + 1)] = own_grad[column]
    for d in range(3):
        for which in range(2):
            board[d + 1, which, :, pl.ds(start, width)] = halves[d][which]
            board[d + 1, which, :, pl.ds(rest, width)] = others[d][which]
    up_total = jnp.zeros(up.shape, F32)
    down_total = jnp.zeros(down.shape, F32)
    for d in range(4):
        rows, grad = board[d, 0], board[d, 1]
        value, slope = gelu_parts(nn(rows, up))
        hidden = value.astype(BF)
        lines[0] = nn(hidden, down)
        up_low = (nt(grad, down) * slope).astype(BF)
        lines[1] = nt(up_low, up)
        for which in range(2):
            spots = slice(104 * (2 * d + which), 104 * (2 * d + which) + rows.shape[0])
            keep[spots, :] = lines[which, :, pl.ds(start, width)].astype(BF)
            give[spots, :] = lines[which, :, pl.ds(rest, width)].astype(BF)
        up_total = up_total + tn(rows, up_low)
        down_total = down_total + tn(hidden, grad)
    size = up.shape[0]
    packed[0:size, :] = up_total.astype(BF)
    packed[size : size + width, :] = down_total[:, :width].astype(BF)
    packed[size + width : size + 2 * width, :] = down_total[:, width:].astype(BF)


def quarter_of(scal, peer):
    one = 1 - scal[8] if peer % 2 else scal[8]
    two = 1 - scal[9] if peer // 2 else scal[9]
    return one + 2 * two


def cut(scal, full, parts):
    rows = parts[0].shape[1]
    for peer in range(4):
        spots = pl.ds(pl.multiple_of(quarter_of(scal, peer) * rows, 16), rows)
        for slot in range(2):
            parts[peer][slot] = full[slot, spots, :]


def sum_planes(*refs):
    one, two = refs[-2:]
    start = 0
    for number in range(len(refs) // 4):
        parts = refs[4 * number : 4 * number + 4]
        rows = parts[0].shape[1]
        for slot, out in ((0, one), (1, two)):
            total = (parts[0][slot].astype(F32) + parts[1][slot].astype(F32)) + (
                parts[2][slot].astype(F32) + parts[3][slot].astype(F32)
            )
            out[start : start + rows, :] = total.astype(BF)
        start += rows


def gather_parts(scal, parts, start, full):
    rows = full.shape[0] // 4
    for peer, part in enumerate(parts):
        spots = pl.ds(pl.multiple_of(quarter_of(scal, peer) * rows, 16), rows)
        full[spots, :] = part[start : start + rows, :].astype(F32)


def put_totals(full, start, pools, memory):
    for field in range(3):
        pools[field] = full[start : start + 27, LANES * field : LANES * field + HD]
    for which in range(2):
        memory[which] = full[start + 32 : start + 32 + FR, LANES * which : LANES * which + HD]


def stack_two(scal, own, other, out):
    turn = scal[1]
    out[turn], out[1 - turn] = own[...], other[...]


def finish_residual(scal, own, own_far, other, other_far, out):
    size, width = own.shape[1:]
    upper = scal[10] // 2
    for core, near, far in ((scal[7], own, own_far), (1 - scal[7], other, other_far)):
        for pair, source in ((upper, near), (1 - upper, far)):
            for parity in range(2):
                rows = pl.ds(pl.multiple_of(2 * size * parity + size * core, 16), size)
                columns = pl.ds(pl.multiple_of(width * pair, LANES), width)
                out[rows, columns] = source[parity].astype(F32)


def take_piece(scal, a, b, c, d, piece):
    half = piece.shape[0]
    start = pl.multiple_of(96 + half * scal[7], 16)
    for peer, part in enumerate((a, b, c, d)):

        @pl.when(quarter_of(scal, peer) == 3)
        def _():
            piece[...] = part[pl.ds(start, half), :]


def finish_two(scal, a, b, c, d, qkv, proj, up, down, pools, memory, gain, full, full_mlp):
    parts = (a, b, c, d)
    gather_parts(scal, parts, 0, full)
    gather_parts(scal, parts, full.shape[0] // 4, full_mlp)
    width = full.shape[1]
    qkv[...] = full[0:576, :]
    proj[:, :width] = full[576:768, :]
    proj[:, width:] = full[768:960, :]
    up[...] = full_mlp[0:384, :]
    down[...] = full_mlp[384:768, :]
    put_totals(full_mlp, 768, pools, memory)
    gain[0:width], gain[width:] = full_mlp[808, :], full_mlp[809, :]


def finish_one(scal, a, b, c, d, qkv, proj, table, second_table, pools, memory, gain, second_gain, third_gain, full):
    gather_parts(scal, (a, b, c, d), 0, full)
    qkv[...] = full[0:288, :]
    proj[...] = full[288:384, :]
    bins = table.shape[1]
    table[...] = full[384:385, :bins]
    second_table[...] = full[385:387, :bins]
    put_totals(full, 400, pools, memory)
    second_gain[...] = full[440, :]
    third_gain[...] = full[441, :]
    gain[...] = full[442, :]


def finish_wide(scal, own, other, up, down):
    first = scal[7] == 0
    one = jnp.where(first, own[...], other[...]).astype(F32)
    two = jnp.where(first, other[...], own[...]).astype(F32)
    size = up.shape[0]
    width = size // 2
    up[:, :width], up[:, width:] = one[:size, :], two[:size, :]
    down[:width, :width], down[:width, width:] = one[size : size + width, :], one[size + width :, :]
    down[width:, :width], down[width:, width:] = two[size : size + width, :], two[size + width :, :]


def add_cores(keep, other, *outs):
    for d in range(4):
        for which in range(2):
            spots = slice(104 * (2 * d + which), 104 * (2 * d + which) + outs[d].shape[1])
            outs[d][which] = (keep[spots, :].astype(F32) + other[spots, :].astype(F32)).astype(BF)


def whole_columns(scal, own, other):
    first = scal[7] == 0
    return jnp.concatenate([pick(first, own, other), pick(first, other, own)], axis=1)


def add_two(one, two, out):
    out[...] = (one[...].astype(F32) + two[...].astype(F32)).astype(BF)


def sum_four(a, b, c, d, out):
    total = (a[...].astype(F32) + b[...].astype(F32)) + (c[...].astype(F32) + d[...].astype(F32))
    out[...] = total.astype(BF)


def back_attend_two(scal, part, other, g, middle, gain, normed, *refs):
    ins, outs = refs[0:10], refs[10:]
    final = (middle[...] + whole_columns(scal, part[0], other[0]).astype(F32)).astype(BF)
    area = (SIDE // 2) ** 2
    outs[10][...] = nn(half_rows(scal[1], area), final).astype(BF)
    outs[11][...] = nn(half_rows(1 - scal[1], area), final).astype(BF)
    grad, gain_grad = norm_back(whole_columns(scal, part[1], other[1]).astype(F32), middle[...], gain[...])
    middle_grad = jnp.concatenate([g[0], g[1]], axis=1).astype(F32) + grad
    outs[0][...] = middle_grad
    outs[1][...] = gain_grad
    width = outs[9].shape[2]
    linear = (0.25 * outs[0][:, pl.ds(pl.multiple_of(scal[7] * width, LANES), width)]).astype(BF)
    high, low = split(nn(cells(), normed[...]))
    found = (tn(high, linear) + tn(low, linear)).astype(BF)
    size = outs[9].shape[1]
    turned = scal[1] == 1
    outs[9][0] = pick(turned, found[size:], found[:size])
    outs[9][1] = pick(turned, found[:size], found[size:])
    attend_back(1, scal, *ins, middle_grad, *outs[2:9])


def put_small(small, pools_grad, memory_grad):
    small[...] = jnp.zeros(small.shape, F32)
    for field in range(3):
        small[0:27, LANES * field : LANES * (field + 1)] = pools_grad[field, 0:27, :]
    for which in range(2):
        small[32 : 32 + FR, LANES * which : LANES * (which + 1)] = memory_grad[which]


def back_front_two(scal, middle_grad, normed_ref, fields, kp, vp, dq, dk, dv, near, far, wa, wb, residual, pools, memory, proj_grad, residual_grad, gain_grad, part_out, keep, one, two, three, small, pools_grad, memory_grad, full, *work):
    weights = (wa, wb)
    normed = normed_ref[...]
    backs = field_back(4, scal[1], (2, 1, 1), fields, (kp, vp), (dq, dk, dv), near, far, pools, memory, pools_grad, memory_grad, work)
    total = jnp.zeros(part_out.shape, F32)
    width = full.shape[2]
    columns = pl.ds(pl.multiple_of(scal[7] * width, LANES), width)
    linear = (0.25 * middle_grad[:, columns]).astype(BF)
    cell = cells()
    for slot in range(2):
        full[slot, 0:576, :] = tn(backs[slot], normed).astype(BF)
        full[slot, 576:960, :] = proj_grad[slot]
        full[slot, 960:1152, :] = residual_grad[slot]
        total = total + nn(backs[slot], weights[slot][...])
    cut(scal, full, (keep, one, two, three))
    high, low = split(nt(linear, residual[:, columns]))
    part_out[...] = (total + tn(cell, high) + tn(cell, low)).astype(BF)
    put_small(small, pools_grad, memory_grad)
    small[40:41, :] = 0.5 * gain_grad[:, :width]
    small[41:42, :] = 0.5 * gain_grad[:, width:]


def back_mlp_one(scal, part, other, x, gain, normed_ref, wa, wb, small, small_other, grad_out, part_out, gain_grad_ref, keep, one, two, three, full):
    weights = (wa, wb)
    grad, gain_grad = norm_back(part[...].astype(F32) + other[...].astype(F32), x[...], gain[...])
    grad_out[...] = grad
    gain_grad_ref[...] = gain_grad
    branch = grad.astype(BF)
    normed = normed_ref[...]
    total = jnp.zeros(part_out.shape, F32)
    whole = (small[...] + small_other[...]).astype(BF)
    size = normed.shape[1]
    for slot in range(2):
        up, down = weights[slot][:size, :], weights[slot][size:, :]
        value, slope = gelu_parts(nn(normed, up))
        up_low = (nt(branch, down) * slope).astype(BF)
        full[slot, 0:size, :] = tn(normed, up_low).astype(BF)
        full[slot, size : 2 * size, :] = tn(value.astype(BF), branch).astype(BF)
        full[slot, 2 * size : 2 * size + 64, :] = whole
        total = total + nt(up_low, up)
    part_out[...] = total.astype(BF)
    cut(scal, full, (keep, one, two, three))


def back_attend_one(scal, part, other, g, middle, gain, *refs):
    ins, outs = refs[0:10], refs[10:]
    grad, gain_grad = norm_back(part[...].astype(F32) + other[...].astype(F32), middle[...], gain[...])
    middle_grad = g[...] + grad
    outs[0][...] = middle_grad
    outs[1][...] = gain_grad
    attend_back(0, scal, *ins, middle_grad, *outs[2:9])


def back_front_one(scal, normed_ref, fields, kp, vp, dq, dk, dv, near, far, wa, wb, pools, memory, gain_two_grad, gain_three_grad, qkv_grad, part_out, small, pools_grad, memory_grad, *work):
    weights = (wa, wb)
    normed = normed_ref[...]
    backs = field_back(2, scal[1], (1, 2, 2), fields, (kp, vp), (dq, dk, dv), near, far, pools, memory, pools_grad, memory_grad, work)
    total = jnp.zeros(part_out.shape, F32)
    for slot in range(2):
        qkv_grad[slot] = tn(backs[slot], normed).astype(BF)
        total = total + nn(backs[slot], weights[slot][: 3 * HD, :])
    part_out[...] = total.astype(BF)
    put_small(small, pools_grad, memory_grad)
    small[40:41, :] = 0.5 * gain_two_grad[...]
    small[41:42, :] = 0.5 * gain_three_grad[...]


def back_tokens(scal, part, other, x, gain, middle_grad, qkv_grad, proj_grad, table_one, table_two, small, small_other, keep_rows, send_rows, keep, one, two, three, full):
    grad, gain_grad = norm_back(part[...].astype(F32) + other[...].astype(F32), x[...].astype(F32), gain[...])
    rows = (middle_grad[...] + grad).astype(BF)
    turn = scal[1]
    keep_rows[...] = nn(half_rows(turn, SIDE * SIDE), rows).astype(BF)
    send_rows[...] = nn(half_rows(1 - turn, SIDE * SIDE), rows).astype(BF)
    line = iota((64, 1), 0)
    whole = jnp.where(line == 42, gain_grad, small[...] + small_other[...]).astype(BF)
    for slot in range(2):
        full[slot, 0:288, :] = qkv_grad[slot]
        full[slot, 288:384, :] = proj_grad[slot]
        lines = jnp.concatenate([table_one[slot : slot + 1, :], table_two[2 * slot : 2 * slot + 2, :], jnp.zeros((13, LANES), F32)], axis=0)
        full[slot, 384:400, :] = jnp.concatenate([lines, jnp.zeros((16, 2 * LANES), F32)], axis=1).astype(BF)
        full[slot, 400:464, :] = whole
        full[slot, 464:512, :] = jnp.zeros((48, full.shape[2]), BF)
    cut(scal, full, (keep, one, two, three))


def scalars(pairs, other_pairs, videos, out):
    plane, core, head = lax.axis_index("plane"), lax.axis_index("core"), lax.axis_index("head")
    upper, turn = lax.div(head, 2), lax.rem(head, 2)
    clip = 4 * plane + 2 * turn + upper
    match = core == turn
    own = videos[clip]
    out[0] = jnp.where(match, 1, 0)
    out[1] = turn
    for j in range(2):
        before = clip - 1 - j
        there = (before >= 0) & (videos[jnp.maximum(before, 0)] == own)
        out[2 + j] = jnp.where(there, 1, 0)
        out[4 + j] = jnp.where(match, pairs[upper, j], other_pairs[upper, j])
    out[6] = jnp.where(upper == core, 1, 0)
    out[7] = core
    out[8] = lax.rem(plane, 2)
    out[9] = lax.rem(lax.div(plane, 2), 2)
    out[10] = head


def pack(tokens, grad_out, table_one, table_two, qkv_one, proj_one, rows, first):
    count, width = tokens.shape
    area = grad_out.shape[0]
    rows[0:count, :] = tokens[...]
    rows[count : count + area, :] = grad_out[:, :width]
    rows[count + area :, :] = grad_out[:, width:]
    lines = []
    for table in (table_one[0:1, :], table_two[0:1, :], table_two[1:2, :]):
        high = table.astype(BF).astype(F32)
        middle = (table - high).astype(BF).astype(F32)
        lines += [high, middle, table - high - middle]
    first[0 : 3 * HD, :] = qkv_one[...]
    first[3 * HD : 4 * HD, :] = proj_one[...]
    stacked = jnp.concatenate(lines + [jnp.zeros((7, lines[0].shape[1]), F32)], axis=0)
    first[4 * HD :, :] = jnp.concatenate([stacked, jnp.zeros((16, width - stacked.shape[1]), F32)], axis=1).astype(BF)


def join(one, two, first, second, third, out):
    out[0 : one.shape[0], :] = one[...]
    out[one.shape[0] :, :] = two[...]


SMEM = pl.BlockSpec(memory_space=pltpu.SMEM)


FAR = pl.BlockSpec(memory_space=pltpu.HBM)
NEAR = pl.BlockSpec(memory_space=pltpu.VMEM)


def moved(body, counts, left, early, late, *refs):
    ins_count, outs_count, work_count = counts
    ins, outs = list(refs[:ins_count]), refs[ins_count : ins_count + outs_count]
    spot = ins_count + outs_count
    saved = refs[spot : spot + len(early) + len(late)]
    spot += len(early) + len(late)
    work = refs[spot : spot + work_count]
    buffers, arrived = refs[spot + work_count : -1], refs[-1]
    brought = [pltpu.make_async_copy(ins[item], buffers[i], arrived.at[i]) for i, item in enumerate(left)]
    first = len(left)
    sent = [pltpu.make_async_copy(ins[item], saved[i], arrived.at[first + i]) for i, item in enumerate(early)]
    for copy in brought + sent:
        copy.start()
    for i, item in enumerate(left):
        brought[i].wait()
        ins[item] = buffers[i]
    body(*ins, *outs, *work)
    first += len(early)
    last = [
        pltpu.make_async_copy(outs[item], saved[len(early) + i], arrived.at[first + i]) for i, item in enumerate(late)
    ]
    for copy in last:
        copy.start()
    for copy in sent + last:
        copy.wait()


def kernel(body, name, outs, ins, work=(), left=(), early=(), late=(), raw=(), far_outs=(), limit=16, flops=2 * 10**8):
    if limit == 16 and (left or early or late):
        found = kernel(body, name, outs, ins, work, (), (), (), raw, far_outs)
        return (*found, *[list(ins)[item] for item in early], *[found[item] for item in late])
    ins = list(ins)
    in_specs = []
    for number, item in enumerate(ins):
        if number == 0 and item.dtype == jnp.int32:
            in_specs.append(SMEM)
        else:
            in_specs.append(FAR if number in left or number in raw else NEAR)
    results = [jax.ShapeDtypeStruct(shape, kind) for shape, kind in outs]
    extra = [jax.ShapeDtypeStruct(ins[item].shape, ins[item].dtype) for item in early] + [results[item] for item in late]
    size = sum(int(np.prod(item.shape)) * item.dtype.itemsize for item in [*ins, *results, *extra])
    work = list(work)
    count = len(work)
    if left or early or late:
        body = functools.partial(moved, body, (len(ins), len(results), count), tuple(left), tuple(early), tuple(late))
        work += [pltpu.VMEM(ins[number].shape, ins[number].dtype) for number in left]
        work.append(pltpu.SemaphoreType.DMA((len(left) + len(early) + len(late),)))
    return pl.pallas_call(
        body,
        out_shape=tuple(results + extra),
        in_specs=in_specs,
        out_specs=tuple([FAR if number in far_outs else NEAR for number in range(len(results))] + [FAR] * len(extra)),
        scratch_shapes=work,
        name=name,
        cost_estimate=pl.CostEstimate(flops=flops, bytes_accessed=size, transcendentals=0),
        compiler_params=pltpu.CompilerParams(vmem_limit_bytes=limit << 20),
    )(*ins)


def scratch(*rows):
    return [pltpu.VMEM((count, LANES), F32) for count in rows]


def field_work(heads):
    groups = 3 * heads // 2
    return [pltpu.VMEM((groups, PADDED, LANES), F32), pltpu.SemaphoreType.DMA((groups,))]


FRONT_WORK = (PADDED, PADDED, 216, 800)
BACK_WORK = (PADDED, PADDED, 216, 800, PADDED, PADDED, PADDED, 216, 400)


def after(values, events):
    return lax.optimization_barrier((values, events))


def swap(values):
    return lax.ppermute(values, "core", [(0, 1), (1, 0)])


def cross_route():
    route = []
    for core in range(2):
        low, other = 2 * core, 2 - 2 * core
        route += [(core * 4 + low + i, core * 4 + other + i) for i in range(2)]
    return route


def beside(values):
    return lax.ppermute(values, "head", [(z, z ^ 1) for z in range(4)])


def choose(scal, own, other, out):
    out[...] = pick(scal[6] == 1, own[...], other[...])


def chosen(scal, own, other):
    return kernel(choose, "choose_shard", [(own.shape, own.dtype)], [scal, own, other])[0]


def over(values, scal):
    return chosen(scal, values, lax.ppermute(values, ("core", "head"), cross_route()))


def spread(values, scal):
    one = over(values, scal)
    return one, beside(one)


def reverse(route):
    return [(end, start) for start, end in route]


def clip_routes(planes, distance):
    def place(clip):
        slot = clip % 4
        return (clip // 4) * 4 + 2 * (slot % 2) + slot // 2

    total = 4 * planes
    return [(place(clip), place(clip + distance)) for clip in range(total) if 0 <= clip + distance < total]


def half_routes():
    def place(core, a, b):
        return core * 4 + 2 * a + b

    one, two, three = [], [], []
    for a in range(2):
        for b in range(2):
            one += [(place(b, a, b), place(1 - b, a, b)), (place(1 - b, a, b), place(1 - b, a, 1 - b))]
            two += [(place(1 - b, a, b), place(b, a, 1 - b))]
            three += [(place(1 - b, a, b), place(b, a, 1 - b))]
    return one, two, three


def turn_by(values, distance):
    return lax.ppermute(values, "head", [(z, (z + distance) % 4) for z in range(4)])


def local(
    planes,
    tokens,
    grad_out,
    video_ids,
    offsets,
    gain_one,
    qkv_one,
    pools_one,
    memory_one,
    table_one,
    proj_one,
    gain_two,
    up_one,
    down_one,
    gain_three,
    qkv_two,
    residual_two,
    pools_two,
    memory_two,
    table_two,
    proj_two,
    gain_four,
    up_two,
    down_two,
):
    match = lax.axis_index("core") == lax.axis_index("head") % 2
    (scal,) = pl.pallas_call(
        scalars,
        out_shape=(jax.ShapeDtypeStruct((16,), jnp.int32),),
        in_specs=[SMEM] * 3,
        out_specs=(SMEM,),
        name="scalars",
    )(offsets, swap(offsets), video_ids)
    gains = [item.reshape(1, -1) for item in (gain_one, gain_two, gain_three, gain_four)]

    half = residual_two.shape[1] // 2
    qkv_one_t, qkv_two_t = qkv_one.T, qkv_two.T
    rows_in, first_bundle = kernel(
        pack,
        "pack",
        [((300, half), BF), ((400, half), BF)],
        [tokens, grad_out, table_one, table_two, qkv_one_t, proj_one],
        left=range(6),
        limit=56,
    )
    route_one, route_two, route_three = half_routes()
    axes = ("core", "head")
    first_over = over(first_bundle, scal)
    first_all = (first_over, beside(first_over))
    tok_one, tok_two = lax.ppermute(rows_in, axes, route_one), lax.ppermute(rows_in, axes, route_two)
    (mlp_bundle,) = kernel(
        join, "join", [((768, half), BF)], [up_one, down_one, first_over, tok_one, tok_two], left=(0, 1), limit=48
    )
    mlp_over = over(mlp_bundle, scal)

    width = qkv_one.shape[0]
    wide = residual_two.shape[1]
    n1, n2 = FR * SIDE * SIDE, FR * SIDE * SIDE // 4
    a1, a2 = n2 // FR, n1 // FR

    x1, _, g, fields1, qp1, kp1, vp1, passed1, *saved = kernel(
        front_one,
        "front_one",
        [
            ((n1, width), BF),
            ((n1, width), BF),
            ((2, n2, half), BF),
            ((3, PADDED, LANES), F32),
            ((2, n1, LANES), F32),
            ((2, n2, LANES), F32),
            ((2, n2, LANES), F32),
            ((2, a1, 2 * HD), BF),
        ],
        [scal, rows_in, tok_one, tok_two, gains[0], *first_all, pools_one, memory_one],
        scratch(*FRONT_WORK) + field_work(2),
        early=(5, 6),
        late=(0, 1, 2, 4, 5, 6),
        far_outs=(3,),
    )
    first_kept, (x1_kept, normed1, g_kept, qp1_kept, kp1_kept, vp1_kept) = saved[:2], saved[2:]
    places = ("plane", "head")
    near1 = lax.ppermute(passed1, places, clip_routes(planes, 1))
    far1 = lax.ppermute(passed1, places, clip_routes(planes, 2))
    (mlp_over, late_qkv), (x1,) = after((mlp_over, qkv_two_t), (x1,))
    mlp_all = (mlp_over, beside(mlp_over))
    qkv_two_all = spread(late_qkv, scal)
    late_proj, (first,) = after(proj_two, qkv_two_all[0:1])
    qkv_two_all = (first, qkv_two_all[1])
    proj_two_all = spread(late_proj, scal)
    attn1_ins = [*first_all, qp1, kp1, vp1, near1, far1, *first_all]
    _, part1, near1_kept, far1_kept, rows1 = kernel(
        functools.partial(attend, 0),
        "attend_one",
        [((2, n1, LANES), BF), ((n1, width), BF)],
        [scal, *attn1_ins],
        early=(6, 7),
        late=(0,),
    )
    middle1, _, part_mlp1, *mlp_kept, middle1_kept, mlp_normed1 = kernel(
        mlp_one,
        "mlp_one",
        [((n1, width), F32), ((n1, width), BF), ((n1, width), BF)],
        [scal, x1, part1, swap(part1), gains[1], *mlp_all],
        early=(5, 6),
        late=(0, 1),
    )
    _, _, skip, fields2, qp2, kp2, vp2, passed2, *saved = kernel(
        front_two,
        "front_two",
        [
            ((n1, width), F32),
            ((n1, width), BF),
            ((n2, wide), F32),
            ((6, PADDED, LANES), F32),
            ((4, n2, LANES), F32),
            ((4, n1, LANES), F32),
            ((4, n1, LANES), F32),
            ((2, a2, 4 * HD), BF),
        ],
        [scal, middle1, part_mlp1, swap(part_mlp1), gains[2], *qkv_two_all, residual_two, pools_two, memory_two],
        scratch(*FRONT_WORK) + field_work(4),
        early=(5, 6),
        late=(0, 1, 4, 5, 6),
        far_outs=(3,),
    )
    qkv_two_kept, (x2, normed2, qp2_kept, kp2_kept, vp2_kept) = saved[:2], saved[2:]
    near2 = lax.ppermute(passed2, places, clip_routes(planes, 1))
    far2 = lax.ppermute(passed2, places, clip_routes(planes, 2))
    attn2_ins = [*first_kept, qp2, kp2, vp2, near2, far2, *proj_two_all]
    _, part2, near2_kept, far2_kept, *proj_two_kept, rows2 = kernel(
        functools.partial(attend, 1),
        "attend_two",
        [((4, n2, LANES), BF), ((n2, wide), BF)],
        [scal, *attn2_ins],
        left=(1, 2),
        early=(6, 7, 8, 9),
        late=(0,),
    )
    _, mlp_normed2, own_half, middle2 = kernel(
        middle_two,
        "middle_two",
        [((n2, wide), F32), ((n2, wide), BF), ((2, n2, half), BF)],
        [scal, skip, part2, swap(part2), gains[3], g_kept],
        left=(5,),
        late=(0,),
    )
    halves = [turn_by(own_half, d) for d in (1, 2, 3)]
    found = kernel(
        mlp_two,
        "mlp_two",
        [((832, half), BF)] * 2 + [((2 * wide, half), BF)],
        [scal, mlp_normed2, g_kept, *halves, *(swap(item) for item in halves), up_two, down_two],
        [pltpu.VMEM((4, 2, n2, wide), BF), pltpu.VMEM((2, n2, wide), F32)],
        left=(2, 9, 10),
    )
    sums = kernel(add_cores, "add_cores", [((2, n2, half), BF)] * 4, [found[0], swap(found[1])])
    sums = [sums[0]] + [turn_by(sums[d], -d) for d in (1, 2, 3)]
    (row_sum,) = kernel(sum_four, "sum_rows", [((2, n2, half), BF)], sums)
    middle_grad2, gain_four_grad, dq2, dk2, dv2, d_near2, d_far2, proj_two_grad, table_two_grad, residual_grad, keep, send = kernel(
        back_attend_two,
        "back_attend_two",
        [
            ((n2, wide), F32),
            ((1, wide), F32),
            ((4, n2, LANES), F32),
            ((4, n1, LANES), F32),
            ((4, n1, LANES), F32),
            ((2, a2, 4 * HD), BF),
            ((2, a2, 4 * HD), BF),
            ((2, 4 * HD, width), BF),
            ((4, LANES), F32),
            ((2, 192, half), BF),
            ((n2 // 2, wide), BF),
            ((n2 // 2, wide), BF),
        ],
        [
            scal, row_sum, swap(row_sum), g_kept, middle2, gains[3], normed2,
            *first_kept, qp2_kept, kp2_kept, vp2_kept, near2_kept, far2_kept, *proj_two_kept, rows2,
        ],
        left=[3, 4, *range(6, 17)],
    )
    near_grad2 = lax.ppermute(d_near2, places, clip_routes(planes, -1))
    far_grad2 = lax.ppermute(d_far2, places, clip_routes(planes, -2))

    def across(values, bit):
        return lax.ppermute(values, "plane", [(i, i ^ bit) for i in range(planes)])

    def peers(parts):
        return [parts[0]] + [across(parts[peer], peer) for peer in (1, 2, 3)]

    def add_wide(values, bit):
        return kernel(add_two, "add_wide", [((2 * wide, half), BF)], [values, across(values, bit)])[0]

    wide_sum = add_wide(found[2], 1)
    (near_grad2, far_grad2), (wide_sum,) = after((near_grad2, far_grad2), (wide_sum,))
    part_back2, *sends2, small2, _, _ = kernel(
        back_front_two,
        "back_front_two",
        [
            ((n1, width), BF),
            *[((2, 288, width), BF)] * 4,
            ((64, width), F32),
            ((3, 32, LANES), F32),
            ((2, FR, LANES), F32),
        ],
        [
            scal, middle_grad2, normed2, fields2, kp2_kept, vp2_kept, dq2, dk2, dv2, near_grad2, far_grad2,
            *qkv_two_kept, residual_two, pools_two, memory_two, proj_two_grad, residual_grad, gain_four_grad,
        ],
        [pltpu.VMEM((2, 1152, width), BF)] + scratch(*BACK_WORK) + field_work(4),
        [2, 4, 5, 11, 12, 13],
        raw=[3],
    )
    received2 = peers(sends2)
    grad1, part_mlp_back, gain_three_grad, *sends_mlp = kernel(
        back_mlp_one,
        "back_mlp_one",
        [((n1, width), F32), ((n1, width), BF), ((1, width), F32)] + [((2, 208, width), BF)] * 4,
        [scal, part_back2, swap(part_back2), x2, gains[2], mlp_normed1, *mlp_kept, small2, swap(small2)],
        [pltpu.VMEM((2, 832, width), BF)],
        [3, 5, 6, 7],
    )
    middle_grad1, gain_two_grad, dq1, dk1, dv1, d_near1, d_far1, proj_one_grad, table_one_grad = kernel(
        back_attend_one,
        "back_attend_one",
        [
            ((n1, width), F32),
            ((1, width), F32),
            ((2, n1, LANES), F32),
            ((2, n2, LANES), F32),
            ((2, n2, LANES), F32),
            ((2, a1, 2 * HD), BF),
            ((2, a1, 2 * HD), BF),
            ((2, HD, width), BF),
            ((2, LANES), F32),
        ],
        [
            scal, part_mlp_back, swap(part_mlp_back), grad1, middle1_kept, gains[1],
            *first_kept, qp1_kept, kp1_kept, vp1_kept, near1_kept, far1_kept, *first_kept, rows1,
        ],
        left=[4, *range(6, 16)],
    )
    near_grad1 = lax.ppermute(d_near1, places, clip_routes(planes, -1))
    far_grad1 = lax.ppermute(d_far1, places, clip_routes(planes, -2))
    bit = 2
    while bit < planes:
        wide_sum = add_wide(wide_sum, bit)
        bit *= 2
    received_mlp = peers(sends_mlp)
    (near_grad1, far_grad1), (wide_sum, received2) = after((near_grad1, far_grad1), (wide_sum, received2))
    qkv_one_grad, part_back1, small1, _, _ = kernel(
        back_front_one,
        "back_front_one",
        [((2, 3 * HD, width), BF), ((n1, width), BF), ((64, width), F32), ((3, 32, LANES), F32), ((2, FR, LANES), F32)],
        [
            scal, normed1, fields1, kp1_kept, vp1_kept, dq1, dk1, dv1, near_grad1, far_grad1,
            *first_kept, pools_one, memory_one, gain_two_grad, gain_three_grad,
        ],
        scratch(*BACK_WORK) + field_work(2),
        [1, 3, 4, 10, 11],
        raw=[2],
    )
    part_back1, (received_mlp,) = after(part_back1, (received_mlp,))
    tok_keep, tok_send, *sends1 = kernel(
        back_tokens,
        "back_tokens",
        [((n1 // 2, width), BF), ((n1 // 2, width), BF)] + [((2, 128, width), BF)] * 4,
        [
            scal, part_back1, swap(part_back1), x1_kept, gains[0], middle_grad1, qkv_one_grad, proj_one_grad,
            table_one_grad, table_two_grad, small1, swap(small1),
        ],
        [pltpu.VMEM((2, 512, width), BF)],
        [3],
    )
    tokens_grad = jnp.where(match, tok_keep, lax.ppermute(tok_send, axes, route_three))

    def combine(body, label, rows, ins, count=1):
        return kernel(body, label, [((rows, width), BF)] * count, ins)

    back_route = reverse(cross_route())
    received1 = peers(sends1)
    rows_two, rows_mlp, rows_one = 288, 208, 128
    one2, two2 = combine(sum_planes, "sum_planes_two", rows_two + rows_mlp, received2 + received_mlp, 2)
    beside2 = beside(two2)
    up_two_sum, down_two_sum = kernel(
        finish_wide, "finish_wide", [((wide, wide), F32), ((wide, wide), F32)], [scal, wide_sum, swap(wide_sum)]
    )
    received1, (up_two_sum, down_two_sum) = after(received1, (up_two_sum, down_two_sum))
    one1, two1 = combine(sum_planes, "sum_planes_one", rows_one, received1, 2)
    beside1 = beside(two1)
    (beside2,), (one1,) = after((beside2,), (one1,))
    (total2,) = combine(add_two, "add_pair_two", rows_two + rows_mlp, [one2, beside2])
    cross2 = lax.ppermute(total2, axes, back_route)
    (beside1,), (total2,) = after((beside1,), (total2,))
    (total1,) = combine(add_two, "add_pair_one", rows_one, [one1, beside1])
    cross1 = lax.ppermute(total1, axes, back_route)
    (cross2,), (total1,) = after((cross2,), (total1,))
    (total2,) = combine(add_two, "add_cross_two", rows_two + rows_mlp, [total2, cross2])
    (total1,) = combine(add_two, "add_cross_one", rows_one, [total1, cross1])
    bit = 4
    while bit < planes:
        (total2,) = combine(add_two, "add_planes_two", rows_two + rows_mlp, [total2, across(total2, bit)])
        (total1,) = combine(add_two, "add_planes_one", rows_one, [total1, across(total1, bit)])
        bit *= 2
    parts2 = peers([chosen(scal, total2, swap(total2))] * 4)
    parts1 = peers([chosen(scal, total1, swap(total1))] * 4)
    parts2, parts1[0:1] = after(parts2, parts1[0:1])
    (piece,) = kernel(take_piece, "take_piece", [((96, width), BF)], [scal, *parts2])
    small_shapes = [(pools_one.shape, F32), (memory_one.shape, F32)]
    qkv_two_sum, proj_two_sum, up_one_sum, down_one_sum, pools_two_sum, memory_two_sum, gain_four_sum = kernel(
        finish_two,
        "finish_two",
        [(qkv_two_t.shape, F32), (proj_two.shape, F32), (up_one.shape, F32), (down_one.shape, F32)]
        + small_shapes
        + [((wide,), F32)],
        [scal, *parts2],
        [pltpu.VMEM((1152, width), F32), pltpu.VMEM((832, width), F32)],
    )
    (qkv_one_sum, proj_one_sum, table_one_sum, table_two_sum, pools_one_sum, memory_one_sum, *gain_sums) = kernel(
        finish_one,
        "finish_one",
        [(qkv_one_t.shape, F32), (proj_one.shape, F32), (table_one.shape, F32), (table_two.shape, F32)]
        + small_shapes
        + [((width,), F32)] * 3,
        [scal, *parts1],
        [pltpu.VMEM((512, width), F32)],
    )
    (pieces,) = kernel(stack_two, "stack_pieces", [((2, 96, width), BF)], [scal, piece, beside(piece)])
    far_pieces = lax.ppermute(pieces, "head", [(z, z ^ 2) for z in range(4)])
    (residual_sum,) = kernel(
        finish_residual,
        "finish_residual",
        [(residual_two.shape, F32)],
        [scal, pieces, far_pieces, swap(pieces), swap(far_pieces)],
    )

    blocks_out = jnp.where(match, keep, lax.ppermute(send, axes, route_three))

    return (
        blocks_out,
        tokens_grad,
        gain_sums[0],
        qkv_one_sum.T,
        pools_one_sum,
        memory_one_sum,
        table_one_sum,
        proj_one_sum,
        gain_sums[1],
        up_one_sum,
        down_one_sum,
        gain_sums[2],
        qkv_two_sum.T,
        residual_sum,
        pools_two_sum,
        memory_two_sum,
        table_two_sum,
        proj_two_sum,
        gain_four_sum,
        up_two_sum,
        down_two_sum,
    )


def solution(mesh):
    planes = mesh.shape["dp"] // 2
    fine = Mesh(mesh.devices.reshape(planes, 2, mesh.shape["head"]), ("plane", "core", "head"))
    dp = ("plane", "core")
    rows = P(("plane", "core", "head"), None)
    columns, lines, free = P(None, "head"), P("head", None), P()
    in_specs = (
        rows, rows, free, P(dp, None),
        free, columns, free, free, lines, lines, free, columns, lines,
        free, columns, free, free, free, lines, lines, free, columns, lines,
    )
    out_specs = (
        rows, rows,
        free, columns, free, free, lines, lines, free, columns, lines,
        free, columns, free, free, free, lines, lines, free, columns, lines,
    )
    return jax.shard_map(
        functools.partial(local, planes), mesh=fine, in_specs=in_specs, out_specs=out_specs, check_vma=False
    )
```

```python
import functools

import jax
import jax.numpy as jnp
import numpy as np
from jax import lax
from jax.experimental import pallas as pl
from jax.experimental.pallas import tpu as pltpu
from jax.sharding import Mesh, PartitionSpec as P

HD = 96
FR = 4
SIDE = 10
LANES = 128
GRID = SIDE + 2
SLAB = GRID * 2 * FR
PADDED = GRID * SLAB
EPSILON = 1e-06
NEGATIVE = -1e30
SCALE = HD**-0.5
GELU_A = float(np.sqrt(2.0 / np.pi))
GELU_B = 0.044715

BF = jnp.bfloat16
F32 = jnp.float32


def nn(a, b):
    return lax.dot_general(a, b, (((1,), (0,)), ((), ())), preferred_element_type=F32)


def nt(a, b):
    return lax.dot_general(a, b, (((1,), (1,)), ((), ())), preferred_element_type=F32)


def tn(a, b):
    return lax.dot_general(a, b, (((0,), (0,)), ((), ())), preferred_element_type=F32)


def iota(shape, dim):
    return lax.broadcasted_iota(jnp.int32, shape, dim)


def widen(values):
    fill = jnp.zeros((values.shape[0], LANES - values.shape[1]), values.dtype)
    return jnp.concatenate([values, fill], axis=1)


def split(values):
    high = values.astype(BF)
    return high, (values - high.astype(F32)).astype(BF)


def norm_parts(values):
    centered = values - jnp.mean(values, axis=-1, keepdims=True)
    variance = jnp.mean(centered * centered, axis=-1, keepdims=True)
    scale = lax.rsqrt(variance + EPSILON)
    return centered * scale, scale


def norm_back(grad, values, gain):
    unit, scale = norm_parts(values)
    scaled = grad * gain
    mean_one = jnp.mean(scaled, axis=-1, keepdims=True)
    mean_two = jnp.mean(scaled * unit, axis=-1, keepdims=True)
    gain_grad = jnp.sum(grad * unit, axis=0, keepdims=True)
    return scale * (scaled - mean_one - unit * mean_two), gain_grad


def gelu_parts(values):
    square = values * values
    bent = jnp.tanh(GELU_A * values * (1.0 + GELU_B * square))
    half = 0.5 * (1.0 + bent)
    slope = half + 0.5 * values * (1.0 - bent * bent) * GELU_A * (1.0 + 3.0 * GELU_B * square)
    return values * half, slope


def pick(flag, one, two):
    return jnp.where(flag, one, two)


def token_rows(half):
    shape = (FR * SIDE * SIDE, 2 * SIDE * SIDE)
    rows, cols = iota(shape, 0), iota(shape, 1)
    frame, place = (rows & (FR - 1)) - 2 * half, rows >> 2
    match = (cols == SIDE * SIDE * frame + place) & (frame >= 0) & (frame < 2)
    return jnp.where(match, 1.0, 0.0).astype(BF)


def half_rows(half, area):
    shape = (2 * area, FR * area)
    rows, cols = iota(shape, 0), iota(shape, 1)
    upper = jnp.where(rows >= area, 1, 0)
    return jnp.where(cols == FR * (rows - area * upper) + 2 * half + upper, 1.0, 0.0).astype(BF)


def cells():
    small = SIDE // 2
    count = FR * small * small
    rows, cols = iota((count, 1), 0), iota((1, FR * SIDE * SIDE), 1)
    place, spot = rows >> 2, cols >> 2
    row_key = FR * place + (rows & (FR - 1))
    line, column = lax.div(spot, 2 * SIDE), lax.div(lax.rem(spot, SIDE), 2)
    col_key = FR * (small * line + column) + (cols & (FR - 1))
    return jnp.where(row_key == col_key, 1.0, 0.0).astype(BF)


def fill_weights(wide, pools, field, flip):
    for tap in range(27):
        source = 26 - tap if flip else tap
        line = widen(pools[field, source : source + 1, :])
        wide[8 * tap : 8 * tap + 8, :] = jnp.broadcast_to(line, (8, LANES))


def frame_shifts():
    lane = iota((8, LANES), 0)
    early, late = lane >= 2, lane < 6
    return (
        lambda values: jnp.where(early, pltpu.roll(values, 2, 0), 0.0),
        lambda values: jnp.where(late, pltpu.roll(values, 6, 0), 0.0),
    )


def load_row(ref, index):
    return ref[pl.ds(pl.multiple_of(SLAB * index, SLAB), SLAB), :].reshape(GRID, 8, LANES)


def tap_of(wide, a, b, e):
    spot = 8 * (9 * a + 3 * b + e)
    return wide[spot : spot + 8, :]


def conv_rows(source, wide, result, stride):
    count = SIDE // stride
    before, after = frame_shifts()

    def one_row(i, carry):
        sums = [[None] * count for _ in range(3)]
        for b in range(3):
            line = load_row(source, stride * i + b)
            for a in range(3):
                for e in range(3):
                    weight = tap_of(wide, a, b, e)
                    for j in range(count):
                        term = weight * line[stride * j + e]
                        sums[a][j] = term if sums[a][j] is None else sums[a][j] + term
        for j in range(count):
            total = sums[1][j] + before(sums[0][j]) + after(sums[2][j])
            result[pl.ds(pl.multiple_of(8 * count * i + 8 * j, 8), 8), :] = total
        return carry

    lax.fori_loop(0, count, one_row, 0)


def conv_back_two(source, wide, result):
    count = SIDE // 2
    before, after = frame_shifts()

    def one_row(m, carry):
        now, later = load_row(source, m + 1), load_row(source, m + 2)
        totals = [None] * (2 * SIDE)
        for a, shift in ((1, None), (0, after), (2, before)):
            sums = [None] * (2 * SIDE)
            for start, b, line in ((0, 1, now), (SIDE, 0, later), (SIDE, 2, now)):
                taps = [tap_of(wide, a, b, e) for e in range(3)]
                for n in range(count):
                    even = taps[1] * line[n + 1]
                    odd = taps[0] * line[n + 2] + taps[2] * line[n + 1]
                    for spot, term in ((start + 2 * n, even), (start + 2 * n + 1, odd)):
                        sums[spot] = term if sums[spot] is None else sums[spot] + term
            for spot in range(2 * SIDE):
                totals[spot] = sums[spot] if shift is None else totals[spot] + shift(sums[spot])
        for spot in range(2 * SIDE):
            result[pl.ds(pl.multiple_of(16 * SIDE * m + 8 * spot, 8), 8), :] = totals[spot]
        return carry

    lax.fori_loop(0, count, one_row, 0)


def conv_weight(source, grads, totals, stride):
    count = SIDE // stride
    before, after = frame_shifts()
    totals[...] = jnp.zeros((27 * 8, LANES), F32)

    def one_row(i, carry):
        line = load_row(grads, i + 1)
        own = [line[j + 1] for j in range(count)]
        cotangents = ([after(item) for item in own], own, [before(item) for item in own])
        for b in range(3):
            line = load_row(source, stride * i + b)
            for e in range(3):
                for a in range(3):
                    spot = 8 * (9 * a + 3 * b + e)
                    terms = [line[stride * j + e] * cotangents[a][j] for j in range(count)]
                    terms.append(totals[spot : spot + 8, :])
                    while len(terms) > 1:
                        terms = [
                            terms[k] + terms[k + 1] if k + 1 < len(terms) else terms[k]
                            for k in range(0, len(terms), 2)
                        ]
                    totals[spot : spot + 8, :] = terms[0]
        return carry

    lax.fori_loop(0, count, one_row, 0)


def weights_of_rows(totals):
    return jnp.sum(totals[...].reshape(27, 8, LANES), axis=1)


def put_rows(target, values, head, count):
    for i in range(count):
        start = ((i + 1) * GRID + 1) * 8 + head
        target[pl.ds(start, FR * count, stride=2), :] = values[FR * count * i : FR * count * (i + 1), :]


def pairs_of(heads):
    return [((0, 0), (1, 0))] if heads == 2 else [((0, 0), (0, 1)), ((1, 0), (1, 1))]


def pack_heads(lines, turn):
    half = len(lines) // 2
    sides = [jnp.concatenate([line[:, :HD] for line in lines[half * i : half * (i + 1)]], axis=1) for i in range(2)]
    flag = turn == 1
    return jnp.concatenate([pick(flag, sides[1], sides[0]), pick(flag, sides[0], sides[1])], axis=1)


def unpack_heads(values, turn):
    heads = values.shape[1] // HD
    lines = [values[:, HD * head : HD * (head + 1)] for head in range(heads)]
    flag, half = turn == 1, heads // 2
    return [widen(pick(flag, lines[(head + half) % heads], lines[head])) for head in range(heads)]


def front_body(heads, turn, strides, normed, weights, pools, memory, fields, pooled, passed, work):
    wide, result, held, sent = work
    copies = []
    lines = [nt(normed, weights[s][: 3 * HD * heads // 2, :]) for s in range(2)]
    for field in range(3):
        fill_weights(wide, pools, field, False)
        stride = strides[field]
        count = SIDE // stride
        for number, pair in enumerate(pairs_of(heads)):
            spot = field * (heads // 2) + number
            group = held.at[spot]
            group[...] = jnp.zeros((PADDED, LANES), F32)
            for head, (slot, place) in enumerate(pair):
                start = HD * (3 * place + field)
                put_rows(group, widen(lines[slot][:, start : start + HD]), head, SIDE)
            copies.append(pltpu.make_async_copy(group, fields.at[spot], sent.at[spot]))
            copies[-1].start()
            conv_rows(group, wide, result, stride)
            for head in range(2):
                pooled[field][2 * number + head] = result[pl.ds(head, FR * count * count, stride=2), :]
    area = (SIDE // strides[1]) ** 2
    for which in range(2):
        lines = []
        for head in range(heads):
            total = jnp.zeros((area, LANES), F32)
            for t in range(FR):
                line = widen(memory[which, t : t + 1, :])
                total = total + line * pooled[1 + which][head, pl.ds(t, area, stride=FR), :]
            lines.append(total)
        passed[which] = pack_heads(lines, turn).astype(BF)
    for copy in copies:
        copy.wait()


def front_one(scal, own, first, second, gain, wa, wb, pools, memory, x_out, normed_out, g_out, fields, qp, kp, vp, passed, *work):
    match, turn = scal[0] == 1, scal[1] == 1
    near = pick(match, own[...], first[...])
    far = pick(match, first[...], second[...])
    low, high = pick(turn, far, near), pick(turn, near, far)
    count, area = 2 * SIDE * SIDE, (SIDE // 2) ** 2
    rows = nn(token_rows(0), low[:count]) + nn(token_rows(1), high[:count])
    x_out[...] = rows.astype(BF)
    turns = [half_rows(half, area) for half in range(2)]
    for column in range(2):
        spots = slice(count + 2 * area * column, count + 2 * area * (column + 1))
        g_out[column] = (tn(turns[0], low[spots]) + tn(turns[1], high[spots])).astype(BF)
    normed = (norm_parts(rows)[0] * gain[...]).astype(BF)
    normed_out[...] = normed
    front_body(2, scal[1], (1, 2, 2), normed, (wa, wb), pools, memory, fields, (qp, kp, vp), passed, work)


def front_two(scal, middle, part, other, gain, wa, wb, residual, pools, memory, x_out, normed_out, skip, fields, qp, kp, vp, passed, *work):
    rows = middle[...] + (part[...].astype(F32) + other[...].astype(F32))
    x_out[...] = rows
    normed = (norm_parts(rows)[0] * gain[...]).astype(BF)
    normed_out[...] = normed
    high, low = split(nn(cells(), normed))
    skip[...] = 0.25 * (nn(high, residual[...]) + nn(low, residual[...]))
    front_body(4, scal[1], (2, 1, 1), normed, (wa, wb), pools, memory, fields, (qp, kp, vp), passed, work)


def table_of(shards, block, slot, place):
    line = shards[slot][4 * HD : 4 * HD + 16, :].astype(F32)
    row = 3 * (place if block == 0 else 1 + place)
    return line[row : row + 1, :] + line[row + 1 : row + 2, :] + line[row + 2 : row + 3, :]


def own_bias(bins, table):
    values = jnp.zeros(bins.shape, F32)
    for number in range(2 * FR - 1):
        values = jnp.where(bins == number, table[:, number : number + 1], values)
    return values


def far_bias(table, offset):
    lanes = iota(table.shape, 1)
    return jnp.sum(jnp.where(lanes == offset + 2 * FR - 1, table, 0.0), axis=1, keepdims=True)


def probs_of(scal, bins, table, query, keys):
    tile = own_bias(bins, table)
    rows = query.shape[0]
    bias = jnp.concatenate([tile] * ((rows + 7) // 8), axis=0)[:rows]
    parts = [nt(query, keys[0]) * SCALE + bias]
    for j in range(2):
        raw = nt(query, keys[1 + j]) * SCALE + far_bias(table, scal[4 + j])
        parts.append(jnp.where(scal[2 + j] == 1, raw, NEGATIVE))
    top = functools.reduce(jnp.maximum, [jnp.max(part, axis=1, keepdims=True) for part in parts])
    parts = [jnp.exp(part - top) for part in parts]
    total = sum(jnp.sum(part, axis=1, keepdims=True) for part in parts)
    return [part / total for part in parts]


def heads_of(heads, block):
    return [(slot, place) for slot in range(2) for place in range(heads // 2)]


def attend(block, scal, ta, tb, qp, kp, vp, near, far, wa, wb, rows_out, part_out):
    heads = qp.shape[0]
    shards, weights = (ta, tb), (wa, wb)
    base = 0 if block else 3 * HD
    shape = (8, kp.shape[1])
    bins = (iota(shape, 0) & (FR - 1)) - (iota(shape, 1) & (FR - 1)) + FR - 1
    total = jnp.zeros(part_out.shape, F32)
    nears, fars = ([unpack_heads(item[which], scal[1]) for which in range(2)] for item in (near, far))
    for head, (slot, place) in enumerate(heads_of(heads, block)):
        table = table_of(shards, block, slot, place)
        pool = qp[head]
        keys = (kp[head].astype(BF), nears[0][head], fars[0][head])
        values = (vp[head].astype(BF), nears[1][head], fars[1][head])
        probs = probs_of(scal, bins, table, pool.astype(BF), keys)
        mixture = sum(nn(p.astype(BF), v) for p, v in zip(probs, values))
        line = (mixture + pool).astype(BF)
        rows_out[head] = line
        total = total + nn(line[:, :HD], weights[slot][base + HD * place : base + HD * place + HD, :])
    part_out[...] = total.astype(BF)


def attend_back(block, scal, ta, tb, qp, kp, vp, near, far, wa, wb, rows, middle_grad, dq, dk, dv, d_near, d_far, proj_grad, table_grad):
    heads = qp.shape[0]
    shards, weights = (ta, tb), (wa, wb)
    base = 0 if block else 3 * HD
    shape = (8, kp.shape[1])
    bins = (iota(shape, 0) & (FR - 1)) - (iota(shape, 1) & (FR - 1)) + FR - 1
    branch = middle_grad.astype(BF)
    lanes = iota((1, LANES), 1)
    table_lines = []
    nears, fars = ([unpack_heads(item[which], scal[1]) for which in range(2)] for item in (near, far))
    near_lines, far_lines = ([], []), ([], [])
    for head, (slot, place) in enumerate(heads_of(heads, block)):
        table = table_of(shards, block, slot, place)
        weight = weights[slot][base + HD * place : base + HD * place + HD, :]
        found = tn(rows[head][:, :HD], branch).astype(BF)
        for column in range(proj_grad.shape[1] // (HD * (heads // 2))):
            start = HD * (heads // 2) * column + HD * place
            proj_grad[slot, start : start + HD, :] = found[:, proj_grad.shape[2] * column : proj_grad.shape[2] * (column + 1)]
        grad = widen(nt(branch, weight).astype(BF))
        query = qp[head].astype(BF)
        keys = (kp[head].astype(BF), nears[0][head], fars[0][head])
        values = (vp[head].astype(BF), nears[1][head], fars[1][head])
        probs = probs_of(scal, bins, table, query, keys)
        grad_probs = [nt(grad, v) for v in values]
        inner = sum(jnp.sum(p * d, axis=1, keepdims=True) for p, d in zip(probs, grad_probs))
        low = [(p * (d - inner)).astype(BF) for p, d in zip(probs, grad_probs)]
        dq[head] = sum(nn(s, k) for s, k in zip(low, keys)) * SCALE + grad.astype(F32)
        key_grads = [tn(s, query) * SCALE for s in low]
        value_grads = [tn(p.astype(BF), grad) for p in probs]
        dk[head], dv[head] = key_grads[0], value_grads[0]
        for which, grads in enumerate((key_grads, value_grads)):
            near_lines[which].append(grads[1])
            far_lines[which].append(grads[2])
        score = low[0].astype(F32)
        count = score.shape[0]
        if count % 8:
            score = jnp.concatenate([score, jnp.zeros((8 - count % 8, score.shape[1]), F32)], axis=0)
        score = jnp.sum(score.reshape(-1, 8, score.shape[1]), axis=0)
        line = jnp.zeros((1, LANES), F32)
        for number in range(2 * FR - 1):
            column = jnp.sum(jnp.where(bins == number, score, 0.0), axis=0, keepdims=True)
            line = line + jnp.where(lanes == number, jnp.sum(column, axis=1, keepdims=True), 0.0)
        for j in range(2):
            column = jnp.sum(low[1 + j].astype(F32), axis=0, keepdims=True)
            value = jnp.sum(column, axis=1, keepdims=True)
            line = line + jnp.where(lanes == scal[4 + j] + 2 * FR - 1, value, 0.0)
        table_lines.append(line)
    for which in range(2):
        d_near[which] = pack_heads(near_lines[which], scal[1]).astype(BF)
        d_far[which] = pack_heads(far_lines[which], scal[1]).astype(BF)
    for head, line in enumerate(table_lines):
        table_grad[head : head + 1, :] = line


def field_back(heads, turn, strides, fields, pooled, grads, near, far, pools, memory, pools_grad, memory_grad, work):
    wide, result, grid, totals, rows, held, arrived = work
    half = heads // 2
    copies = [pltpu.make_async_copy(fields.at[i], held.at[i], arrived.at[i]) for i in range(3 * half)]
    for copy in copies:
        copy.start()
    back = {}
    area = (SIDE // strides[1]) ** 2
    for field in range(3):
        stride = strides[field]
        count = SIDE // stride
        fill_weights(wide, pools, field, stride == 1)
        weight_sum = jnp.zeros((27, LANES), F32)
        memory_lines = [jnp.zeros((1, LANES), F32) for _ in range(FR)]
        if field:
            passed = unpack_heads(near[field - 1].astype(F32) + far[field - 1].astype(F32), turn)
        for number, pair in enumerate(pairs_of(heads)):
            grid[...] = jnp.zeros((PADDED, LANES), F32)
            for place in range(2):
                head = 2 * number + place
                if field == 0:
                    put_rows(grid, grads[0][head], place, count)
                else:
                    cotangent = passed[head]
                    for t in range(FR):
                        spot = pl.ds(t, area, stride=FR)
                        line = widen(memory[field - 1, t : t + 1, :])
                        rows[spot, :] = grads[field][head, spot, :] + line * cotangent
                        product = pooled[field - 1][head, spot, :] * cotangent
                        memory_lines[t] = memory_lines[t] + jnp.sum(product, axis=0, keepdims=True)
                    put_rows(grid, rows[0 : FR * area, :], place, count)
            group = held.at[field * half + number]
            copies[field * half + number].wait()
            conv_weight(group, grid, totals, stride)
            weight_sum = weight_sum + weights_of_rows(totals)
            if stride == 1:
                conv_rows(grid, wide, result, 1)
            else:
                conv_back_two(grid, wide, result)
            for place, key in enumerate(pair):
                back[key + (field,)] = result[pl.ds(place, FR * SIDE * SIDE, stride=2), :][:, :HD]
        pools_grad[field, 0:27, :] = weight_sum
        if field:
            for t in range(FR):
                memory_grad[field - 1, t : t + 1, :] = memory_lines[t]
    outs = []
    for slot in range(2):
        columns = [back[(slot, place, field)] for place in range(half) for field in range(3)]
        outs.append(jnp.concatenate(columns, axis=1).astype(BF))
    return outs


def mlp_one(scal, x, part, other, gain, wa, wb, middle_out, normed_out, part_out):
    weights = (wa, wb)
    middle = x[...].astype(F32) + (part[...].astype(F32) + other[...].astype(F32))
    middle_out[...] = middle
    normed = (norm_parts(middle)[0] * gain[...]).astype(BF)
    normed_out[...] = normed
    size = normed.shape[1]
    total = jnp.zeros(part_out.shape, F32)
    for slot in range(2):
        hidden = gelu_parts(nn(normed, weights[slot][:size, :]))[0].astype(BF)
        total = total + nn(hidden, weights[slot][size:, :])
    part_out[...] = total.astype(BF)


def middle_two(scal, skip, part, other, gain, g, middle_out, normed_out, half_out):
    middle = skip[...] + (part[...].astype(F32) + other[...].astype(F32))
    middle_out[...] = middle
    normed_out[...] = (norm_parts(middle)[0] * gain[...]).astype(BF)
    width = half_out.shape[2]
    half_out[0] = normed_out[:, pl.ds(pl.multiple_of(scal[7] * width, LANES), width)]
    half_out[1] = g[scal[7]]


def mlp_two(scal, own, own_grad, *refs):
    halves, others = refs[0:3], refs[3:6]
    up_ref, down_ref = refs[6:8]
    keep, give = refs[8:10]
    packed, packed_down, board, lines = refs[10:14]
    width = up_ref.shape[1] // 2
    core = scal[7]
    start = pl.multiple_of(core * width, LANES)
    rest = pl.multiple_of((1 - core) * width, LANES)
    up, down = up_ref[:, pl.ds(start, width)], down_ref[pl.ds(start, width), :]
    board[0, 0] = own[...]
    for column in range(2):
        board[0, 1, :, width * column : width * (column + 1)] = own_grad[column]
    for d in range(3):
        for which in range(2):
            board[d + 1, which, :, pl.ds(start, width)] = halves[d][which]
            board[d + 1, which, :, pl.ds(rest, width)] = others[d][which]
    up_total = jnp.zeros(up.shape, F32)
    down_total = jnp.zeros(down.shape, F32)
    for d in range(4):
        rows, grad = board[d, 0], board[d, 1]
        value, slope = gelu_parts(nn(rows, up))
        hidden = value.astype(BF)
        lines[0] = nn(hidden, down)
        up_low = (nt(grad, down) * slope).astype(BF)
        lines[1] = nt(up_low, up)
        for which in range(2):
            spots = slice(104 * (2 * d + which), 104 * (2 * d + which) + rows.shape[0])
            keep[spots, :] = lines[which, :, pl.ds(start, width)].astype(BF)
            give[spots, :] = lines[which, :, pl.ds(rest, width)].astype(BF)
        up_total = up_total + tn(rows, up_low)
        down_total = down_total + tn(hidden, grad)
    packed[...] = up_total.astype(BF)
    packed_down[0:width, :] = down_total[:, :width].astype(BF)
    packed_down[width:, :] = down_total[:, width:].astype(BF)


def quarter_of(scal, peer):
    one = 1 - scal[8] if peer % 2 else scal[8]
    two = 1 - scal[9] if peer // 2 else scal[9]
    return one + 2 * two


def cut(scal, full, parts):
    rows = parts[0].shape[1]
    for peer in range(4):
        spots = pl.ds(pl.multiple_of(quarter_of(scal, peer) * rows, 16), rows)
        for slot in range(2):
            parts[peer][slot] = full[slot, spots, :]


def sum_planes(*refs):
    one, two = refs[-2:]
    start = 0
    for number in range(len(refs) // 4):
        parts = refs[4 * number : 4 * number + 4]
        rows = parts[0].shape[1]
        for slot, out in ((0, one), (1, two)):
            total = (parts[0][slot].astype(F32) + parts[1][slot].astype(F32)) + (
                parts[2][slot].astype(F32) + parts[3][slot].astype(F32)
            )
            out[start : start + rows, :] = total.astype(BF)
        start += rows


def gather_parts(scal, parts, start, full):
    rows = full.shape[0] // 8
    for number, part in enumerate(parts):
        core = scal[7] if number < 4 else 1 - scal[7]
        spots = pl.ds(pl.multiple_of((2 * quarter_of(scal, number % 4) + core) * rows, 16), rows)
        full[spots, :] = part[start : start + rows, :].astype(F32)


def put_totals(full, start, pools, memory):
    for field in range(3):
        pools[field] = full[start : start + 27, LANES * field : LANES * field + HD]
    for which in range(2):
        memory[which] = full[start + 32 : start + 32 + FR, LANES * which : LANES * which + HD]


def stack_four(scal, own, beside, far, last, out):
    z = scal[10]
    turn, upper = lax.rem(z, 2), lax.div(z, 2)
    for piece, parity, pair in (
        (own, turn, upper),
        (beside, 1 - turn, upper),
        (far, turn, 1 - upper),
        (last, 1 - turn, 1 - upper),
    ):
        out[2 * pair + parity] = piece[...]


def finish_residual(scal, own, other, out):
    size, width = own.shape[1:]
    for core, source in ((scal[7], own), (1 - scal[7], other)):
        for shard in range(4):
            rows = pl.ds(pl.multiple_of(2 * size * (shard % 2) + size * core, 16), size)
            columns = slice(width * (shard // 2), width * (shard // 2 + 1))
            out[rows, columns] = source[shard].astype(F32)


def take_piece(scal, a, b, c, d, piece):
    half = piece.shape[0]
    start = pl.multiple_of(48 * scal[7], 16)
    for peer, part in enumerate((a, b, c, d)):

        @pl.when(quarter_of(scal, peer) == 3)
        def _():
            piece[...] = part[pl.ds(start, half), :]


def finish_two(scal, *refs):
    parts = refs[0:8]
    qkv, proj, up, down, pools, memory, gain, full, full_mlp = refs[8:]
    gather_parts(scal, parts, 0, full)
    gather_parts(scal, parts, full.shape[0] // 8, full_mlp)
    width = full.shape[1]
    qkv[...] = full[0:576, :]
    proj[:, :width] = full[576:768, :]
    proj[0:96, width:] = full[768:864, :]
    proj[96:192, width:] = full[960:1056, :]
    up[...] = full_mlp[0:384, :]
    down[...] = full_mlp[384:768, :]
    put_totals(full_mlp, 768, pools, memory)
    gain[0:width], gain[width:] = full_mlp[808, :], full_mlp[809, :]


def finish_one(scal, *refs):
    qkv, proj, table, second_table, pools, memory, gain, second_gain, third_gain, full = refs[8:]
    gather_parts(scal, refs[0:8], 0, full)
    qkv[...] = full[0:288, :]
    proj[...] = full[288:384, :]
    bins = table.shape[1]
    table[...] = full[384:385, :bins]
    second_table[...] = full[385:387, :bins]
    put_totals(full, 400, pools, memory)
    second_gain[...] = full[440, :]
    third_gain[...] = full[441, :]
    gain[...] = full[442, :]


def finish_wide(scal, own_up, other_up, own_down, other_down, up, down):
    first = scal[7] == 0
    size = up.shape[0]
    width = size // 2
    up[:, :width] = pick(first, own_up[...], other_up[...]).astype(F32)
    up[:, width:] = pick(first, other_up[...], own_up[...]).astype(F32)
    one = pick(first, own_down[...], other_down[...]).astype(F32)
    two = pick(first, other_down[...], own_down[...]).astype(F32)
    down[:width, :width], down[:width, width:] = one[:width, :], one[width:, :]
    down[width:, :width], down[width:, width:] = two[:width, :], two[width:, :]


def add_cores(keep, other, *outs):
    for d in range(4):
        for which in range(2):
            spots = slice(104 * (2 * d + which), 104 * (2 * d + which) + outs[d].shape[1])
            outs[d][which] = (keep[spots, :].astype(F32) + other[spots, :].astype(F32)).astype(BF)


def whole_columns(scal, own, other):
    first = scal[7] == 0
    return jnp.concatenate([pick(first, own, other), pick(first, other, own)], axis=1)


def add_both(one, one_other, two, two_other, one_out, two_out):
    one_out[...] = (one[...].astype(F32) + one_other[...].astype(F32)).astype(BF)
    two_out[...] = (two[...].astype(F32) + two_other[...].astype(F32)).astype(BF)


def add_two(one, two, out):
    out[...] = (one[...].astype(F32) + two[...].astype(F32)).astype(BF)


def sum_four(a, b, c, d, out):
    total = (a[...].astype(F32) + b[...].astype(F32)) + (c[...].astype(F32) + d[...].astype(F32))
    out[...] = total.astype(BF)


def back_attend_two(scal, part, other, g, middle, gain, normed, *refs):
    ins, outs = refs[0:10], refs[10:]
    final = (middle[...] + whole_columns(scal, part[0], other[0]).astype(F32)).astype(BF)
    area = (SIDE // 2) ** 2
    outs[10][...] = nn(half_rows(scal[1], area), final).astype(BF)
    outs[11][...] = nn(half_rows(1 - scal[1], area), final).astype(BF)
    grad, gain_grad = norm_back(whole_columns(scal, part[1], other[1]).astype(F32), middle[...], gain[...])
    middle_grad = jnp.concatenate([g[0], g[1]], axis=1).astype(F32) + grad
    outs[0][...] = middle_grad
    outs[1][...] = gain_grad
    width = outs[9].shape[2]
    linear = (0.25 * outs[0][:, pl.ds(pl.multiple_of(scal[7] * width, LANES), width)]).astype(BF)
    high, low = split(nn(cells(), normed[...]))
    found = (tn(high, linear) + tn(low, linear)).astype(BF)
    size = outs[9].shape[1]
    turned = scal[1] == 1
    outs[9][0] = pick(turned, found[size:], found[:size])
    outs[9][1] = pick(turned, found[:size], found[size:])
    attend_back(1, scal, *ins, middle_grad, *outs[2:9])


def put_small(small, pools_grad, memory_grad):
    small[...] = jnp.zeros(small.shape, F32)
    for field in range(3):
        small[0:27, LANES * field : LANES * (field + 1)] = pools_grad[field, 0:27, :]
    for which in range(2):
        small[32 : 32 + FR, LANES * which : LANES * (which + 1)] = memory_grad[which]


def back_front_two(scal, middle_grad, normed_ref, fields, kp, vp, dq, dk, dv, near, far, wa, wb, residual, pools, memory, proj_grad, residual_grad, gain_grad, part_out, keep, one, two, three, small, pools_grad, memory_grad, full, *work):
    weights = (wa, wb)
    normed = normed_ref[...]
    backs = field_back(4, scal[1], (2, 1, 1), fields, (kp, vp), (dq, dk, dv), near, far, pools, memory, pools_grad, memory_grad, work)
    total = jnp.zeros(part_out.shape, F32)
    width = full.shape[2]
    columns = pl.ds(pl.multiple_of(scal[7] * width, LANES), width)
    linear = (0.25 * middle_grad[:, columns]).astype(BF)
    cell = cells()
    for slot in range(2):
        full[slot, 0:576, :] = tn(backs[slot], normed).astype(BF)
        full[slot, 576:864, :] = proj_grad[slot, 0:288, :]
        full[slot, 864:960, :] = residual_grad[slot, 0:96, :]
        full[slot, 960:1056, :] = proj_grad[slot, 288:384, :]
        full[slot, 1056:1152, :] = residual_grad[slot, 96:192, :]
        total = total + nn(backs[slot], weights[slot][...])
    cut(scal, full, (keep, one, two, three))
    high, low = split(nt(linear, residual[:, columns]))
    part_out[...] = (total + tn(cell, high) + tn(cell, low)).astype(BF)
    put_small(small, pools_grad, memory_grad)
    small[40:41, :] = 0.5 * gain_grad[:, :width]
    small[41:42, :] = 0.5 * gain_grad[:, width:]


def back_mlp_one(scal, part, other, x, gain, normed_ref, wa, wb, small, small_other, grad_out, part_out, gain_grad_ref, keep, one, two, three, full):
    weights = (wa, wb)
    grad, gain_grad = norm_back(part[...].astype(F32) + other[...].astype(F32), x[...], gain[...])
    grad_out[...] = grad
    gain_grad_ref[...] = gain_grad
    branch = grad.astype(BF)
    normed = normed_ref[...]
    total = jnp.zeros(part_out.shape, F32)
    whole = (small[...] + small_other[...]).astype(BF)
    size = normed.shape[1]
    for slot in range(2):
        up, down = weights[slot][:size, :], weights[slot][size:, :]
        value, slope = gelu_parts(nn(normed, up))
        up_low = (nt(branch, down) * slope).astype(BF)
        full[slot, 0:size, :] = tn(normed, up_low).astype(BF)
        full[slot, size : 2 * size, :] = tn(value.astype(BF), branch).astype(BF)
        full[slot, 2 * size : 2 * size + 64, :] = whole
        full[slot, 2 * size + 64 :, :] = jnp.zeros((64, size), BF)
        total = total + nt(up_low, up)
    part_out[...] = total.astype(BF)
    cut(scal, full, (keep, one, two, three))


def back_attend_one(scal, part, other, g, middle, gain, *refs):
    ins, outs = refs[0:10], refs[10:]
    grad, gain_grad = norm_back(part[...].astype(F32) + other[...].astype(F32), middle[...], gain[...])
    middle_grad = g[...] + grad
    outs[0][...] = middle_grad
    outs[1][...] = gain_grad
    attend_back(0, scal, *ins, middle_grad, *outs[2:9])


def back_front_one(scal, normed_ref, fields, kp, vp, dq, dk, dv, near, far, wa, wb, pools, memory, gain_two_grad, gain_three_grad, qkv_grad, part_out, small, pools_grad, memory_grad, *work):
    weights = (wa, wb)
    normed = normed_ref[...]
    backs = field_back(2, scal[1], (1, 2, 2), fields, (kp, vp), (dq, dk, dv), near, far, pools, memory, pools_grad, memory_grad, work)
    total = jnp.zeros(part_out.shape, F32)
    for slot in range(2):
        qkv_grad[slot] = tn(backs[slot], normed).astype(BF)
        total = total + nn(backs[slot], weights[slot][: 3 * HD, :])
    part_out[...] = total.astype(BF)
    put_small(small, pools_grad, memory_grad)
    small[40:41, :] = 0.5 * gain_two_grad[...]
    small[41:42, :] = 0.5 * gain_three_grad[...]


def back_tokens(scal, part, other, x, gain, middle_grad, qkv_grad, proj_grad, table_one, table_two, small, small_other, keep_rows, send_rows, keep, one, two, three, full):
    grad, gain_grad = norm_back(part[...].astype(F32) + other[...].astype(F32), x[...].astype(F32), gain[...])
    rows = (middle_grad[...] + grad).astype(BF)
    turn = scal[1]
    keep_rows[...] = nn(half_rows(turn, SIDE * SIDE), rows).astype(BF)
    send_rows[...] = nn(half_rows(1 - turn, SIDE * SIDE), rows).astype(BF)
    line = iota((64, 1), 0)
    whole = jnp.where(line == 42, gain_grad, small[...] + small_other[...]).astype(BF)
    for slot in range(2):
        full[slot, 0:288, :] = qkv_grad[slot]
        full[slot, 288:384, :] = proj_grad[slot]
        lines = jnp.concatenate([table_one[slot : slot + 1, :], table_two[2 * slot : 2 * slot + 2, :], jnp.zeros((13, LANES), F32)], axis=0)
        full[slot, 384:400, :] = jnp.concatenate([lines, jnp.zeros((16, 2 * LANES), F32)], axis=1).astype(BF)
        full[slot, 400:464, :] = whole
        full[slot, 464:512, :] = jnp.zeros((48, full.shape[2]), BF)
    cut(scal, full, (keep, one, two, three))


def scalars(pairs, other_pairs, videos, out):
    plane, core, head = lax.axis_index("plane"), lax.axis_index("core"), lax.axis_index("head")
    upper, turn = lax.div(head, 2), lax.rem(head, 2)
    clip = 4 * plane + 2 * turn + upper
    match = core == turn
    own = videos[clip]
    out[0] = jnp.where(match, 1, 0)
    out[1] = turn
    for j in range(2):
        before = clip - 1 - j
        there = (before >= 0) & (videos[jnp.maximum(before, 0)] == own)
        out[2 + j] = jnp.where(there, 1, 0)
        out[4 + j] = jnp.where(match, pairs[upper, j], other_pairs[upper, j])
    out[6] = jnp.where(upper == core, 1, 0)
    out[7] = core
    out[8] = lax.rem(plane, 2)
    out[9] = lax.rem(lax.div(plane, 2), 2)
    out[10] = head


def pack(tokens, grad_out, table_one, table_two, qkv_one, proj_one, rows, first):
    count, width = tokens.shape
    area = grad_out.shape[0]
    rows[0:count, :] = tokens[...]
    rows[count : count + area, :] = grad_out[:, :width]
    rows[count + area :, :] = grad_out[:, width:]
    lines = []
    for table in (table_one[0:1, :], table_two[0:1, :], table_two[1:2, :]):
        high = table.astype(BF).astype(F32)
        middle = (table - high).astype(BF).astype(F32)
        lines += [high, middle, table - high - middle]
    first[0 : 3 * HD, :] = qkv_one[...]
    first[3 * HD : 4 * HD, :] = proj_one[...]
    stacked = jnp.concatenate(lines + [jnp.zeros((7, lines[0].shape[1]), F32)], axis=0)
    first[4 * HD :, :] = jnp.concatenate([stacked, jnp.zeros((16, width - stacked.shape[1]), F32)], axis=1).astype(BF)


def join(one, two, first, second, third, out):
    out[0 : one.shape[0], :] = one[...]
    out[one.shape[0] :, :] = two[...]


SMEM = pl.BlockSpec(memory_space=pltpu.SMEM)


FAR = pl.BlockSpec(memory_space=pltpu.HBM)
NEAR = pl.BlockSpec(memory_space=pltpu.VMEM)


def moved(body, counts, left, early, late, *refs):
    ins_count, outs_count, work_count = counts
    ins, outs = list(refs[:ins_count]), refs[ins_count : ins_count + outs_count]
    spot = ins_count + outs_count
    saved = refs[spot : spot + len(early) + len(late)]
    spot += len(early) + len(late)
    work = refs[spot : spot + work_count]
    buffers, arrived = refs[spot + work_count : -1], refs[-1]
    brought = [pltpu.make_async_copy(ins[item], buffers[i], arrived.at[i]) for i, item in enumerate(left)]
    first = len(left)
    sent = [pltpu.make_async_copy(ins[item], saved[i], arrived.at[first + i]) for i, item in enumerate(early)]
    for copy in brought + sent:
        copy.start()
    for i, item in enumerate(left):
        brought[i].wait()
        ins[item] = buffers[i]
    body(*ins, *outs, *work)
    first += len(early)
    last = [
        pltpu.make_async_copy(outs[item], saved[len(early) + i], arrived.at[first + i]) for i, item in enumerate(late)
    ]
    for copy in last:
        copy.start()
    for copy in sent + last:
        copy.wait()


def kernel(body, name, outs, ins, work=(), left=(), early=(), late=(), raw=(), far_outs=(), limit=16, flops=2 * 10**8):
    if limit == 16 and (left or early or late):
        found = kernel(body, name, outs, ins, work, (), (), (), raw, far_outs)
        return (*found, *[list(ins)[item] for item in early], *[found[item] for item in late])
    ins = list(ins)
    in_specs = []
    for number, item in enumerate(ins):
        if number == 0 and item.dtype == jnp.int32:
            in_specs.append(SMEM)
        else:
            in_specs.append(FAR if number in left or number in raw else NEAR)
    results = [jax.ShapeDtypeStruct(shape, kind) for shape, kind in outs]
    extra = [jax.ShapeDtypeStruct(ins[item].shape, ins[item].dtype) for item in early] + [results[item] for item in late]
    size = sum(int(np.prod(item.shape)) * item.dtype.itemsize for item in [*ins, *results, *extra])
    work = list(work)
    count = len(work)
    if left or early or late:
        body = functools.partial(moved, body, (len(ins), len(results), count), tuple(left), tuple(early), tuple(late))
        work += [pltpu.VMEM(ins[number].shape, ins[number].dtype) for number in left]
        work.append(pltpu.SemaphoreType.DMA((len(left) + len(early) + len(late),)))
    return pl.pallas_call(
        body,
        out_shape=tuple(results + extra),
        in_specs=in_specs,
        out_specs=tuple([FAR if number in far_outs else NEAR for number in range(len(results))] + [FAR] * len(extra)),
        scratch_shapes=work,
        name=name,
        cost_estimate=pl.CostEstimate(flops=flops, bytes_accessed=size, transcendentals=0),
        compiler_params=pltpu.CompilerParams(vmem_limit_bytes=limit << 20),
    )(*ins)


def scratch(*rows):
    return [pltpu.VMEM((count, LANES), F32) for count in rows]


def field_work(heads):
    groups = 3 * heads // 2
    return [pltpu.VMEM((groups, PADDED, LANES), F32), pltpu.SemaphoreType.DMA((groups,))]


FRONT_WORK = (216, 800)
BACK_WORK = (216, 800, PADDED, 216, 400)


def after(values, events):
    return lax.optimization_barrier((values, events))


def swap(values):
    return lax.ppermute(values, "core", [(0, 1), (1, 0)])


def cross_route():
    route = []
    for core in range(2):
        low, other = 2 * core, 2 - 2 * core
        route += [(core * 4 + low + i, core * 4 + other + i) for i in range(2)]
    return route


def beside(values):
    return lax.ppermute(values, "head", [(z, z ^ 1) for z in range(4)])


def choose(scal, own, other, out):
    out[...] = pick(scal[6] == 1, own[...], other[...])


def choose_half(sizes, scal, own, other, out):
    start, put = 0, 0
    for size in sizes:
        half = size // 2
        spots = pl.ds(pl.multiple_of(start + half * scal[7], 16), half)
        out[put : put + half, :] = pick(scal[6] == 1, own[spots, :], other[spots, :])
        start, put = start + size, put + half


def chosen(scal, own, other):
    return kernel(choose, "choose_shard", [(own.shape, own.dtype)], [scal, own, other])[0]


def over(values, scal):
    return chosen(scal, values, lax.ppermute(values, ("core", "head"), cross_route()))


def spread(values, scal):
    one = over(values, scal)
    return one, beside(one)


def reverse(route):
    return [(end, start) for start, end in route]


def clip_routes(planes, distance):
    def place(clip):
        slot = clip % 4
        return (clip // 4) * 4 + 2 * (slot % 2) + slot // 2

    total = 4 * planes
    return [(place(clip), place(clip + distance)) for clip in range(total) if 0 <= clip + distance < total]


def half_routes():
    def place(core, a, b):
        return core * 4 + 2 * a + b

    one, two, three = [], [], []
    for a in range(2):
        for b in range(2):
            one += [(place(b, a, b), place(1 - b, a, b)), (place(1 - b, a, b), place(1 - b, a, 1 - b))]
            two += [(place(1 - b, a, b), place(b, a, 1 - b))]
            three += [(place(1 - b, a, b), place(b, a, 1 - b))]
    return one, two, three


def turn_by(values, distance):
    return lax.ppermute(values, "head", [(z, (z + distance) % 4) for z in range(4)])


def local(
    planes,
    tokens,
    grad_out,
    video_ids,
    offsets,
    gain_one,
    qkv_one,
    pools_one,
    memory_one,
    table_one,
    proj_one,
    gain_two,
    up_one,
    down_one,
    gain_three,
    qkv_two,
    residual_two,
    pools_two,
    memory_two,
    table_two,
    proj_two,
    gain_four,
    up_two,
    down_two,
):
    match = lax.axis_index("core") == lax.axis_index("head") % 2
    (scal,) = pl.pallas_call(
        scalars,
        out_shape=(jax.ShapeDtypeStruct((16,), jnp.int32),),
        in_specs=[SMEM] * 3,
        out_specs=(SMEM,),
        name="scalars",
    )(offsets, swap(offsets), video_ids)
    gains = [item.reshape(1, -1) for item in (gain_one, gain_two, gain_three, gain_four)]

    half = residual_two.shape[1] // 2
    qkv_one_t, qkv_two_t = qkv_one.T, qkv_two.T
    rows_in, first_bundle = kernel(
        pack,
        "pack",
        [((300, half), BF), ((400, half), BF)],
        [tokens, grad_out, table_one, table_two, qkv_one_t, proj_one],
        left=range(6),
        limit=56,
    )
    route_one, route_two, route_three = half_routes()
    axes = ("core", "head")
    first_over = over(first_bundle, scal)
    first_all = (first_over, beside(first_over))
    tok_one, tok_two = lax.ppermute(rows_in, axes, route_one), lax.ppermute(rows_in, axes, route_two)
    (mlp_bundle,) = kernel(
        join, "join", [((768, half), BF)], [up_one, down_one, first_over, tok_one, tok_two], left=(0, 1), limit=48
    )
    mlp_over = over(mlp_bundle, scal)

    width = qkv_one.shape[0]
    wide = residual_two.shape[1]
    n1, n2 = FR * SIDE * SIDE, FR * SIDE * SIDE // 4
    a1, a2 = n2 // FR, n1 // FR

    x1, _, g, fields1, qp1, kp1, vp1, passed1, *saved = kernel(
        front_one,
        "front_one",
        [
            ((n1, width), BF),
            ((n1, width), BF),
            ((2, n2, half), BF),
            ((3, PADDED, LANES), F32),
            ((2, n1, LANES), F32),
            ((2, n2, LANES), F32),
            ((2, n2, LANES), F32),
            ((2, a1, 2 * HD), BF),
        ],
        [scal, rows_in, tok_one, tok_two, gains[0], *first_all, pools_one, memory_one],
        scratch(*FRONT_WORK) + field_work(2),
        early=(5, 6),
        late=(0, 1, 2, 4, 5, 6),
        far_outs=(3,),
    )
    first_kept, (x1_kept, normed1, g_kept, qp1_kept, kp1_kept, vp1_kept) = saved[:2], saved[2:]
    places = ("plane", "head")
    near1 = lax.ppermute(passed1, places, clip_routes(planes, 1))
    far1 = lax.ppermute(passed1, places, clip_routes(planes, 2))
    (mlp_over, late_qkv), (x1,) = after((mlp_over, qkv_two_t), (x1,))
    mlp_all = (mlp_over, beside(mlp_over))
    qkv_two_all = spread(late_qkv, scal)
    late_proj, (first,) = after(proj_two, qkv_two_all[0:1])
    qkv_two_all = (first, qkv_two_all[1])
    proj_two_all = spread(late_proj, scal)
    attn1_ins = [*first_all, qp1, kp1, vp1, near1, far1, *first_all]
    _, part1, near1_kept, far1_kept, rows1 = kernel(
        functools.partial(attend, 0),
        "attend_one",
        [((2, n1, LANES), BF), ((n1, width), BF)],
        [scal, *attn1_ins],
        early=(6, 7),
        late=(0,),
    )
    middle1, _, part_mlp1, *mlp_kept, middle1_kept, mlp_normed1 = kernel(
        mlp_one,
        "mlp_one",
        [((n1, width), F32), ((n1, width), BF), ((n1, width), BF)],
        [scal, x1, part1, swap(part1), gains[1], *mlp_all],
        early=(5, 6),
        late=(0, 1),
    )
    _, _, skip, fields2, qp2, kp2, vp2, passed2, *saved = kernel(
        front_two,
        "front_two",
        [
            ((n1, width), F32),
            ((n1, width), BF),
            ((n2, wide), F32),
            ((6, PADDED, LANES), F32),
            ((4, n2, LANES), F32),
            ((4, n1, LANES), F32),
            ((4, n1, LANES), F32),
            ((2, a2, 4 * HD), BF),
        ],
        [scal, middle1, part_mlp1, swap(part_mlp1), gains[2], *qkv_two_all, residual_two, pools_two, memory_two],
        scratch(*FRONT_WORK) + field_work(4),
        early=(5, 6),
        late=(0, 1, 4, 5, 6),
        far_outs=(3,),
    )
    qkv_two_kept, (x2, normed2, qp2_kept, kp2_kept, vp2_kept) = saved[:2], saved[2:]
    near2 = lax.ppermute(passed2, places, clip_routes(planes, 1))
    far2 = lax.ppermute(passed2, places, clip_routes(planes, 2))
    attn2_ins = [*first_kept, qp2, kp2, vp2, near2, far2, *proj_two_all]
    _, part2, near2_kept, far2_kept, *proj_two_kept, rows2 = kernel(
        functools.partial(attend, 1),
        "attend_two",
        [((4, n2, LANES), BF), ((n2, wide), BF)],
        [scal, *attn2_ins],
        left=(1, 2),
        early=(6, 7, 8, 9),
        late=(0,),
    )
    _, mlp_normed2, own_half, middle2 = kernel(
        middle_two,
        "middle_two",
        [((n2, wide), F32), ((n2, wide), BF), ((2, n2, half), BF)],
        [scal, skip, part2, swap(part2), gains[3], g_kept],
        left=(5,),
        late=(0,),
    )
    halves = [turn_by(own_half, d) for d in (1, 2, 3)]
    found = kernel(
        mlp_two,
        "mlp_two",
        [((832, half), BF)] * 2 + [((wide, half), BF)] * 2,
        [scal, mlp_normed2, g_kept, *halves, *(swap(item) for item in halves), up_two, down_two],
        [pltpu.VMEM((4, 2, n2, wide), BF), pltpu.VMEM((2, n2, wide), F32)],
        left=(2, 9, 10),
    )
    sums = kernel(add_cores, "add_cores", [((2, n2, half), BF)] * 4, [found[0], swap(found[1])])
    sums = [sums[0]] + [turn_by(sums[d], -d) for d in (1, 2, 3)]
    def across(values, bit):
        return lax.ppermute(values, "plane", [(i, i ^ bit) for i in range(planes)])

    def peers(parts):
        return [parts[0]] + [across(parts[peer], peer) for peer in (1, 2, 3)]

    def add_wide(pair, bits):
        received = [across(item, bit) for item, bit in zip(pair, bits)]
        return kernel(add_both, "add_wide", [((wide, half), BF)] * 2, [pair[0], received[0], pair[1], received[1]])

    wide_sum = add_wide(found[2:4], (1, 2))
    (row_sum,) = kernel(sum_four, "sum_rows", [((2, n2, half), BF)], sums)
    row_sum, (wide_sum,) = after(row_sum, (wide_sum,))
    middle_grad2, gain_four_grad, dq2, dk2, dv2, d_near2, d_far2, proj_two_grad, table_two_grad, residual_grad, keep, send = kernel(
        back_attend_two,
        "back_attend_two",
        [
            ((n2, wide), F32),
            ((1, wide), F32),
            ((4, n2, LANES), F32),
            ((4, n1, LANES), F32),
            ((4, n1, LANES), F32),
            ((2, a2, 4 * HD), BF),
            ((2, a2, 4 * HD), BF),
            ((2, 4 * HD, width), BF),
            ((4, LANES), F32),
            ((2, 192, half), BF),
            ((n2 // 2, wide), BF),
            ((n2 // 2, wide), BF),
        ],
        [
            scal, row_sum, swap(row_sum), g_kept, middle2, gains[3], normed2,
            *first_kept, qp2_kept, kp2_kept, vp2_kept, near2_kept, far2_kept, *proj_two_kept, rows2,
        ],
        left=[3, 4, *range(6, 17)],
    )
    near_grad2 = lax.ppermute(d_near2, places, clip_routes(planes, -1))
    far_grad2 = lax.ppermute(d_far2, places, clip_routes(planes, -2))

    wide_sum = add_wide(wide_sum, (2, 1))
    (near_grad2, far_grad2), (wide_sum,) = after((near_grad2, far_grad2), (wide_sum,))
    part_back2, *sends2, small2, _, _ = kernel(
        back_front_two,
        "back_front_two",
        [
            ((n1, width), BF),
            *[((2, 288, width), BF)] * 4,
            ((64, width), F32),
            ((3, 32, LANES), F32),
            ((2, FR, LANES), F32),
        ],
        [
            scal, middle_grad2, normed2, fields2, kp2_kept, vp2_kept, dq2, dk2, dv2, near_grad2, far_grad2,
            *qkv_two_kept, residual_two, pools_two, memory_two, proj_two_grad, residual_grad, gain_four_grad,
        ],
        [pltpu.VMEM((2, 1152, width), BF)] + scratch(*BACK_WORK) + field_work(4),
        [2, 4, 5, 11, 12, 13],
        raw=[3],
    )
    received2 = peers(sends2)
    grad1, part_mlp_back, gain_three_grad, *sends_mlp = kernel(
        back_mlp_one,
        "back_mlp_one",
        [((n1, width), F32), ((n1, width), BF), ((1, width), F32)] + [((2, 224, width), BF)] * 4,
        [scal, part_back2, swap(part_back2), x2, gains[2], mlp_normed1, *mlp_kept, small2, swap(small2)],
        [pltpu.VMEM((2, 896, width), BF)],
        [3, 5, 6, 7],
    )
    middle_grad1, gain_two_grad, dq1, dk1, dv1, d_near1, d_far1, proj_one_grad, table_one_grad = kernel(
        back_attend_one,
        "back_attend_one",
        [
            ((n1, width), F32),
            ((1, width), F32),
            ((2, n1, LANES), F32),
            ((2, n2, LANES), F32),
            ((2, n2, LANES), F32),
            ((2, a1, 2 * HD), BF),
            ((2, a1, 2 * HD), BF),
            ((2, HD, width), BF),
            ((2, LANES), F32),
        ],
        [
            scal, part_mlp_back, swap(part_mlp_back), grad1, middle1_kept, gains[1],
            *first_kept, qp1_kept, kp1_kept, vp1_kept, near1_kept, far1_kept, *first_kept, rows1,
        ],
        left=[4, *range(6, 16)],
    )
    near_grad1 = lax.ppermute(d_near1, places, clip_routes(planes, -1))
    far_grad1 = lax.ppermute(d_far1, places, clip_routes(planes, -2))
    bit = 4
    while bit < planes:
        wide_sum = add_wide(wide_sum, (bit, bit))
        bit *= 2
    received_mlp = peers(sends_mlp)
    rows_received = lax.ppermute(send, axes, route_three)
    (near_grad1, far_grad1), (wide_sum, received2, rows_received) = after(
        (near_grad1, far_grad1), (wide_sum, received2, rows_received)
    )
    qkv_one_grad, part_back1, small1, _, _ = kernel(
        back_front_one,
        "back_front_one",
        [((2, 3 * HD, width), BF), ((n1, width), BF), ((64, width), F32), ((3, 32, LANES), F32), ((2, FR, LANES), F32)],
        [
            scal, normed1, fields1, kp1_kept, vp1_kept, dq1, dk1, dv1, near_grad1, far_grad1,
            *first_kept, pools_one, memory_one, gain_two_grad, gain_three_grad,
        ],
        scratch(*BACK_WORK) + field_work(2),
        [1, 3, 4, 10, 11],
        raw=[2],
    )
    part_back1, (received_mlp,) = after(part_back1, (received_mlp,))
    tok_keep, tok_send, *sends1 = kernel(
        back_tokens,
        "back_tokens",
        [((n1 // 2, width), BF), ((n1 // 2, width), BF)] + [((2, 128, width), BF)] * 4,
        [
            scal, part_back1, swap(part_back1), x1_kept, gains[0], middle_grad1, qkv_one_grad, proj_one_grad,
            table_one_grad, table_two_grad, small1, swap(small1),
        ],
        [pltpu.VMEM((2, 512, width), BF)],
        [3],
    )
    tok_received = lax.ppermute(tok_send, axes, route_three)

    def combine(body, label, rows, ins, count=1):
        return kernel(body, label, [((rows, width), BF)] * count, ins)

    back_route = reverse(cross_route())
    received1 = peers(sends1)
    rows_two, rows_mlp, rows_one = 288, 224, 128
    one2, two2 = combine(sum_planes, "sum_planes_two", rows_two + rows_mlp, received2 + received_mlp, 2)
    beside2 = beside(two2)
    up_two_sum, down_two_sum = kernel(
        finish_wide, "finish_wide", [((wide, wide), F32), ((wide, wide), F32)], [scal, wide_sum[0], swap(wide_sum[0]), wide_sum[1], swap(wide_sum[1])]
    )
    received1, (up_two_sum, down_two_sum) = after(received1, (up_two_sum, down_two_sum))
    one1, two1 = combine(sum_planes, "sum_planes_one", rows_one, received1, 2)
    beside1 = beside(two1)
    (beside2,), (one1, tok_received) = after((beside2,), (one1, tok_received))
    tokens_grad = jnp.where(match, tok_keep, tok_received)
    (total2,) = combine(add_two, "add_pair_two", rows_two + rows_mlp, [one2, beside2])
    cross2 = lax.ppermute(total2, axes, back_route)
    (beside1,), (total2,) = after((beside1,), (total2,))
    (total1,) = combine(add_two, "add_pair_one", rows_one, [one1, beside1])
    cross1 = lax.ppermute(total1, axes, back_route)
    (cross2,), (cross1,) = after((cross2,), (cross1,))
    (total2,) = combine(add_two, "add_cross_two", rows_two + rows_mlp, [total2, cross2])
    bit = 4
    while bit < planes:
        (total2,) = combine(add_two, "add_planes_two", rows_two + rows_mlp, [total2, across(total2, bit)])
        bit *= 2

    def halves_of(total, sizes):
        body = functools.partial(choose_half, sizes)
        return combine(body, "choose_half", sum(sizes) // 2, [scal, total, swap(total)])

    half2 = halves_of(total2, (rows_two, rows_mlp))
    (total1,) = combine(add_two, "add_cross_one", rows_one, [total1, cross1])
    bit = 4
    while bit < planes:
        (total1,) = combine(add_two, "add_planes_one", rows_one, [total1, across(total1, bit)])
        bit *= 2
    parts2 = peers(list(half2) * 4)
    parts1 = peers(halves_of(total1, (rows_one,)) * 4)
    parts2, parts1 = after(parts2, parts1)
    (piece,) = kernel(take_piece, "take_piece", [((96, width), BF)], [scal, *parts2])
    small_shapes = [(pools_one.shape, F32), (memory_one.shape, F32)]
    qkv_two_sum, proj_two_sum, up_one_sum, down_one_sum, pools_two_sum, memory_two_sum, gain_four_sum = kernel(
        finish_two,
        "finish_two",
        [(qkv_two_t.shape, F32), (proj_two.shape, F32), (up_one.shape, F32), (down_one.shape, F32)]
        + small_shapes
        + [((wide,), F32)],
        [scal, *parts2, *(swap(part) for part in parts2)],
        [pltpu.VMEM((1152, width), F32), pltpu.VMEM((896, width), F32)],
    )
    (qkv_one_sum, proj_one_sum, table_one_sum, table_two_sum, pools_one_sum, memory_one_sum, *gain_sums) = kernel(
        finish_one,
        "finish_one",
        [(qkv_one_t.shape, F32), (proj_one.shape, F32), (table_one.shape, F32), (table_two.shape, F32)]
        + small_shapes
        + [((width,), F32)] * 3,
        [scal, *parts1, *(swap(part) for part in parts1)],
        [pltpu.VMEM((512, width), F32)],
    )
    others = [lax.ppermute(piece, "head", [(z, z ^ bit) for z in range(4)]) for bit in (1, 2, 3)]
    (pieces,) = kernel(stack_four, "stack_pieces", [((4, 96, width), BF)], [scal, piece, *others])
    (residual_sum,) = kernel(
        finish_residual, "finish_residual", [(residual_two.shape, F32)], [scal, pieces, swap(pieces)]
    )

    blocks_out = jnp.where(match, keep, rows_received)

    return (
        blocks_out,
        tokens_grad,
        gain_sums[0],
        qkv_one_sum.T,
        pools_one_sum,
        memory_one_sum,
        table_one_sum,
        proj_one_sum,
        gain_sums[1],
        up_one_sum,
        down_one_sum,
        gain_sums[2],
        qkv_two_sum.T,
        residual_sum,
        pools_two_sum,
        memory_two_sum,
        table_two_sum,
        proj_two_sum,
        gain_four_sum,
        up_two_sum,
        down_two_sum,
    )


def solution(mesh):
    planes = mesh.shape["dp"] // 2
    fine = Mesh(mesh.devices.reshape(planes, 2, mesh.shape["head"]), ("plane", "core", "head"))
    dp = ("plane", "core")
    rows = P(("plane", "core", "head"), None)
    columns, lines, free = P(None, "head"), P("head", None), P()
    in_specs = (
        rows, rows, free, P(dp, None),
        free, columns, free, free, lines, lines, free, columns, lines,
        free, columns, free, free, free, lines, lines, free, columns, lines,
    )
    out_specs = (
        rows, rows,
        free, columns, free, free, lines, lines, free, columns, lines,
        free, columns, free, free, free, lines, lines, free, columns, lines,
    )
    return jax.shard_map(
        functools.partial(local, planes), mesh=fine, in_specs=in_specs, out_specs=out_specs, check_vma=False
    )
```

```python
import functools

import jax
import jax.numpy as jnp
import numpy as np
from jax import lax
from jax.experimental import pallas as pl
from jax.experimental.pallas import tpu as pltpu
from jax.sharding import Mesh, PartitionSpec as P

HD = 96
FR = 4
SIDE = 10
LANES = 128
GRID = SIDE + 2
SLAB = GRID * 2 * FR
PADDED = GRID * SLAB
EPSILON = 1e-06
NEGATIVE = -1e30
SCALE = HD**-0.5
GELU_A = float(np.sqrt(2.0 / np.pi))
GELU_B = 0.044715

BF = jnp.bfloat16
F32 = jnp.float32


def nn(a, b):
    return lax.dot_general(a, b, (((1,), (0,)), ((), ())), preferred_element_type=F32)


def nt(a, b):
    return lax.dot_general(a, b, (((1,), (1,)), ((), ())), preferred_element_type=F32)


def tn(a, b):
    return lax.dot_general(a, b, (((0,), (0,)), ((), ())), preferred_element_type=F32)


def iota(shape, dim):
    return lax.broadcasted_iota(jnp.int32, shape, dim)


def widen(values):
    fill = jnp.zeros((values.shape[0], LANES - values.shape[1]), values.dtype)
    return jnp.concatenate([values, fill], axis=1)


def split(values):
    high = values.astype(BF)
    return high, (values - high.astype(F32)).astype(BF)


def norm_parts(values):
    centered = values - jnp.mean(values, axis=-1, keepdims=True)
    variance = jnp.mean(centered * centered, axis=-1, keepdims=True)
    scale = lax.rsqrt(variance + EPSILON)
    return centered * scale, scale


def norm_back(grad, values, gain):
    unit, scale = norm_parts(values)
    scaled = grad * gain
    mean_one = jnp.mean(scaled, axis=-1, keepdims=True)
    mean_two = jnp.mean(scaled * unit, axis=-1, keepdims=True)
    gain_grad = jnp.sum(grad * unit, axis=0, keepdims=True)
    return scale * (scaled - mean_one - unit * mean_two), gain_grad


def gelu_parts(values):
    square = values * values
    bent = jnp.tanh(GELU_A * values * (1.0 + GELU_B * square))
    half = 0.5 * (1.0 + bent)
    slope = half + 0.5 * values * (1.0 - bent * bent) * GELU_A * (1.0 + 3.0 * GELU_B * square)
    return values * half, slope


def pick(flag, one, two):
    return jnp.where(flag, one, two)


def token_rows(half):
    shape = (FR * SIDE * SIDE, 2 * SIDE * SIDE)
    rows, cols = iota(shape, 0), iota(shape, 1)
    frame, place = (rows & (FR - 1)) - 2 * half, rows >> 2
    match = (cols == SIDE * SIDE * frame + place) & (frame >= 0) & (frame < 2)
    return jnp.where(match, 1.0, 0.0).astype(BF)


def half_rows(half, area):
    shape = (2 * area, FR * area)
    rows, cols = iota(shape, 0), iota(shape, 1)
    upper = jnp.where(rows >= area, 1, 0)
    return jnp.where(cols == FR * (rows - area * upper) + 2 * half + upper, 1.0, 0.0).astype(BF)


def cells():
    small = SIDE // 2
    count = FR * small * small
    rows, cols = iota((count, 1), 0), iota((1, FR * SIDE * SIDE), 1)
    place, spot = rows >> 2, cols >> 2
    row_key = FR * place + (rows & (FR - 1))
    line, column = lax.div(spot, 2 * SIDE), lax.div(lax.rem(spot, SIDE), 2)
    col_key = FR * (small * line + column) + (cols & (FR - 1))
    return jnp.where(row_key == col_key, 1.0, 0.0).astype(BF)


def fill_weights(wide, pools, field, flip):
    for tap in range(27):
        source = 26 - tap if flip else tap
        line = widen(pools[field, source : source + 1, :])
        wide[8 * tap : 8 * tap + 8, :] = jnp.broadcast_to(line, (8, LANES))


def frame_shifts():
    lane = iota((8, LANES), 0)
    early, late = lane >= 2, lane < 6
    return (
        lambda values: jnp.where(early, pltpu.roll(values, 2, 0), 0.0),
        lambda values: jnp.where(late, pltpu.roll(values, 6, 0), 0.0),
    )


def load_row(ref, index):
    return ref[pl.ds(pl.multiple_of(SLAB * index, SLAB), SLAB), :].reshape(GRID, 8, LANES)


def tap_of(wide, a, b, e):
    spot = 8 * (9 * a + 3 * b + e)
    return wide[spot : spot + 8, :]


def conv_rows(source, wide, result, stride):
    count = SIDE // stride
    before, after = frame_shifts()

    def one_row(i, carry):
        sums = [[None] * count for _ in range(3)]
        for b in range(3):
            line = load_row(source, stride * i + b)
            for a in range(3):
                for e in range(3):
                    weight = tap_of(wide, a, b, e)
                    for j in range(count):
                        term = weight * line[stride * j + e]
                        sums[a][j] = term if sums[a][j] is None else sums[a][j] + term
        for j in range(count):
            total = sums[1][j] + before(sums[0][j]) + after(sums[2][j])
            result[pl.ds(pl.multiple_of(8 * count * i + 8 * j, 8), 8), :] = total
        return carry

    lax.fori_loop(0, count, one_row, 0)


def conv_back_two(source, wide, result):
    count = SIDE // 2
    before, after = frame_shifts()

    def one_row(m, carry):
        now, later = load_row(source, m + 1), load_row(source, m + 2)
        totals = [None] * (2 * SIDE)
        for a, shift in ((1, None), (0, after), (2, before)):
            sums = [None] * (2 * SIDE)
            for start, b, line in ((0, 1, now), (SIDE, 0, later), (SIDE, 2, now)):
                taps = [tap_of(wide, a, b, e) for e in range(3)]
                for n in range(count):
                    even = taps[1] * line[n + 1]
                    odd = taps[0] * line[n + 2] + taps[2] * line[n + 1]
                    for spot, term in ((start + 2 * n, even), (start + 2 * n + 1, odd)):
                        sums[spot] = term if sums[spot] is None else sums[spot] + term
            for spot in range(2 * SIDE):
                totals[spot] = sums[spot] if shift is None else totals[spot] + shift(sums[spot])
        for spot in range(2 * SIDE):
            result[pl.ds(pl.multiple_of(16 * SIDE * m + 8 * spot, 8), 8), :] = totals[spot]
        return carry

    lax.fori_loop(0, count, one_row, 0)


def conv_weight(source, grads, totals, stride):
    count = SIDE // stride
    before, after = frame_shifts()
    totals[...] = jnp.zeros((27 * 8, LANES), F32)

    def one_row(i, carry):
        line = load_row(grads, i + 1)
        own = [line[j + 1] for j in range(count)]
        cotangents = ([after(item) for item in own], own, [before(item) for item in own])
        for b in range(3):
            line = load_row(source, stride * i + b)
            for e in range(3):
                for a in range(3):
                    spot = 8 * (9 * a + 3 * b + e)
                    terms = [line[stride * j + e] * cotangents[a][j] for j in range(count)]
                    terms.append(totals[spot : spot + 8, :])
                    while len(terms) > 1:
                        terms = [
                            terms[k] + terms[k + 1] if k + 1 < len(terms) else terms[k]
                            for k in range(0, len(terms), 2)
                        ]
                    totals[spot : spot + 8, :] = terms[0]
        return carry

    lax.fori_loop(0, count, one_row, 0)


def weights_of_rows(totals):
    return jnp.sum(totals[...].reshape(27, 8, LANES), axis=1)


def put_rows(target, values, head, count):
    for i in range(count):
        start = ((i + 1) * GRID + 1) * 8 + head
        target[pl.ds(start, FR * count, stride=2), :] = values[FR * count * i : FR * count * (i + 1), :]


def pairs_of(heads):
    return [((0, 0), (1, 0))] if heads == 2 else [((0, 0), (0, 1)), ((1, 0), (1, 1))]


def pack_heads(lines, turn):
    half = len(lines) // 2
    sides = [jnp.concatenate([line[:, :HD] for line in lines[half * i : half * (i + 1)]], axis=1) for i in range(2)]
    flag = turn == 1
    return jnp.concatenate([pick(flag, sides[1], sides[0]), pick(flag, sides[0], sides[1])], axis=1)


def unpack_heads(values, turn):
    heads = values.shape[1] // HD
    lines = [values[:, HD * head : HD * (head + 1)] for head in range(heads)]
    flag, half = turn == 1, heads // 2
    return [widen(pick(flag, lines[(head + half) % heads], lines[head])) for head in range(heads)]


def front_body(heads, turn, strides, normed, weights, pools, memory, fields, pooled, passed, work):
    wide, result, held, sent = work
    copies = []
    lines = [nt(normed, weights[s][: 3 * HD * heads // 2, :]) for s in range(2)]
    for field in range(3):
        fill_weights(wide, pools, field, False)
        stride = strides[field]
        count = SIDE // stride
        for number, pair in enumerate(pairs_of(heads)):
            spot = field * (heads // 2) + number
            group = held.at[spot]
            group[...] = jnp.zeros((PADDED, LANES), F32)
            for head, (slot, place) in enumerate(pair):
                start = HD * (3 * place + field)
                put_rows(group, widen(lines[slot][:, start : start + HD]), head, SIDE)
            copies.append(pltpu.make_async_copy(group, fields.at[spot], sent.at[spot]))
            copies[-1].start()
            conv_rows(group, wide, result, stride)
            for head in range(2):
                pooled[field][2 * number + head] = result[pl.ds(head, FR * count * count, stride=2), :]
    area = (SIDE // strides[1]) ** 2
    for which in range(2):
        lines = []
        for head in range(heads):
            total = jnp.zeros((area, LANES), F32)
            for t in range(FR):
                line = widen(memory[which, t : t + 1, :])
                total = total + line * pooled[1 + which][head, pl.ds(t, area, stride=FR), :]
            lines.append(total)
        passed[which] = pack_heads(lines, turn).astype(BF)
    for copy in copies:
        copy.wait()


def front_one(scal, own, first, second, gain, wa, wb, pools, memory, x_out, normed_out, g_out, fields, qp, kp, vp, passed, *work):
    match, turn = scal[0] == 1, scal[1] == 1
    near = pick(match, own[...], first[...])
    far = pick(match, first[...], second[...])
    low, high = pick(turn, far, near), pick(turn, near, far)
    count, area = 2 * SIDE * SIDE, (SIDE // 2) ** 2
    rows = nn(token_rows(0), low[:count]) + nn(token_rows(1), high[:count])
    x_out[...] = rows.astype(BF)
    turns = [half_rows(half, area) for half in range(2)]
    for column in range(2):
        spots = slice(count + 2 * area * column, count + 2 * area * (column + 1))
        g_out[column] = (tn(turns[0], low[spots]) + tn(turns[1], high[spots])).astype(BF)
    normed = (norm_parts(rows)[0] * gain[...]).astype(BF)
    normed_out[...] = normed
    front_body(2, scal[1], (1, 2, 2), normed, (wa, wb), pools, memory, fields, (qp, kp, vp), passed, work)


def front_two(scal, middle, part, other, gain, wa, wb, pools, memory, x_out, normed_out, fields, qp, kp, vp, passed, *work):
    rows = middle[...] + (part[...].astype(F32) + other[...].astype(F32))
    x_out[...] = rows
    normed = (norm_parts(rows)[0] * gain[...]).astype(BF)
    normed_out[...] = normed
    front_body(4, scal[1], (2, 1, 1), normed, (wa, wb), pools, memory, fields, (qp, kp, vp), passed, work)


def skip_two(normed, residual, skip):
    high, low = split(nn(cells(), normed[...]))
    skip[...] = 0.25 * (nn(high, residual[...]) + nn(low, residual[...]))


def table_of(shards, block, slot, place):
    line = shards[slot][4 * HD : 4 * HD + 16, :].astype(F32)
    row = 3 * (place if block == 0 else 1 + place)
    return line[row : row + 1, :] + line[row + 1 : row + 2, :] + line[row + 2 : row + 3, :]


def own_bias(bins, table):
    values = jnp.zeros(bins.shape, F32)
    for number in range(2 * FR - 1):
        values = jnp.where(bins == number, table[:, number : number + 1], values)
    return values


def far_bias(table, offset):
    lanes = iota(table.shape, 1)
    return jnp.sum(jnp.where(lanes == offset + 2 * FR - 1, table, 0.0), axis=1, keepdims=True)


def probs_of(scal, bins, table, query, keys):
    tile = own_bias(bins, table)
    rows = query.shape[0]
    bias = jnp.concatenate([tile] * ((rows + 7) // 8), axis=0)[:rows]
    parts = [nt(query, keys[0]) * SCALE + bias]
    for j in range(2):
        raw = nt(query, keys[1 + j]) * SCALE + far_bias(table, scal[4 + j])
        parts.append(jnp.where(scal[2 + j] == 1, raw, NEGATIVE))
    top = functools.reduce(jnp.maximum, [jnp.max(part, axis=1, keepdims=True) for part in parts])
    parts = [jnp.exp(part - top) for part in parts]
    total = sum(jnp.sum(part, axis=1, keepdims=True) for part in parts)
    return [part / total for part in parts]


def heads_of(heads, block):
    return [(slot, place) for slot in range(2) for place in range(heads // 2)]


def attend(block, scal, ta, tb, qp, kp, vp, near, far, wa, wb, rows_out, part_out):
    heads = qp.shape[0]
    shards, weights = (ta, tb), (wa, wb)
    base = 0 if block else 3 * HD
    shape = (8, kp.shape[1])
    bins = (iota(shape, 0) & (FR - 1)) - (iota(shape, 1) & (FR - 1)) + FR - 1
    total = jnp.zeros(part_out.shape, F32)
    nears, fars = ([unpack_heads(item[which], scal[1]) for which in range(2)] for item in (near, far))
    for head, (slot, place) in enumerate(heads_of(heads, block)):
        table = table_of(shards, block, slot, place)
        pool = qp[head]
        keys = (kp[head].astype(BF), nears[0][head], fars[0][head])
        values = (vp[head].astype(BF), nears[1][head], fars[1][head])
        probs = probs_of(scal, bins, table, pool.astype(BF), keys)
        mixture = sum(nn(p.astype(BF), v) for p, v in zip(probs, values))
        line = (mixture + pool).astype(BF)
        rows_out[head] = line
        total = total + nn(line[:, :HD], weights[slot][base + HD * place : base + HD * place + HD, :])
    part_out[...] = total.astype(BF)


def attend_back(block, scal, ta, tb, qp, kp, vp, near, far, wa, wb, rows, middle_grad, dq, dk, dv, d_near, d_far, proj_grad, table_grad):
    heads = qp.shape[0]
    shards, weights = (ta, tb), (wa, wb)
    base = 0 if block else 3 * HD
    shape = (8, kp.shape[1])
    bins = (iota(shape, 0) & (FR - 1)) - (iota(shape, 1) & (FR - 1)) + FR - 1
    branch = middle_grad.astype(BF)
    lanes = iota((1, LANES), 1)
    table_lines = []
    nears, fars = ([unpack_heads(item[which], scal[1]) for which in range(2)] for item in (near, far))
    near_lines, far_lines = ([], []), ([], [])
    for head, (slot, place) in enumerate(heads_of(heads, block)):
        table = table_of(shards, block, slot, place)
        weight = weights[slot][base + HD * place : base + HD * place + HD, :]
        if proj_grad is not None:
            proj_grad[slot, HD * place : HD * place + HD, :] = tn(rows[head][:, :HD], branch).astype(BF)
        grad = widen(nt(branch, weight).astype(BF))
        query = qp[head].astype(BF)
        keys = (kp[head].astype(BF), nears[0][head], fars[0][head])
        values = (vp[head].astype(BF), nears[1][head], fars[1][head])
        probs = probs_of(scal, bins, table, query, keys)
        grad_probs = [nt(grad, v) for v in values]
        inner = sum(jnp.sum(p * d, axis=1, keepdims=True) for p, d in zip(probs, grad_probs))
        low = [(p * (d - inner)).astype(BF) for p, d in zip(probs, grad_probs)]
        dq[head] = sum(nn(s, k) for s, k in zip(low, keys)) * SCALE + grad.astype(F32)
        key_grads = [tn(s, query) * SCALE for s in low]
        value_grads = [tn(p.astype(BF), grad) for p in probs]
        dk[head], dv[head] = key_grads[0], value_grads[0]
        for which, grads in enumerate((key_grads, value_grads)):
            near_lines[which].append(grads[1])
            far_lines[which].append(grads[2])
        score = low[0].astype(F32)
        count = score.shape[0]
        if count % 8:
            score = jnp.concatenate([score, jnp.zeros((8 - count % 8, score.shape[1]), F32)], axis=0)
        score = jnp.sum(score.reshape(-1, 8, score.shape[1]), axis=0)
        line = jnp.zeros((1, LANES), F32)
        for number in range(2 * FR - 1):
            column = jnp.sum(jnp.where(bins == number, score, 0.0), axis=0, keepdims=True)
            line = line + jnp.where(lanes == number, jnp.sum(column, axis=1, keepdims=True), 0.0)
        for j in range(2):
            column = jnp.sum(low[1 + j].astype(F32), axis=0, keepdims=True)
            value = jnp.sum(column, axis=1, keepdims=True)
            line = line + jnp.where(lanes == scal[4 + j] + 2 * FR - 1, value, 0.0)
        table_lines.append(line)
    for which in range(2):
        d_near[which] = pack_heads(near_lines[which], scal[1]).astype(BF)
        d_far[which] = pack_heads(far_lines[which], scal[1]).astype(BF)
    for head, line in enumerate(table_lines):
        table_grad[head : head + 1, :] = line


def field_back(heads, turn, strides, fields, pooled, grads, near, far, pools, memory, pools_grad, memory_grad, work):
    wide, result, grid, totals, rows, held, arrived = work
    half = heads // 2
    copies = [pltpu.make_async_copy(fields.at[i], held.at[i], arrived.at[i]) for i in range(3 * half)]
    for copy in copies:
        copy.start()
    back = {}
    area = (SIDE // strides[1]) ** 2
    for field in range(3):
        stride = strides[field]
        count = SIDE // stride
        fill_weights(wide, pools, field, stride == 1)
        weight_sum = jnp.zeros((27, LANES), F32)
        memory_lines = [jnp.zeros((1, LANES), F32) for _ in range(FR)]
        if field:
            passed = unpack_heads(near[field - 1].astype(F32) + far[field - 1].astype(F32), turn)
        for number, pair in enumerate(pairs_of(heads)):
            grid[...] = jnp.zeros((PADDED, LANES), F32)
            for place in range(2):
                head = 2 * number + place
                if field == 0:
                    put_rows(grid, grads[0][head], place, count)
                else:
                    cotangent = passed[head]
                    for t in range(FR):
                        spot = pl.ds(t, area, stride=FR)
                        line = widen(memory[field - 1, t : t + 1, :])
                        rows[spot, :] = grads[field][head, spot, :] + line * cotangent
                        product = pooled[field - 1][head, spot, :] * cotangent
                        memory_lines[t] = memory_lines[t] + jnp.sum(product, axis=0, keepdims=True)
                    put_rows(grid, rows[0 : FR * area, :], place, count)
            group = held.at[field * half + number]
            copies[field * half + number].wait()
            conv_weight(group, grid, totals, stride)
            weight_sum = weight_sum + weights_of_rows(totals)
            if stride == 1:
                conv_rows(grid, wide, result, 1)
            else:
                conv_back_two(grid, wide, result)
            for place, key in enumerate(pair):
                back[key + (field,)] = result[pl.ds(place, FR * SIDE * SIDE, stride=2), :][:, :HD]
        pools_grad[field, 0:27, :] = weight_sum
        if field:
            for t in range(FR):
                memory_grad[field - 1, t : t + 1, :] = memory_lines[t]
    outs = []
    for slot in range(2):
        columns = [back[(slot, place, field)] for place in range(half) for field in range(3)]
        outs.append(jnp.concatenate(columns, axis=1).astype(BF))
    return outs


def mlp_one(scal, x, part, other, gain, wa, wb, middle_out, normed_out, part_out):
    weights = (wa, wb)
    middle = x[...].astype(F32) + (part[...].astype(F32) + other[...].astype(F32))
    middle_out[...] = middle
    normed = (norm_parts(middle)[0] * gain[...]).astype(BF)
    normed_out[...] = normed
    size = normed.shape[1]
    total = jnp.zeros(part_out.shape, F32)
    for slot in range(2):
        hidden = gelu_parts(nn(normed, weights[slot][:size, :]))[0].astype(BF)
        total = total + nn(hidden, weights[slot][size:, :])
    part_out[...] = total.astype(BF)


def middle_two(scal, skip, part, other, gain, g, middle_out, normed_out, half_out):
    middle = skip[...] + (part[...].astype(F32) + other[...].astype(F32))
    middle_out[...] = middle
    normed_out[...] = (norm_parts(middle)[0] * gain[...]).astype(BF)
    width = half_out.shape[2]
    half_out[0] = normed_out[:, pl.ds(pl.multiple_of(scal[7] * width, LANES), width)]
    half_out[1] = g[scal[7]]


def mlp_rows(scal, own, own_grad, *refs):
    halves, others = refs[0:3], refs[3:6]
    up_ref, down_ref = refs[6:8]
    keep, give, hidden_out, low_out, board, lines = refs[8:14]
    width = up_ref.shape[1] // 2
    core = scal[7]
    start = pl.multiple_of(core * width, LANES)
    rest = pl.multiple_of((1 - core) * width, LANES)
    up, down = up_ref[:, pl.ds(start, width)], down_ref[pl.ds(start, width), :]
    board[0, 0] = own[...]
    for column in range(2):
        board[0, 1, :, width * column : width * (column + 1)] = own_grad[column]
    for d in range(3):
        for which in range(2):
            board[d + 1, which, :, pl.ds(start, width)] = halves[d][which]
            board[d + 1, which, :, pl.ds(rest, width)] = others[d][which]
    for d in range(4):
        rows, grad = board[d, 0], board[d, 1]
        value, slope = gelu_parts(nn(rows, up))
        hidden = value.astype(BF)
        up_low = (nt(grad, down) * slope).astype(BF)
        hidden_out[d], low_out[d] = hidden, up_low
        lines[0] = nn(hidden, down)
        lines[1] = nt(up_low, up)
        for which in range(2):
            spots = slice(104 * (2 * d + which), 104 * (2 * d + which) + rows.shape[0])
            keep[spots, :] = lines[which, :, pl.ds(start, width)].astype(BF)
            give[spots, :] = lines[which, :, pl.ds(rest, width)].astype(BF)


def mlp_sums(hidden, low, board, packed, packed_down):
    up_total = sum(tn(board[d, 0], low[d]) for d in range(4))
    down_total = sum(tn(hidden[d], board[d, 1]) for d in range(4))
    width = packed.shape[1]
    packed[...] = up_total.astype(BF)
    packed_down[0:width, :] = down_total[:, :width].astype(BF)
    packed_down[width:, :] = down_total[:, width:].astype(BF)


def quarter_of(scal, peer):
    one = 1 - scal[8] if peer % 2 else scal[8]
    two = 1 - scal[9] if peer // 2 else scal[9]
    return one + 2 * two


def cut(scal, full, parts):
    rows = parts[0].shape[1]
    for peer in range(4):
        spots = pl.ds(pl.multiple_of(quarter_of(scal, peer) * rows, 16), rows)
        for slot in range(2):
            parts[peer][slot] = full[slot, spots, :]


def sum_planes(*refs):
    one, two = refs[-2:]
    start = 0
    for number in range(len(refs) // 4):
        parts = refs[4 * number : 4 * number + 4]
        rows = parts[0].shape[1]
        for slot, out in ((0, one), (1, two)):
            total = (parts[0][slot].astype(F32) + parts[1][slot].astype(F32)) + (
                parts[2][slot].astype(F32) + parts[3][slot].astype(F32)
            )
            out[start : start + rows, :] = total.astype(BF)
        start += rows


def gather_parts(scal, parts, start, full):
    rows = full.shape[0] // 8
    for number, part in enumerate(parts):
        core = scal[7] if number < 4 else 1 - scal[7]
        spots = pl.ds(pl.multiple_of((2 * quarter_of(scal, number % 4) + core) * rows, 16), rows)
        full[spots, :] = part[start : start + rows, :].astype(F32)


def put_totals(full, start, pools, memory):
    for field in range(3):
        pools[field] = full[start : start + 27, LANES * field : LANES * field + HD]
    for which in range(2):
        memory[which] = full[start + 32 : start + 32 + FR, LANES * which : LANES * which + HD]


def stack_four(scal, own, beside, far, last, out):
    z = scal[10]
    turn, upper = lax.rem(z, 2), lax.div(z, 2)
    for piece, parity, pair in (
        (own, turn, upper),
        (beside, 1 - turn, upper),
        (far, turn, 1 - upper),
        (last, 1 - turn, 1 - upper),
    ):
        out[2 * pair + parity] = piece[...]


def finish_residual(scal, own, other, out):
    size, width = own.shape[1:]
    for core, source in ((scal[7], own), (1 - scal[7], other)):
        for shard in range(4):
            rows = pl.ds(pl.multiple_of(2 * size * (shard % 2) + size * core, 16), size)
            columns = slice(width * (shard // 2), width * (shard // 2 + 1))
            out[rows, columns] = source[shard].astype(F32)


def take_piece(scal, a, b, c, d, piece):
    half = piece.shape[0]
    start = pl.multiple_of(48 * scal[7], 16)
    for peer, part in enumerate((a, b, c, d)):

        @pl.when(quarter_of(scal, peer) == 3)
        def _():
            piece[...] = part[pl.ds(start, half), :]


def finish_two(scal, *refs):
    parts = refs[0:8]
    qkv, proj, up, down, pools, memory, gain, full, full_mlp = refs[8:]
    gather_parts(scal, parts, 0, full)
    gather_parts(scal, parts, full.shape[0] // 8, full_mlp)
    width = full.shape[1]
    qkv[...] = full[0:576, :]
    proj[:, :width] = full[576:768, :]
    proj[0:96, width:] = full[768:864, :]
    proj[96:192, width:] = full[960:1056, :]
    up[...] = full_mlp[0:384, :]
    down[...] = full_mlp[384:768, :]
    put_totals(full_mlp, 768, pools, memory)
    gain[0:width], gain[width:] = full_mlp[808, :], full_mlp[809, :]


def finish_one(scal, *refs):
    qkv, proj, table, second_table, pools, memory, gain, second_gain, third_gain, full = refs[8:]
    gather_parts(scal, refs[0:8], 0, full)
    qkv[...] = full[0:288, :]
    proj[...] = full[288:384, :]
    bins = table.shape[1]
    table[...] = full[384:385, :bins]
    second_table[...] = full[385:387, :bins]
    put_totals(full, 400, pools, memory)
    second_gain[...] = full[440, :]
    third_gain[...] = full[441, :]
    gain[...] = full[442, :]


def finish_wide(scal, own_up, other_up, own_down, other_down, up, down):
    first = scal[7] == 0
    size = up.shape[0]
    width = size // 2
    up[:, :width] = pick(first, own_up[...], other_up[...]).astype(F32)
    up[:, width:] = pick(first, other_up[...], own_up[...]).astype(F32)
    one = pick(first, own_down[...], other_down[...]).astype(F32)
    two = pick(first, other_down[...], own_down[...]).astype(F32)
    down[:width, :width], down[:width, width:] = one[:width, :], one[width:, :]
    down[width:, :width], down[width:, width:] = two[:width, :], two[width:, :]


def add_cores(keep, other, *outs):
    for d in range(4):
        for which in range(2):
            spots = slice(104 * (2 * d + which), 104 * (2 * d + which) + outs[d].shape[1])
            outs[d][which] = (keep[spots, :].astype(F32) + other[spots, :].astype(F32)).astype(BF)


def whole_columns(scal, own, other):
    first = scal[7] == 0
    return jnp.concatenate([pick(first, own, other), pick(first, other, own)], axis=1)


def add_both(one, one_other, two, two_other, one_out, two_out):
    one_out[...] = (one[...].astype(F32) + one_other[...].astype(F32)).astype(BF)
    two_out[...] = (two[...].astype(F32) + two_other[...].astype(F32)).astype(BF)


def add_two(one, two, out):
    out[...] = (one[...].astype(F32) + two[...].astype(F32)).astype(BF)


def sum_four(a, b, c, d, out):
    total = (a[...].astype(F32) + b[...].astype(F32)) + (c[...].astype(F32) + d[...].astype(F32))
    out[...] = total.astype(BF)


def back_attend_two(scal, part, other, g, middle, gain, *refs):
    ins, outs = refs[0:10], refs[10:]
    grad, gain_grad = norm_back(whole_columns(scal, part[1], other[1]).astype(F32), middle[...], gain[...])
    middle_grad = jnp.concatenate([g[0], g[1]], axis=1).astype(F32) + grad
    outs[0][...] = middle_grad
    outs[1][...] = gain_grad
    attend_back(1, scal, *ins, middle_grad, *outs[2:7], None, outs[7])


def back_rest_two(scal, part, other, middle, normed, middle_grad, rows, proj_grad, residual_grad, keep, send):
    final = (middle[...] + whole_columns(scal, part[0], other[0]).astype(F32)).astype(BF)
    area = (SIDE // 2) ** 2
    keep[...] = nn(half_rows(scal[1], area), final).astype(BF)
    send[...] = nn(half_rows(1 - scal[1], area), final).astype(BF)
    branch = middle_grad[...].astype(BF)
    width = residual_grad.shape[2]
    for head, (slot, place) in enumerate(heads_of(4, 1)):
        found = tn(rows[head][:, :HD], branch).astype(BF)
        for column in range(2):
            start = 2 * HD * column + HD * place
            proj_grad[slot, start : start + HD, :] = found[:, width * column : width * (column + 1)]
    linear = (0.25 * middle_grad[:, pl.ds(pl.multiple_of(scal[7] * width, LANES), width)]).astype(BF)
    high, low = split(nn(cells(), normed[...]))
    found = (tn(high, linear) + tn(low, linear)).astype(BF)
    size = residual_grad.shape[1]
    turned = scal[1] == 1
    residual_grad[0] = pick(turned, found[size:], found[:size])
    residual_grad[1] = pick(turned, found[:size], found[size:])


def put_small(small, pools_grad, memory_grad):
    small[...] = jnp.zeros(small.shape, F32)
    for field in range(3):
        small[0:27, LANES * field : LANES * (field + 1)] = pools_grad[field, 0:27, :]
    for which in range(2):
        small[32 : 32 + FR, LANES * which : LANES * (which + 1)] = memory_grad[which]


def back_front_two(scal, middle_grad, normed_ref, fields, kp, vp, dq, dk, dv, near, far, wa, wb, residual, pools, memory, proj_grad, residual_grad, gain_grad, part_out, keep, one, two, three, small, pools_grad, memory_grad, full, *work):
    weights = (wa, wb)
    normed = normed_ref[...]
    backs = field_back(4, scal[1], (2, 1, 1), fields, (kp, vp), (dq, dk, dv), near, far, pools, memory, pools_grad, memory_grad, work)
    total = jnp.zeros(part_out.shape, F32)
    width = full.shape[2]
    columns = pl.ds(pl.multiple_of(scal[7] * width, LANES), width)
    linear = (0.25 * middle_grad[:, columns]).astype(BF)
    cell = cells()
    for slot in range(2):
        full[slot, 0:576, :] = tn(backs[slot], normed).astype(BF)
        full[slot, 576:864, :] = proj_grad[slot, 0:288, :]
        full[slot, 864:960, :] = residual_grad[slot, 0:96, :]
        full[slot, 960:1056, :] = proj_grad[slot, 288:384, :]
        full[slot, 1056:1152, :] = residual_grad[slot, 96:192, :]
        total = total + nn(backs[slot], weights[slot][...])
    cut(scal, full, (keep, one, two, three))
    high, low = split(nt(linear, residual[:, columns]))
    part_out[...] = (total + tn(cell, high) + tn(cell, low)).astype(BF)
    put_small(small, pools_grad, memory_grad)
    small[40:41, :] = 0.5 * gain_grad[:, :width]
    small[41:42, :] = 0.5 * gain_grad[:, width:]


def back_mlp_one(scal, part, other, x, gain, normed_ref, wa, wb, small, small_other, grad_out, part_out, gain_grad_ref, keep, one, two, three, full):
    weights = (wa, wb)
    grad, gain_grad = norm_back(part[...].astype(F32) + other[...].astype(F32), x[...], gain[...])
    grad_out[...] = grad
    gain_grad_ref[...] = gain_grad
    branch = grad.astype(BF)
    normed = normed_ref[...]
    total = jnp.zeros(part_out.shape, F32)
    whole = (small[...] + small_other[...]).astype(BF)
    size = normed.shape[1]
    for slot in range(2):
        up, down = weights[slot][:size, :], weights[slot][size:, :]
        value, slope = gelu_parts(nn(normed, up))
        up_low = (nt(branch, down) * slope).astype(BF)
        full[slot, 0:size, :] = tn(normed, up_low).astype(BF)
        full[slot, size : 2 * size, :] = tn(value.astype(BF), branch).astype(BF)
        full[slot, 2 * size : 2 * size + 64, :] = whole
        full[slot, 2 * size + 64 :, :] = jnp.zeros((64, size), BF)
        total = total + nt(up_low, up)
    part_out[...] = total.astype(BF)
    cut(scal, full, (keep, one, two, three))


def back_attend_one(scal, part, other, g, middle, gain, *refs):
    ins, outs = refs[0:10], refs[10:]
    grad, gain_grad = norm_back(part[...].astype(F32) + other[...].astype(F32), middle[...], gain[...])
    middle_grad = g[...] + grad
    outs[0][...] = middle_grad
    outs[1][...] = gain_grad
    attend_back(0, scal, *ins, middle_grad, *outs[2:9])


def back_front_one(scal, normed_ref, fields, kp, vp, dq, dk, dv, near, far, wa, wb, pools, memory, gain_two_grad, gain_three_grad, qkv_grad, part_out, small, pools_grad, memory_grad, *work):
    weights = (wa, wb)
    normed = normed_ref[...]
    backs = field_back(2, scal[1], (1, 2, 2), fields, (kp, vp), (dq, dk, dv), near, far, pools, memory, pools_grad, memory_grad, work)
    total = jnp.zeros(part_out.shape, F32)
    for slot in range(2):
        qkv_grad[slot] = tn(backs[slot], normed).astype(BF)
        total = total + nn(backs[slot], weights[slot][: 3 * HD, :])
    part_out[...] = total.astype(BF)
    put_small(small, pools_grad, memory_grad)
    small[40:41, :] = 0.5 * gain_two_grad[...]
    small[41:42, :] = 0.5 * gain_three_grad[...]


def back_tokens(scal, part, other, x, gain, middle_grad, qkv_grad, proj_grad, table_one, table_two, small, small_other, keep_rows, send_rows, keep, one, two, three, full):
    grad, gain_grad = norm_back(part[...].astype(F32) + other[...].astype(F32), x[...].astype(F32), gain[...])
    rows = (middle_grad[...] + grad).astype(BF)
    turn = scal[1]
    keep_rows[...] = nn(half_rows(turn, SIDE * SIDE), rows).astype(BF)
    send_rows[...] = nn(half_rows(1 - turn, SIDE * SIDE), rows).astype(BF)
    line = iota((64, 1), 0)
    whole = jnp.where(line == 42, gain_grad, small[...] + small_other[...]).astype(BF)
    for slot in range(2):
        full[slot, 0:288, :] = qkv_grad[slot]
        full[slot, 288:384, :] = proj_grad[slot]
        lines = jnp.concatenate([table_one[slot : slot + 1, :], table_two[2 * slot : 2 * slot + 2, :], jnp.zeros((13, LANES), F32)], axis=0)
        full[slot, 384:400, :] = jnp.concatenate([lines, jnp.zeros((16, 2 * LANES), F32)], axis=1).astype(BF)
        full[slot, 400:464, :] = whole
        full[slot, 464:512, :] = jnp.zeros((48, full.shape[2]), BF)
    cut(scal, full, (keep, one, two, three))


def scalars(pairs, other_pairs, videos, out):
    plane, core, head = lax.axis_index("plane"), lax.axis_index("core"), lax.axis_index("head")
    upper, turn = lax.div(head, 2), lax.rem(head, 2)
    clip = 4 * plane + 2 * turn + upper
    match = core == turn
    own = videos[clip]
    out[0] = jnp.where(match, 1, 0)
    out[1] = turn
    for j in range(2):
        before = clip - 1 - j
        there = (before >= 0) & (videos[jnp.maximum(before, 0)] == own)
        out[2 + j] = jnp.where(there, 1, 0)
        out[4 + j] = jnp.where(match, pairs[upper, j], other_pairs[upper, j])
    out[6] = jnp.where(upper == core, 1, 0)
    out[7] = core
    out[8] = lax.rem(plane, 2)
    out[9] = lax.rem(lax.div(plane, 2), 2)
    out[10] = head


def pack(tokens, grad_out, table_one, table_two, qkv_one, proj_one, rows, first):
    count, width = tokens.shape
    area = grad_out.shape[0]
    rows[0:count, :] = tokens[...]
    rows[count : count + area, :] = grad_out[:, :width]
    rows[count + area :, :] = grad_out[:, width:]
    lines = []
    for table in (table_one[0:1, :], table_two[0:1, :], table_two[1:2, :]):
        high = table.astype(BF).astype(F32)
        middle = (table - high).astype(BF).astype(F32)
        lines += [high, middle, table - high - middle]
    first[0 : 3 * HD, :] = qkv_one[...]
    first[3 * HD : 4 * HD, :] = proj_one[...]
    stacked = jnp.concatenate(lines + [jnp.zeros((7, lines[0].shape[1]), F32)], axis=0)
    first[4 * HD :, :] = jnp.concatenate([stacked, jnp.zeros((16, width - stacked.shape[1]), F32)], axis=1).astype(BF)


def join(one, two, first, second, third, out):
    out[0 : one.shape[0], :] = one[...]
    out[one.shape[0] :, :] = two[...]


SMEM = pl.BlockSpec(memory_space=pltpu.SMEM)


FAR = pl.BlockSpec(memory_space=pltpu.HBM)
NEAR = pl.BlockSpec(memory_space=pltpu.VMEM)


def moved(body, counts, left, early, late, *refs):
    ins_count, outs_count, work_count = counts
    ins, outs = list(refs[:ins_count]), refs[ins_count : ins_count + outs_count]
    spot = ins_count + outs_count
    saved = refs[spot : spot + len(early) + len(late)]
    spot += len(early) + len(late)
    work = refs[spot : spot + work_count]
    buffers, arrived = refs[spot + work_count : -1], refs[-1]
    brought = [pltpu.make_async_copy(ins[item], buffers[i], arrived.at[i]) for i, item in enumerate(left)]
    first = len(left)
    sent = [pltpu.make_async_copy(ins[item], saved[i], arrived.at[first + i]) for i, item in enumerate(early)]
    for copy in brought + sent:
        copy.start()
    for i, item in enumerate(left):
        brought[i].wait()
        ins[item] = buffers[i]
    body(*ins, *outs, *work)
    first += len(early)
    last = [
        pltpu.make_async_copy(outs[item], saved[len(early) + i], arrived.at[first + i]) for i, item in enumerate(late)
    ]
    for copy in last:
        copy.start()
    for copy in sent + last:
        copy.wait()


def kernel(body, name, outs, ins, work=(), left=(), early=(), late=(), raw=(), far_outs=(), limit=16, flops=2 * 10**8):
    if limit == 16 and (left or early or late):
        found = kernel(body, name, outs, ins, work, (), (), (), raw, far_outs)
        return (*found, *[list(ins)[item] for item in early], *[found[item] for item in late])
    ins = list(ins)
    in_specs = []
    for number, item in enumerate(ins):
        if number == 0 and item.dtype == jnp.int32:
            in_specs.append(SMEM)
        else:
            in_specs.append(FAR if number in left or number in raw else NEAR)
    results = [jax.ShapeDtypeStruct(shape, kind) for shape, kind in outs]
    extra = [jax.ShapeDtypeStruct(ins[item].shape, ins[item].dtype) for item in early] + [results[item] for item in late]
    size = sum(int(np.prod(item.shape)) * item.dtype.itemsize for item in [*ins, *results, *extra])
    work = list(work)
    count = len(work)
    if left or early or late:
        body = functools.partial(moved, body, (len(ins), len(results), count), tuple(left), tuple(early), tuple(late))
        work += [pltpu.VMEM(ins[number].shape, ins[number].dtype) for number in left]
        work.append(pltpu.SemaphoreType.DMA((len(left) + len(early) + len(late),)))
    return pl.pallas_call(
        body,
        out_shape=tuple(results + extra),
        in_specs=in_specs,
        out_specs=tuple([FAR if number in far_outs else NEAR for number in range(len(results))] + [FAR] * len(extra)),
        scratch_shapes=work,
        name=name,
        cost_estimate=pl.CostEstimate(flops=flops, bytes_accessed=size, transcendentals=0),
        compiler_params=pltpu.CompilerParams(vmem_limit_bytes=limit << 20),
    )(*ins)


def scratch(*rows):
    return [pltpu.VMEM((count, LANES), F32) for count in rows]


def field_work(heads):
    groups = 3 * heads // 2
    return [pltpu.VMEM((groups, PADDED, LANES), F32), pltpu.SemaphoreType.DMA((groups,))]


FRONT_WORK = (216, 800)
BACK_WORK = (216, 800, PADDED, 216, 400)


def after(values, events):
    return lax.optimization_barrier((values, events))


def swap(values):
    return lax.ppermute(values, "core", [(0, 1), (1, 0)])


def cross_route():
    route = []
    for core in range(2):
        low, other = 2 * core, 2 - 2 * core
        route += [(core * 4 + low + i, core * 4 + other + i) for i in range(2)]
    return route


def beside(values):
    return lax.ppermute(values, "head", [(z, z ^ 1) for z in range(4)])


def choose(scal, own, other, out):
    out[...] = pick(scal[6] == 1, own[...], other[...])


def choose_half(sizes, scal, own, other, out):
    start, put = 0, 0
    for size in sizes:
        half = size // 2
        spots = pl.ds(pl.multiple_of(start + half * scal[7], 16), half)
        out[put : put + half, :] = pick(scal[6] == 1, own[spots, :], other[spots, :])
        start, put = start + size, put + half


def chosen(scal, own, other):
    return kernel(choose, "choose_shard", [(own.shape, own.dtype)], [scal, own, other])[0]


def over(values, scal):
    return chosen(scal, values, lax.ppermute(values, ("core", "head"), cross_route()))


def spread(values, scal):
    one = over(values, scal)
    return one, beside(one)


def reverse(route):
    return [(end, start) for start, end in route]


def clip_routes(planes, distance):
    def place(clip):
        slot = clip % 4
        return (clip // 4) * 4 + 2 * (slot % 2) + slot // 2

    total = 4 * planes
    return [(place(clip), place(clip + distance)) for clip in range(total) if 0 <= clip + distance < total]


def half_routes():
    def place(core, a, b):
        return core * 4 + 2 * a + b

    one, two, three = [], [], []
    for a in range(2):
        for b in range(2):
            one += [(place(b, a, b), place(1 - b, a, b)), (place(1 - b, a, b), place(1 - b, a, 1 - b))]
            two += [(place(1 - b, a, b), place(b, a, 1 - b))]
            three += [(place(1 - b, a, b), place(b, a, 1 - b))]
    return one, two, three


def turn_by(values, distance):
    return lax.ppermute(values, "head", [(z, (z + distance) % 4) for z in range(4)])


def local(
    planes,
    tokens,
    grad_out,
    video_ids,
    offsets,
    gain_one,
    qkv_one,
    pools_one,
    memory_one,
    table_one,
    proj_one,
    gain_two,
    up_one,
    down_one,
    gain_three,
    qkv_two,
    residual_two,
    pools_two,
    memory_two,
    table_two,
    proj_two,
    gain_four,
    up_two,
    down_two,
):
    match = lax.axis_index("core") == lax.axis_index("head") % 2
    (scal,) = pl.pallas_call(
        scalars,
        out_shape=(jax.ShapeDtypeStruct((16,), jnp.int32),),
        in_specs=[SMEM] * 3,
        out_specs=(SMEM,),
        name="scalars",
    )(offsets, swap(offsets), video_ids)
    gains = [item.reshape(1, -1) for item in (gain_one, gain_two, gain_three, gain_four)]

    half = residual_two.shape[1] // 2
    qkv_one_t, qkv_two_t = qkv_one.T, qkv_two.T
    rows_in, first_bundle = kernel(
        pack,
        "pack",
        [((300, half), BF), ((400, half), BF)],
        [tokens, grad_out, table_one, table_two, qkv_one_t, proj_one],
        left=range(6),
        limit=56,
    )
    route_one, route_two, route_three = half_routes()
    axes = ("core", "head")
    first_over = over(first_bundle, scal)
    first_all = (first_over, beside(first_over))
    tok_one, tok_two = lax.ppermute(rows_in, axes, route_one), lax.ppermute(rows_in, axes, route_two)
    (mlp_bundle,) = kernel(
        join, "join", [((768, half), BF)], [up_one, down_one, first_over, tok_one, tok_two], left=(0, 1), limit=48
    )
    mlp_over = over(mlp_bundle, scal)

    width = qkv_one.shape[0]
    wide = residual_two.shape[1]
    n1, n2 = FR * SIDE * SIDE, FR * SIDE * SIDE // 4
    a1, a2 = n2 // FR, n1 // FR

    x1, _, g, fields1, qp1, kp1, vp1, passed1, *saved = kernel(
        front_one,
        "front_one",
        [
            ((n1, width), BF),
            ((n1, width), BF),
            ((2, n2, half), BF),
            ((3, PADDED, LANES), F32),
            ((2, n1, LANES), F32),
            ((2, n2, LANES), F32),
            ((2, n2, LANES), F32),
            ((2, a1, 2 * HD), BF),
        ],
        [scal, rows_in, tok_one, tok_two, gains[0], *first_all, pools_one, memory_one],
        scratch(*FRONT_WORK) + field_work(2),
        early=(5, 6),
        late=(0, 1, 2, 4, 5, 6),
        far_outs=(3,),
    )
    first_kept, (x1_kept, normed1, g_kept, qp1_kept, kp1_kept, vp1_kept) = saved[:2], saved[2:]
    places = ("plane", "head")
    near1 = lax.ppermute(passed1, places, clip_routes(planes, 1))
    far1 = lax.ppermute(passed1, places, clip_routes(planes, 2))
    (mlp_over, late_qkv), (x1,) = after((mlp_over, qkv_two_t), (x1,))
    mlp_all = (mlp_over, beside(mlp_over))
    qkv_two_all = spread(late_qkv, scal)
    attn1_ins = [*first_all, qp1, kp1, vp1, near1, far1, *first_all]
    _, part1, near1_kept, far1_kept, rows1 = kernel(
        functools.partial(attend, 0),
        "attend_one",
        [((2, n1, LANES), BF), ((n1, width), BF)],
        [scal, *attn1_ins],
        early=(6, 7),
        late=(0,),
    )
    middle1, _, part_mlp1, *mlp_kept, middle1_kept, mlp_normed1 = kernel(
        mlp_one,
        "mlp_one",
        [((n1, width), F32), ((n1, width), BF), ((n1, width), BF)],
        [scal, x1, part1, swap(part1), gains[1], *mlp_all],
        early=(5, 6),
        late=(0, 1),
    )
    late_proj, (part_mlp1,) = after(proj_two, (part_mlp1,))
    proj_two_all = spread(late_proj, scal)
    _, _, fields2, qp2, kp2, vp2, passed2, *saved = kernel(
        front_two,
        "front_two",
        [
            ((n1, width), F32),
            ((n1, width), BF),
            ((6, PADDED, LANES), F32),
            ((4, n2, LANES), F32),
            ((4, n1, LANES), F32),
            ((4, n1, LANES), F32),
            ((2, a2, 4 * HD), BF),
        ],
        [scal, middle1, part_mlp1, swap(part_mlp1), gains[2], *qkv_two_all, pools_two, memory_two],
        scratch(*FRONT_WORK) + field_work(4),
        early=(5, 6),
        late=(0, 1, 3, 4, 5),
        far_outs=(2,),
    )
    qkv_two_kept, (x2, normed2, qp2_kept, kp2_kept, vp2_kept) = saved[:2], saved[2:]
    (skip,) = kernel(skip_two, "skip_two", [((n2, wide), F32)], [normed2, residual_two])
    near2 = lax.ppermute(passed2, places, clip_routes(planes, 1))
    far2 = lax.ppermute(passed2, places, clip_routes(planes, 2))
    attn2_ins = [*first_kept, qp2, kp2, vp2, near2, far2, *proj_two_all]
    _, part2, near2_kept, far2_kept, *proj_two_kept, rows2 = kernel(
        functools.partial(attend, 1),
        "attend_two",
        [((4, n2, LANES), BF), ((n2, wide), BF)],
        [scal, *attn2_ins],
        left=(1, 2),
        early=(6, 7, 8, 9),
        late=(0,),
    )
    _, mlp_normed2, own_half, middle2 = kernel(
        middle_two,
        "middle_two",
        [((n2, wide), F32), ((n2, wide), BF), ((2, n2, half), BF)],
        [scal, skip, part2, swap(part2), gains[3], g_kept],
        left=(5,),
        late=(0,),
    )
    halves = [turn_by(own_half, d) for d in (1, 2, 3)]
    found = kernel(
        mlp_rows,
        "mlp_rows",
        [((832, half), BF)] * 2 + [((4, n2, half), BF)] * 2 + [((4, 2, n2, wide), BF)],
        [scal, mlp_normed2, g_kept, *halves, *(swap(item) for item in halves), up_two, down_two],
        [pltpu.VMEM((2, n2, wide), F32)],
    )
    wide_grads = kernel(mlp_sums, "mlp_sums", [((wide, half), BF)] * 2, found[2:5])
    sums = kernel(add_cores, "add_cores", [((2, n2, half), BF)] * 4, [found[0], swap(found[1])])
    sums = [sums[0]] + [turn_by(sums[d], -d) for d in (1, 2, 3)]
    def across(values, bit):
        return lax.ppermute(values, "plane", [(i, i ^ bit) for i in range(planes)])

    def peers(parts):
        return [parts[0]] + [across(parts[peer], peer) for peer in (1, 2, 3)]

    def add_wide(pair, bits):
        received = [across(item, bit) for item, bit in zip(pair, bits)]
        return kernel(add_both, "add_wide", [((wide, half), BF)] * 2, [pair[0], received[0], pair[1], received[1]])

    wide_sum = add_wide(wide_grads, (1, 2))
    (row_sum,) = kernel(sum_four, "sum_rows", [((2, n2, half), BF)], sums)
    row_sum, (wide_sum,) = after(row_sum, (wide_sum,))
    row_other = swap(row_sum)
    middle_grad2, gain_four_grad, dq2, dk2, dv2, d_near2, d_far2, table_two_grad = kernel(
        back_attend_two,
        "back_attend_two",
        [
            ((n2, wide), F32),
            ((1, wide), F32),
            ((4, n2, LANES), F32),
            ((4, n1, LANES), F32),
            ((4, n1, LANES), F32),
            ((2, a2, 4 * HD), BF),
            ((2, a2, 4 * HD), BF),
            ((4, LANES), F32),
        ],
        [
            scal, row_sum, row_other, g_kept, middle2, gains[3],
            *first_kept, qp2_kept, kp2_kept, vp2_kept, near2_kept, far2_kept, *proj_two_kept, rows2,
        ],
    )
    proj_two_grad, residual_grad, keep, send = kernel(
        back_rest_two,
        "back_rest_two",
        [((2, 4 * HD, width), BF), ((2, 192, half), BF), ((n2 // 2, wide), BF), ((n2 // 2, wide), BF)],
        [scal, row_sum, row_other, middle2, normed2, middle_grad2, rows2],
    )
    near_grad2 = lax.ppermute(d_near2, places, clip_routes(planes, -1))
    far_grad2 = lax.ppermute(d_far2, places, clip_routes(planes, -2))

    wide_sum = add_wide(wide_sum, (2, 1))
    (near_grad2, far_grad2), (wide_sum,) = after((near_grad2, far_grad2), (wide_sum,))
    part_back2, *sends2, small2, _, _ = kernel(
        back_front_two,
        "back_front_two",
        [
            ((n1, width), BF),
            *[((2, 288, width), BF)] * 4,
            ((64, width), F32),
            ((3, 32, LANES), F32),
            ((2, FR, LANES), F32),
        ],
        [
            scal, middle_grad2, normed2, fields2, kp2_kept, vp2_kept, dq2, dk2, dv2, near_grad2, far_grad2,
            *qkv_two_kept, residual_two, pools_two, memory_two, proj_two_grad, residual_grad, gain_four_grad,
        ],
        [pltpu.VMEM((2, 1152, width), BF)] + scratch(*BACK_WORK) + field_work(4),
        [2, 4, 5, 11, 12, 13],
        raw=[3],
    )
    received2 = peers(sends2)
    grad1, part_mlp_back, gain_three_grad, *sends_mlp = kernel(
        back_mlp_one,
        "back_mlp_one",
        [((n1, width), F32), ((n1, width), BF), ((1, width), F32)] + [((2, 224, width), BF)] * 4,
        [scal, part_back2, swap(part_back2), x2, gains[2], mlp_normed1, *mlp_kept, small2, swap(small2)],
        [pltpu.VMEM((2, 896, width), BF)],
        [3, 5, 6, 7],
    )
    middle_grad1, gain_two_grad, dq1, dk1, dv1, d_near1, d_far1, proj_one_grad, table_one_grad = kernel(
        back_attend_one,
        "back_attend_one",
        [
            ((n1, width), F32),
            ((1, width), F32),
            ((2, n1, LANES), F32),
            ((2, n2, LANES), F32),
            ((2, n2, LANES), F32),
            ((2, a1, 2 * HD), BF),
            ((2, a1, 2 * HD), BF),
            ((2, HD, width), BF),
            ((2, LANES), F32),
        ],
        [
            scal, part_mlp_back, swap(part_mlp_back), grad1, middle1_kept, gains[1],
            *first_kept, qp1_kept, kp1_kept, vp1_kept, near1_kept, far1_kept, *first_kept, rows1,
        ],
        left=[4, *range(6, 16)],
    )
    near_grad1 = lax.ppermute(d_near1, places, clip_routes(planes, -1))
    far_grad1 = lax.ppermute(d_far1, places, clip_routes(planes, -2))
    bit = 4
    while bit < planes:
        wide_sum = add_wide(wide_sum, (bit, bit))
        bit *= 2
    received_mlp = peers(sends_mlp)
    rows_received = lax.ppermute(send, axes, route_three)
    (near_grad1, far_grad1), (wide_sum, received2, rows_received) = after(
        (near_grad1, far_grad1), (wide_sum, received2, rows_received)
    )
    qkv_one_grad, part_back1, small1, _, _ = kernel(
        back_front_one,
        "back_front_one",
        [((2, 3 * HD, width), BF), ((n1, width), BF), ((64, width), F32), ((3, 32, LANES), F32), ((2, FR, LANES), F32)],
        [
            scal, normed1, fields1, kp1_kept, vp1_kept, dq1, dk1, dv1, near_grad1, far_grad1,
            *first_kept, pools_one, memory_one, gain_two_grad, gain_three_grad,
        ],
        scratch(*BACK_WORK) + field_work(2),
        [1, 3, 4, 10, 11],
        raw=[2],
    )
    part_back1, (received_mlp,) = after(part_back1, (received_mlp,))
    tok_keep, tok_send, *sends1 = kernel(
        back_tokens,
        "back_tokens",
        [((n1 // 2, width), BF), ((n1 // 2, width), BF)] + [((2, 128, width), BF)] * 4,
        [
            scal, part_back1, swap(part_back1), x1_kept, gains[0], middle_grad1, qkv_one_grad, proj_one_grad,
            table_one_grad, table_two_grad, small1, swap(small1),
        ],
        [pltpu.VMEM((2, 512, width), BF)],
        [3],
    )
    tok_received = lax.ppermute(tok_send, axes, route_three)

    def combine(body, label, rows, ins, count=1):
        return kernel(body, label, [((rows, width), BF)] * count, ins)

    back_route = reverse(cross_route())
    received1 = peers(sends1)
    rows_two, rows_mlp, rows_one = 288, 224, 128
    one2, two2 = combine(sum_planes, "sum_planes_two", rows_two + rows_mlp, received2 + received_mlp, 2)
    beside2 = beside(two2)
    up_two_sum, down_two_sum = kernel(
        finish_wide, "finish_wide", [((wide, wide), F32), ((wide, wide), F32)], [scal, wide_sum[0], swap(wide_sum[0]), wide_sum[1], swap(wide_sum[1])]
    )
    received1, (up_two_sum, down_two_sum) = after(received1, (up_two_sum, down_two_sum))
    one1, two1 = combine(sum_planes, "sum_planes_one", rows_one, received1, 2)
    beside1 = beside(two1)
    (beside2,), (one1, tok_received) = after((beside2,), (one1, tok_received))
    tokens_grad = jnp.where(match, tok_keep, tok_received)
    (total2,) = combine(add_two, "add_pair_two", rows_two + rows_mlp, [one2, beside2])
    cross2 = lax.ppermute(total2, axes, back_route)
    (beside1,), (total2,) = after((beside1,), (total2,))
    (total1,) = combine(add_two, "add_pair_one", rows_one, [one1, beside1])
    cross1 = lax.ppermute(total1, axes, back_route)
    (cross2,), (cross1,) = after((cross2,), (cross1,))
    (total2,) = combine(add_two, "add_cross_two", rows_two + rows_mlp, [total2, cross2])
    bit = 4
    while bit < planes:
        (total2,) = combine(add_two, "add_planes_two", rows_two + rows_mlp, [total2, across(total2, bit)])
        bit *= 2

    def halves_of(total, sizes):
        body = functools.partial(choose_half, sizes)
        return combine(body, "choose_half", sum(sizes) // 2, [scal, total, swap(total)])

    half2 = halves_of(total2, (rows_two, rows_mlp))
    (total1,) = combine(add_two, "add_cross_one", rows_one, [total1, cross1])
    bit = 4
    while bit < planes:
        (total1,) = combine(add_two, "add_planes_one", rows_one, [total1, across(total1, bit)])
        bit *= 2
    parts2 = peers(list(half2) * 4)
    parts1 = peers(halves_of(total1, (rows_one,)) * 4)
    parts2, parts1 = after(parts2, parts1)
    (piece,) = kernel(take_piece, "take_piece", [((96, width), BF)], [scal, *parts2])
    small_shapes = [(pools_one.shape, F32), (memory_one.shape, F32)]
    qkv_two_sum, proj_two_sum, up_one_sum, down_one_sum, pools_two_sum, memory_two_sum, gain_four_sum = kernel(
        finish_two,
        "finish_two",
        [(qkv_two_t.shape, F32), (proj_two.shape, F32), (up_one.shape, F32), (down_one.shape, F32)]
        + small_shapes
        + [((wide,), F32)],
        [scal, *parts2, *(swap(part) for part in parts2)],
        [pltpu.VMEM((1152, width), F32), pltpu.VMEM((896, width), F32)],
    )
    (qkv_one_sum, proj_one_sum, table_one_sum, table_two_sum, pools_one_sum, memory_one_sum, *gain_sums) = kernel(
        finish_one,
        "finish_one",
        [(qkv_one_t.shape, F32), (proj_one.shape, F32), (table_one.shape, F32), (table_two.shape, F32)]
        + small_shapes
        + [((width,), F32)] * 3,
        [scal, *parts1, *(swap(part) for part in parts1)],
        [pltpu.VMEM((512, width), F32)],
    )
    others = [lax.ppermute(piece, "head", [(z, z ^ bit) for z in range(4)]) for bit in (1, 2, 3)]
    blocks_out, tokens_out = jnp.where(match, keep, rows_received), tokens_grad
    others, (gain_four_sum, first_gain, blocks_out, tokens_out) = after(
        others, (gain_four_sum, gain_sums[0], blocks_out, tokens_out)
    )
    (pieces,) = kernel(stack_four, "stack_pieces", [((4, 96, width), BF)], [scal, piece, *others])
    (residual_sum,) = kernel(
        finish_residual, "finish_residual", [(residual_two.shape, F32)], [scal, pieces, swap(pieces)]
    )

    return (
        blocks_out,
        tokens_out,
        first_gain,
        qkv_one_sum.T,
        pools_one_sum,
        memory_one_sum,
        table_one_sum,
        proj_one_sum,
        gain_sums[1],
        up_one_sum,
        down_one_sum,
        gain_sums[2],
        qkv_two_sum.T,
        residual_sum,
        pools_two_sum,
        memory_two_sum,
        table_two_sum,
        proj_two_sum,
        gain_four_sum,
        up_two_sum,
        down_two_sum,
    )


def solution(mesh):
    planes = mesh.shape["dp"] // 2
    fine = Mesh(mesh.devices.reshape(planes, 2, mesh.shape["head"]), ("plane", "core", "head"))
    dp = ("plane", "core")
    rows = P(("plane", "core", "head"), None)
    columns, lines, free = P(None, "head"), P("head", None), P()
    in_specs = (
        rows, rows, free, P(dp, None),
        free, columns, free, free, lines, lines, free, columns, lines,
        free, columns, free, free, free, lines, lines, free, columns, lines,
    )
    out_specs = (
        rows, rows,
        free, columns, free, free, lines, lines, free, columns, lines,
        free, columns, free, free, free, lines, lines, free, columns, lines,
    )
    return jax.shard_map(
        functools.partial(local, planes), mesh=fine, in_specs=in_specs, out_specs=out_specs, check_vma=False
    )
```

```python
import functools

import jax
import jax.numpy as jnp
import numpy as np
from jax import lax
from jax.experimental import pallas as pl
from jax.experimental.pallas import tpu as pltpu
from jax.sharding import Mesh, PartitionSpec as P

HD = 96
FR = 4
SIDE = 10
LANES = 128
GRID = SIDE + 2
SLAB = GRID * 2 * FR
PADDED = GRID * SLAB
EPSILON = 1e-06
NEGATIVE = -1e30
SCALE = HD**-0.5
GELU_A = float(np.sqrt(2.0 / np.pi))
GELU_B = 0.044715

BF = jnp.bfloat16
F32 = jnp.float32


def nn(a, b):
    return lax.dot_general(a, b, (((1,), (0,)), ((), ())), preferred_element_type=F32)


def nt(a, b):
    return lax.dot_general(a, b, (((1,), (1,)), ((), ())), preferred_element_type=F32)


def tn(a, b):
    return lax.dot_general(a, b, (((0,), (0,)), ((), ())), preferred_element_type=F32)


def iota(shape, dim):
    return lax.broadcasted_iota(jnp.int32, shape, dim)


def widen(values):
    fill = jnp.zeros((values.shape[0], LANES - values.shape[1]), values.dtype)
    return jnp.concatenate([values, fill], axis=1)


def split(values):
    high = values.astype(BF)
    return high, (values - high.astype(F32)).astype(BF)


def norm_parts(values):
    centered = values - jnp.mean(values, axis=-1, keepdims=True)
    variance = jnp.mean(centered * centered, axis=-1, keepdims=True)
    scale = lax.rsqrt(variance + EPSILON)
    return centered * scale, scale


def norm_back(grad, values, gain):
    unit, scale = norm_parts(values)
    scaled = grad * gain
    mean_one = jnp.mean(scaled, axis=-1, keepdims=True)
    mean_two = jnp.mean(scaled * unit, axis=-1, keepdims=True)
    gain_grad = jnp.sum(grad * unit, axis=0, keepdims=True)
    return scale * (scaled - mean_one - unit * mean_two), gain_grad


def gelu_parts(values):
    square = values * values
    bent = jnp.tanh(GELU_A * values * (1.0 + GELU_B * square))
    half = 0.5 * (1.0 + bent)
    slope = half + 0.5 * values * (1.0 - bent * bent) * GELU_A * (1.0 + 3.0 * GELU_B * square)
    return values * half, slope


def pick(flag, one, two):
    return jnp.where(flag, one, two)


def token_rows(half):
    shape = (FR * SIDE * SIDE, 2 * SIDE * SIDE)
    rows, cols = iota(shape, 0), iota(shape, 1)
    frame, place = (rows & (FR - 1)) - 2 * half, rows >> 2
    match = (cols == SIDE * SIDE * frame + place) & (frame >= 0) & (frame < 2)
    return jnp.where(match, 1.0, 0.0).astype(BF)


def half_rows(half, area):
    shape = (2 * area, FR * area)
    rows, cols = iota(shape, 0), iota(shape, 1)
    upper = jnp.where(rows >= area, 1, 0)
    return jnp.where(cols == FR * (rows - area * upper) + 2 * half + upper, 1.0, 0.0).astype(BF)


def cells():
    small = SIDE // 2
    count = FR * small * small
    rows, cols = iota((count, 1), 0), iota((1, FR * SIDE * SIDE), 1)
    place, spot = rows >> 2, cols >> 2
    row_key = FR * place + (rows & (FR - 1))
    line, column = lax.div(spot, 2 * SIDE), lax.div(lax.rem(spot, SIDE), 2)
    col_key = FR * (small * line + column) + (cols & (FR - 1))
    return jnp.where(row_key == col_key, 1.0, 0.0).astype(BF)


def fill_weights(wide, pools, field, flip):
    for tap in range(27):
        source = 26 - tap if flip else tap
        line = widen(pools[field, source : source + 1, :])
        wide[8 * tap : 8 * tap + 8, :] = jnp.broadcast_to(line, (8, LANES))


def frame_shifts():
    lane = iota((8, LANES), 0)
    early, late = lane >= 2, lane < 6
    return (
        lambda values: jnp.where(early, pltpu.roll(values, 2, 0), 0.0),
        lambda values: jnp.where(late, pltpu.roll(values, 6, 0), 0.0),
    )


def load_row(ref, index):
    return ref[pl.ds(pl.multiple_of(SLAB * index, SLAB), SLAB), :].reshape(GRID, 8, LANES)


def tap_of(wide, a, b, e):
    spot = 8 * (9 * a + 3 * b + e)
    return wide[spot : spot + 8, :]


def conv_rows(source, wide, result, stride):
    count = SIDE // stride
    before, after = frame_shifts()

    def one_row(i, carry):
        sums = [[None] * count for _ in range(3)]
        for b in range(3):
            line = load_row(source, stride * i + b)
            for a in range(3):
                for e in range(3):
                    weight = tap_of(wide, a, b, e)
                    for j in range(count):
                        term = weight * line[stride * j + e]
                        sums[a][j] = term if sums[a][j] is None else sums[a][j] + term
        for j in range(count):
            total = sums[1][j] + before(sums[0][j]) + after(sums[2][j])
            result[pl.ds(pl.multiple_of(8 * count * i + 8 * j, 8), 8), :] = total
        return carry

    lax.fori_loop(0, count, one_row, 0)


def conv_back_two(source, wide, result):
    count = SIDE // 2
    before, after = frame_shifts()

    def one_row(m, carry):
        now, later = load_row(source, m + 1), load_row(source, m + 2)
        totals = [None] * (2 * SIDE)
        for a, shift in ((1, None), (0, after), (2, before)):
            sums = [None] * (2 * SIDE)
            for start, b, line in ((0, 1, now), (SIDE, 0, later), (SIDE, 2, now)):
                taps = [tap_of(wide, a, b, e) for e in range(3)]
                for n in range(count):
                    even = taps[1] * line[n + 1]
                    odd = taps[0] * line[n + 2] + taps[2] * line[n + 1]
                    for spot, term in ((start + 2 * n, even), (start + 2 * n + 1, odd)):
                        sums[spot] = term if sums[spot] is None else sums[spot] + term
            for spot in range(2 * SIDE):
                totals[spot] = sums[spot] if shift is None else totals[spot] + shift(sums[spot])
        for spot in range(2 * SIDE):
            result[pl.ds(pl.multiple_of(16 * SIDE * m + 8 * spot, 8), 8), :] = totals[spot]
        return carry

    lax.fori_loop(0, count, one_row, 0)


def conv_weight(source, grads, totals, stride):
    count = SIDE // stride
    before, after = frame_shifts()
    totals[...] = jnp.zeros((27 * 8, LANES), F32)

    def one_row(i, carry):
        line = load_row(grads, i + 1)
        own = [line[j + 1] for j in range(count)]
        cotangents = ([after(item) for item in own], own, [before(item) for item in own])
        for b in range(3):
            line = load_row(source, stride * i + b)
            for e in range(3):
                for a in range(3):
                    spot = 8 * (9 * a + 3 * b + e)
                    terms = [line[stride * j + e] * cotangents[a][j] for j in range(count)]
                    terms.append(totals[spot : spot + 8, :])
                    while len(terms) > 1:
                        terms = [
                            terms[k] + terms[k + 1] if k + 1 < len(terms) else terms[k]
                            for k in range(0, len(terms), 2)
                        ]
                    totals[spot : spot + 8, :] = terms[0]
        return carry

    lax.fori_loop(0, count, one_row, 0)


def weights_of_rows(totals):
    return jnp.sum(totals[...].reshape(27, 8, LANES), axis=1)


def put_rows(target, values, head, count):
    for i in range(count):
        start = ((i + 1) * GRID + 1) * 8 + head
        target[pl.ds(start, FR * count, stride=2), :] = values[FR * count * i : FR * count * (i + 1), :]


def pairs_of(heads):
    return [((0, 0), (1, 0))] if heads == 2 else [((0, 0), (0, 1)), ((1, 0), (1, 1))]


def pack_heads(lines, turn):
    half = len(lines) // 2
    sides = [jnp.concatenate([line[:, :HD] for line in lines[half * i : half * (i + 1)]], axis=1) for i in range(2)]
    flag = turn == 1
    return jnp.concatenate([pick(flag, sides[1], sides[0]), pick(flag, sides[0], sides[1])], axis=1)


def unpack_heads(values, turn):
    heads = values.shape[1] // HD
    lines = [values[:, HD * head : HD * (head + 1)] for head in range(heads)]
    flag, half = turn == 1, heads // 2
    return [widen(pick(flag, lines[(head + half) % heads], lines[head])) for head in range(heads)]


def front_body(heads, turn, strides, normed, weights, pools, memory, fields, pooled, passed, work):
    wide, result, held, sent = work
    copies = []
    lines = [nt(normed, weights[s][: 3 * HD * heads // 2, :]) for s in range(2)]
    for field in range(3):
        fill_weights(wide, pools, field, False)
        stride = strides[field]
        count = SIDE // stride
        for number, pair in enumerate(pairs_of(heads)):
            spot = field * (heads // 2) + number
            group = held.at[spot]
            group[...] = jnp.zeros((PADDED, LANES), F32)
            for head, (slot, place) in enumerate(pair):
                start = HD * (3 * place + field)
                put_rows(group, widen(lines[slot][:, start : start + HD]), head, SIDE)
            copies.append(pltpu.make_async_copy(group, fields.at[spot], sent.at[spot]))
            copies[-1].start()
            conv_rows(group, wide, result, stride)
            for head in range(2):
                pooled[field][2 * number + head] = result[pl.ds(head, FR * count * count, stride=2), :]
    area = (SIDE // strides[1]) ** 2
    for which in range(2):
        lines = []
        for head in range(heads):
            total = jnp.zeros((area, LANES), F32)
            for t in range(FR):
                line = widen(memory[which, t : t + 1, :])
                total = total + line * pooled[1 + which][head, pl.ds(t, area, stride=FR), :]
            lines.append(total)
        passed[which] = pack_heads(lines, turn).astype(BF)
    for copy in copies:
        copy.wait()


def front_one(scal, own, first, second, gain, wa, wb, pools, memory, x_out, normed_out, g_out, fields, qp, kp, vp, passed, *work):
    match, turn = scal[0] == 1, scal[1] == 1
    near = pick(match, own[...], first[...])
    far = pick(match, first[...], second[...])
    low, high = pick(turn, far, near), pick(turn, near, far)
    count, area = 2 * SIDE * SIDE, (SIDE // 2) ** 2
    rows = nn(token_rows(0), low[:count]) + nn(token_rows(1), high[:count])
    x_out[...] = rows.astype(BF)
    turns = [half_rows(half, area) for half in range(2)]
    for column in range(2):
        spots = slice(count + 2 * area * column, count + 2 * area * (column + 1))
        g_out[column] = (tn(turns[0], low[spots]) + tn(turns[1], high[spots])).astype(BF)
    normed = (norm_parts(rows)[0] * gain[...]).astype(BF)
    normed_out[...] = normed
    front_body(2, scal[1], (1, 2, 2), normed, (wa, wb), pools, memory, fields, (qp, kp, vp), passed, work)


def front_two(scal, middle, part, other, gain, wa, wb, pools, memory, x_out, normed_out, fields, qp, kp, vp, passed, *work):
    rows = middle[...] + (part[...].astype(F32) + other[...].astype(F32))
    x_out[...] = rows
    normed = (norm_parts(rows)[0] * gain[...]).astype(BF)
    normed_out[...] = normed
    front_body(4, scal[1], (2, 1, 1), normed, (wa, wb), pools, memory, fields, (qp, kp, vp), passed, work)


def skip_two(normed, residual, skip):
    high, low = split(nn(cells(), normed[...]))
    skip[...] = 0.25 * (nn(high, residual[...]) + nn(low, residual[...]))


def table_of(shards, block, slot, place):
    line = shards[slot][4 * HD : 4 * HD + 16, :].astype(F32)
    row = 3 * (place if block == 0 else 1 + place)
    return line[row : row + 1, :] + line[row + 1 : row + 2, :] + line[row + 2 : row + 3, :]


def own_bias(bins, table):
    values = jnp.zeros(bins.shape, F32)
    for number in range(2 * FR - 1):
        values = jnp.where(bins == number, table[:, number : number + 1], values)
    return values


def far_bias(table, offset):
    lanes = iota(table.shape, 1)
    return jnp.sum(jnp.where(lanes == offset + 2 * FR - 1, table, 0.0), axis=1, keepdims=True)


def probs_of(scal, bins, table, query, keys):
    tile = own_bias(bins, table)
    rows = query.shape[0]
    bias = jnp.concatenate([tile] * ((rows + 7) // 8), axis=0)[:rows]
    parts = [nt(query, keys[0]) * SCALE + bias]
    for j in range(2):
        raw = nt(query, keys[1 + j]) * SCALE + far_bias(table, scal[4 + j])
        parts.append(jnp.where(scal[2 + j] == 1, raw, NEGATIVE))
    top = functools.reduce(jnp.maximum, [jnp.max(part, axis=1, keepdims=True) for part in parts])
    parts = [jnp.exp(part - top) for part in parts]
    total = sum(jnp.sum(part, axis=1, keepdims=True) for part in parts)
    return [part / total for part in parts]


def heads_of(heads, block):
    return [(slot, place) for slot in range(2) for place in range(heads // 2)]


def attend(block, scal, ta, tb, qp, kp, vp, near, far, wa, wb, rows_out, part_out):
    heads = qp.shape[0]
    shards, weights = (ta, tb), (wa, wb)
    base = 0 if block else 3 * HD
    shape = (8, kp.shape[1])
    bins = (iota(shape, 0) & (FR - 1)) - (iota(shape, 1) & (FR - 1)) + FR - 1
    total = jnp.zeros(part_out.shape, F32)
    nears, fars = ([unpack_heads(item[which], scal[1]) for which in range(2)] for item in (near, far))
    for head, (slot, place) in enumerate(heads_of(heads, block)):
        table = table_of(shards, block, slot, place)
        pool = qp[head]
        keys = (kp[head].astype(BF), nears[0][head], fars[0][head])
        values = (vp[head].astype(BF), nears[1][head], fars[1][head])
        probs = probs_of(scal, bins, table, pool.astype(BF), keys)
        mixture = sum(nn(p.astype(BF), v) for p, v in zip(probs, values))
        line = (mixture + pool).astype(BF)
        rows_out[head] = line
        total = total + nn(line[:, :HD], weights[slot][base + HD * place : base + HD * place + HD, :])
    part_out[...] = total.astype(BF)


def attend_back(block, scal, ta, tb, qp, kp, vp, near, far, wa, wb, rows, middle_grad, dq, dk, dv, d_near, d_far, proj_grad, table_grad):
    heads = qp.shape[0]
    shards, weights = (ta, tb), (wa, wb)
    base = 0 if block else 3 * HD
    shape = (8, kp.shape[1])
    bins = (iota(shape, 0) & (FR - 1)) - (iota(shape, 1) & (FR - 1)) + FR - 1
    branch = middle_grad.astype(BF)
    lanes = iota((1, LANES), 1)
    table_lines = []
    nears, fars = ([unpack_heads(item[which], scal[1]) for which in range(2)] for item in (near, far))
    near_lines, far_lines = ([], []), ([], [])
    for head, (slot, place) in enumerate(heads_of(heads, block)):
        table = table_of(shards, block, slot, place)
        weight = weights[slot][base + HD * place : base + HD * place + HD, :]
        if proj_grad is not None:
            proj_grad[slot, HD * place : HD * place + HD, :] = tn(rows[head][:, :HD], branch).astype(BF)
        grad = widen(nt(branch, weight).astype(BF))
        query = qp[head].astype(BF)
        keys = (kp[head].astype(BF), nears[0][head], fars[0][head])
        values = (vp[head].astype(BF), nears[1][head], fars[1][head])
        probs = probs_of(scal, bins, table, query, keys)
        grad_probs = [nt(grad, v) for v in values]
        inner = sum(jnp.sum(p * d, axis=1, keepdims=True) for p, d in zip(probs, grad_probs))
        low = [(p * (d - inner)).astype(BF) for p, d in zip(probs, grad_probs)]
        dq[head] = sum(nn(s, k) for s, k in zip(low, keys)) * SCALE + grad.astype(F32)
        key_grads = [tn(s, query) * SCALE for s in low]
        value_grads = [tn(p.astype(BF), grad) for p in probs]
        dk[head], dv[head] = key_grads[0], value_grads[0]
        for which, grads in enumerate((key_grads, value_grads)):
            near_lines[which].append(grads[1])
            far_lines[which].append(grads[2])
        score = low[0].astype(F32)
        count = score.shape[0]
        if count % 8:
            score = jnp.concatenate([score, jnp.zeros((8 - count % 8, score.shape[1]), F32)], axis=0)
        score = jnp.sum(score.reshape(-1, 8, score.shape[1]), axis=0)
        line = jnp.zeros((1, LANES), F32)
        for number in range(2 * FR - 1):
            column = jnp.sum(jnp.where(bins == number, score, 0.0), axis=0, keepdims=True)
            line = line + jnp.where(lanes == number, jnp.sum(column, axis=1, keepdims=True), 0.0)
        for j in range(2):
            column = jnp.sum(low[1 + j].astype(F32), axis=0, keepdims=True)
            value = jnp.sum(column, axis=1, keepdims=True)
            line = line + jnp.where(lanes == scal[4 + j] + 2 * FR - 1, value, 0.0)
        table_lines.append(line)
    for which in range(2):
        d_near[which] = pack_heads(near_lines[which], scal[1]).astype(BF)
        d_far[which] = pack_heads(far_lines[which], scal[1]).astype(BF)
    for head, line in enumerate(table_lines):
        table_grad[head : head + 1, :] = line


def field_back(heads, turn, strides, fields, pooled, grads, near, far, pools, memory, pools_grad, memory_grad, work):
    wide, result, grid, totals, rows, held, arrived = work
    half = heads // 2
    copies = [pltpu.make_async_copy(fields.at[i], held.at[i], arrived.at[i]) for i in range(3 * half)]
    for copy in copies:
        copy.start()
    back = {}
    area = (SIDE // strides[1]) ** 2
    for field in range(3):
        stride = strides[field]
        count = SIDE // stride
        fill_weights(wide, pools, field, stride == 1)
        weight_sum = jnp.zeros((27, LANES), F32)
        memory_lines = [jnp.zeros((1, LANES), F32) for _ in range(FR)]
        if field:
            passed = unpack_heads(near[field - 1].astype(F32) + far[field - 1].astype(F32), turn)
        for number, pair in enumerate(pairs_of(heads)):
            grid[...] = jnp.zeros((PADDED, LANES), F32)
            for place in range(2):
                head = 2 * number + place
                if field == 0:
                    put_rows(grid, grads[0][head], place, count)
                else:
                    cotangent = passed[head]
                    for t in range(FR):
                        spot = pl.ds(t, area, stride=FR)
                        line = widen(memory[field - 1, t : t + 1, :])
                        rows[spot, :] = grads[field][head, spot, :] + line * cotangent
                        product = pooled[field - 1][head, spot, :] * cotangent
                        memory_lines[t] = memory_lines[t] + jnp.sum(product, axis=0, keepdims=True)
                    put_rows(grid, rows[0 : FR * area, :], place, count)
            group = held.at[field * half + number]
            copies[field * half + number].wait()
            conv_weight(group, grid, totals, stride)
            weight_sum = weight_sum + weights_of_rows(totals)
            if stride == 1:
                conv_rows(grid, wide, result, 1)
            else:
                conv_back_two(grid, wide, result)
            for place, key in enumerate(pair):
                back[key + (field,)] = result[pl.ds(place, FR * SIDE * SIDE, stride=2), :][:, :HD]
        pools_grad[field, 0:27, :] = weight_sum
        if field:
            for t in range(FR):
                memory_grad[field - 1, t : t + 1, :] = memory_lines[t]
    outs = []
    for slot in range(2):
        columns = [back[(slot, place, field)] for place in range(half) for field in range(3)]
        outs.append(jnp.concatenate(columns, axis=1).astype(BF))
    return outs


def mlp_one(scal, x, part, other, gain, wa, wb, middle_out, normed_out, part_out):
    weights = (wa, wb)
    middle = x[...].astype(F32) + (part[...].astype(F32) + other[...].astype(F32))
    middle_out[...] = middle
    normed = (norm_parts(middle)[0] * gain[...]).astype(BF)
    normed_out[...] = normed
    size = normed.shape[1]
    total = jnp.zeros(part_out.shape, F32)
    for slot in range(2):
        hidden = gelu_parts(nn(normed, weights[slot][:size, :]))[0].astype(BF)
        total = total + nn(hidden, weights[slot][size:, :])
    part_out[...] = total.astype(BF)


def middle_two(scal, skip, part, other, gain, g, middle_out, normed_out, half_out):
    middle = skip[...] + (part[...].astype(F32) + other[...].astype(F32))
    middle_out[...] = middle
    normed_out[...] = (norm_parts(middle)[0] * gain[...]).astype(BF)
    width = half_out.shape[2]
    half_out[0] = normed_out[:, pl.ds(pl.multiple_of(scal[7] * width, LANES), width)]
    half_out[1] = g[scal[7]]


def mlp_rows(scal, own, own_grad, *refs):
    halves, others = refs[0:3], refs[3:6]
    up_ref, down_ref = refs[6:8]
    keep, give, hidden_out, low_out, board, lines = refs[8:14]
    width = up_ref.shape[1] // 2
    core = scal[7]
    start = pl.multiple_of(core * width, LANES)
    rest = pl.multiple_of((1 - core) * width, LANES)
    up, down = up_ref[:, pl.ds(start, width)], down_ref[pl.ds(start, width), :]
    board[0, 0] = own[...]
    for column in range(2):
        board[0, 1, :, width * column : width * (column + 1)] = own_grad[column]
    for d in range(3):
        for which in range(2):
            board[d + 1, which, :, pl.ds(start, width)] = halves[d][which]
            board[d + 1, which, :, pl.ds(rest, width)] = others[d][which]
    for d in range(4):
        rows, grad = board[d, 0], board[d, 1]
        value, slope = gelu_parts(nn(rows, up))
        hidden = value.astype(BF)
        up_low = (nt(grad, down) * slope).astype(BF)
        hidden_out[d], low_out[d] = hidden, up_low
        lines[0] = nn(hidden, down)
        lines[1] = nt(up_low, up)
        for which in range(2):
            spots = slice(104 * (2 * d + which), 104 * (2 * d + which) + rows.shape[0])
            keep[spots, :] = lines[which, :, pl.ds(start, width)].astype(BF)
            give[spots, :] = lines[which, :, pl.ds(rest, width)].astype(BF)


def mlp_sums(hidden, low, board, packed, packed_down):
    up_total = sum(tn(board[d, 0], low[d]) for d in range(4))
    down_total = sum(tn(hidden[d], board[d, 1]) for d in range(4))
    width = packed.shape[1]
    packed[...] = up_total.astype(BF)
    packed_down[0:width, :] = down_total[:, :width].astype(BF)
    packed_down[width:, :] = down_total[:, width:].astype(BF)


def quarter_of(scal, peer):
    one = 1 - scal[8] if peer % 2 else scal[8]
    two = 1 - scal[9] if peer // 2 else scal[9]
    return one + 2 * two


def cut(scal, full, parts):
    rows = parts[0].shape[1]
    for peer in range(4):
        spots = pl.ds(pl.multiple_of(quarter_of(scal, peer) * rows, 16), rows)
        for slot in range(2):
            parts[peer][slot] = full[slot, spots, :]


def sum_planes(*refs):
    one, two = refs[-2:]
    start = 0
    for number in range(len(refs) // 4):
        parts = refs[4 * number : 4 * number + 4]
        rows = parts[0].shape[1]
        for slot, out in ((0, one), (1, two)):
            total = (parts[0][slot].astype(F32) + parts[1][slot].astype(F32)) + (
                parts[2][slot].astype(F32) + parts[3][slot].astype(F32)
            )
            out[start : start + rows, :] = total.astype(BF)
        start += rows


def gather_parts(scal, parts, start, full):
    rows = full.shape[0] // 8
    for number, part in enumerate(parts):
        core = scal[7] if number < 4 else 1 - scal[7]
        spots = pl.ds(pl.multiple_of((2 * quarter_of(scal, number % 4) + core) * rows, 16), rows)
        full[spots, :] = part[start : start + rows, :].astype(F32)


def put_totals(full, start, pools, memory):
    for field in range(3):
        pools[field] = full[start : start + 27, LANES * field : LANES * field + HD]
    for which in range(2):
        memory[which] = full[start + 32 : start + 32 + FR, LANES * which : LANES * which + HD]


def stack_four(scal, own, beside, far, last, out):
    z = scal[10]
    turn, upper = lax.rem(z, 2), lax.div(z, 2)
    for piece, parity, pair in (
        (own, turn, upper),
        (beside, 1 - turn, upper),
        (far, turn, 1 - upper),
        (last, 1 - turn, 1 - upper),
    ):
        out[2 * pair + parity] = piece[...]


def finish_residual(scal, own, other, out):
    size, width = own.shape[1:]
    for core, source in ((scal[7], own), (1 - scal[7], other)):
        for shard in range(4):
            rows = pl.ds(pl.multiple_of(2 * size * (shard % 2) + size * core, 16), size)
            columns = slice(width * (shard // 2), width * (shard // 2 + 1))
            out[rows, columns] = source[shard].astype(F32)


def take_piece(scal, a, b, c, d, piece):
    half = piece.shape[0]
    start = pl.multiple_of(48 * scal[7], 16)
    for peer, part in enumerate((a, b, c, d)):

        @pl.when(quarter_of(scal, peer) == 3)
        def _():
            piece[...] = part[pl.ds(start, half), :]


def finish_two(scal, *refs):
    parts = refs[0:8]
    qkv, proj, up, down, pools, memory, gain, full, full_mlp = refs[8:]
    gather_parts(scal, parts, 0, full)
    gather_parts(scal, parts, full.shape[0] // 8, full_mlp)
    width = full.shape[1]
    qkv[...] = full[0:576, :]
    proj[:, :width] = full[576:768, :]
    proj[0:96, width:] = full[768:864, :]
    proj[96:192, width:] = full[960:1056, :]
    up[...] = full_mlp[0:384, :]
    down[...] = full_mlp[384:768, :]
    put_totals(full_mlp, 768, pools, memory)
    gain[0:width], gain[width:] = full_mlp[808, :], full_mlp[809, :]


def finish_one(scal, *refs):
    qkv, proj, table, second_table, pools, memory, gain, second_gain, third_gain, full = refs[8:]
    gather_parts(scal, refs[0:8], 0, full)
    qkv[...] = full[0:288, :]
    proj[...] = full[288:384, :]
    bins = table.shape[1]
    table[...] = full[384:385, :bins]
    second_table[...] = full[385:387, :bins]
    put_totals(full, 400, pools, memory)
    second_gain[...] = full[440, :]
    third_gain[...] = full[441, :]
    gain[...] = full[442, :]


def finish_wide(scal, own_up, other_up, own_down, other_down, up, down):
    first = scal[7] == 0
    size = up.shape[0]
    width = size // 2
    up[:, :width] = pick(first, own_up[...], other_up[...]).astype(F32)
    up[:, width:] = pick(first, other_up[...], own_up[...]).astype(F32)
    one = pick(first, own_down[...], other_down[...]).astype(F32)
    two = pick(first, other_down[...], own_down[...]).astype(F32)
    down[:width, :width], down[:width, width:] = one[:width, :], one[width:, :]
    down[width:, :width], down[width:, width:] = two[:width, :], two[width:, :]


def add_cores(keep, other, *outs):
    for d in range(4):
        for which in range(2):
            spots = slice(104 * (2 * d + which), 104 * (2 * d + which) + outs[d].shape[1])
            outs[d][which] = (keep[spots, :].astype(F32) + other[spots, :].astype(F32)).astype(BF)


def whole_columns(scal, own, other):
    first = scal[7] == 0
    return jnp.concatenate([pick(first, own, other), pick(first, other, own)], axis=1)


def add_both(one, one_other, two, two_other, one_out, two_out):
    one_out[...] = (one[...].astype(F32) + one_other[...].astype(F32)).astype(BF)
    two_out[...] = (two[...].astype(F32) + two_other[...].astype(F32)).astype(BF)


def add_two(one, two, out):
    out[...] = (one[...].astype(F32) + two[...].astype(F32)).astype(BF)


def sum_four(a, b, c, d, out):
    total = (a[...].astype(F32) + b[...].astype(F32)) + (c[...].astype(F32) + d[...].astype(F32))
    out[...] = total.astype(BF)


def back_attend_two(scal, part, other, g, middle, gain, *refs):
    ins, outs = refs[0:10], refs[10:]
    grad, gain_grad = norm_back(whole_columns(scal, part[1], other[1]).astype(F32), middle[...], gain[...])
    middle_grad = jnp.concatenate([g[0], g[1]], axis=1).astype(F32) + grad
    outs[0][...] = middle_grad
    outs[1][...] = gain_grad
    attend_back(1, scal, *ins, middle_grad, *outs[2:7], None, outs[7])


def back_rest_two(scal, part, other, middle, normed, middle_grad, rows, proj_grad, residual_grad, keep, send):
    final = (middle[...] + whole_columns(scal, part[0], other[0]).astype(F32)).astype(BF)
    area = (SIDE // 2) ** 2
    keep[...] = nn(half_rows(scal[1], area), final).astype(BF)
    send[...] = nn(half_rows(1 - scal[1], area), final).astype(BF)
    branch = middle_grad[...].astype(BF)
    width = residual_grad.shape[2]
    for head, (slot, place) in enumerate(heads_of(4, 1)):
        found = tn(rows[head][:, :HD], branch).astype(BF)
        for column in range(2):
            start = 2 * HD * column + HD * place
            proj_grad[slot, start : start + HD, :] = found[:, width * column : width * (column + 1)]
    linear = (0.25 * middle_grad[:, pl.ds(pl.multiple_of(scal[7] * width, LANES), width)]).astype(BF)
    high, low = split(nn(cells(), normed[...]))
    found = (tn(high, linear) + tn(low, linear)).astype(BF)
    size = residual_grad.shape[1]
    turned = scal[1] == 1
    residual_grad[0] = pick(turned, found[size:], found[:size])
    residual_grad[1] = pick(turned, found[:size], found[size:])


def put_small(small, pools_grad, memory_grad):
    small[...] = jnp.zeros(small.shape, F32)
    for field in range(3):
        small[0:27, LANES * field : LANES * (field + 1)] = pools_grad[field, 0:27, :]
    for which in range(2):
        small[32 : 32 + FR, LANES * which : LANES * (which + 1)] = memory_grad[which]


def back_front_two(scal, middle_grad, normed_ref, fields, kp, vp, dq, dk, dv, near, far, wa, wb, residual, pools, memory, proj_grad, residual_grad, gain_grad, part_out, keep, one, two, three, small, pools_grad, memory_grad, full, *work):
    weights = (wa, wb)
    normed = normed_ref[...]
    backs = field_back(4, scal[1], (2, 1, 1), fields, (kp, vp), (dq, dk, dv), near, far, pools, memory, pools_grad, memory_grad, work)
    count = normed.shape[0]
    total = jnp.zeros(normed.shape, F32)
    width = full.shape[2]
    columns = pl.ds(pl.multiple_of(scal[7] * width, LANES), width)
    linear = (0.25 * middle_grad[:, columns]).astype(BF)
    cell = cells()
    for slot in range(2):
        full[slot, 0:576, :] = tn(backs[slot], normed).astype(BF)
        full[slot, 576:864, :] = proj_grad[slot, 0:288, :]
        full[slot, 864:960, :] = residual_grad[slot, 0:96, :]
        full[slot, 960:1056, :] = proj_grad[slot, 288:384, :]
        full[slot, 1056:1152, :] = residual_grad[slot, 96:192, :]
        total = total + nn(backs[slot], weights[slot][...])
    cut(scal, full, (keep, one, two, three))
    high, low = split(nt(linear, residual[:, columns]))
    part_out[0:count, :] = (total + tn(cell, high) + tn(cell, low)).astype(BF)
    put_small(small, pools_grad, memory_grad)
    small[40:41, :] = 0.5 * gain_grad[:, :width]
    small[41:42, :] = 0.5 * gain_grad[:, width:]
    part_out[count:, :] = small[...].astype(BF)


def back_mlp_one(scal, part, other, x, gain, normed_ref, wa, wb, grad_out, part_out, gain_grad_ref, keep, one, two, three, full):
    weights = (wa, wb)
    grad, gain_grad = norm_back(part[: x.shape[0], :].astype(F32) + other[: x.shape[0], :].astype(F32), x[...], gain[...])
    grad_out[...] = grad
    gain_grad_ref[...] = gain_grad
    branch = grad.astype(BF)
    normed = normed_ref[...]
    total = jnp.zeros(part_out.shape, F32)
    whole = (part[x.shape[0] :, :].astype(F32) + other[x.shape[0] :, :].astype(F32)).astype(BF)
    size = normed.shape[1]
    for slot in range(2):
        up, down = weights[slot][:size, :], weights[slot][size:, :]
        value, slope = gelu_parts(nn(normed, up))
        up_low = (nt(branch, down) * slope).astype(BF)
        full[slot, 0:size, :] = tn(normed, up_low).astype(BF)
        full[slot, size : 2 * size, :] = tn(value.astype(BF), branch).astype(BF)
        full[slot, 2 * size : 2 * size + 64, :] = whole
        full[slot, 2 * size + 64 :, :] = jnp.zeros((64, size), BF)
        total = total + nt(up_low, up)
    part_out[...] = total.astype(BF)
    cut(scal, full, (keep, one, two, three))


def back_attend_one(scal, part, other, g, middle, gain, *refs):
    ins, outs = refs[0:10], refs[10:]
    grad, gain_grad = norm_back(part[...].astype(F32) + other[...].astype(F32), middle[...], gain[...])
    middle_grad = g[...] + grad
    outs[0][...] = middle_grad
    outs[1][...] = gain_grad
    attend_back(0, scal, *ins, middle_grad, *outs[2:9])


def back_front_one(scal, normed_ref, fields, kp, vp, dq, dk, dv, near, far, wa, wb, pools, memory, gain_two_grad, gain_three_grad, qkv_grad, part_out, small, pools_grad, memory_grad, *work):
    weights = (wa, wb)
    normed = normed_ref[...]
    backs = field_back(2, scal[1], (1, 2, 2), fields, (kp, vp), (dq, dk, dv), near, far, pools, memory, pools_grad, memory_grad, work)
    count = normed.shape[0]
    total = jnp.zeros(normed.shape, F32)
    for slot in range(2):
        qkv_grad[slot] = tn(backs[slot], normed).astype(BF)
        total = total + nn(backs[slot], weights[slot][: 3 * HD, :])
    part_out[0:count, :] = total.astype(BF)
    put_small(small, pools_grad, memory_grad)
    small[40:41, :] = 0.5 * gain_two_grad[...]
    small[41:42, :] = 0.5 * gain_three_grad[...]
    part_out[count:, :] = small[...].astype(BF)


def back_tokens(scal, part, other, x, gain, middle_grad, qkv_grad, proj_grad, table_one, table_two, keep_rows, send_rows, keep, one, two, three, full):
    grad, gain_grad = norm_back(part[: x.shape[0], :].astype(F32) + other[: x.shape[0], :].astype(F32), x[...].astype(F32), gain[...])
    rows = (middle_grad[...] + grad).astype(BF)
    turn = scal[1]
    keep_rows[...] = nn(half_rows(turn, SIDE * SIDE), rows).astype(BF)
    send_rows[...] = nn(half_rows(1 - turn, SIDE * SIDE), rows).astype(BF)
    line = iota((64, 1), 0)
    whole = jnp.where(
        line == 42, gain_grad, part[x.shape[0] :, :].astype(F32) + other[x.shape[0] :, :].astype(F32)
    ).astype(BF)
    for slot in range(2):
        full[slot, 0:288, :] = qkv_grad[slot]
        full[slot, 288:384, :] = proj_grad[slot]
        lines = jnp.concatenate([table_one[slot : slot + 1, :], table_two[2 * slot : 2 * slot + 2, :], jnp.zeros((13, LANES), F32)], axis=0)
        full[slot, 384:400, :] = jnp.concatenate([lines, jnp.zeros((16, 2 * LANES), F32)], axis=1).astype(BF)
        full[slot, 400:464, :] = whole
        full[slot, 464:512, :] = jnp.zeros((48, full.shape[2]), BF)
    cut(scal, full, (keep, one, two, three))


def scalars(pairs, other_pairs, videos, out):
    plane, core, head = lax.axis_index("plane"), lax.axis_index("core"), lax.axis_index("head")
    upper, turn = lax.div(head, 2), lax.rem(head, 2)
    clip = 4 * plane + 2 * turn + upper
    match = core == turn
    own = videos[clip]
    out[0] = jnp.where(match, 1, 0)
    out[1] = turn
    for j in range(2):
        before = clip - 1 - j
        there = (before >= 0) & (videos[jnp.maximum(before, 0)] == own)
        out[2 + j] = jnp.where(there, 1, 0)
        out[4 + j] = jnp.where(match, pairs[upper, j], other_pairs[upper, j])
    out[6] = jnp.where(upper == core, 1, 0)
    out[7] = core
    out[8] = lax.rem(plane, 2)
    out[9] = lax.rem(lax.div(plane, 2), 2)
    out[10] = head


def pack(tokens, grad_out, table_one, table_two, qkv_one, proj_one, rows, first):
    count, width = tokens.shape
    area = grad_out.shape[0]
    rows[0:count, :] = tokens[...]
    rows[count : count + area, :] = grad_out[:, :width]
    rows[count + area :, :] = grad_out[:, width:]
    lines = []
    for table in (table_one[0:1, :], table_two[0:1, :], table_two[1:2, :]):
        high = table.astype(BF).astype(F32)
        middle = (table - high).astype(BF).astype(F32)
        lines += [high, middle, table - high - middle]
    first[0 : 3 * HD, :] = qkv_one[...]
    first[3 * HD : 4 * HD, :] = proj_one[...]
    stacked = jnp.concatenate(lines + [jnp.zeros((7, lines[0].shape[1]), F32)], axis=0)
    first[4 * HD :, :] = jnp.concatenate([stacked, jnp.zeros((16, width - stacked.shape[1]), F32)], axis=1).astype(BF)


def join(one, two, first, second, third, out):
    out[0 : one.shape[0], :] = one[...]
    out[one.shape[0] :, :] = two[...]


SMEM = pl.BlockSpec(memory_space=pltpu.SMEM)


FAR = pl.BlockSpec(memory_space=pltpu.HBM)
NEAR = pl.BlockSpec(memory_space=pltpu.VMEM)


def moved(body, counts, left, early, late, *refs):
    ins_count, outs_count, work_count = counts
    ins, outs = list(refs[:ins_count]), refs[ins_count : ins_count + outs_count]
    spot = ins_count + outs_count
    saved = refs[spot : spot + len(early) + len(late)]
    spot += len(early) + len(late)
    work = refs[spot : spot + work_count]
    buffers, arrived = refs[spot + work_count : -1], refs[-1]
    brought = [pltpu.make_async_copy(ins[item], buffers[i], arrived.at[i]) for i, item in enumerate(left)]
    first = len(left)
    sent = [pltpu.make_async_copy(ins[item], saved[i], arrived.at[first + i]) for i, item in enumerate(early)]
    for copy in brought + sent:
        copy.start()
    for i, item in enumerate(left):
        brought[i].wait()
        ins[item] = buffers[i]
    body(*ins, *outs, *work)
    first += len(early)
    last = [
        pltpu.make_async_copy(outs[item], saved[len(early) + i], arrived.at[first + i]) for i, item in enumerate(late)
    ]
    for copy in last:
        copy.start()
    for copy in sent + last:
        copy.wait()


def kernel(body, name, outs, ins, work=(), left=(), early=(), late=(), raw=(), far_outs=(), limit=16, flops=2 * 10**8):
    if limit == 16 and (left or early or late):
        found = kernel(body, name, outs, ins, work, (), (), (), raw, far_outs)
        return (*found, *[list(ins)[item] for item in early], *[found[item] for item in late])
    ins = list(ins)
    in_specs = []
    for number, item in enumerate(ins):
        if number == 0 and item.dtype == jnp.int32:
            in_specs.append(SMEM)
        else:
            in_specs.append(FAR if number in left or number in raw else NEAR)
    results = [jax.ShapeDtypeStruct(shape, kind) for shape, kind in outs]
    extra = [jax.ShapeDtypeStruct(ins[item].shape, ins[item].dtype) for item in early] + [results[item] for item in late]
    size = sum(int(np.prod(item.shape)) * item.dtype.itemsize for item in [*ins, *results, *extra])
    work = list(work)
    count = len(work)
    if left or early or late:
        body = functools.partial(moved, body, (len(ins), len(results), count), tuple(left), tuple(early), tuple(late))
        work += [pltpu.VMEM(ins[number].shape, ins[number].dtype) for number in left]
        work.append(pltpu.SemaphoreType.DMA((len(left) + len(early) + len(late),)))
    return pl.pallas_call(
        body,
        out_shape=tuple(results + extra),
        in_specs=in_specs,
        out_specs=tuple([FAR if number in far_outs else NEAR for number in range(len(results))] + [FAR] * len(extra)),
        scratch_shapes=work,
        name=name,
        cost_estimate=pl.CostEstimate(flops=flops, bytes_accessed=size, transcendentals=0),
        compiler_params=pltpu.CompilerParams(vmem_limit_bytes=limit << 20),
    )(*ins)


def scratch(*rows):
    return [pltpu.VMEM((count, LANES), F32) for count in rows]


def field_work(heads):
    groups = 3 * heads // 2
    return [pltpu.VMEM((groups, PADDED, LANES), F32), pltpu.SemaphoreType.DMA((groups,))]


FRONT_WORK = (216, 800)
BACK_WORK = (216, 800, PADDED, 216, 400)


def after(values, events):
    return lax.optimization_barrier((values, events))


def swap(values):
    return lax.ppermute(values, "core", [(0, 1), (1, 0)])


def cross_route():
    route = []
    for core in range(2):
        low, other = 2 * core, 2 - 2 * core
        route += [(core * 4 + low + i, core * 4 + other + i) for i in range(2)]
    return route


def beside(values):
    return lax.ppermute(values, "head", [(z, z ^ 1) for z in range(4)])


def choose(scal, own, other, out):
    out[...] = pick(scal[6] == 1, own[...], other[...])


def choose_half(sizes, scal, own, other, out):
    start, put = 0, 0
    for size in sizes:
        half = size // 2
        spots = pl.ds(pl.multiple_of(start + half * scal[7], 16), half)
        out[put : put + half, :] = pick(scal[6] == 1, own[spots, :], other[spots, :])
        start, put = start + size, put + half


def chosen(scal, own, other):
    return kernel(choose, "choose_shard", [(own.shape, own.dtype)], [scal, own, other])[0]


def over(values, scal):
    return chosen(scal, values, lax.ppermute(values, ("core", "head"), cross_route()))


def spread(values, scal):
    one = over(values, scal)
    return one, beside(one)


def reverse(route):
    return [(end, start) for start, end in route]


def clip_routes(planes, distance):
    def place(clip):
        slot = clip % 4
        return (clip // 4) * 4 + 2 * (slot % 2) + slot // 2

    total = 4 * planes
    return [(place(clip), place(clip + distance)) for clip in range(total) if 0 <= clip + distance < total]


def half_routes():
    def place(core, a, b):
        return core * 4 + 2 * a + b

    one, two, three = [], [], []
    for a in range(2):
        for b in range(2):
            one += [(place(b, a, b), place(1 - b, a, b)), (place(1 - b, a, b), place(1 - b, a, 1 - b))]
            two += [(place(1 - b, a, b), place(b, a, 1 - b))]
            three += [(place(1 - b, a, b), place(b, a, 1 - b))]
    return one, two, three


def turn_by(values, distance):
    return lax.ppermute(values, "head", [(z, (z + distance) % 4) for z in range(4)])


def local(
    planes,
    tokens,
    grad_out,
    video_ids,
    offsets,
    gain_one,
    qkv_one,
    pools_one,
    memory_one,
    table_one,
    proj_one,
    gain_two,
    up_one,
    down_one,
    gain_three,
    qkv_two,
    residual_two,
    pools_two,
    memory_two,
    table_two,
    proj_two,
    gain_four,
    up_two,
    down_two,
):
    match = lax.axis_index("core") == lax.axis_index("head") % 2
    (scal,) = pl.pallas_call(
        scalars,
        out_shape=(jax.ShapeDtypeStruct((16,), jnp.int32),),
        in_specs=[SMEM] * 3,
        out_specs=(SMEM,),
        name="scalars",
    )(offsets, swap(offsets), video_ids)
    gains = [item.reshape(1, -1) for item in (gain_one, gain_two, gain_three, gain_four)]

    half = residual_two.shape[1] // 2
    qkv_one_t, qkv_two_t = qkv_one.T, qkv_two.T
    rows_in, first_bundle = kernel(
        pack,
        "pack",
        [((300, half), BF), ((400, half), BF)],
        [tokens, grad_out, table_one, table_two, qkv_one_t, proj_one],
        left=range(6),
        limit=56,
    )
    route_one, route_two, route_three = half_routes()
    axes = ("core", "head")
    first_over = over(first_bundle, scal)
    first_all = (first_over, beside(first_over))
    tok_one, tok_two = lax.ppermute(rows_in, axes, route_one), lax.ppermute(rows_in, axes, route_two)
    (mlp_bundle,) = kernel(
        join, "join", [((768, half), BF)], [up_one, down_one, first_over, tok_one, tok_two], left=(0, 1), limit=48
    )
    mlp_over = over(mlp_bundle, scal)

    width = qkv_one.shape[0]
    wide = residual_two.shape[1]
    n1, n2 = FR * SIDE * SIDE, FR * SIDE * SIDE // 4
    a1, a2 = n2 // FR, n1 // FR

    x1, _, g, fields1, qp1, kp1, vp1, passed1, *saved = kernel(
        front_one,
        "front_one",
        [
            ((n1, width), BF),
            ((n1, width), BF),
            ((2, n2, half), BF),
            ((3, PADDED, LANES), F32),
            ((2, n1, LANES), F32),
            ((2, n2, LANES), F32),
            ((2, n2, LANES), F32),
            ((2, a1, 2 * HD), BF),
        ],
        [scal, rows_in, tok_one, tok_two, gains[0], *first_all, pools_one, memory_one],
        scratch(*FRONT_WORK) + field_work(2),
        early=(5, 6),
        late=(0, 1, 2, 4, 5, 6),
        far_outs=(3,),
    )
    first_kept, (x1_kept, normed1, g_kept, qp1_kept, kp1_kept, vp1_kept) = saved[:2], saved[2:]
    places = ("plane", "head")
    near1 = lax.ppermute(passed1, places, clip_routes(planes, 1))
    far1 = lax.ppermute(passed1, places, clip_routes(planes, 2))
    (mlp_over, late_qkv), (x1,) = after((mlp_over, qkv_two_t), (x1,))
    mlp_all = (mlp_over, beside(mlp_over))
    qkv_two_all = spread(late_qkv, scal)
    attn1_ins = [*first_all, qp1, kp1, vp1, near1, far1, *first_all]
    _, part1, near1_kept, far1_kept, rows1 = kernel(
        functools.partial(attend, 0),
        "attend_one",
        [((2, n1, LANES), BF), ((n1, width), BF)],
        [scal, *attn1_ins],
        early=(6, 7),
        late=(0,),
    )
    middle1, _, part_mlp1, *mlp_kept, middle1_kept, mlp_normed1 = kernel(
        mlp_one,
        "mlp_one",
        [((n1, width), F32), ((n1, width), BF), ((n1, width), BF)],
        [scal, x1, part1, swap(part1), gains[1], *mlp_all],
        early=(5, 6),
        late=(0, 1),
    )
    late_proj, (part_mlp1,) = after(proj_two, (part_mlp1,))
    proj_two_all = spread(late_proj, scal)
    _, _, fields2, qp2, kp2, vp2, passed2, *saved = kernel(
        front_two,
        "front_two",
        [
            ((n1, width), F32),
            ((n1, width), BF),
            ((6, PADDED, LANES), F32),
            ((4, n2, LANES), F32),
            ((4, n1, LANES), F32),
            ((4, n1, LANES), F32),
            ((2, a2, 4 * HD), BF),
        ],
        [scal, middle1, part_mlp1, swap(part_mlp1), gains[2], *qkv_two_all, pools_two, memory_two],
        scratch(*FRONT_WORK) + field_work(4),
        early=(5, 6),
        late=(0, 1, 3, 4, 5),
        far_outs=(2,),
    )
    qkv_two_kept, (x2, normed2, qp2_kept, kp2_kept, vp2_kept) = saved[:2], saved[2:]
    (skip,) = kernel(skip_two, "skip_two", [((n2, wide), F32)], [normed2, residual_two])
    near2 = lax.ppermute(passed2, places, clip_routes(planes, 1))
    far2 = lax.ppermute(passed2, places, clip_routes(planes, 2))
    attn2_ins = [*first_kept, qp2, kp2, vp2, near2, far2, *proj_two_all]
    _, part2, near2_kept, far2_kept, *proj_two_kept, rows2 = kernel(
        functools.partial(attend, 1),
        "attend_two",
        [((4, n2, LANES), BF), ((n2, wide), BF)],
        [scal, *attn2_ins],
        left=(1, 2),
        early=(6, 7, 8, 9),
        late=(0,),
    )
    _, mlp_normed2, own_half, middle2 = kernel(
        middle_two,
        "middle_two",
        [((n2, wide), F32), ((n2, wide), BF), ((2, n2, half), BF)],
        [scal, skip, part2, swap(part2), gains[3], g_kept],
        left=(5,),
        late=(0,),
    )
    halves = [turn_by(own_half, d) for d in (1, 2, 3)]
    found = kernel(
        mlp_rows,
        "mlp_rows",
        [((832, half), BF)] * 2 + [((4, n2, half), BF)] * 2 + [((4, 2, n2, wide), BF)],
        [scal, mlp_normed2, g_kept, *halves, *(swap(item) for item in halves), up_two, down_two],
        [pltpu.VMEM((2, n2, wide), F32)],
    )
    wide_grads = kernel(mlp_sums, "mlp_sums", [((wide, half), BF)] * 2, found[2:5])
    sums = kernel(add_cores, "add_cores", [((2, n2, half), BF)] * 4, [found[0], swap(found[1])])
    sums = [sums[0]] + [turn_by(sums[d], -d) for d in (1, 2, 3)]
    def across(values, bit):
        return lax.ppermute(values, "plane", [(i, i ^ bit) for i in range(planes)])

    def peers(parts):
        return [parts[0]] + [across(parts[peer], peer) for peer in (1, 2, 3)]

    def add_wide(pair, bits):
        received = [across(item, bit) for item, bit in zip(pair, bits)]
        return kernel(add_both, "add_wide", [((wide, half), BF)] * 2, [pair[0], received[0], pair[1], received[1]])

    wide_sum = add_wide(wide_grads, (1, 2))
    (row_sum,) = kernel(sum_four, "sum_rows", [((2, n2, half), BF)], sums)
    row_sum, (wide_sum,) = after(row_sum, (wide_sum,))
    row_other = swap(row_sum)
    middle_grad2, gain_four_grad, dq2, dk2, dv2, d_near2, d_far2, table_two_grad = kernel(
        back_attend_two,
        "back_attend_two",
        [
            ((n2, wide), F32),
            ((1, wide), F32),
            ((4, n2, LANES), F32),
            ((4, n1, LANES), F32),
            ((4, n1, LANES), F32),
            ((2, a2, 4 * HD), BF),
            ((2, a2, 4 * HD), BF),
            ((4, LANES), F32),
        ],
        [
            scal, row_sum, row_other, g_kept, middle2, gains[3],
            *first_kept, qp2_kept, kp2_kept, vp2_kept, near2_kept, far2_kept, *proj_two_kept, rows2,
        ],
    )
    proj_two_grad, residual_grad, keep, send = kernel(
        back_rest_two,
        "back_rest_two",
        [((2, 4 * HD, width), BF), ((2, 192, half), BF), ((n2 // 2, wide), BF), ((n2 // 2, wide), BF)],
        [scal, row_sum, row_other, middle2, normed2, middle_grad2, rows2],
    )
    near_grad2 = lax.ppermute(d_near2, places, clip_routes(planes, -1))
    far_grad2 = lax.ppermute(d_far2, places, clip_routes(planes, -2))

    wide_sum = add_wide(wide_sum, (2, 1))
    (near_grad2, far_grad2), (wide_sum,) = after((near_grad2, far_grad2), (wide_sum,))
    part_back2, *sends2, _, _, _ = kernel(
        back_front_two,
        "back_front_two",
        [
            ((n1 + 64, width), BF),
            *[((2, 288, width), BF)] * 4,
            ((64, width), F32),
            ((3, 32, LANES), F32),
            ((2, FR, LANES), F32),
        ],
        [
            scal, middle_grad2, normed2, fields2, kp2_kept, vp2_kept, dq2, dk2, dv2, near_grad2, far_grad2,
            *qkv_two_kept, residual_two, pools_two, memory_two, proj_two_grad, residual_grad, gain_four_grad,
        ],
        [pltpu.VMEM((2, 1152, width), BF)] + scratch(*BACK_WORK) + field_work(4),
        [2, 4, 5, 11, 12, 13],
        raw=[3],
    )
    received2 = peers(sends2)
    grad1, part_mlp_back, gain_three_grad, *sends_mlp = kernel(
        back_mlp_one,
        "back_mlp_one",
        [((n1, width), F32), ((n1, width), BF), ((1, width), F32)] + [((2, 224, width), BF)] * 4,
        [scal, part_back2, swap(part_back2), x2, gains[2], mlp_normed1, *mlp_kept],
        [pltpu.VMEM((2, 896, width), BF)],
        [3, 5, 6, 7],
    )
    middle_grad1, gain_two_grad, dq1, dk1, dv1, d_near1, d_far1, proj_one_grad, table_one_grad = kernel(
        back_attend_one,
        "back_attend_one",
        [
            ((n1, width), F32),
            ((1, width), F32),
            ((2, n1, LANES), F32),
            ((2, n2, LANES), F32),
            ((2, n2, LANES), F32),
            ((2, a1, 2 * HD), BF),
            ((2, a1, 2 * HD), BF),
            ((2, HD, width), BF),
            ((2, LANES), F32),
        ],
        [
            scal, part_mlp_back, swap(part_mlp_back), grad1, middle1_kept, gains[1],
            *first_kept, qp1_kept, kp1_kept, vp1_kept, near1_kept, far1_kept, *first_kept, rows1,
        ],
        left=[4, *range(6, 16)],
    )
    near_grad1 = lax.ppermute(d_near1, places, clip_routes(planes, -1))
    far_grad1 = lax.ppermute(d_far1, places, clip_routes(planes, -2))
    bit = 4
    while bit < planes:
        wide_sum = add_wide(wide_sum, (bit, bit))
        bit *= 2
    received_mlp = peers(sends_mlp)
    rows_received = lax.ppermute(send, axes, route_three)
    (near_grad1, far_grad1), (wide_sum, received2, rows_received) = after(
        (near_grad1, far_grad1), (wide_sum, received2, rows_received)
    )
    qkv_one_grad, part_back1, _, _, _ = kernel(
        back_front_one,
        "back_front_one",
        [((2, 3 * HD, width), BF), ((n1 + 64, width), BF), ((64, width), F32), ((3, 32, LANES), F32), ((2, FR, LANES), F32)],
        [
            scal, normed1, fields1, kp1_kept, vp1_kept, dq1, dk1, dv1, near_grad1, far_grad1,
            *first_kept, pools_one, memory_one, gain_two_grad, gain_three_grad,
        ],
        scratch(*BACK_WORK) + field_work(2),
        [1, 3, 4, 10, 11],
        raw=[2],
    )
    part_back1, (received_mlp,) = after(part_back1, (received_mlp,))
    tok_keep, tok_send, *sends1 = kernel(
        back_tokens,
        "back_tokens",
        [((n1 // 2, width), BF), ((n1 // 2, width), BF)] + [((2, 128, width), BF)] * 4,
        [
            scal, part_back1, swap(part_back1), x1_kept, gains[0], middle_grad1, qkv_one_grad, proj_one_grad,
            table_one_grad, table_two_grad,
        ],
        [pltpu.VMEM((2, 512, width), BF)],
        [3],
    )
    tok_received = lax.ppermute(tok_send, axes, route_three)

    def combine(body, label, rows, ins, count=1):
        return kernel(body, label, [((rows, width), BF)] * count, ins)

    back_route = reverse(cross_route())
    received1 = peers(sends1)
    rows_two, rows_mlp, rows_one = 288, 224, 128
    one2, two2 = combine(sum_planes, "sum_planes_two", rows_two + rows_mlp, received2 + received_mlp, 2)
    beside2 = beside(two2)
    up_two_sum, down_two_sum = kernel(
        finish_wide, "finish_wide", [((wide, wide), F32), ((wide, wide), F32)], [scal, wide_sum[0], swap(wide_sum[0]), wide_sum[1], swap(wide_sum[1])]
    )
    received1, (up_two_sum, down_two_sum) = after(received1, (up_two_sum, down_two_sum))
    one1, two1 = combine(sum_planes, "sum_planes_one", rows_one, received1, 2)
    beside1 = beside(two1)
    (beside2,), (one1, tok_received) = after((beside2,), (one1, tok_received))
    tokens_grad = jnp.where(match, tok_keep, tok_received)
    (total2,) = combine(add_two, "add_pair_two", rows_two + rows_mlp, [one2, beside2])
    cross2 = lax.ppermute(total2, axes, back_route)
    (beside1,), (total2,) = after((beside1,), (total2,))
    (total1,) = combine(add_two, "add_pair_one", rows_one, [one1, beside1])
    cross1 = lax.ppermute(total1, axes, back_route)
    (cross2,), (cross1,) = after((cross2,), (cross1,))
    (total2,) = combine(add_two, "add_cross_two", rows_two + rows_mlp, [total2, cross2])
    bit = 4
    while bit < planes:
        (total2,) = combine(add_two, "add_planes_two", rows_two + rows_mlp, [total2, across(total2, bit)])
        bit *= 2

    def halves_of(total, sizes):
        body = functools.partial(choose_half, sizes)
        return combine(body, "choose_half", sum(sizes) // 2, [scal, total, swap(total)])

    half2 = halves_of(total2, (rows_two, rows_mlp))
    (total1,) = combine(add_two, "add_cross_one", rows_one, [total1, cross1])
    bit = 4
    while bit < planes:
        (total1,) = combine(add_two, "add_planes_one", rows_one, [total1, across(total1, bit)])
        bit *= 2
    parts2 = peers(list(half2) * 4)
    parts1 = peers(halves_of(total1, (rows_one,)) * 4)
    parts2, parts1 = after(parts2, parts1)
    (piece,) = kernel(take_piece, "take_piece", [((96, width), BF)], [scal, *parts2])
    small_shapes = [(pools_one.shape, F32), (memory_one.shape, F32)]
    qkv_two_sum, proj_two_sum, up_one_sum, down_one_sum, pools_two_sum, memory_two_sum, gain_four_sum = kernel(
        finish_two,
        "finish_two",
        [(qkv_two_t.shape, F32), (proj_two.shape, F32), (up_one.shape, F32), (down_one.shape, F32)]
        + small_shapes
        + [((wide,), F32)],
        [scal, *parts2, *(swap(part) for part in parts2)],
        [pltpu.VMEM((1152, width), F32), pltpu.VMEM((896, width), F32)],
    )
    (qkv_one_sum, proj_one_sum, table_one_sum, table_two_sum, pools_one_sum, memory_one_sum, *gain_sums) = kernel(
        finish_one,
        "finish_one",
        [(qkv_one_t.shape, F32), (proj_one.shape, F32), (table_one.shape, F32), (table_two.shape, F32)]
        + small_shapes
        + [((width,), F32)] * 3,
        [scal, *parts1, *(swap(part) for part in parts1)],
        [pltpu.VMEM((512, width), F32)],
    )
    others = [lax.ppermute(piece, "head", [(z, z ^ bit) for z in range(4)]) for bit in (1, 2, 3)]
    blocks_out, tokens_out = jnp.where(match, keep, rows_received), tokens_grad
    others, (gain_four_sum, first_gain, blocks_out, tokens_out) = after(
        others, (gain_four_sum, gain_sums[0], blocks_out, tokens_out)
    )
    (pieces,) = kernel(stack_four, "stack_pieces", [((4, 96, width), BF)], [scal, piece, *others])
    (residual_sum,) = kernel(
        finish_residual, "finish_residual", [(residual_two.shape, F32)], [scal, pieces, swap(pieces)]
    )

    return (
        blocks_out,
        tokens_out,
        first_gain,
        qkv_one_sum.T,
        pools_one_sum,
        memory_one_sum,
        table_one_sum,
        proj_one_sum,
        gain_sums[1],
        up_one_sum,
        down_one_sum,
        gain_sums[2],
        qkv_two_sum.T,
        residual_sum,
        pools_two_sum,
        memory_two_sum,
        table_two_sum,
        proj_two_sum,
        gain_four_sum,
        up_two_sum,
        down_two_sum,
    )


def solution(mesh):
    planes = mesh.shape["dp"] // 2
    fine = Mesh(mesh.devices.reshape(planes, 2, mesh.shape["head"]), ("plane", "core", "head"))
    dp = ("plane", "core")
    rows = P(("plane", "core", "head"), None)
    columns, lines, free = P(None, "head"), P("head", None), P()
    in_specs = (
        rows, rows, free, P(dp, None),
        free, columns, free, free, lines, lines, free, columns, lines,
        free, columns, free, free, free, lines, lines, free, columns, lines,
    )
    out_specs = (
        rows, rows,
        free, columns, free, free, lines, lines, free, columns, lines,
        free, columns, free, free, free, lines, lines, free, columns, lines,
    )
    return jax.shard_map(
        functools.partial(local, planes), mesh=fine, in_specs=in_specs, out_specs=out_specs, check_vma=False
    )
```

```python
import functools

import jax
import jax.numpy as jnp
import numpy as np
from jax import lax
from jax.experimental import pallas as pl
from jax.experimental.pallas import tpu as pltpu
from jax.sharding import Mesh, PartitionSpec as P

HD = 96
FR = 4
SIDE = 10
LANES = 128
GRID = SIDE + 2
SLAB = GRID * 2 * FR
PADDED = GRID * SLAB
EPSILON = 1e-06
NEGATIVE = -1e30
SCALE = HD**-0.5
GELU_A = float(np.sqrt(2.0 / np.pi))
GELU_B = 0.044715

BF = jnp.bfloat16
F32 = jnp.float32


def nn(a, b):
    return lax.dot_general(a, b, (((1,), (0,)), ((), ())), preferred_element_type=F32)


def nt(a, b):
    return lax.dot_general(a, b, (((1,), (1,)), ((), ())), preferred_element_type=F32)


def tn(a, b):
    return lax.dot_general(a, b, (((0,), (0,)), ((), ())), preferred_element_type=F32)


def iota(shape, dim):
    return lax.broadcasted_iota(jnp.int32, shape, dim)


def widen(values):
    fill = jnp.zeros((values.shape[0], LANES - values.shape[1]), values.dtype)
    return jnp.concatenate([values, fill], axis=1)


def split(values):
    high = values.astype(BF)
    return high, (values - high.astype(F32)).astype(BF)


def norm_parts(values):
    centered = values - jnp.mean(values, axis=-1, keepdims=True)
    variance = jnp.mean(centered * centered, axis=-1, keepdims=True)
    scale = lax.rsqrt(variance + EPSILON)
    return centered * scale, scale


def norm_back(grad, values, gain):
    unit, scale = norm_parts(values)
    scaled = grad * gain
    mean_one = jnp.mean(scaled, axis=-1, keepdims=True)
    mean_two = jnp.mean(scaled * unit, axis=-1, keepdims=True)
    gain_grad = jnp.sum(grad * unit, axis=0, keepdims=True)
    return scale * (scaled - mean_one - unit * mean_two), gain_grad


def gelu_parts(values):
    square = values * values
    bent = jnp.tanh(GELU_A * values * (1.0 + GELU_B * square))
    half = 0.5 * (1.0 + bent)
    slope = half + 0.5 * values * (1.0 - bent * bent) * GELU_A * (1.0 + 3.0 * GELU_B * square)
    return values * half, slope


def pick(flag, one, two):
    return jnp.where(flag, one, two)


def token_rows(half):
    shape = (FR * SIDE * SIDE, 2 * SIDE * SIDE)
    rows, cols = iota(shape, 0), iota(shape, 1)
    frame, place = (rows & (FR - 1)) - 2 * half, rows >> 2
    match = (cols == SIDE * SIDE * frame + place) & (frame >= 0) & (frame < 2)
    return jnp.where(match, 1.0, 0.0).astype(BF)


def half_rows(half, area):
    shape = (2 * area, FR * area)
    rows, cols = iota(shape, 0), iota(shape, 1)
    upper = jnp.where(rows >= area, 1, 0)
    return jnp.where(cols == FR * (rows - area * upper) + 2 * half + upper, 1.0, 0.0).astype(BF)


def cells():
    small = SIDE // 2
    count = FR * small * small
    rows, cols = iota((count, 1), 0), iota((1, FR * SIDE * SIDE), 1)
    place, spot = rows >> 2, cols >> 2
    row_key = FR * place + (rows & (FR - 1))
    line, column = lax.div(spot, 2 * SIDE), lax.div(lax.rem(spot, SIDE), 2)
    col_key = FR * (small * line + column) + (cols & (FR - 1))
    return jnp.where(row_key == col_key, 1.0, 0.0).astype(BF)


def fill_weights(wide, pools, field, flip):
    for tap in range(27):
        source = 26 - tap if flip else tap
        line = widen(pools[field, source : source + 1, :])
        wide[8 * tap : 8 * tap + 8, :] = jnp.broadcast_to(line, (8, LANES))


def frame_shifts():
    lane = iota((8, LANES), 0)
    early, late = lane >= 2, lane < 6
    return (
        lambda values: jnp.where(early, pltpu.roll(values, 2, 0), 0.0),
        lambda values: jnp.where(late, pltpu.roll(values, 6, 0), 0.0),
    )


def load_row(ref, index):
    return ref[pl.ds(pl.multiple_of(SLAB * index, SLAB), SLAB), :].reshape(GRID, 8, LANES)


def tap_of(wide, a, b, e):
    spot = 8 * (9 * a + 3 * b + e)
    return wide[spot : spot + 8, :]


def conv_rows(source, wide, result, stride):
    count = SIDE // stride
    before, after = frame_shifts()

    def one_row(i, carry):
        sums = [[None] * count for _ in range(3)]
        for b in range(3):
            line = load_row(source, stride * i + b)
            for a in range(3):
                for e in range(3):
                    weight = tap_of(wide, a, b, e)
                    for j in range(count):
                        term = weight * line[stride * j + e]
                        sums[a][j] = term if sums[a][j] is None else sums[a][j] + term
        for j in range(count):
            total = sums[1][j] + before(sums[0][j]) + after(sums[2][j])
            result[pl.ds(pl.multiple_of(8 * count * i + 8 * j, 8), 8), :] = total
        return carry

    lax.fori_loop(0, count, one_row, 0)


def conv_back_two(source, wide, result):
    count = SIDE // 2
    before, after = frame_shifts()

    def one_row(m, carry):
        now, later = load_row(source, m + 1), load_row(source, m + 2)
        totals = [None] * (2 * SIDE)
        for a, shift in ((1, None), (0, after), (2, before)):
            sums = [None] * (2 * SIDE)
            for start, b, line in ((0, 1, now), (SIDE, 0, later), (SIDE, 2, now)):
                taps = [tap_of(wide, a, b, e) for e in range(3)]
                for n in range(count):
                    even = taps[1] * line[n + 1]
                    odd = taps[0] * line[n + 2] + taps[2] * line[n + 1]
                    for spot, term in ((start + 2 * n, even), (start + 2 * n + 1, odd)):
                        sums[spot] = term if sums[spot] is None else sums[spot] + term
            for spot in range(2 * SIDE):
                totals[spot] = sums[spot] if shift is None else totals[spot] + shift(sums[spot])
        for spot in range(2 * SIDE):
            result[pl.ds(pl.multiple_of(16 * SIDE * m + 8 * spot, 8), 8), :] = totals[spot]
        return carry

    lax.fori_loop(0, count, one_row, 0)


def conv_weight(source, grads, totals, stride):
    count = SIDE // stride
    before, after = frame_shifts()
    totals[...] = jnp.zeros((27 * 8, LANES), F32)

    def one_row(i, carry):
        line = load_row(grads, i + 1)
        own = [line[j + 1] for j in range(count)]
        cotangents = ([after(item) for item in own], own, [before(item) for item in own])
        for b in range(3):
            line = load_row(source, stride * i + b)
            for e in range(3):
                for a in range(3):
                    spot = 8 * (9 * a + 3 * b + e)
                    terms = [line[stride * j + e] * cotangents[a][j] for j in range(count)]
                    terms.append(totals[spot : spot + 8, :])
                    while len(terms) > 1:
                        terms = [
                            terms[k] + terms[k + 1] if k + 1 < len(terms) else terms[k]
                            for k in range(0, len(terms), 2)
                        ]
                    totals[spot : spot + 8, :] = terms[0]
        return carry

    lax.fori_loop(0, count, one_row, 0)


def weights_of_rows(totals):
    return jnp.sum(totals[...].reshape(27, 8, LANES), axis=1)


def put_rows(target, values, head, count):
    for i in range(count):
        start = ((i + 1) * GRID + 1) * 8 + head
        target[pl.ds(start, FR * count, stride=2), :] = values[FR * count * i : FR * count * (i + 1), :]


def pairs_of(heads):
    return [((0, 0), (1, 0))] if heads == 2 else [((0, 0), (0, 1)), ((1, 0), (1, 1))]


def pack_heads(lines, turn):
    half = len(lines) // 2
    sides = [jnp.concatenate([line[:, :HD] for line in lines[half * i : half * (i + 1)]], axis=1) for i in range(2)]
    flag = turn == 1
    return jnp.concatenate([pick(flag, sides[1], sides[0]), pick(flag, sides[0], sides[1])], axis=1)


def unpack_heads(values, turn):
    heads = values.shape[1] // HD
    lines = [values[:, HD * head : HD * (head + 1)] for head in range(heads)]
    flag, half = turn == 1, heads // 2
    return [widen(pick(flag, lines[(head + half) % heads], lines[head])) for head in range(heads)]


def front_body(heads, turn, strides, normed, weights, pools, memory, fields, pooled, passed, work):
    wide, result, held, sent = work
    copies = []
    lines = [nt(normed, weights[s][: 3 * HD * heads // 2, :]) for s in range(2)]
    for field in range(3):
        fill_weights(wide, pools, field, False)
        stride = strides[field]
        count = SIDE // stride
        for number, pair in enumerate(pairs_of(heads)):
            spot = field * (heads // 2) + number
            group = held.at[spot]
            group[...] = jnp.zeros((PADDED, LANES), F32)
            for head, (slot, place) in enumerate(pair):
                start = HD * (3 * place + field)
                put_rows(group, widen(lines[slot][:, start : start + HD]), head, SIDE)
            copies.append(pltpu.make_async_copy(group, fields.at[spot], sent.at[spot]))
            copies[-1].start()
            conv_rows(group, wide, result, stride)
            for head in range(2):
                pooled[field][2 * number + head] = result[pl.ds(head, FR * count * count, stride=2), :]
    area = (SIDE // strides[1]) ** 2
    for which in range(2):
        lines = []
        for head in range(heads):
            total = jnp.zeros((area, LANES), F32)
            for t in range(FR):
                line = widen(memory[which, t : t + 1, :])
                total = total + line * pooled[1 + which][head, pl.ds(t, area, stride=FR), :]
            lines.append(total)
        passed[which] = pack_heads(lines, turn).astype(BF)
    for copy in copies:
        copy.wait()


def front_one(scal, own, first, second, gain, wa, wb, pools, memory, x_out, normed_out, g_out, fields, qp, kp, vp, passed, *work):
    match, turn = scal[0] == 1, scal[1] == 1
    near = pick(match, own[...], first[...])
    far = pick(match, first[...], second[...])
    low, high = pick(turn, far, near), pick(turn, near, far)
    count, area = 2 * SIDE * SIDE, (SIDE // 2) ** 2
    rows = nn(token_rows(0), low[:count]) + nn(token_rows(1), high[:count])
    x_out[...] = rows.astype(BF)
    turns = [half_rows(half, area) for half in range(2)]
    for column in range(2):
        spots = slice(count + 2 * area * column, count + 2 * area * (column + 1))
        g_out[column] = (tn(turns[0], low[spots]) + tn(turns[1], high[spots])).astype(BF)
    normed = (norm_parts(rows)[0] * gain[...]).astype(BF)
    normed_out[...] = normed
    front_body(2, scal[1], (1, 2, 2), normed, (wa, wb), pools, memory, fields, (qp, kp, vp), passed, work)


def front_two(scal, middle, part, other, gain, wa, wb, pools, memory, x_out, normed_out, fields, qp, kp, vp, passed, *work):
    rows = middle[...] + (part[...].astype(F32) + other[...].astype(F32))
    x_out[...] = rows
    normed = (norm_parts(rows)[0] * gain[...]).astype(BF)
    normed_out[...] = normed
    front_body(4, scal[1], (2, 1, 1), normed, (wa, wb), pools, memory, fields, (qp, kp, vp), passed, work)


def skip_two(normed, residual, skip):
    high, low = split(nn(cells(), normed[...]))
    skip[...] = 0.25 * (nn(high, residual[...]) + nn(low, residual[...]))


def table_of(shards, block, slot, place):
    line = shards[slot][4 * HD : 4 * HD + 16, :].astype(F32)
    row = 3 * (place if block == 0 else 1 + place)
    return line[row : row + 1, :] + line[row + 1 : row + 2, :] + line[row + 2 : row + 3, :]


def own_bias(bins, table):
    values = jnp.zeros(bins.shape, F32)
    for number in range(2 * FR - 1):
        values = jnp.where(bins == number, table[:, number : number + 1], values)
    return values


def far_bias(table, offset):
    lanes = iota(table.shape, 1)
    return jnp.sum(jnp.where(lanes == offset + 2 * FR - 1, table, 0.0), axis=1, keepdims=True)


def probs_of(scal, bins, table, query, keys):
    tile = own_bias(bins, table)
    rows = query.shape[0]
    bias = jnp.concatenate([tile] * ((rows + 7) // 8), axis=0)[:rows]
    parts = [nt(query, keys[0]) * SCALE + bias]
    for j in range(2):
        raw = nt(query, keys[1 + j]) * SCALE + far_bias(table, scal[4 + j])
        parts.append(jnp.where(scal[2 + j] == 1, raw, NEGATIVE))
    top = functools.reduce(jnp.maximum, [jnp.max(part, axis=1, keepdims=True) for part in parts])
    parts = [jnp.exp(part - top) for part in parts]
    total = sum(jnp.sum(part, axis=1, keepdims=True) for part in parts)
    return [part / total for part in parts]


def heads_of(heads, block):
    return [(slot, place) for slot in range(2) for place in range(heads // 2)]


def attend(block, scal, ta, tb, qp, kp, vp, near, far, wa, wb, rows_out, part_out):
    heads = qp.shape[0]
    shards, weights = (ta, tb), (wa, wb)
    base = 0 if block else 3 * HD
    shape = (8, kp.shape[1])
    bins = (iota(shape, 0) & (FR - 1)) - (iota(shape, 1) & (FR - 1)) + FR - 1
    total = jnp.zeros(part_out.shape, F32)
    nears, fars = ([unpack_heads(item[which], scal[1]) for which in range(2)] for item in (near, far))
    for head, (slot, place) in enumerate(heads_of(heads, block)):
        table = table_of(shards, block, slot, place)
        pool = qp[head]
        keys = (kp[head].astype(BF), nears[0][head], fars[0][head])
        values = (vp[head].astype(BF), nears[1][head], fars[1][head])
        probs = probs_of(scal, bins, table, pool.astype(BF), keys)
        mixture = sum(nn(p.astype(BF), v) for p, v in zip(probs, values))
        line = (mixture + pool).astype(BF)
        rows_out[head] = line
        total = total + nn(line[:, :HD], weights[slot][base + HD * place : base + HD * place + HD, :])
    part_out[...] = total.astype(BF)


def attend_back(block, scal, ta, tb, qp, kp, vp, near, far, wa, wb, rows, middle_grad, dq, dk, dv, d_near, d_far, proj_grad, table_grad):
    heads = qp.shape[0]
    shards, weights = (ta, tb), (wa, wb)
    base = 0 if block else 3 * HD
    shape = (8, kp.shape[1])
    bins = (iota(shape, 0) & (FR - 1)) - (iota(shape, 1) & (FR - 1)) + FR - 1
    branch = middle_grad.astype(BF)
    lanes = iota((1, LANES), 1)
    table_lines = []
    nears, fars = ([unpack_heads(item[which], scal[1]) for which in range(2)] for item in (near, far))
    near_lines, far_lines = ([], []), ([], [])
    for head, (slot, place) in enumerate(heads_of(heads, block)):
        table = table_of(shards, block, slot, place)
        weight = weights[slot][base + HD * place : base + HD * place + HD, :]
        if proj_grad is not None:
            proj_grad[slot, HD * place : HD * place + HD, :] = tn(rows[head][:, :HD], branch).astype(BF)
        grad = widen(nt(branch, weight).astype(BF))
        query = qp[head].astype(BF)
        keys = (kp[head].astype(BF), nears[0][head], fars[0][head])
        values = (vp[head].astype(BF), nears[1][head], fars[1][head])
        probs = probs_of(scal, bins, table, query, keys)
        grad_probs = [nt(grad, v) for v in values]
        inner = sum(jnp.sum(p * d, axis=1, keepdims=True) for p, d in zip(probs, grad_probs))
        low = [(p * (d - inner)).astype(BF) for p, d in zip(probs, grad_probs)]
        dq[head] = sum(nn(s, k) for s, k in zip(low, keys)) * SCALE + grad.astype(F32)
        key_grads = [tn(s, query) * SCALE for s in low]
        value_grads = [tn(p.astype(BF), grad) for p in probs]
        dk[head], dv[head] = key_grads[0], value_grads[0]
        for which, grads in enumerate((key_grads, value_grads)):
            near_lines[which].append(grads[1])
            far_lines[which].append(grads[2])
        score = low[0].astype(F32)
        count = score.shape[0]
        if count % 8:
            score = jnp.concatenate([score, jnp.zeros((8 - count % 8, score.shape[1]), F32)], axis=0)
        score = jnp.sum(score.reshape(-1, 8, score.shape[1]), axis=0)
        line = jnp.zeros((1, LANES), F32)
        for number in range(2 * FR - 1):
            column = jnp.sum(jnp.where(bins == number, score, 0.0), axis=0, keepdims=True)
            line = line + jnp.where(lanes == number, jnp.sum(column, axis=1, keepdims=True), 0.0)
        for j in range(2):
            column = jnp.sum(low[1 + j].astype(F32), axis=0, keepdims=True)
            value = jnp.sum(column, axis=1, keepdims=True)
            line = line + jnp.where(lanes == scal[4 + j] + 2 * FR - 1, value, 0.0)
        table_lines.append(line)
    for which in range(2):
        d_near[which] = pack_heads(near_lines[which], scal[1]).astype(BF)
        d_far[which] = pack_heads(far_lines[which], scal[1]).astype(BF)
    for head, line in enumerate(table_lines):
        table_grad[head : head + 1, :] = line


def field_back(heads, turn, strides, fields, pooled, grads, near, far, pools, memory, pools_grad, memory_grad, work):
    wide, result, grid, totals, rows, held, arrived = work
    half = heads // 2
    copies = [pltpu.make_async_copy(fields.at[i], held.at[i], arrived.at[i]) for i in range(3 * half)]
    for copy in copies:
        copy.start()
    back = {}
    area = (SIDE // strides[1]) ** 2
    for field in range(3):
        stride = strides[field]
        count = SIDE // stride
        fill_weights(wide, pools, field, stride == 1)
        weight_sum = jnp.zeros((27, LANES), F32)
        memory_lines = [jnp.zeros((1, LANES), F32) for _ in range(FR)]
        if field:
            passed = unpack_heads(near[field - 1].astype(F32) + far[field - 1].astype(F32), turn)
        for number, pair in enumerate(pairs_of(heads)):
            grid[...] = jnp.zeros((PADDED, LANES), F32)
            for place in range(2):
                head = 2 * number + place
                if field == 0:
                    put_rows(grid, grads[0][head], place, count)
                else:
                    cotangent = passed[head]
                    for t in range(FR):
                        spot = pl.ds(t, area, stride=FR)
                        line = widen(memory[field - 1, t : t + 1, :])
                        rows[spot, :] = grads[field][head, spot, :] + line * cotangent
                        product = pooled[field - 1][head, spot, :] * cotangent
                        memory_lines[t] = memory_lines[t] + jnp.sum(product, axis=0, keepdims=True)
                    put_rows(grid, rows[0 : FR * area, :], place, count)
            group = held.at[field * half + number]
            copies[field * half + number].wait()
            conv_weight(group, grid, totals, stride)
            weight_sum = weight_sum + weights_of_rows(totals)
            if stride == 1:
                conv_rows(grid, wide, result, 1)
            else:
                conv_back_two(grid, wide, result)
            for place, key in enumerate(pair):
                back[key + (field,)] = result[pl.ds(place, FR * SIDE * SIDE, stride=2), :][:, :HD]
        pools_grad[field, 0:27, :] = weight_sum
        if field:
            for t in range(FR):
                memory_grad[field - 1, t : t + 1, :] = memory_lines[t]
    outs = []
    for slot in range(2):
        columns = [back[(slot, place, field)] for place in range(half) for field in range(3)]
        outs.append(jnp.concatenate(columns, axis=1).astype(BF))
    return outs


def mlp_one(scal, x, part, other, gain, wa, wb, middle_out, normed_out, part_out):
    weights = (wa, wb)
    middle = x[...].astype(F32) + (part[...].astype(F32) + other[...].astype(F32))
    middle_out[...] = middle
    normed = (norm_parts(middle)[0] * gain[...]).astype(BF)
    normed_out[...] = normed
    size = normed.shape[1]
    total = jnp.zeros(part_out.shape, F32)
    for slot in range(2):
        hidden = gelu_parts(nn(normed, weights[slot][:size, :]))[0].astype(BF)
        total = total + nn(hidden, weights[slot][size:, :])
    part_out[...] = total.astype(BF)


def middle_two(scal, skip, part, other, gain, g, middle_out, normed_out, half_out):
    middle = skip[...] + (part[...].astype(F32) + other[...].astype(F32))
    middle_out[...] = middle
    normed_out[...] = (norm_parts(middle)[0] * gain[...]).astype(BF)
    width = half_out.shape[2]
    half_out[0] = normed_out[:, pl.ds(pl.multiple_of(scal[7] * width, LANES), width)]
    half_out[1] = g[scal[7]]


def mlp_rows(scal, own, own_grad, *refs):
    halves, others = refs[0:3], refs[3:6]
    up_ref, down_ref = refs[6:8]
    keep, give, hidden_out, low_out, board, lines = refs[8:14]
    width = up_ref.shape[1] // 2
    core = scal[7]
    start = pl.multiple_of(core * width, LANES)
    rest = pl.multiple_of((1 - core) * width, LANES)
    up, down = up_ref[:, pl.ds(start, width)], down_ref[pl.ds(start, width), :]
    board[0, 0] = own[...]
    for column in range(2):
        board[0, 1, :, width * column : width * (column + 1)] = own_grad[column]
    for d in range(3):
        for which in range(2):
            board[d + 1, which, :, pl.ds(start, width)] = halves[d][which]
            board[d + 1, which, :, pl.ds(rest, width)] = others[d][which]
    for d in range(4):
        rows, grad = board[d, 0], board[d, 1]
        value, slope = gelu_parts(nn(rows, up))
        hidden = value.astype(BF)
        up_low = (nt(grad, down) * slope).astype(BF)
        hidden_out[d], low_out[d] = hidden, up_low
        lines[0] = nn(hidden, down)
        lines[1] = nt(up_low, up)
        for which in range(2):
            spots = slice(104 * (2 * d + which), 104 * (2 * d + which) + rows.shape[0])
            keep[spots, :] = lines[which, :, pl.ds(start, width)].astype(BF)
            give[spots, :] = lines[which, :, pl.ds(rest, width)].astype(BF)


def mlp_sums(hidden, low, board, packed, packed_down):
    up_total = sum(tn(board[d, 0], low[d]) for d in range(4))
    down_total = sum(tn(hidden[d], board[d, 1]) for d in range(4))
    width = packed.shape[1]
    packed[...] = up_total.astype(BF)
    packed_down[0:width, :] = down_total[:, :width].astype(BF)
    packed_down[width:, :] = down_total[:, width:].astype(BF)


def quarter_of(scal, peer):
    one = 1 - scal[8] if peer % 2 else scal[8]
    two = 1 - scal[9] if peer // 2 else scal[9]
    return one + 2 * two


def cut(scal, full, parts):
    rows = parts[0].shape[1]
    for peer in range(4):
        spots = pl.ds(pl.multiple_of(quarter_of(scal, peer) * rows, 16), rows)
        for slot in range(2):
            parts[peer][slot] = full[slot, spots, :]


def sum_planes(*refs):
    one, two = refs[-2:]
    start = 0
    for number in range(len(refs) // 4):
        parts = refs[4 * number : 4 * number + 4]
        rows = parts[0].shape[1]
        for slot, out in ((0, one), (1, two)):
            total = (parts[0][slot].astype(F32) + parts[1][slot].astype(F32)) + (
                parts[2][slot].astype(F32) + parts[3][slot].astype(F32)
            )
            out[start : start + rows, :] = total.astype(BF)
        start += rows


def gather_parts(scal, parts, start, full):
    rows = full.shape[0] // 8
    for number, part in enumerate(parts):
        core = scal[7] if number < 4 else 1 - scal[7]
        spots = pl.ds(pl.multiple_of((2 * quarter_of(scal, number % 4) + core) * rows, 16), rows)
        full[spots, :] = part[start : start + rows, :].astype(F32)


def put_totals(full, start, pools, memory):
    for field in range(3):
        pools[field] = full[start : start + 27, LANES * field : LANES * field + HD]
    for which in range(2):
        memory[which] = full[start + 32 : start + 32 + FR, LANES * which : LANES * which + HD]


def stack_four(scal, own, beside, far, last, out):
    z = scal[10]
    turn, upper = lax.rem(z, 2), lax.div(z, 2)
    for piece, parity, pair in (
        (own, turn, upper),
        (beside, 1 - turn, upper),
        (far, turn, 1 - upper),
        (last, 1 - turn, 1 - upper),
    ):
        out[2 * pair + parity] = piece[...]


def finish_residual(scal, own, other, out):
    size, width = own.shape[1:]
    for core, source in ((scal[7], own), (1 - scal[7], other)):
        for shard in range(4):
            rows = pl.ds(pl.multiple_of(2 * size * (shard % 2) + size * core, 16), size)
            columns = slice(width * (shard // 2), width * (shard // 2 + 1))
            out[rows, columns] = source[shard].astype(F32)


def take_piece(scal, a, b, c, d, piece):
    half = piece.shape[0]
    start = pl.multiple_of(48 * scal[7], 16)
    for peer, part in enumerate((a, b, c, d)):

        @pl.when(quarter_of(scal, peer) == 3)
        def _():
            piece[...] = part[pl.ds(start, half), :]


def finish_two(scal, *refs):
    parts = refs[0:8]
    qkv, proj, up, down, pools, memory, gain, full, full_mlp = refs[8:]
    gather_parts(scal, parts, 0, full)
    gather_parts(scal, parts, full.shape[0] // 8, full_mlp)
    width = full.shape[1]
    qkv[...] = full[0:576, :]
    proj[:, :width] = full[576:768, :]
    proj[0:96, width:] = full[768:864, :]
    proj[96:192, width:] = full[960:1056, :]
    up[...] = full_mlp[0:384, :]
    down[...] = full_mlp[384:768, :]
    put_totals(full_mlp, 768, pools, memory)
    gain[0:width], gain[width:] = full_mlp[808, :], full_mlp[809, :]


def finish_one(scal, *refs):
    qkv, proj, table, second_table, pools, memory, gain, second_gain, third_gain, full = refs[8:]
    gather_parts(scal, refs[0:8], 0, full)
    qkv[...] = full[0:288, :]
    proj[...] = full[288:384, :]
    bins = table.shape[1]
    table[...] = full[384:385, :bins]
    second_table[...] = full[385:387, :bins]
    put_totals(full, 400, pools, memory)
    second_gain[...] = full[440, :]
    third_gain[...] = full[441, :]
    gain[...] = full[442, :]


def finish_wide(scal, own_up, other_up, own_down, other_down, up, down):
    first = scal[7] == 0
    size = up.shape[0]
    width = size // 2
    up[:, :width] = pick(first, own_up[...], other_up[...]).astype(F32)
    up[:, width:] = pick(first, other_up[...], own_up[...]).astype(F32)
    one = pick(first, own_down[...], other_down[...]).astype(F32)
    two = pick(first, other_down[...], own_down[...]).astype(F32)
    down[:width, :width], down[:width, width:] = one[:width, :], one[width:, :]
    down[width:, :width], down[width:, width:] = two[:width, :], two[width:, :]


def add_cores(keep, other, *outs):
    for d in range(4):
        for which in range(2):
            spots = slice(104 * (2 * d + which), 104 * (2 * d + which) + outs[d].shape[1])
            outs[d][which] = (keep[spots, :].astype(F32) + other[spots, :].astype(F32)).astype(BF)


def whole_columns(scal, own, other):
    first = scal[7] == 0
    return jnp.concatenate([pick(first, own, other), pick(first, other, own)], axis=1)


def add_both(one, one_other, two, two_other, one_out, two_out):
    one_out[...] = (one[...].astype(F32) + one_other[...].astype(F32)).astype(BF)
    two_out[...] = (two[...].astype(F32) + two_other[...].astype(F32)).astype(BF)


def add_two(one, two, out):
    out[...] = (one[...].astype(F32) + two[...].astype(F32)).astype(BF)


def sum_four(a, b, c, d, out):
    total = (a[...].astype(F32) + b[...].astype(F32)) + (c[...].astype(F32) + d[...].astype(F32))
    out[...] = total.astype(BF)


def back_attend_two(scal, part, other, g, middle, gain, *refs):
    ins, outs = refs[0:10], refs[10:]
    grad, gain_grad = norm_back(whole_columns(scal, part[1], other[1]).astype(F32), middle[...], gain[...])
    middle_grad = jnp.concatenate([g[0], g[1]], axis=1).astype(F32) + grad
    outs[0][...] = middle_grad
    outs[1][...] = gain_grad
    attend_back(1, scal, *ins, middle_grad, *outs[2:7], None, outs[7])


def back_rest_two(scal, part, other, middle, normed, middle_grad, rows, proj_grad, residual_grad, keep, send):
    final = (middle[...] + whole_columns(scal, part[0], other[0]).astype(F32)).astype(BF)
    area = (SIDE // 2) ** 2
    keep[...] = nn(half_rows(scal[1], area), final).astype(BF)
    send[...] = nn(half_rows(1 - scal[1], area), final).astype(BF)
    branch = middle_grad[...].astype(BF)
    width = residual_grad.shape[2]
    for head, (slot, place) in enumerate(heads_of(4, 1)):
        found = tn(rows[head][:, :HD], branch).astype(BF)
        for column in range(2):
            start = 2 * HD * column + HD * place
            proj_grad[slot, start : start + HD, :] = found[:, width * column : width * (column + 1)]
    linear = (0.25 * middle_grad[:, pl.ds(pl.multiple_of(scal[7] * width, LANES), width)]).astype(BF)
    high, low = split(nn(cells(), normed[...]))
    found = (tn(high, linear) + tn(low, linear)).astype(BF)
    size = residual_grad.shape[1]
    turned = scal[1] == 1
    residual_grad[0] = pick(turned, found[size:], found[:size])
    residual_grad[1] = pick(turned, found[:size], found[size:])


def put_small(small, pools_grad, memory_grad):
    small[...] = jnp.zeros(small.shape, F32)
    for field in range(3):
        small[0:27, LANES * field : LANES * (field + 1)] = pools_grad[field, 0:27, :]
    for which in range(2):
        small[32 : 32 + FR, LANES * which : LANES * (which + 1)] = memory_grad[which]


def back_front_two(scal, middle_grad, normed_ref, fields, kp, vp, dq, dk, dv, near, far, wa, wb, residual, pools, memory, proj_grad, residual_grad, gain_grad, part_out, keep, one, two, three, small, pools_grad, memory_grad, full, *work):
    weights = (wa, wb)
    normed = normed_ref[...]
    backs = field_back(4, scal[1], (2, 1, 1), fields, (kp, vp), (dq, dk, dv), near, far, pools, memory, pools_grad, memory_grad, work)
    count = normed.shape[0]
    total = jnp.zeros(normed.shape, F32)
    width = full.shape[2]
    columns = pl.ds(pl.multiple_of(scal[7] * width, LANES), width)
    linear = (0.25 * middle_grad[:, columns]).astype(BF)
    cell = cells()
    for slot in range(2):
        full[slot, 0:576, :] = tn(backs[slot], normed).astype(BF)
        full[slot, 576:864, :] = proj_grad[slot, 0:288, :]
        full[slot, 864:960, :] = residual_grad[slot, 0:96, :]
        full[slot, 960:1056, :] = proj_grad[slot, 288:384, :]
        full[slot, 1056:1152, :] = residual_grad[slot, 96:192, :]
        total = total + nn(backs[slot], weights[slot][...])
    cut(scal, full, (keep, one, two, three))
    high, low = split(nt(linear, residual[:, columns]))
    part_out[0:count, :] = (total + tn(cell, high) + tn(cell, low)).astype(BF)
    put_small(small, pools_grad, memory_grad)
    small[40:41, :] = 0.5 * gain_grad[:, :width]
    small[41:42, :] = 0.5 * gain_grad[:, width:]
    part_out[count:, :] = small[...].astype(BF)


def back_mlp_one(scal, part, other, x, gain, normed_ref, wa, wb, grad_out, part_out, gain_grad_ref, keep, one, two, three, full):
    weights = (wa, wb)
    grad, gain_grad = norm_back(part[: x.shape[0], :].astype(F32) + other[: x.shape[0], :].astype(F32), x[...], gain[...])
    grad_out[...] = grad
    gain_grad_ref[...] = gain_grad
    branch = grad.astype(BF)
    normed = normed_ref[...]
    total = jnp.zeros(part_out.shape, F32)
    whole = (part[x.shape[0] :, :].astype(F32) + other[x.shape[0] :, :].astype(F32)).astype(BF)
    size = normed.shape[1]
    for slot in range(2):
        up, down = weights[slot][:size, :], weights[slot][size:, :]
        value, slope = gelu_parts(nn(normed, up))
        up_low = (nt(branch, down) * slope).astype(BF)
        full[slot, 0:size, :] = tn(normed, up_low).astype(BF)
        full[slot, size : 2 * size, :] = tn(value.astype(BF), branch).astype(BF)
        full[slot, 2 * size : 2 * size + 64, :] = whole
        full[slot, 2 * size + 64 :, :] = jnp.zeros((64, size), BF)
        total = total + nt(up_low, up)
    part_out[...] = total.astype(BF)
    cut(scal, full, (keep, one, two, three))


def back_attend_one(scal, part, other, g, middle, gain, *refs):
    ins, outs = refs[0:10], refs[10:]
    grad, gain_grad = norm_back(part[...].astype(F32) + other[...].astype(F32), middle[...], gain[...])
    middle_grad = g[...] + grad
    outs[0][...] = middle_grad
    outs[1][...] = gain_grad
    attend_back(0, scal, *ins, middle_grad, *outs[2:9])


def back_front_one(scal, normed_ref, fields, kp, vp, dq, dk, dv, near, far, wa, wb, pools, memory, gain_two_grad, gain_three_grad, qkv_grad, part_out, small, pools_grad, memory_grad, *work):
    weights = (wa, wb)
    normed = normed_ref[...]
    backs = field_back(2, scal[1], (1, 2, 2), fields, (kp, vp), (dq, dk, dv), near, far, pools, memory, pools_grad, memory_grad, work)
    count = normed.shape[0]
    total = jnp.zeros(normed.shape, F32)
    for slot in range(2):
        qkv_grad[slot] = tn(backs[slot], normed).astype(BF)
        total = total + nn(backs[slot], weights[slot][: 3 * HD, :])
    part_out[0:count, :] = total.astype(BF)
    put_small(small, pools_grad, memory_grad)
    small[40:41, :] = 0.5 * gain_two_grad[...]
    small[41:42, :] = 0.5 * gain_three_grad[...]
    part_out[count:, :] = small[...].astype(BF)


def back_tokens(scal, part, other, x, gain, middle_grad, qkv_grad, proj_grad, table_one, table_two, keep_rows, send_rows, keep, one, two, three, full):
    grad, gain_grad = norm_back(part[: x.shape[0], :].astype(F32) + other[: x.shape[0], :].astype(F32), x[...].astype(F32), gain[...])
    rows = (middle_grad[...] + grad).astype(BF)
    turn = scal[1]
    keep_rows[...] = nn(half_rows(turn, SIDE * SIDE), rows).astype(BF)
    send_rows[...] = nn(half_rows(1 - turn, SIDE * SIDE), rows).astype(BF)
    line = iota((64, 1), 0)
    whole = jnp.where(
        line == 42, gain_grad, part[x.shape[0] :, :].astype(F32) + other[x.shape[0] :, :].astype(F32)
    ).astype(BF)
    for slot in range(2):
        full[slot, 0:288, :] = qkv_grad[slot]
        full[slot, 288:384, :] = proj_grad[slot]
        lines = jnp.concatenate([table_one[slot : slot + 1, :], table_two[2 * slot : 2 * slot + 2, :], jnp.zeros((13, LANES), F32)], axis=0)
        full[slot, 384:400, :] = jnp.concatenate([lines, jnp.zeros((16, 2 * LANES), F32)], axis=1).astype(BF)
        full[slot, 400:464, :] = whole
        full[slot, 464:512, :] = jnp.zeros((48, full.shape[2]), BF)
    cut(scal, full, (keep, one, two, three))


def scalars(pairs, other_pairs, videos, out):
    plane, core, head = lax.axis_index("plane"), lax.axis_index("core"), lax.axis_index("head")
    upper, turn = lax.div(head, 2), lax.rem(head, 2)
    clip = 4 * plane + 2 * turn + upper
    match = core == turn
    own = videos[clip]
    out[0] = jnp.where(match, 1, 0)
    out[1] = turn
    for j in range(2):
        before = clip - 1 - j
        there = (before >= 0) & (videos[jnp.maximum(before, 0)] == own)
        out[2 + j] = jnp.where(there, 1, 0)
        out[4 + j] = jnp.where(match, pairs[upper, j], other_pairs[upper, j])
    out[6] = jnp.where(upper == core, 1, 0)
    out[7] = core
    out[8] = lax.rem(plane, 2)
    out[9] = lax.rem(lax.div(plane, 2), 2)
    out[10] = head


def pack(tokens, grad_out, table_one, table_two, qkv_one, proj_one, rows, first):
    count, width = tokens.shape
    area = grad_out.shape[0]
    rows[0:count, :] = tokens[...]
    rows[count : count + area, :] = grad_out[:, :width]
    rows[count + area :, :] = grad_out[:, width:]
    lines = []
    for table in (table_one[0:1, :], table_two[0:1, :], table_two[1:2, :]):
        high = table.astype(BF).astype(F32)
        middle = (table - high).astype(BF).astype(F32)
        lines += [high, middle, table - high - middle]
    first[0 : 3 * HD, :] = qkv_one[...]
    first[3 * HD : 4 * HD, :] = proj_one[...]
    stacked = jnp.concatenate(lines + [jnp.zeros((7, lines[0].shape[1]), F32)], axis=0)
    first[4 * HD :, :] = jnp.concatenate([stacked, jnp.zeros((16, width - stacked.shape[1]), F32)], axis=1).astype(BF)


def join(one, two, first, second, third, out):
    out[0 : one.shape[0], :] = one[...]
    out[one.shape[0] :, :] = two[...]


SMEM = pl.BlockSpec(memory_space=pltpu.SMEM)


FAR = pl.BlockSpec(memory_space=pltpu.HBM)
NEAR = pl.BlockSpec(memory_space=pltpu.VMEM)


def moved(body, counts, left, early, late, *refs):
    ins_count, outs_count, work_count = counts
    ins, outs = list(refs[:ins_count]), refs[ins_count : ins_count + outs_count]
    spot = ins_count + outs_count
    saved = refs[spot : spot + len(early) + len(late)]
    spot += len(early) + len(late)
    work = refs[spot : spot + work_count]
    buffers, arrived = refs[spot + work_count : -1], refs[-1]
    brought = [pltpu.make_async_copy(ins[item], buffers[i], arrived.at[i]) for i, item in enumerate(left)]
    first = len(left)
    sent = [pltpu.make_async_copy(ins[item], saved[i], arrived.at[first + i]) for i, item in enumerate(early)]
    for copy in brought + sent:
        copy.start()
    for i, item in enumerate(left):
        brought[i].wait()
        ins[item] = buffers[i]
    body(*ins, *outs, *work)
    first += len(early)
    last = [
        pltpu.make_async_copy(outs[item], saved[len(early) + i], arrived.at[first + i]) for i, item in enumerate(late)
    ]
    for copy in last:
        copy.start()
    for copy in sent + last:
        copy.wait()


def kernel(body, name, outs, ins, work=(), left=(), early=(), late=(), raw=(), far_outs=(), limit=16, flops=2 * 10**8):
    if limit == 16 and (left or early or late):
        found = kernel(body, name, outs, ins, work, (), (), (), raw, far_outs)
        return (*found, *[list(ins)[item] for item in early], *[found[item] for item in late])
    ins = list(ins)
    in_specs = []
    for number, item in enumerate(ins):
        if number == 0 and item.dtype == jnp.int32:
            in_specs.append(SMEM)
        else:
            in_specs.append(FAR if number in left or number in raw else NEAR)
    results = [jax.ShapeDtypeStruct(shape, kind) for shape, kind in outs]
    extra = [jax.ShapeDtypeStruct(ins[item].shape, ins[item].dtype) for item in early] + [results[item] for item in late]
    size = sum(int(np.prod(item.shape)) * item.dtype.itemsize for item in [*ins, *results, *extra])
    work = list(work)
    count = len(work)
    if left or early or late:
        body = functools.partial(moved, body, (len(ins), len(results), count), tuple(left), tuple(early), tuple(late))
        work += [pltpu.VMEM(ins[number].shape, ins[number].dtype) for number in left]
        work.append(pltpu.SemaphoreType.DMA((len(left) + len(early) + len(late),)))
    return pl.pallas_call(
        body,
        out_shape=tuple(results + extra),
        in_specs=in_specs,
        out_specs=tuple([FAR if number in far_outs else NEAR for number in range(len(results))] + [FAR] * len(extra)),
        scratch_shapes=work,
        name=name,
        cost_estimate=pl.CostEstimate(flops=flops, bytes_accessed=size, transcendentals=0),
        compiler_params=pltpu.CompilerParams(vmem_limit_bytes=limit << 20),
    )(*ins)


def scratch(*rows):
    return [pltpu.VMEM((count, LANES), F32) for count in rows]


def field_work(heads):
    groups = 3 * heads // 2
    return [pltpu.VMEM((groups, PADDED, LANES), F32), pltpu.SemaphoreType.DMA((groups,))]


FRONT_WORK = (216, 800)
BACK_WORK = (216, 800, PADDED, 216, 400)


def after(values, events):
    return lax.optimization_barrier((values, events))


def swap(values):
    return lax.ppermute(values, "core", [(0, 1), (1, 0)])


def cross_route():
    route = []
    for core in range(2):
        low, other = 2 * core, 2 - 2 * core
        route += [(core * 4 + low + i, core * 4 + other + i) for i in range(2)]
    return route


def beside(values):
    return lax.ppermute(values, "head", [(z, z ^ 1) for z in range(4)])


def choose(scal, own, other, out):
    out[...] = pick(scal[6] == 1, own[...], other[...])


def choose_half(sizes, scal, own, other, out):
    start, put = 0, 0
    for size in sizes:
        half = size // 2
        spots = pl.ds(pl.multiple_of(start + half * scal[7], 16), half)
        out[put : put + half, :] = pick(scal[6] == 1, own[spots, :], other[spots, :])
        start, put = start + size, put + half


def chosen(scal, own, other):
    return kernel(choose, "choose_shard", [(own.shape, own.dtype)], [scal, own, other])[0]


def over(values, scal):
    return chosen(scal, values, lax.ppermute(values, ("core", "head"), cross_route()))


def spread(values, scal):
    one = over(values, scal)
    return one, beside(one)


def reverse(route):
    return [(end, start) for start, end in route]


def clip_routes(planes, distance):
    def place(clip):
        slot = clip % 4
        return (clip // 4) * 4 + 2 * (slot % 2) + slot // 2

    total = 4 * planes
    return [(place(clip), place(clip + distance)) for clip in range(total) if 0 <= clip + distance < total]


def half_routes():
    def place(core, a, b):
        return core * 4 + 2 * a + b

    one, two, three = [], [], []
    for a in range(2):
        for b in range(2):
            one += [(place(b, a, b), place(1 - b, a, b)), (place(1 - b, a, b), place(1 - b, a, 1 - b))]
            two += [(place(1 - b, a, b), place(b, a, 1 - b))]
            three += [(place(1 - b, a, b), place(b, a, 1 - b))]
    return one, two, three


def turn_by(values, distance):
    return lax.ppermute(values, "head", [(z, (z + distance) % 4) for z in range(4)])


def local(
    planes,
    tokens,
    grad_out,
    video_ids,
    offsets,
    gain_one,
    qkv_one,
    pools_one,
    memory_one,
    table_one,
    proj_one,
    gain_two,
    up_one,
    down_one,
    gain_three,
    qkv_two,
    residual_two,
    pools_two,
    memory_two,
    table_two,
    proj_two,
    gain_four,
    up_two,
    down_two,
):
    match = lax.axis_index("core") == lax.axis_index("head") % 2
    (scal,) = pl.pallas_call(
        scalars,
        out_shape=(jax.ShapeDtypeStruct((16,), jnp.int32),),
        in_specs=[SMEM] * 3,
        out_specs=(SMEM,),
        name="scalars",
    )(offsets, swap(offsets), video_ids)
    gains = [item.reshape(1, -1) for item in (gain_one, gain_two, gain_three, gain_four)]

    half = residual_two.shape[1] // 2
    qkv_one_t, qkv_two_t = qkv_one.T, qkv_two.T
    rows_in, first_bundle = kernel(
        pack,
        "pack",
        [((300, half), BF), ((400, half), BF)],
        [tokens, grad_out, table_one, table_two, qkv_one_t, proj_one],
        left=range(6),
        limit=56,
    )
    route_one, route_two, route_three = half_routes()
    axes = ("core", "head")
    first_over = over(first_bundle, scal)
    first_all = (first_over, beside(first_over))
    tok_one, tok_two = lax.ppermute(rows_in, axes, route_one), lax.ppermute(rows_in, axes, route_two)
    (mlp_bundle,) = kernel(
        join, "join", [((768, half), BF)], [up_one, down_one, first_over, tok_one, tok_two], left=(0, 1), limit=48
    )
    mlp_over = over(mlp_bundle, scal)

    width = qkv_one.shape[0]
    wide = residual_two.shape[1]
    n1, n2 = FR * SIDE * SIDE, FR * SIDE * SIDE // 4
    a1, a2 = n2 // FR, n1 // FR

    x1, _, g, fields1, qp1, kp1, vp1, passed1, *saved = kernel(
        front_one,
        "front_one",
        [
            ((n1, width), BF),
            ((n1, width), BF),
            ((2, n2, half), BF),
            ((3, PADDED, LANES), F32),
            ((2, n1, LANES), F32),
            ((2, n2, LANES), F32),
            ((2, n2, LANES), F32),
            ((2, a1, 2 * HD), BF),
        ],
        [scal, rows_in, tok_one, tok_two, gains[0], *first_all, pools_one, memory_one],
        scratch(*FRONT_WORK) + field_work(2),
        early=(5, 6),
        late=(0, 1, 2, 4, 5, 6),
        far_outs=(3,),
    )
    first_kept, (x1_kept, normed1, g_kept, qp1_kept, kp1_kept, vp1_kept) = saved[:2], saved[2:]
    places = ("plane", "head")
    near1 = lax.ppermute(passed1, places, clip_routes(planes, 1))
    far1 = lax.ppermute(passed1, places, clip_routes(planes, 2))
    (mlp_over, late_qkv), (x1,) = after((mlp_over, qkv_two_t), (x1,))
    mlp_all = (mlp_over, beside(mlp_over))
    qkv_two_all = spread(late_qkv, scal)
    attn1_ins = [*first_all, qp1, kp1, vp1, near1, far1, *first_all]
    _, part1, near1_kept, far1_kept, rows1 = kernel(
        functools.partial(attend, 0),
        "attend_one",
        [((2, n1, LANES), BF), ((n1, width), BF)],
        [scal, *attn1_ins],
        early=(6, 7),
        late=(0,),
    )
    middle1, _, part_mlp1, *mlp_kept, middle1_kept, mlp_normed1 = kernel(
        mlp_one,
        "mlp_one",
        [((n1, width), F32), ((n1, width), BF), ((n1, width), BF)],
        [scal, x1, part1, swap(part1), gains[1], *mlp_all],
        early=(5, 6),
        late=(0, 1),
    )
    late_proj, (part_mlp1,) = after(proj_two, (part_mlp1,))
    proj_two_all = spread(late_proj, scal)
    _, _, fields2, qp2, kp2, vp2, passed2, *saved = kernel(
        front_two,
        "front_two",
        [
            ((n1, width), F32),
            ((n1, width), BF),
            ((6, PADDED, LANES), F32),
            ((4, n2, LANES), F32),
            ((4, n1, LANES), F32),
            ((4, n1, LANES), F32),
            ((2, a2, 4 * HD), BF),
        ],
        [scal, middle1, part_mlp1, swap(part_mlp1), gains[2], *qkv_two_all, pools_two, memory_two],
        scratch(*FRONT_WORK) + field_work(4),
        early=(5, 6),
        late=(0, 1, 3, 4, 5),
        far_outs=(2,),
    )
    qkv_two_kept, (x2, normed2, qp2_kept, kp2_kept, vp2_kept) = saved[:2], saved[2:]
    (skip,) = kernel(skip_two, "skip_two", [((n2, wide), F32)], [normed2, residual_two])
    near2 = lax.ppermute(passed2, places, clip_routes(planes, 1))
    far2 = lax.ppermute(passed2, places, clip_routes(planes, 2))
    attn2_ins = [*first_kept, qp2, kp2, vp2, near2, far2, *proj_two_all]
    _, part2, near2_kept, far2_kept, *proj_two_kept, rows2 = kernel(
        functools.partial(attend, 1),
        "attend_two",
        [((4, n2, LANES), BF), ((n2, wide), BF)],
        [scal, *attn2_ins],
        left=(1, 2),
        early=(6, 7, 8, 9),
        late=(0,),
    )
    _, mlp_normed2, own_half, middle2 = kernel(
        middle_two,
        "middle_two",
        [((n2, wide), F32), ((n2, wide), BF), ((2, n2, half), BF)],
        [scal, skip, part2, swap(part2), gains[3], g_kept],
        left=(5,),
        late=(0,),
    )
    halves = [turn_by(own_half, d) for d in (1, 2, 3)]
    found = kernel(
        mlp_rows,
        "mlp_rows",
        [((832, half), BF)] * 2 + [((4, n2, half), BF)] * 2 + [((4, 2, n2, wide), BF)],
        [scal, mlp_normed2, g_kept, *halves, *(swap(item) for item in halves), up_two, down_two],
        [pltpu.VMEM((2, n2, wide), F32)],
    )
    wide_grads = kernel(mlp_sums, "mlp_sums", [((wide, half), BF)] * 2, found[2:5])
    sums = kernel(add_cores, "add_cores", [((2, n2, half), BF)] * 4, [found[0], swap(found[1])])
    sums = [sums[0]] + [turn_by(sums[d], -d) for d in (1, 2, 3)]
    def across(values, bit):
        return lax.ppermute(values, "plane", [(i, i ^ bit) for i in range(planes)])

    def peers(parts):
        return [parts[0]] + [across(parts[peer], peer) for peer in (1, 2, 3)]

    def add_wide(pair, bits):
        received = [across(item, bit) for item, bit in zip(pair, bits)]
        return kernel(add_both, "add_wide", [((wide, half), BF)] * 2, [pair[0], received[0], pair[1], received[1]])

    wide_sum = add_wide(wide_grads, (1, 2))
    (row_sum,) = kernel(sum_four, "sum_rows", [((2, n2, half), BF)], sums)
    row_sum, (wide_sum,) = after(row_sum, (wide_sum,))
    row_other = swap(row_sum)
    middle_grad2, gain_four_grad, dq2, dk2, dv2, d_near2, d_far2, table_two_grad = kernel(
        back_attend_two,
        "back_attend_two",
        [
            ((n2, wide), F32),
            ((1, wide), F32),
            ((4, n2, LANES), F32),
            ((4, n1, LANES), F32),
            ((4, n1, LANES), F32),
            ((2, a2, 4 * HD), BF),
            ((2, a2, 4 * HD), BF),
            ((4, LANES), F32),
        ],
        [
            scal, row_sum, row_other, g_kept, middle2, gains[3],
            *first_kept, qp2_kept, kp2_kept, vp2_kept, near2_kept, far2_kept, *proj_two_kept, rows2,
        ],
    )
    proj_two_grad, residual_grad, keep, send = kernel(
        back_rest_two,
        "back_rest_two",
        [((2, 4 * HD, width), BF), ((2, 192, half), BF), ((n2 // 2, wide), BF), ((n2 // 2, wide), BF)],
        [scal, row_sum, row_other, middle2, normed2, middle_grad2, rows2],
    )
    near_grad2 = lax.ppermute(d_near2, places, clip_routes(planes, -1))
    far_grad2 = lax.ppermute(d_far2, places, clip_routes(planes, -2))

    wide_sum = add_wide(wide_sum, (2, 1))
    (near_grad2, far_grad2), (wide_sum,) = after((near_grad2, far_grad2), (wide_sum,))
    part_back2, *sends2, _, _, _ = kernel(
        back_front_two,
        "back_front_two",
        [
            ((n1 + 64, width), BF),
            *[((2, 288, width), BF)] * 4,
            ((64, width), F32),
            ((3, 32, LANES), F32),
            ((2, FR, LANES), F32),
        ],
        [
            scal, middle_grad2, normed2, fields2, kp2_kept, vp2_kept, dq2, dk2, dv2, near_grad2, far_grad2,
            *qkv_two_kept, residual_two, pools_two, memory_two, proj_two_grad, residual_grad, gain_four_grad,
        ],
        [pltpu.VMEM((2, 1152, width), BF)] + scratch(*BACK_WORK) + field_work(4),
        [2, 4, 5, 11, 12, 13],
        raw=[3],
    )
    received2 = peers(sends2)
    grad1, part_mlp_back, gain_three_grad, *sends_mlp = kernel(
        back_mlp_one,
        "back_mlp_one",
        [((n1, width), F32), ((n1, width), BF), ((1, width), F32)] + [((2, 224, width), BF)] * 4,
        [scal, part_back2, swap(part_back2), x2, gains[2], mlp_normed1, *mlp_kept],
        [pltpu.VMEM((2, 896, width), BF)],
        [3, 5, 6, 7],
    )
    middle_grad1, gain_two_grad, dq1, dk1, dv1, d_near1, d_far1, proj_one_grad, table_one_grad = kernel(
        back_attend_one,
        "back_attend_one",
        [
            ((n1, width), F32),
            ((1, width), F32),
            ((2, n1, LANES), F32),
            ((2, n2, LANES), F32),
            ((2, n2, LANES), F32),
            ((2, a1, 2 * HD), BF),
            ((2, a1, 2 * HD), BF),
            ((2, HD, width), BF),
            ((2, LANES), F32),
        ],
        [
            scal, part_mlp_back, swap(part_mlp_back), grad1, middle1_kept, gains[1],
            *first_kept, qp1_kept, kp1_kept, vp1_kept, near1_kept, far1_kept, *first_kept, rows1,
        ],
        left=[4, *range(6, 16)],
    )
    near_grad1 = lax.ppermute(d_near1, places, clip_routes(planes, -1))
    far_grad1 = lax.ppermute(d_far1, places, clip_routes(planes, -2))
    bit = 4
    while bit < planes:
        wide_sum = add_wide(wide_sum, (bit, bit))
        bit *= 2
    received_mlp = peers(sends_mlp)
    rows_received = lax.ppermute(send, axes, route_three)
    (near_grad1, far_grad1), (wide_sum, received2) = after(
        (near_grad1, far_grad1), (wide_sum, received2)
    )
    qkv_one_grad, part_back1, _, _, _ = kernel(
        back_front_one,
        "back_front_one",
        [((2, 3 * HD, width), BF), ((n1 + 64, width), BF), ((64, width), F32), ((3, 32, LANES), F32), ((2, FR, LANES), F32)],
        [
            scal, normed1, fields1, kp1_kept, vp1_kept, dq1, dk1, dv1, near_grad1, far_grad1,
            *first_kept, pools_one, memory_one, gain_two_grad, gain_three_grad,
        ],
        scratch(*BACK_WORK) + field_work(2),
        [1, 3, 4, 10, 11],
        raw=[2],
    )
    part_back1, (received_mlp,) = after(part_back1, (received_mlp,))
    tok_keep, tok_send, *sends1 = kernel(
        back_tokens,
        "back_tokens",
        [((n1 // 2, width), BF), ((n1 // 2, width), BF)] + [((2, 128, width), BF)] * 4,
        [
            scal, part_back1, swap(part_back1), x1_kept, gains[0], middle_grad1, qkv_one_grad, proj_one_grad,
            table_one_grad, table_two_grad,
        ],
        [pltpu.VMEM((2, 512, width), BF)],
        [3],
    )
    tok_received = lax.ppermute(tok_send, axes, route_three)

    def combine(body, label, rows, ins, count=1):
        return kernel(body, label, [((rows, width), BF)] * count, ins)

    back_route = reverse(cross_route())
    received1 = peers(sends1)
    rows_two, rows_mlp, rows_one = 288, 224, 128
    one2, two2 = combine(sum_planes, "sum_planes_two", rows_two + rows_mlp, received2 + received_mlp, 2)
    beside2 = beside(two2)
    up_two_sum, down_two_sum = kernel(
        finish_wide, "finish_wide", [((wide, wide), F32), ((wide, wide), F32)], [scal, wide_sum[0], swap(wide_sum[0]), wide_sum[1], swap(wide_sum[1])]
    )
    received1, (up_two_sum, down_two_sum) = after(received1, (up_two_sum, down_two_sum))
    one1, two1 = combine(sum_planes, "sum_planes_one", rows_one, received1, 2)
    beside1 = beside(two1)
    (beside2,), (one1, tok_received, rows_received) = after((beside2,), (one1, tok_received, rows_received))
    tokens_grad = jnp.where(match, tok_keep, tok_received)
    (total2,) = combine(add_two, "add_pair_two", rows_two + rows_mlp, [one2, beside2])
    cross2 = lax.ppermute(total2, axes, back_route)
    (beside1,), (total2,) = after((beside1,), (total2,))
    (total1,) = combine(add_two, "add_pair_one", rows_one, [one1, beside1])
    cross1 = lax.ppermute(total1, axes, back_route)
    (cross2,), (cross1,) = after((cross2,), (cross1,))
    (total2,) = combine(add_two, "add_cross_two", rows_two + rows_mlp, [total2, cross2])
    bit = 4
    while bit < planes:
        (total2,) = combine(add_two, "add_planes_two", rows_two + rows_mlp, [total2, across(total2, bit)])
        bit *= 2

    def halves_of(total, sizes):
        body = functools.partial(choose_half, sizes)
        return combine(body, "choose_half", sum(sizes) // 2, [scal, total, swap(total)])

    half2 = halves_of(total2, (rows_two, rows_mlp))
    (total1,) = combine(add_two, "add_cross_one", rows_one, [total1, cross1])
    bit = 4
    while bit < planes:
        (total1,) = combine(add_two, "add_planes_one", rows_one, [total1, across(total1, bit)])
        bit *= 2
    parts2 = peers(list(half2) * 4)
    parts1 = peers(halves_of(total1, (rows_one,)) * 4)
    parts2, parts1 = after(parts2, parts1)
    (piece,) = kernel(take_piece, "take_piece", [((96, width), BF)], [scal, *parts2])
    small_shapes = [(pools_one.shape, F32), (memory_one.shape, F32)]
    qkv_two_sum, proj_two_sum, up_one_sum, down_one_sum, pools_two_sum, memory_two_sum, gain_four_sum = kernel(
        finish_two,
        "finish_two",
        [(qkv_two_t.shape, F32), (proj_two.shape, F32), (up_one.shape, F32), (down_one.shape, F32)]
        + small_shapes
        + [((wide,), F32)],
        [scal, *parts2, *(swap(part) for part in parts2)],
        [pltpu.VMEM((1152, width), F32), pltpu.VMEM((896, width), F32)],
    )
    (qkv_one_sum, proj_one_sum, table_one_sum, table_two_sum, pools_one_sum, memory_one_sum, *gain_sums) = kernel(
        finish_one,
        "finish_one",
        [(qkv_one_t.shape, F32), (proj_one.shape, F32), (table_one.shape, F32), (table_two.shape, F32)]
        + small_shapes
        + [((width,), F32)] * 3,
        [scal, *parts1, *(swap(part) for part in parts1)],
        [pltpu.VMEM((512, width), F32)],
    )
    others = [lax.ppermute(piece, "head", [(z, z ^ bit) for z in range(4)]) for bit in (1, 2, 3)]
    blocks_out, tokens_out = jnp.where(match, keep, rows_received), tokens_grad
    others, (gain_four_sum, first_gain, blocks_out, tokens_out) = after(
        others, (gain_four_sum, gain_sums[0], blocks_out, tokens_out)
    )
    (pieces,) = kernel(stack_four, "stack_pieces", [((4, 96, width), BF)], [scal, piece, *others])
    (residual_sum,) = kernel(
        finish_residual, "finish_residual", [(residual_two.shape, F32)], [scal, pieces, swap(pieces)]
    )

    return (
        blocks_out,
        tokens_out,
        first_gain,
        qkv_one_sum.T,
        pools_one_sum,
        memory_one_sum,
        table_one_sum,
        proj_one_sum,
        gain_sums[1],
        up_one_sum,
        down_one_sum,
        gain_sums[2],
        qkv_two_sum.T,
        residual_sum,
        pools_two_sum,
        memory_two_sum,
        table_two_sum,
        proj_two_sum,
        gain_four_sum,
        up_two_sum,
        down_two_sum,
    )


def solution(mesh):
    planes = mesh.shape["dp"] // 2
    fine = Mesh(mesh.devices.reshape(planes, 2, mesh.shape["head"]), ("plane", "core", "head"))
    dp = ("plane", "core")
    rows = P(("plane", "core", "head"), None)
    columns, lines, free = P(None, "head"), P("head", None), P()
    in_specs = (
        rows, rows, free, P(dp, None),
        free, columns, free, free, lines, lines, free, columns, lines,
        free, columns, free, free, free, lines, lines, free, columns, lines,
    )
    out_specs = (
        rows, rows,
        free, columns, free, free, lines, lines, free, columns, lines,
        free, columns, free, free, free, lines, lines, free, columns, lines,
    )
    return jax.shard_map(
        functools.partial(local, planes), mesh=fine, in_specs=in_specs, out_specs=out_specs, check_vma=False
    )
```
